32 devices in a mesh: rep: 4 (over y, core), exp: 8 (over z, x).
Axes of the slice: x: 2, y: 2, z: 4, core: 2. Of those that a mesh axis runs over, the one named last changes fastest.
Arguments:
- tokens: bfloat16 [8192, 1024], P(('rep', 'exp')), may hold values from -6 to 6
- cotangent: bfloat16 [8192, 1024], P(('rep', 'exp')), may hold values from -6 to 6
- doc_lengths: int32 [32, 4], P(('rep', 'exp')), may hold values from 1 to 128, 256 in all within a row
- expert_of_token: int32 [8192], P(('rep', 'exp')), may hold values from 0 to 3, as said below
- w_query: bfloat16 [1024, 1024], P('exp'), may hold values from -0.25 to 0.25
- w_key: bfloat16 [1024, 1024], P('exp'), may hold values from -0.25 to 0.25
- w_value: bfloat16 [1024, 1024], P('exp'), may hold values from -0.1875 to 0.1875
- w_output: bfloat16 [1024, 1024], P('exp'), may hold values from -0.75 to 0.75
- attn_gain: bfloat16 [1024], P('exp'), may hold values from 0.25 to 1.75
- w_inner: bfloat16 [8, 1024, 4096], P('exp', 'rep'), may hold values from -0.1875 to 0.1875
- w_outer: bfloat16 [8, 4096, 1024], P('exp', 'rep'), may hold values from -0.125 to 0.125
- expert_gain: bfloat16 [8, 1024], P('exp', 'rep'), may hold values from 0.25 to 1.75
- centroids: bfloat16 [8, 512], P('exp', 'rep'), may hold values from -0.08984375 to 0.08984375
Outputs:
- output: bfloat16 [8192, 1024], P(('rep', 'exp'))
- grad_tokens: float32 [8192, 1024], P(('rep', 'exp'))
- grad_w_query: float32 [1024, 1024], P('exp')
- grad_w_key: float32 [1024, 1024], P('exp')
- grad_w_value: float32 [1024, 1024], P('exp')
- grad_w_output: float32 [1024, 1024], P('exp')
- grad_attn_gain: float32 [1024], P('exp')
- grad_w_inner: float32 [8, 1024, 4096], P('exp', 'rep')
- grad_w_outer: float32 [8, 4096, 1024], P('exp', 'rep')
- grad_expert_gain: float32 [8, 1024], P('exp', 'rep')
- grad_centroids: float32 [8, 512], P('exp', 'rep')
The draws below stay inside these ranges and needn't reach their ends.
Inputs may be any that keep to these rules, and one draw needn't show every extreme that they name: `expert_of_token`: among the tokens of one device every expert is named an even number of times, at most 96, and in every index of rep some device names some expert exactly 2 * 48 times; the devices of one index of rep name every expert exactly 2 * 256 times in all.
All inputs are finite; a program needn't handle non-finite values.
Results may differ from the reference program's by a relative error of at most 0.015.
Values may be sent and summed in bfloat16 or wider, within the bound.
A program may use at most 320 MiB of HBM per device.

```python
import math
import jax
import jax.numpy as jnp
import numpy as np
from jax import lax

D = 1024
HEADS = 16
HEAD_DIM = 64
FF = 4096
TOK_DEV = 256
DOCS = 4
EXPERTS = 4
SEQS = 32
TOKENS = 8192


def group_loads(group_key):
    first_key, second_key, third_key = jax.random.split(group_key, 3)
    expert_total = EXPERTS
    mean_load = TOK_DEV // EXPERTS
    quarter_load = mean_load // 4
    pair_sizes = jax.random.randint(first_key, (expert_total // 2,), 0, quarter_load + 1).astype(jnp.int32)
    pair_sizes = pair_sizes.at[0].set(quarter_load)
    signed_sizes = jnp.concatenate([2 * pair_sizes, -2 * pair_sizes])
    sorting = jax.random.permutation(second_key, expert_total)
    offsets = jnp.zeros((expert_total,), jnp.int32).at[sorting].set(signed_sizes)
    column_perm = jax.random.permutation(third_key, expert_total)
    source_ids = jnp.arange(2 * expert_total)[:, None]
    return mean_load + offsets[(column_perm[None, :] - source_ids) % expert_total]


def draw_expert_of_token(key, part):
    group_total = TOKENS // (TOK_DEV * 2 * EXPERTS)
    device_total = group_total * 2 * EXPERTS
    loads = jax.vmap(group_loads)(jax.random.split(key, group_total)).reshape(device_total, EXPERTS)
    positions = jnp.arange(TOK_DEV, dtype=jnp.int32)

    def device_row(device_key, load_row):
        bounds = jnp.cumsum(load_row)
        expert_ids = jnp.sum((positions[:, None] >= bounds[None, :]).astype(jnp.int32), axis=1)
        return jax.random.permutation(device_key, expert_ids)
    device_keys = jax.random.split(jax.random.fold_in(key, 11), device_total)
    return jax.vmap(device_row)(device_keys, loads).reshape(TOKENS).astype(jnp.int32)


def level_of(rng, extent, shards, smallest, high):
    level = 1.0
    for axis_at, parts in shards:
        heights = jax.random.uniform(jax.random.fold_in(jax.random.fold_in(rng, 6), axis_at), (parts,), jnp.float32, smallest / len(shards), high / len(shards))
        level = level * jnp.repeat(jnp.exp(heights), extent[axis_at] // parts).reshape((-1,) + (1,) * (len(extent) - 1 - axis_at))
    return level


def profile(number_of, total, most, lean):
    portions = [(1 << 20) // math.isqrt(grade ** lean) + 1 for grade in range(2, number_of + 1)]
    spare, given = total - most - (number_of - 1), [1] * (number_of - 1)
    while spare > 0:
        candidates = [i for i in range(number_of - 1) if given[i] < most]
        whole, remaining = sum([portions[i] for i in candidates]), spare
        for i in candidates:
            more = min(most - given[i], max(1, remaining * portions[i] // whole), spare)
            given[i] = given[i] + more
            spare = spare - more
    return np.array([most] + given)


def uneven_parts(rng, number_of, total, limit, slope):
    if number_of == 2:
        one = jax.random.randint(rng, (), max(1, total - limit), min(limit, total - 1) + 1)
        return jnp.stack([one, total - one])
    sizes = jnp.asarray(profile(number_of, total, limit, slope), jnp.int32)
    couples = (number_of - 1) // 2
    giver, sink = sizes[1:1 + 2 * couples:2], sizes[2:2 + 2 * couples:2]
    slack = jnp.minimum(giver - 1, limit - sink)
    moved = jax.random.randint(jax.random.fold_in(rng, 1), (couples,), 0, 1 << 20) % (slack + 1)
    sizes = sizes.at[1:1 + 2 * couples:2].set(giver - moved).at[2:2 + 2 * couples:2].set(sink + moved)
    return sizes[jax.random.permutation(jax.random.fold_in(rng, 2), number_of)]


def gaussian(stream_key, dims, spread, reach, cuts=(), kind=jnp.bfloat16):
    entries = spread * jax.random.normal(stream_key, dims, jnp.float32)
    if cuts:
        entries = entries * level_of(stream_key, dims, cuts, -0.22, 0.18)
    return jnp.clip(entries, -reach, reach).astype(kind)


def setup_inputs(seed: int = 0) -> dict:
    arg_keys = jax.random.split(jax.random.key(seed), 14)
    tokens = gaussian(arg_keys[0], (TOKENS, D), 1.0, 6.0, ((0, 32),))
    cotangent = gaussian(arg_keys[1], (TOKENS, D), 1.0, 6.0, ((0, 32),))
    doc_lengths = jax.vmap(lambda own: uneven_parts(own, DOCS, TOK_DEV, TOK_DEV // 2, 2))(jax.random.split(arg_keys[2], SEQS)).reshape((SEQS, DOCS)).astype(jnp.int32)
    expert_of_token = draw_expert_of_token(jax.random.fold_in(arg_keys[13], 71), 0)
    w_query = gaussian(arg_keys[4], (D, D), (D // 2) ** -0.5, 0.25, ((0, 8),))
    w_key = gaussian(arg_keys[5], (D, D), (D // 2) ** -0.5, 0.25, ((0, 8),))
    w_value = gaussian(arg_keys[6], (D, D), D ** -0.5, 0.1875, ((0, 8),))
    w_output = gaussian(arg_keys[7], (D, D), (D // 16) ** -0.5, 0.75, ((0, 8),))
    attn_gain = jnp.clip(1.0 + 0.15 * jax.random.normal(arg_keys[8], (D,), jnp.float32), 0.25, 1.75).astype(jnp.bfloat16)
    w_inner = gaussian(arg_keys[9], (2 * EXPERTS, D, FF), D ** -0.5, 0.1875, ((0, 8), (1, 4)))
    w_outer = gaussian(arg_keys[10], (2 * EXPERTS, FF, D), (FF // 2) ** -0.5, 0.125, ((0, 8), (1, 4)))
    expert_gain = jnp.clip(1.0 + 0.15 * jax.random.normal(arg_keys[11], (2 * EXPERTS, D), jnp.float32), 0.25, 1.75).astype(jnp.bfloat16)
    centroids = gaussian(arg_keys[12], (2 * EXPERTS, D // 2), 0.015, 0.08984375, ((0, 8), (1, 4)))
    return dict(tokens=tokens, cotangent=cotangent, doc_lengths=doc_lengths, expert_of_token=expert_of_token, w_query=w_query, w_key=w_key, w_value=w_value, w_output=w_output, attn_gain=attn_gain, w_inner=w_inner, w_outer=w_outer, expert_gain=expert_gain, centroids=centroids)


EPS = 1e-05
PRECISE = lax.Precision.HIGHEST

@jax.custom_vjp
def low(v):
    return lax.optimization_barrier(v.astype(jnp.bfloat16)).astype(jnp.float32)

@jax.custom_vjp
def low_back(v):
    return v

def low_keep(v):
    return (low(v), None)

def low_pass(kept, grad):
    return (grad,)

def back_keep(v):
    return (v, None)

def back_low(kept, grad):
    return (low(grad),)
low.defvjp(low_keep, low_pass)
low_back.defvjp(back_keep, back_low)

def high_dot(left_mat, right_mat):
    return jnp.dot(left_mat, right_mat, precision=PRECISE)

def layer_norm(inputs_row, gain_row):
    row_mean = lax.optimization_barrier(jnp.mean(inputs_row, axis=-1, keepdims=True))
    centered = inputs_row - row_mean
    variance = lax.optimization_barrier(jnp.mean(centered * centered, axis=-1, keepdims=True))
    return centered * lax.rsqrt(variance + EPS) * gain_row

def attend_group(members):
    queries, keys_in, values_in, segment = members
    seq_span = queries.shape[1]
    scores = jnp.einsum('gqhe,gkhe->ghqk', queries, keys_in, precision=PRECISE) * HEAD_DIM ** (-0.5)
    scores = low_back(scores)
    positions = jnp.arange(seq_span, dtype=jnp.int32)
    allowed = (segment[:, :, None] == segment[:, None, :]) & (positions[None, :, None] >= positions[None, None, :])
    scores = jnp.where(allowed[:, None], scores, -1e+30)
    attn_probs = low(jax.nn.softmax(scores, axis=-1))
    return jnp.einsum('ghqk,gkhe->gqhe', attn_probs, values_in, precision=PRECISE)

def expert_rows(members):
    rows_in, inner_pair, outer_pair, gain_pair, centroid = members
    gates = jax.nn.sigmoid(high_dot(rows_in, centroid))
    carried = rows_in
    for sublayer in range(2):
        normed = low(layer_norm(carried, gain_pair[sublayer]))
        inner_pre = low_back(high_dot(normed, inner_pair[sublayer]))
        active = low(jax.nn.gelu(inner_pre, approximate=False))
        carried = carried + low_back(high_dot(active, outer_pair[sublayer]))
    return low(low_back(gates[:, None] * carried))

def forward(tokens, w_query, w_key, w_value, w_output, attn_gain, w_inner, w_outer, expert_gain, centroids, segment, sorting, inverse):
    normed = low(layer_norm(tokens, attn_gain))

    def project(weight_mat):
        projected = low(low_back(high_dot(normed, weight_mat)))
        return projected.reshape(SEQS // 8, 8, TOK_DEV, HEADS, HEAD_DIM)
    context = lax.map(jax.checkpoint(attend_group), (project(w_query), project(w_key), project(w_value), segment.reshape(SEQS // 8, 8, TOK_DEV)))
    context = low(low_back(context.reshape(TOKENS, HEADS * HEAD_DIM)))
    hidden = tokens + low_back(high_dot(context, w_output))
    sent_rows = low_back(low(hidden))
    grouped = sent_rows[sorting].reshape(EXPERTS, TOKENS // EXPERTS, HEADS * HEAD_DIM)
    inner_all = w_inner.reshape(EXPERTS, 2, HEADS * HEAD_DIM, FF)
    outer_all = w_outer.reshape(EXPERTS, 2, FF, HEADS * HEAD_DIM)
    gain_all = expert_gain.reshape(EXPERTS, 2, HEADS * HEAD_DIM)
    centre_all = centroids.reshape(EXPERTS, HEADS * HEAD_DIM)
    branch = lax.map(jax.checkpoint(expert_rows), (grouped, inner_all, outer_all, gain_all, centre_all))
    return hidden + branch.reshape(TOKENS, HEADS * HEAD_DIM)[inverse]

def reference(tokens, cotangent, doc_lengths, expert_of_token, w_query, w_key, w_value, w_output, attn_gain, w_inner, w_outer, expert_gain, centroids):
    doc_ends = jnp.cumsum(doc_lengths, axis=1)
    positions = jnp.arange(TOK_DEV, dtype=jnp.int32)
    segment = lax.optimization_barrier(jnp.sum((positions[None, :, None] >= doc_ends[:, None, :]).astype(jnp.int32), axis=2))
    sorting = jnp.argsort(expert_of_token, stable=True).astype(jnp.int32)
    inverse = jnp.argsort(sorting).astype(jnp.int32)
    arrays = tuple((array_in.astype(jnp.float32) for array_in in (tokens, w_query, w_key, w_value, w_output, attn_gain, w_inner, w_outer, expert_gain, centroids)))

    def layer_of(tokens_f, query_f, key_f, value_f, output_f, gain_a, inner_f, outer_f, gain_e, centroid_f):
        return forward(tokens_f, query_f, key_f, value_f, output_f, gain_a, inner_f, outer_f, gain_e, centroid_f, segment, sorting, inverse)
    output, pullback = jax.vjp(layer_of, *arrays)
    gradients = pullback(cotangent.astype(jnp.float32))
    return (output.astype(jnp.bfloat16), gradients[0], gradients[1], gradients[2], gradients[3], gradients[4], gradients[5], gradients[6], gradients[7], gradients[8], gradients[9])
```

```python
import jax
import jax.numpy as jnp
from jax import lax
from jax.sharding import PartitionSpec as P

HEADS = 16
EPS = 1e-05
ROOT_HALF = 0.7071067811865476
INV_ROOT_TAU = 0.3989422804014327
CHUNKS = 2


def swap(shard, axis, mask):
    return lax.ppermute(shard, axis, [(i, i ^ mask) for i in range(lax.axis_size(axis))])


def plain_product(left_mat, right_mat):
    return jnp.dot(left_mat, right_mat, preferred_element_type=jnp.float32)


def tn_product(left_mat, right_mat):
    return lax.dot_general(
        left_mat, right_mat, (((0,), (0,)), ((), ())), preferred_element_type=jnp.float32
    )


def nt_product(left_mat, right_mat):
    return lax.dot_general(
        left_mat, right_mat, (((1,), (1,)), ((), ())), preferred_element_type=jnp.float32
    )


def xor_order(array, axis, index, count):
    bits = count.bit_length() - 1
    shape = array.shape
    array = array.reshape(shape[:axis] + (2,) * bits + (shape[axis] // count,) + shape[axis + 1 :])
    for at in range(bits):
        flag = (index >> (bits - 1 - at)) & 1
        if isinstance(flag, int):
            array = jnp.flip(array, axis + at) if flag else array
        else:
            array = jnp.where(flag == 1, jnp.flip(array, axis + at), array)
    return array.reshape(shape)


def norm_stats(rows):
    row_mean = jnp.mean(rows, axis=-1, keepdims=True)
    centered = rows - row_mean
    variance = jnp.mean(centered * centered, axis=-1, keepdims=True)
    inv_scale = lax.rsqrt(variance + EPS)
    return centered * inv_scale, inv_scale


def norm_back(grad_out, unit_rows, inv_scale, gain_row):
    grad_unit = grad_out * gain_row
    centred_grad = grad_unit - jnp.mean(grad_unit, axis=-1, keepdims=True)
    return (
        centred_grad - unit_rows * jnp.mean(grad_unit * unit_rows, axis=-1, keepdims=True)
    ) * inv_scale


def gather_weights(stack, core, exp_bits):
    half = stack.shape[2] // 2
    pair = stack.reshape(stack.shape[0], stack.shape[1], 2, half)
    mine = jnp.where(core == 0, pair[:, :, 0], pair[:, :, 1])
    for bit in range(1, exp_bits):
        got = swap(mine, "exp", 1 << bit)
        mine = jnp.stack([mine[:, None], got[:, None]], axis=1)
        mine = mine.reshape((stack.shape[0], -1) + stack.shape[1:2] + (half,))
    mine = mine.reshape((stack.shape[0], -1) + stack.shape[1:2] + (half,))
    got = swap(mine, "exp", 1)
    mine = jnp.stack([mine, got], axis=2).reshape(stack.shape[0], -1, half)
    other = swap(mine, "rep", 1)
    return jnp.concatenate([mine, other], axis=2)


def reduce_weights(grads, exp_bits):
    count, rows, cols = grads.shape
    half = cols // 2
    total = grads[:, :, :half] + swap(grads[:, :, half:].astype(jnp.bfloat16), "rep", 1).astype(
        jnp.float32
    )
    total = total.reshape(count, -1, 2, rows >> exp_bits, half)
    total = total[:, :, 0] + swap(total[:, :, 1].astype(jnp.bfloat16), "exp", 1).astype(
        jnp.float32
    )
    for bit in range(exp_bits - 1, 0, -1):
        keep = total.shape[1] // 2
        total = total[:, :keep] + swap(
            total[:, keep:].astype(jnp.bfloat16), "exp", 1 << bit
        ).astype(jnp.float32)
    total = total[:, 0]
    total = total + swap(total.astype(jnp.bfloat16), "rep", 2).astype(jnp.float32)
    other = swap(total.astype(jnp.bfloat16), "rep", 1).astype(jnp.float32)
    return total, other


def masked_scores(queries3, keys3, allowed, factor):
    scores = (
        jnp.einsum("qhe,khe->hqk", queries3, keys3, preferred_element_type=jnp.float32) * factor
    )
    return jnp.where(allowed[None], scores, -1e30)


def shards(
    tokens,
    cotangent,
    doc_lengths,
    expert_of_token,
    w_query,
    w_key,
    w_value,
    w_output,
    attn_gain,
    w_inner,
    w_outer,
    expert_gain,
    centroids,
):
    exp_size = lax.axis_size("exp")
    rep_size = lax.axis_size("rep")
    exp_bits = exp_size.bit_length() - 1
    experts = exp_size // 2
    rep_at = lax.axis_index("rep")
    exp_at = lax.axis_index("exp")
    core = rep_at % 2
    first = exp_at % 2 == 0
    group = exp_at // 2
    row_count, width = tokens.shape
    head_dim = width // HEADS
    factor = head_dim ** (-0.5)
    half_width = width // 2
    low = jnp.bfloat16
    wide = jnp.float32

    inner_own = w_inner[0]
    block = inner_own.shape[1] // rep_size

    def inner_for(mask):
        dest = rep_at ^ mask
        return jnp.concatenate(
            [
                lax.dynamic_slice_in_dim(inner_own, dest * block, block, 1),
                lax.dynamic_slice_in_dim(inner_own, (dest ^ 2) * block, block, 1),
            ],
            axis=1,
        )

    inner_w = jnp.concatenate(
        [inner_for(0)] + [swap(inner_for(mask), "rep", mask) for mask in range(1, rep_size)], axis=0
    )
    outer_w = jnp.concatenate([w_outer[0], swap(w_outer[0], "rep", 2)], axis=0)

    expert_ids = jnp.arange(experts, dtype=jnp.int32)
    onehot = expert_of_token[:, None] == expert_ids[None, :]
    counts = jnp.sum(onehot.astype(wide), axis=0)
    pieces = [centroids[0], expert_gain[0], attn_gain, counts.astype(low)]
    small = lax.all_gather(jnp.concatenate(pieces), ("rep", "exp"), axis=0, tiled=False)
    small = small.reshape(rep_size, exp_size, -1)
    edges = [0]
    for piece in pieces:
        edges.append(edges[-1] + piece.shape[0])
    gain_attn = small[0, :, edges[2] : edges[3]].reshape(width).astype(wide)
    own_small = lax.dynamic_slice_in_dim(small, exp_at - exp_at % 2, 2, 1)
    centroid = jnp.swapaxes(own_small[:, :, edges[0] : edges[1]], 0, 1).reshape(width)
    gain_pair = own_small[:, :, edges[1] : edges[2]]
    gain_row = jnp.where(first, gain_pair[:, 0], gain_pair[:, 1]).reshape(width).astype(wide)
    group_counts = lax.dynamic_index_in_dim(small, rep_at, 0, False)[:, edges[3] : edges[4]]
    group_counts = jnp.sum(
        jnp.where(expert_ids[None, :] == group, group_counts.astype(wide), 0.0), axis=1
    ).astype(jnp.int32)

    qkv_w = gather_weights(jnp.stack([w_query, w_key, w_value]), core, exp_bits)
    out_w = gather_weights(w_output[None], core, exp_bits)[0]
    inputs = tokens.astype(wide)
    unit_a, scale_a = norm_stats(inputs)
    act_a = xor_order((unit_a * gain_attn).astype(low), 1, exp_at, exp_size)
    queries, keys_low, values_low = [plain_product(act_a, qkv_w[i]).astype(low) for i in range(3)]
    queries3 = queries.reshape(row_count, HEADS, head_dim)
    keys3 = keys_low.reshape(row_count, HEADS, head_dim)
    values3 = values_low.reshape(row_count, HEADS, head_dim)
    doc_ends = jnp.cumsum(doc_lengths[0])
    positions = jnp.arange(row_count, dtype=jnp.int32)
    segment = jnp.sum((positions[:, None] >= doc_ends[None, :]).astype(jnp.int32), axis=1)
    allowed = (segment[:, None] == segment[None, :]) & (positions[:, None] >= positions[None, :])
    scores = masked_scores(queries3, keys3, allowed, factor)
    row_top = jnp.max(scores, axis=-1, keepdims=True)
    row_total = jnp.sum(jnp.exp(scores - row_top), axis=-1, keepdims=True)
    log_total = row_top + jnp.log(row_total)
    probs_low = jnp.exp(scores - log_total).astype(low)
    context = jnp.einsum("hqk,khe->qhe", probs_low, values3, preferred_element_type=wide)
    context = context.reshape(row_count, width).astype(low)
    context_x = xor_order(xor_order(context, 1, core, 2), 1, exp_at, exp_size)
    hidden = inputs + xor_order(plain_product(context_x, out_w), 1, core, 2)

    slots = 3 * row_count // exp_size
    lower = (positions[:, None] > positions[None, :]).astype(low)
    earlier = plain_product(lower, onehot.astype(low))
    rank_in = jnp.sum(jnp.where(onehot, earlier, 0.0), axis=1).astype(jnp.int32)
    position = expert_of_token * slots + rank_in
    all_slots = experts * slots
    pick = (jnp.arange(all_slots, dtype=jnp.int32)[:, None] == position[None, :]).astype(low)
    sent_rows = hidden.astype(low)
    packed_sent = plain_product(pick, sent_rows).astype(low).reshape(experts, 1, slots, width)
    packed_cot = plain_product(pick, cotangent).astype(low).reshape(experts, 1, slots, width)
    packed = jnp.concatenate([packed_sent, packed_cot], axis=1).reshape(exp_size, slots, width)
    arrived = lax.all_to_all(packed, "exp", split_axis=0, concat_axis=0, tiled=True)
    arrived = arrived.reshape(exp_size * slots, width)
    starts = jnp.cumsum(group_counts) - group_counts
    slot_at = jnp.arange(slots, dtype=jnp.int32)
    row_of_slot = jnp.where(
        slot_at[None, :] < group_counts[:, None], starts[:, None] + slot_at[None, :], -1
    ).reshape(-1)
    own_rows = 2 * row_count
    compact = (jnp.arange(own_rows, dtype=jnp.int32)[:, None] == row_of_slot[None, :]).astype(low)
    rows_own = plain_product(compact, arrived).astype(low)

    part = own_rows // CHUNKS

    def chunk_of(array, at):
        return array[at * part : (at + 1) * part]

    own_f = rows_own.astype(wide)
    gates = swap(jax.nn.sigmoid(plain_product(rows_own, centroid[:, None])[:, 0]), "exp", 1)
    gates_zero = jax.nn.sigmoid(plain_product(rows_own, centroid[:, None])[:, 0])
    gates = jnp.where(first, gates_zero, gates)
    kept = []
    handed = None
    finals = []
    for at in range(CHUNKS + 1):
        if at == 0:
            own_in = chunk_of(rows_own, 0)
        elif at == CHUNKS:
            own_in = handed
        else:
            own_in = jnp.where(first, chunk_of(rows_own, at), handed)
        other_in = swap(own_in, "rep", 1)
        rows_in = jnp.concatenate([own_in, other_in], axis=0).astype(wide)
        unit_rows, inv_scale = norm_stats(rows_in)
        normed_low = xor_order((unit_rows * gain_row).astype(low), 1, rep_at, rep_size)
        inner_pre = plain_product(normed_low, inner_w)
        normal = 0.5 * (1.0 + lax.erf(inner_pre * ROOT_HALF))
        active = (inner_pre * normal).astype(low)
        slope = (
            normal + inner_pre * jnp.exp(-0.5 * inner_pre * inner_pre) * INV_ROOT_TAU
        ).astype(low)
        product = plain_product(active, outer_w)
        got = swap(product[part:].astype(low), "rep", 1)
        result = rows_in[:part] + product[:part] + got.astype(wide)
        kept.append((normed_low, active, slope, own_in))
        finals.append(result)
        if at < CHUNKS:
            handed = swap(result.astype(low), "exp", 1)
    final_rows = jnp.concatenate(finals[1:], axis=0)
    grad_gate = jnp.sum(own_f * final_rows, axis=1)
    branch = (gates[:, None] * final_rows).astype(low)
    grad_gate = swap(grad_gate, "exp", 1)
    grad_logit = grad_gate * gates * (1.0 - gates)

    gain_grad = jnp.zeros((width,), wide)
    states = []
    inners = []
    outs = []
    handed = None
    for at in range(CHUNKS + 1):

        def kept_of(which):
            if at == 0:
                return kept[1][which]
            if at == CHUNKS:
                return kept[CHUNKS - 1][which]
            return jnp.where(first, kept[at - 1][which], kept[at + 1][which])

        if at < CHUNKS:
            fresh = chunk_of(gates, at)[:, None] * chunk_of(own_f, at)
        if at == 0:
            state = fresh
        elif at == CHUNKS:
            state = handed.astype(wide)
        else:
            state = jnp.where(first, handed.astype(wide), fresh)
        grad_own = state.astype(low)
        grad_outer = jnp.concatenate([grad_own, swap(grad_own, "rep", 1)], axis=0)
        grad_active = nt_product(grad_outer, outer_w)
        grad_inner = (grad_active * kept_of(2).astype(wide)).astype(low)
        grad_normed = nt_product(grad_inner, inner_w)
        got = swap(grad_normed[part:].astype(low), "rep", 1)
        got = xor_order(got, 1, 1, rep_size)
        grad_normed = xor_order(grad_normed[:part] + got.astype(wide), 1, rep_at, rep_size)
        unit_rows, inv_scale = norm_stats(kept_of(3).astype(wide))
        share = jnp.sum(grad_normed * unit_rows, axis=0)
        if at == 0:
            share = jnp.where(first, 0.0, share)
        elif at == CHUNKS:
            share = jnp.where(first, share, 0.0)
        gain_grad = gain_grad + share
        grad_state = state + norm_back(grad_normed, unit_rows, inv_scale, gain_row)
        states.append(grad_outer)
        inners.append(grad_inner)
        outs.append(grad_state)
        if at < CHUNKS:
            handed = swap(grad_state.astype(low), "exp", 1)
    grad_wide = jnp.concatenate(outs[1:], axis=0)
    grad_sent = (grad_wide + grad_logit[:, None] * centroid.astype(wide)[None, :]).astype(low)
    back_rows = jnp.where(first, grad_sent, branch)
    spread = tn_product(compact, back_rows).astype(low).reshape(exp_size, slots, width)
    home = lax.all_to_all(spread, "exp", split_axis=0, concat_axis=0, tiled=True)
    home = home.reshape(experts, 2, slots, width)
    grad_home = tn_product(pick, home[:, 0].reshape(all_slots, width))
    branch_home = tn_product(pick, home[:, 1].reshape(all_slots, width))
    output = (hidden + branch_home).astype(low)

    def both(items, of_first, of_second):
        return jnp.concatenate(
            [
                jnp.where(first, items[of_first + k], items[of_second + k])
                for k in range(CHUNKS)
            ],
            axis=0,
        )

    normed_all = both([k[0] for k in kept], 0, 1)
    active_all = both([k[1] for k in kept], 0, 1)
    state_all = both(states, 1, 0)
    inner_all = both(inners, 1, 0)
    grad_outer_w = tn_product(active_all, state_all)
    grad_inner_w = tn_product(normed_all, inner_all)
    outer_rows = w_outer.shape[1]
    grad_w_outer = (
        grad_outer_w[:outer_rows]
        + swap(grad_outer_w[outer_rows:].astype(low), "rep", 2).astype(wide)
    )[None]
    shares = grad_inner_w.reshape(rep_size, width // rep_size, 2, block)
    got = [swap(shares[mask].astype(low), "rep", mask).astype(wide) for mask in (1, 2, 3)]
    mine = shares[0]
    ordered = jnp.stack(
        [
            mine[:, 0] + got[1][:, 1],
            got[0][:, 0] + got[2][:, 1],
            mine[:, 1] + got[1][:, 0],
            got[0][:, 1] + got[2][:, 0],
        ],
        axis=1,
    )
    grad_w_inner = xor_order(ordered.reshape(width // rep_size, -1), 1, rep_at, rep_size)[None]

    grad_centre = jnp.dot(grad_logit, own_f, precision=lax.Precision.HIGHEST)
    other_centre = swap(grad_centre[half_width:], "exp", 1)
    centre_half = jnp.where(first, grad_centre[:half_width], other_centre)

    grad_hidden = cotangent.astype(wide) + grad_home
    grad_attn = grad_hidden.astype(low)
    grad_attn_c = xor_order(grad_attn, 1, core, 2)
    grad_w_o = tn_product(context_x, grad_attn_c)
    share_o = reduce_weights(grad_w_o[None], exp_bits)
    grad_context = nt_product(grad_attn_c, out_w).astype(low)
    grad_context = xor_order(xor_order(grad_context, 1, exp_at, exp_size), 1, core, 2)
    grad_context3 = grad_context.reshape(row_count, HEADS, head_dim)
    again_scores = masked_scores(queries3, keys3, allowed, factor)
    attn_probs = jnp.exp(again_scores - log_total)
    grad_probs = jnp.einsum("qhe,khe->hqk", grad_context3, values3, preferred_element_type=wide)
    inner_sum = jnp.sum(attn_probs * grad_probs, axis=-1, keepdims=True)
    grad_scores = (attn_probs * (grad_probs - inner_sum)).astype(low)
    grad_query = (
        jnp.einsum("hqk,khe->qhe", grad_scores, keys3, preferred_element_type=wide) * factor
    ).astype(low)
    grad_key = (
        jnp.einsum("hqk,qhe->khe", grad_scores, queries3, preferred_element_type=wide) * factor
    ).astype(low)
    grad_value = jnp.einsum(
        "hqk,qhe->khe", attn_probs.astype(low), grad_context3, preferred_element_type=wide
    ).astype(low)
    grads3 = [g.reshape(row_count, width) for g in (grad_query, grad_key, grad_value)]
    grad_w_qkv = jnp.stack([tn_product(act_a, g) for g in grads3])
    share_qkv = reduce_weights(grad_w_qkv, exp_bits)
    grad_act = sum(nt_product(g, qkv_w[i]) for i, g in enumerate(grads3))
    grad_act = xor_order(grad_act, 1, exp_at, exp_size)
    grad_gain_a = jnp.sum(grad_act * unit_a, axis=0)
    grad_tokens = grad_hidden + norm_back(grad_act, unit_a, scale_a, gain_attn)

    def true_halves(pair):
        mine_half, other_half = pair
        return xor_order(jnp.concatenate([mine_half, other_half], axis=-1), 2, core, 2)

    full_o = true_halves(share_o)[0]
    full_qkv = true_halves(share_qkv)

    rep_sums = lax.psum(jnp.concatenate([gain_grad, centre_half]), "rep")
    gain_len = width // rep_size
    centre_len = half_width // rep_size
    grad_expert_gain = lax.dynamic_slice_in_dim(rep_sums, rep_at * gain_len, gain_len)[None]
    grad_centroids = lax.dynamic_slice_in_dim(
        rep_sums, width + rep_at * centre_len, centre_len
    )[None]
    attn_sums = lax.psum(grad_gain_a, ("rep", "exp"))
    attn_len = width // exp_size
    share_gain = lax.dynamic_slice_in_dim(attn_sums, exp_at * attn_len, attn_len)
    return (
        output,
        grad_tokens,
        full_qkv[0],
        full_qkv[1],
        full_qkv[2],
        full_o,
        share_gain,
        grad_w_inner,
        grad_w_outer,
        grad_expert_gain,
        grad_centroids,
    )


def solution(mesh):
    placed = (
        P(("rep", "exp"), None),
        P(("rep", "exp"), None),
        P(("rep", "exp"), None),
        P(("rep", "exp")),
        P("exp", None),
        P("exp", None),
        P("exp", None),
        P("exp", None),
        P("exp"),
        P("exp", "rep", None),
        P("exp", "rep", None),
        P("exp", "rep"),
        P("exp", "rep"),
    )
    return jax.shard_map(
        shards,
        mesh=mesh,
        in_specs=placed,
        out_specs=(
            P(("rep", "exp"), None),
            P(("rep", "exp"), None),
            P("exp", None),
            P("exp", None),
            P("exp", None),
            P("exp", None),
            P("exp"),
            P("exp", "rep", None),
            P("exp", "rep", None),
            P("exp", "rep"),
            P("exp", "rep"),
        ),
        check_vma=False,
    )
```

```python
import functools

import jax
import jax.numpy as jnp
from jax import lax
from jax.experimental import pallas as pl
from jax.experimental.pallas import tpu as pltpu
from jax.sharding import PartitionSpec as P

HEADS = 16
EPS = 1e-05
ROOT_HALF = 0.7071067811865476
INV_ROOT_TAU = 0.3989422804014327
CHUNKS = 2


def swap(shard, axis, mask):
    return lax.ppermute(shard, axis, [(i, i ^ mask) for i in range(lax.axis_size(axis))])


def plain_product(left_mat, right_mat):
    return jnp.dot(left_mat, right_mat, preferred_element_type=jnp.float32)


def tn_product(left_mat, right_mat):
    return lax.dot_general(
        left_mat, right_mat, (((0,), (0,)), ((), ())), preferred_element_type=jnp.float32
    )


def nt_product(left_mat, right_mat):
    return lax.dot_general(
        left_mat, right_mat, (((1,), (1,)), ((), ())), preferred_element_type=jnp.float32
    )


def xor_order(array, axis, index, count):
    bits = count.bit_length() - 1
    shape = array.shape
    array = array.reshape(shape[:axis] + (2,) * bits + (shape[axis] // count,) + shape[axis + 1 :])
    for at in range(bits):
        flag = (index >> (bits - 1 - at)) & 1
        if isinstance(flag, int):
            array = jnp.flip(array, axis + at) if flag else array
        else:
            array = jnp.where(flag == 1, jnp.flip(array, axis + at), array)
    return array.reshape(shape)


def norm_stats(rows):
    row_mean = jnp.mean(rows, axis=-1, keepdims=True)
    centered = rows - row_mean
    variance = jnp.mean(centered * centered, axis=-1, keepdims=True)
    inv_scale = lax.rsqrt(variance + EPS)
    return centered * inv_scale, inv_scale


def norm_back(grad_out, unit_rows, inv_scale, gain_row):
    grad_unit = grad_out * gain_row
    centred_grad = grad_unit - jnp.mean(grad_unit, axis=-1, keepdims=True)
    return (
        centred_grad - unit_rows * jnp.mean(grad_unit * unit_rows, axis=-1, keepdims=True)
    ) * inv_scale


MESH = pl.DeviceIdType.MESH
TILE = 256
ROWS = 64


def remote(src, dst, send_sem, recv_sem, device):
    return pltpu.make_async_remote_copy(
        src_ref=src,
        dst_ref=dst,
        send_sem=send_sem,
        recv_sem=recv_sem,
        device_id=device,
        device_id_type=MESH,
    )


def expert_kernel(
    exp_size,
    rep_size,
    slots,
    packed,
    compact,
    spread_m,
    own_in,
    in_one,
    in_two,
    in_three,
    own_out,
    out_two,
    gain,
    cent,
    cent_wide,
    home,
    outer_keep,
    outer_send,
    inner_keep,
    inner_send,
    gain_grad,
    centre_grad,
    arrived,
    inner_w,
    outer_w,
    own_x,
    own_cot,
    normed,
    active,
    slope,
    states,
    fwd_send,
    fwd_recv,
    bwd_send,
    bwd_recv,
    hop,
    back,
    spread,
    acc,
    gates,
    gate_grads,
    outer_keep_v,
    outer_send_v,
    inner_keep_v,
    inner_send_v,
    disp_s,
    disp_r,
    load_sem,
    norm_s,
    norm_r,
    state_s,
    state_r,
    fwd_s,
    fwd_r,
    bwd_s,
    bwd_r,
    hop_s,
    hop_r,
    gate_s,
    gate_r,
    ret_s,
    ret_r,
    out_sem,
):
    low = jnp.bfloat16
    wide = jnp.float32
    rep_at = lax.axis_index("rep")
    exp_at = lax.axis_index("exp")
    first = exp_at % 2 == 0
    second = exp_at % 2 == 1
    core_peer = (rep_at ^ 1, exp_at)
    side_peer = (rep_at, exp_at ^ 1)
    width = own_x.shape[1]
    own_rows = own_x.shape[0]
    part = own_rows // CHUNKS
    wide_ff = inner_w.shape[1]
    block = wide_ff // 2
    depth = width // rep_size

    def slot_rows(at):
        return pl.ds(pl.multiple_of(at * slots, slots), slots)

    def inner_rows(mask):
        return pl.ds(pl.multiple_of((rep_at ^ mask) * depth, depth), depth)

    def own_cols(mask):
        return pl.ds(pl.multiple_of((rep_at ^ mask) * block, block), block)

    loads = [
        pltpu.make_async_copy(
            own_in.at[:, own_cols(0)], inner_w.at[inner_rows(0), :block], load_sem.at[0]
        ),
        pltpu.make_async_copy(
            own_in.at[:, own_cols(2)], inner_w.at[inner_rows(0), block:], load_sem.at[1]
        ),
        pltpu.make_async_copy(in_one, inner_w.at[inner_rows(1)], load_sem.at[2]),
        pltpu.make_async_copy(in_two, inner_w.at[inner_rows(2)], load_sem.at[3]),
        pltpu.make_async_copy(in_three, inner_w.at[inner_rows(3)], load_sem.at[4]),
        pltpu.make_async_copy(own_out, outer_w.at[:block], load_sem.at[5]),
        pltpu.make_async_copy(out_two, outer_w.at[block:], load_sem.at[6]),
    ]
    for load in loads:
        load.start()

    barrier = pltpu.get_barrier_semaphore()
    pl.semaphore_signal(barrier, inc=1, device_id=core_peer, device_id_type=MESH)

    @pl.loop(1, exp_size)
    def _(at):
        pl.semaphore_signal(barrier, inc=1, device_id=(rep_at, exp_at ^ at), device_id_type=MESH)

    pl.semaphore_wait(barrier, exp_size)

    def disp_copy(dest):
        return remote(
            packed.at[slot_rows(dest)],
            arrived.at[slot_rows(exp_at)],
            disp_s.at[dest],
            disp_r.at[exp_at],
            (rep_at, dest),
        )

    own_copy = pltpu.make_async_copy(
        packed.at[slot_rows(exp_at)], arrived.at[slot_rows(exp_at)], disp_s.at[exp_at]
    )
    own_copy.start()
    for side in range(2):

        @pl.loop(0, exp_size // 2)
        def _(at):
            dest = 2 * ((exp_at // 2) ^ at) + side

            @pl.when(dest != exp_at)
            def _():
                disp_copy(dest).start()

    own_copy.wait()

    @pl.loop(1, exp_size)
    def _(at):
        source = exp_at ^ at
        remote(
            packed.at[slot_rows(source)],
            arrived.at[slot_rows(source)],
            disp_s.at[source],
            disp_r.at[source],
            (rep_at, source),
        ).wait()

    for at in range(width // TILE):
        cols = slice(at * TILE, (at + 1) * TILE)
        rows_low = jnp.dot(
            compact[...], arrived[:, cols], preferred_element_type=wide
        ).astype(low)

        @pl.when(first)
        def _():
            own_x[:, cols] = rows_low

        @pl.when(second)
        def _():
            own_cot[:, cols] = rows_low

    gate_copy = remote(gates, gates, gate_s.at[0], gate_r.at[0], side_peer)
    grad_copy = remote(gate_grads, gate_grads, gate_s.at[1], gate_r.at[1], side_peer)

    @pl.when(first)
    def _():
        logit = jnp.dot(own_x[...], cent_wide[...], preferred_element_type=wide)
        gates[...] = jax.nn.sigmoid(logit)
        gate_copy.start()

    def stats(rows):
        row_mean = jnp.mean(rows, axis=-1, keepdims=True)
        centered = rows - row_mean
        variance = jnp.mean(centered * centered, axis=-1, keepdims=True)
        inv_scale = lax.rsqrt(variance + EPS)
        return centered * inv_scale, inv_scale

    def hop_forward(at):
        rows = pl.ds(at * part, part)
        return remote(hop.at[rows], own_x.at[rows], hop_s.at[at], hop_r.at[at], side_peer)

    def own_slice(at):
        return pl.ds(at * 2 * part + part, part)

    def other_slice(at):
        return pl.ds(at * 2 * part, part)

    def hop_backward(at):
        rows = pl.ds(at * part, part)
        return remote(
            hop.at[rows], states.at[own_slice(at)], hop_s.at[at], hop_r.at[at], side_peer
        )

    for load in loads:
        load.wait()

    def forward(at):
        base = at * part

        @pl.when(second)
        def _():
            hop_forward(at).wait_recv()

        @pl.loop(0, part // ROWS)
        def _(step):
            off = pl.multiple_of(step * ROWS, ROWS)
            unit, _ = stats(own_x[pl.ds(base + off, ROWS), :].astype(wide))
            normed[pl.ds(at * 2 * part + part + off, ROWS), :] = (unit * gain[...]).astype(low)

        norm_copy = remote(
            normed.at[own_slice(at)], normed.at[other_slice(at)], norm_s.at[at], norm_r.at[at], core_peer
        )
        norm_copy.start()
        norm_copy.wait_recv()

        @pl.loop(0, wide_ff // TILE)
        def _(step):
            cols = pl.ds(pl.multiple_of(step * TILE, TILE), TILE)
            inner = jnp.dot(
                normed[pl.ds(at * 2 * part, 2 * part), :],
                inner_w[:, cols],
                preferred_element_type=wide,
            )
            normal = 0.5 * (1.0 + lax.erf(inner * ROOT_HALF))
            active[pl.ds(at * 2 * part, 2 * part), cols] = (inner * normal).astype(low)
            slope[pl.ds(at * 2 * part, 2 * part), cols] = (
                normal + inner * jnp.exp(-0.5 * inner * inner) * INV_ROOT_TAU
            ).astype(low)

        @pl.loop(0, width // TILE)
        def _(step):
            cols = pl.ds(pl.multiple_of(step * TILE, TILE), TILE)
            fwd_send[pl.ds(base, part), cols] = jnp.dot(
                active[other_slice(at), :], outer_w[:, cols], preferred_element_type=wide
            ).astype(low)

        rows = pl.ds(base, part)
        copy = remote(fwd_send.at[rows], fwd_recv.at[rows], fwd_s.at[at], fwd_r.at[at], core_peer)
        copy.start()

        @pl.loop(0, width // TILE)
        def _(step):
            cols = pl.ds(pl.multiple_of(step * TILE, TILE), TILE)
            acc[:, cols] = jnp.dot(
                active[own_slice(at), :], outer_w[:, cols], preferred_element_type=wide
            )

        copy.wait_recv()

        @pl.when(first)
        def _():
            @pl.loop(0, part // ROWS)
            def _(step):
                off = pl.multiple_of(step * ROWS, ROWS)
                here = pl.ds(base + off, ROWS)
                result = (
                    own_x[here, :].astype(wide)
                    + acc[pl.ds(off, ROWS), :]
                    + fwd_recv[here, :].astype(wide)
                )
                hop[here, :] = result.astype(low)

            hop_forward(at).start()

        @pl.when(second)
        def _():
            if at == 0:
                gate_copy.wait_recv()

            @pl.loop(0, part // ROWS)
            def _(step):
                off = pl.multiple_of(step * ROWS, ROWS)
                here = pl.ds(base + off, ROWS)
                result = (
                    own_x[here, :].astype(wide)
                    + acc[pl.ds(off, ROWS), :]
                    + fwd_recv[here, :].astype(wide)
                )
                cot = own_cot[here, :].astype(wide)
                gate = gates[here, :][:, :1]
                back[here, :] = (gate * result).astype(low)
                gate_grads[here, :] = jnp.broadcast_to(
                    jnp.sum(cot * result, axis=1, keepdims=True), (ROWS, gate_grads.shape[1])
                )
                states[pl.ds(at * 2 * part + part + off, ROWS), :] = (gate * cot).astype(low)

    for at in range(CHUNKS):
        forward(at)

    def ret_copy(dest):
        return remote(
            spread.at[slot_rows(dest)],
            home.at[slot_rows(exp_at)],
            ret_s.at[dest],
            ret_r.at[exp_at],
            (rep_at, dest),
        )

    ret_own = pltpu.make_async_copy(
        spread.at[slot_rows(exp_at)], home.at[slot_rows(exp_at)], ret_s.at[exp_at]
    )

    def send_back():
        @pl.loop(0, width // TILE)
        def _(step):
            cols = pl.ds(pl.multiple_of(step * TILE, TILE), TILE)
            spread[:, cols] = jnp.dot(
                spread_m[...], back[:, cols], preferred_element_type=wide
            ).astype(low)

        @pl.loop(1, exp_size)
        def _(step):
            ret_copy(exp_at ^ step).start()

        ret_own.start()

    @pl.when(second)
    def _():
        grad_copy.start()
        send_back()

    gain_grad[...] = jnp.zeros_like(gain_grad)
    centre_grad[...] = jnp.zeros_like(centre_grad)

    def backward(at):
        base = at * part

        @pl.when(first)
        def _():
            hop_backward(at).wait_recv()

        copy = remote(
            states.at[own_slice(at)], states.at[other_slice(at)], state_s.at[at], state_r.at[at], core_peer
        )
        copy.start()
        copy.wait_recv()

        @pl.loop(0, wide_ff // TILE)
        def _(step):
            rows = pl.ds(pl.multiple_of(step * TILE, TILE), TILE)
            grad_active = lax.dot_general(
                states[pl.ds(at * 2 * part, 2 * part), :],
                outer_w[rows, :],
                (((1,), (1,)), ((), ())),
                preferred_element_type=wide,
            )
            here = pl.ds(at * 2 * part, 2 * part)
            slope[here, rows] = (grad_active * slope[here, rows].astype(wide)).astype(low)

        @pl.loop(0, width // TILE)
        def _(step):
            cols = pl.ds(pl.multiple_of(step * TILE, TILE), TILE)
            bwd_send[pl.ds(base, part), cols] = lax.dot_general(
                slope[other_slice(at), :],
                inner_w[cols, :],
                (((1,), (1,)), ((), ())),
                preferred_element_type=wide,
            ).astype(low)

        rows = pl.ds(base, part)
        back_copy = remote(
            bwd_send.at[rows], bwd_recv.at[rows], bwd_s.at[at], bwd_r.at[at], core_peer
        )
        back_copy.start()

        @pl.loop(0, width // TILE)
        def _(step):
            cols = pl.ds(pl.multiple_of(step * TILE, TILE), TILE)
            acc[:, cols] = lax.dot_general(
                slope[own_slice(at), :],
                inner_w[cols, :],
                (((1,), (1,)), ((), ())),
                preferred_element_type=wide,
            )

        back_copy.wait_recv()
        if at == 0:

            @pl.when(first)
            def _():
                grad_copy.wait_recv()

        @pl.when(first)
        def _():
            hop_forward(at).wait_send()

        @pl.loop(0, part // ROWS)
        def _(step):
            off = pl.multiple_of(step * ROWS, ROWS)
            here = pl.ds(base + off, ROWS)
            rows_in = own_x[here, :].astype(wide)
            unit, inv_scale = stats(rows_in)
            grad_normed = acc[pl.ds(off, ROWS), :] + bwd_recv[here, :].astype(wide)
            gain_grad[...] += jnp.sum(grad_normed * unit, axis=0, keepdims=True)
            grad_unit = grad_normed * gain[...]
            grad_in = (
                grad_unit
                - jnp.mean(grad_unit, axis=-1, keepdims=True)
                - unit * jnp.mean(grad_unit * unit, axis=-1, keepdims=True)
            ) * inv_scale
            gate = gates[here, :][:, :1]

            @pl.when(second)
            def _():
                state = gate * own_cot[here, :].astype(wide) + grad_in
                hop[here, :] = state.astype(low)

            @pl.when(first)
            def _():
                state = states[pl.ds(at * 2 * part + part + off, ROWS), :].astype(wide) + grad_in
                grad_logit = gate_grads[here, :][:, :1] * gate * (1.0 - gate)
                back[here, :] = (state + grad_logit * cent[...]).astype(low)
                centre_grad[...] += jnp.sum(grad_logit * rows_in, axis=0, keepdims=True)

        @pl.when(second)
        def _():
            hop_backward(at).start()

    for at in range(CHUNKS):
        backward(at)

    @pl.when(first)
    def _():
        send_back()

    outs = []
    for at in range(2 * block // TILE):
        rows = slice(at * TILE, (at + 1) * TILE)
        grad = lax.dot_general(
            active[:, rows], states[...], (((0,), (0,)), ((), ())), preferred_element_type=wide
        )
        if (at + 1) * TILE <= block:
            outer_keep_v[rows, :] = grad
            outs.append((outer_keep_v.at[rows], outer_keep.at[rows]))
        else:
            rows = slice(at * TILE - block, (at + 1) * TILE - block)
            outer_send_v[rows, :] = grad.astype(low)
            outs.append((outer_send_v.at[rows], outer_send.at[rows]))
        pltpu.make_async_copy(outs[-1][0], outs[-1][1], out_sem.at[len(outs) - 1]).start()
    for mask in range(rep_size):
        for side in range(2):
            cols = slice(side * block, (side + 1) * block)
            grad = lax.dot_general(
                normed[:, inner_rows(mask)],
                slope[:, cols],
                (((0,), (0,)), ((), ())),
                preferred_element_type=wide,
            )
            if mask == 0:
                inner_keep_v[:, cols] = grad
                outs.append((inner_keep_v.at[:, cols], inner_keep.at[:, cols]))
            else:
                rows = slice((mask - 1) * depth, mask * depth)
                inner_send_v[rows, cols] = grad.astype(low)
                outs.append((inner_send_v.at[rows, cols], inner_send.at[mask - 1, :, cols]))
            pltpu.make_async_copy(outs[-1][0], outs[-1][1], out_sem.at[len(outs) - 1]).start()

    for at, (source, target) in enumerate(outs):
        pltpu.make_async_copy(source, target, out_sem.at[at]).wait()
    for at in range(CHUNKS):
        rows = pl.ds(at * part, part)
        remote(
            normed.at[own_slice(at)], normed.at[other_slice(at)], norm_s.at[at], norm_r.at[at], core_peer
        ).wait_send()
        remote(
            states.at[own_slice(at)], states.at[other_slice(at)], state_s.at[at], state_r.at[at], core_peer
        ).wait_send()
        remote(
            fwd_send.at[rows], fwd_recv.at[rows], fwd_s.at[at], fwd_r.at[at], core_peer
        ).wait_send()
        remote(
            bwd_send.at[rows], bwd_recv.at[rows], bwd_s.at[at], bwd_r.at[at], core_peer
        ).wait_send()

        @pl.when(second)
        def _():
            hop_backward(at).wait_send()

    @pl.when(first)
    def _():
        gate_copy.wait_send()

    @pl.when(second)
    def _():
        grad_copy.wait_send()

    ret_own.wait()

    @pl.loop(1, exp_size)
    def _(step):
        source = exp_at ^ step
        remote(
            spread.at[slot_rows(source)],
            home.at[slot_rows(source)],
            ret_s.at[source],
            ret_r.at[source],
            (rep_at, source),
        ).wait()


def run_experts(exp_size, rep_size, slots, packed, compact, spread_m, weights, gain, cent, cent_wide):
    width = packed.shape[1]
    own_rows = compact.shape[0]
    depth = width // rep_size
    block = weights[0].shape[1] // rep_size
    low = jnp.bfloat16
    wide = jnp.float32
    total = exp_size * slots
    all_rows = 2 * own_rows
    part = own_rows // CHUNKS
    anyplace = pl.BlockSpec(memory_space=pl.ANY)
    inside = pl.BlockSpec(memory_space=pltpu.VMEM)
    dma = pltpu.SemaphoreType.DMA
    n_out = 2 * block // TILE + 2 * rep_size
    scratch = [
        pltpu.VMEM((total, width), low),
        pltpu.VMEM((width, 2 * block), low),
        pltpu.VMEM((2 * block, width), low),
        pltpu.VMEM((own_rows, width), low),
        pltpu.VMEM((own_rows, width), low),
        pltpu.VMEM((all_rows, width), low),
        pltpu.VMEM((all_rows, 2 * block), low),
        pltpu.VMEM((all_rows, 2 * block), low),
        pltpu.VMEM((all_rows, width), low),
        pltpu.VMEM((own_rows, width), low),
        pltpu.VMEM((own_rows, width), low),
        pltpu.VMEM((own_rows, width), low),
        pltpu.VMEM((own_rows, width), low),
        pltpu.VMEM((own_rows, width), low),
        pltpu.VMEM((own_rows, width), low),
        pltpu.VMEM((total, width), low),
        pltpu.VMEM((part, width), wide),
        pltpu.VMEM((own_rows, 128), wide),
        pltpu.VMEM((own_rows, 128), wide),
        pltpu.VMEM((block, width), wide),
        pltpu.VMEM((block, width), low),
        pltpu.VMEM((depth, 2 * block), wide),
        pltpu.VMEM(((rep_size - 1) * depth, 2 * block), low),
        dma((exp_size,)),
        dma((exp_size,)),
        dma((7,)),
    ]
    scratch += [dma((CHUNKS,)) for _ in range(10)]
    scratch += [dma((2,)), dma((2,)), dma((exp_size,)), dma((exp_size,)), dma((n_out,))]
    flops = 2 * all_rows * width * 2 * block * 6
    return pl.pallas_call(
        functools.partial(expert_kernel, exp_size, rep_size, slots),
        out_shape=(
            jax.ShapeDtypeStruct((total, width), low),
            jax.ShapeDtypeStruct((block, width), wide),
            jax.ShapeDtypeStruct((block, width), low),
            jax.ShapeDtypeStruct((depth, 2 * block), wide),
            jax.ShapeDtypeStruct((rep_size - 1, depth, 2 * block), low),
            jax.ShapeDtypeStruct((1, width), wide),
            jax.ShapeDtypeStruct((1, width), wide),
        ),
        in_specs=[anyplace, inside, inside] + [anyplace] * 6 + [inside] * 3,
        out_specs=(anyplace,) * 5 + (inside, inside),
        scratch_shapes=scratch,
        compiler_params=pltpu.CompilerParams(
            collective_id=0, has_side_effects=True, vmem_limit_bytes=62 << 20
        ),
        cost_estimate=pl.CostEstimate(
            flops=flops, bytes_accessed=40 << 20, transcendentals=2 * all_rows * 2 * block
        ),
        name="experts",
    )(packed, compact, spread_m, *weights, gain, cent, cent_wide)


def gather_weights(stack, core, exp_bits):
    half = stack.shape[2] // 2
    pair = stack.reshape(stack.shape[0], stack.shape[1], 2, half)
    mine = jnp.where(core == 0, pair[:, :, 0], pair[:, :, 1])
    for bit in range(1, exp_bits):
        got = swap(mine, "exp", 1 << bit)
        mine = jnp.stack([mine[:, None], got[:, None]], axis=1)
        mine = mine.reshape((stack.shape[0], -1) + stack.shape[1:2] + (half,))
    mine = mine.reshape((stack.shape[0], -1) + stack.shape[1:2] + (half,))
    got = swap(mine, "exp", 1)
    mine = jnp.stack([mine, got], axis=2).reshape(stack.shape[0], -1, half)
    other = swap(mine, "rep", 1)
    return jnp.concatenate([mine, other], axis=2)


def reduce_weights(grads, exp_bits):
    count, rows, cols = grads.shape
    half = cols // 2
    total = grads[:, :, :half] + swap(grads[:, :, half:].astype(jnp.bfloat16), "rep", 1).astype(
        jnp.float32
    )
    total = total.reshape(count, -1, 2, rows >> exp_bits, half)
    total = total[:, :, 0] + swap(total[:, :, 1].astype(jnp.bfloat16), "exp", 1).astype(
        jnp.float32
    )
    for bit in range(exp_bits - 1, 0, -1):
        keep = total.shape[1] // 2
        total = total[:, :keep] + swap(
            total[:, keep:].astype(jnp.bfloat16), "exp", 1 << bit
        ).astype(jnp.float32)
    total = total[:, 0]
    total = total + swap(total.astype(jnp.bfloat16), "rep", 2).astype(jnp.float32)
    other = swap(total.astype(jnp.bfloat16), "rep", 1).astype(jnp.float32)
    return total, other


def masked_scores(queries3, keys3, allowed, factor):
    scores = (
        jnp.einsum("qhe,khe->hqk", queries3, keys3, preferred_element_type=jnp.float32) * factor
    )
    return jnp.where(allowed[None], scores, -1e30)


def shards(
    tokens,
    cotangent,
    doc_lengths,
    expert_of_token,
    w_query,
    w_key,
    w_value,
    w_output,
    attn_gain,
    w_inner,
    w_outer,
    expert_gain,
    centroids,
):
    exp_size = lax.axis_size("exp")
    rep_size = lax.axis_size("rep")
    exp_bits = exp_size.bit_length() - 1
    experts = exp_size // 2
    rep_at = lax.axis_index("rep")
    exp_at = lax.axis_index("exp")
    core = rep_at % 2
    first = exp_at % 2 == 0
    group = exp_at // 2
    row_count, width = tokens.shape
    head_dim = width // HEADS
    factor = head_dim ** (-0.5)
    half_width = width // 2
    low = jnp.bfloat16
    wide = jnp.float32

    inner_own = w_inner[0]
    block = inner_own.shape[1] // rep_size

    def inner_for(mask):
        dest = rep_at ^ mask
        return jnp.concatenate(
            [
                lax.dynamic_slice_in_dim(inner_own, dest * block, block, 1),
                lax.dynamic_slice_in_dim(inner_own, (dest ^ 2) * block, block, 1),
            ],
            axis=1,
        )

    weights = [inner_own]
    weights += [swap(inner_for(mask), "rep", mask) for mask in range(1, rep_size)]
    weights += [w_outer[0], swap(w_outer[0], "rep", 2)]

    expert_ids = jnp.arange(experts, dtype=jnp.int32)
    onehot = expert_of_token[:, None] == expert_ids[None, :]
    counts = jnp.sum(onehot.astype(wide), axis=0)
    pieces = [centroids[0], expert_gain[0], attn_gain, counts.astype(low)]
    small = lax.all_gather(jnp.concatenate(pieces), ("rep", "exp"), axis=0, tiled=False)
    small = small.reshape(rep_size, exp_size, -1)
    edges = [0]
    for piece in pieces:
        edges.append(edges[-1] + piece.shape[0])
    gain_attn = small[0, :, edges[2] : edges[3]].reshape(width).astype(wide)
    own_small = lax.dynamic_slice_in_dim(small, exp_at - exp_at % 2, 2, 1)
    centroid = jnp.swapaxes(own_small[:, :, edges[0] : edges[1]], 0, 1).reshape(width)
    gain_pair = own_small[:, :, edges[1] : edges[2]]
    gain_row = jnp.where(first, gain_pair[:, 0], gain_pair[:, 1]).reshape(width).astype(wide)
    group_counts = lax.dynamic_index_in_dim(small, rep_at, 0, False)[:, edges[3] : edges[4]]
    group_counts = jnp.sum(
        jnp.where(expert_ids[None, :] == group, group_counts.astype(wide), 0.0), axis=1
    ).astype(jnp.int32)

    qkv_w = gather_weights(jnp.stack([w_query, w_key, w_value]), core, exp_bits)
    out_w = gather_weights(w_output[None], core, exp_bits)[0]
    inputs = tokens.astype(wide)
    unit_a, scale_a = norm_stats(inputs)
    act_a = xor_order((unit_a * gain_attn).astype(low), 1, exp_at, exp_size)
    queries, keys_low, values_low = [plain_product(act_a, qkv_w[i]).astype(low) for i in range(3)]
    queries3 = queries.reshape(row_count, HEADS, head_dim)
    keys3 = keys_low.reshape(row_count, HEADS, head_dim)
    values3 = values_low.reshape(row_count, HEADS, head_dim)
    doc_ends = jnp.cumsum(doc_lengths[0])
    positions = jnp.arange(row_count, dtype=jnp.int32)
    segment = jnp.sum((positions[:, None] >= doc_ends[None, :]).astype(jnp.int32), axis=1)
    allowed = (segment[:, None] == segment[None, :]) & (positions[:, None] >= positions[None, :])
    scores = masked_scores(queries3, keys3, allowed, factor)
    row_top = jnp.max(scores, axis=-1, keepdims=True)
    row_total = jnp.sum(jnp.exp(scores - row_top), axis=-1, keepdims=True)
    log_total = row_top + jnp.log(row_total)
    probs_low = jnp.exp(scores - log_total).astype(low)
    context = jnp.einsum("hqk,khe->qhe", probs_low, values3, preferred_element_type=wide)
    context = context.reshape(row_count, width).astype(low)
    context_x = xor_order(xor_order(context, 1, core, 2), 1, exp_at, exp_size)
    hidden = inputs + xor_order(plain_product(context_x, out_w), 1, core, 2)

    slots = -(-3 * row_count // exp_size // 16) * 16
    lower = (positions[:, None] > positions[None, :]).astype(low)
    earlier = plain_product(lower, onehot.astype(low))
    rank_in = jnp.sum(jnp.where(onehot, earlier, 0.0), axis=1).astype(jnp.int32)
    position = expert_of_token * slots + rank_in
    all_slots = experts * slots
    pick = (jnp.arange(all_slots, dtype=jnp.int32)[:, None] == position[None, :]).astype(low)
    sent_rows = hidden.astype(low)
    packed_sent = plain_product(pick, sent_rows).astype(low).reshape(experts, 1, slots, width)
    packed_cot = plain_product(pick, cotangent).astype(low).reshape(experts, 1, slots, width)
    packed = jnp.concatenate([packed_sent, packed_cot], axis=1).reshape(exp_size, slots, width)
    starts = jnp.cumsum(group_counts) - group_counts
    slot_at = jnp.arange(slots, dtype=jnp.int32)
    row_of_slot = jnp.where(
        slot_at[None, :] < group_counts[:, None], starts[:, None] + slot_at[None, :], -1
    ).reshape(-1)
    own_rows = 2 * row_count
    compact = (jnp.arange(own_rows, dtype=jnp.int32)[:, None] == row_of_slot[None, :]).astype(low)
    spread_m = (row_of_slot[:, None] == jnp.arange(own_rows, dtype=jnp.int32)[None, :]).astype(low)
    cent_wide = jnp.broadcast_to(centroid[:, None], (width, 128))
    home, outer_keep, outer_send, inner_keep, inner_send, gain_grad, grad_centre = run_experts(
        exp_size,
        rep_size,
        slots,
        packed.reshape(exp_size * slots, width),
        compact,
        spread_m,
        weights,
        gain_row[None],
        centroid.astype(wide)[None],
        cent_wide,
    )
    gain_grad = gain_grad[0]
    grad_centre = grad_centre[0]
    home = home.reshape(experts, 2, slots, width)
    grad_home = tn_product(pick, home[:, 0].reshape(all_slots, width))
    branch_home = tn_product(pick, home[:, 1].reshape(all_slots, width))
    output = (hidden + branch_home).astype(low)

    grad_w_outer = (outer_keep + swap(outer_send, "rep", 2).astype(wide))[None]
    mine = inner_keep.reshape(width // rep_size, 2, block)
    got = [
        swap(inner_send[mask - 1], "rep", mask).astype(wide).reshape(mine.shape)
        for mask in range(1, rep_size)
    ]
    ordered = jnp.stack(
        [
            mine[:, 0] + got[1][:, 1],
            got[0][:, 0] + got[2][:, 1],
            mine[:, 1] + got[1][:, 0],
            got[0][:, 1] + got[2][:, 0],
        ],
        axis=1,
    )
    grad_w_inner = xor_order(ordered.reshape(width // rep_size, -1), 1, rep_at, rep_size)[None]

    other_centre = swap(grad_centre[half_width:], "exp", 1)
    centre_half = jnp.where(first, grad_centre[:half_width], other_centre)

    grad_hidden = cotangent.astype(wide) + grad_home
    grad_attn = grad_hidden.astype(low)
    grad_attn_c = xor_order(grad_attn, 1, core, 2)
    grad_w_o = tn_product(context_x, grad_attn_c)
    share_o = reduce_weights(grad_w_o[None], exp_bits)
    grad_context = nt_product(grad_attn_c, out_w).astype(low)
    grad_context = xor_order(xor_order(grad_context, 1, exp_at, exp_size), 1, core, 2)
    grad_context3 = grad_context.reshape(row_count, HEADS, head_dim)
    again_scores = masked_scores(queries3, keys3, allowed, factor)
    attn_probs = jnp.exp(again_scores - log_total)
    grad_probs = jnp.einsum("qhe,khe->hqk", grad_context3, values3, preferred_element_type=wide)
    inner_sum = jnp.sum(attn_probs * grad_probs, axis=-1, keepdims=True)
    grad_scores = (attn_probs * (grad_probs - inner_sum)).astype(low)
    grad_query = (
        jnp.einsum("hqk,khe->qhe", grad_scores, keys3, preferred_element_type=wide) * factor
    ).astype(low)
    grad_key = (
        jnp.einsum("hqk,qhe->khe", grad_scores, queries3, preferred_element_type=wide) * factor
    ).astype(low)
    grad_value = jnp.einsum(
        "hqk,qhe->khe", attn_probs.astype(low), grad_context3, preferred_element_type=wide
    ).astype(low)
    grads3 = [g.reshape(row_count, width) for g in (grad_query, grad_key, grad_value)]
    grad_w_qkv = jnp.stack([tn_product(act_a, g) for g in grads3])
    share_qkv = reduce_weights(grad_w_qkv, exp_bits)
    grad_act = sum(nt_product(g, qkv_w[i]) for i, g in enumerate(grads3))
    grad_act = xor_order(grad_act, 1, exp_at, exp_size)
    grad_gain_a = jnp.sum(grad_act * unit_a, axis=0)
    grad_tokens = grad_hidden + norm_back(grad_act, unit_a, scale_a, gain_attn)

    def true_halves(pair):
        mine_half, other_half = pair
        return xor_order(jnp.concatenate([mine_half, other_half], axis=-1), 2, core, 2)

    full_o = true_halves(share_o)[0]
    full_qkv = true_halves(share_qkv)

    rep_sums = lax.psum(jnp.concatenate([gain_grad, centre_half]), "rep")
    gain_len = width // rep_size
    centre_len = half_width // rep_size
    grad_expert_gain = lax.dynamic_slice_in_dim(rep_sums, rep_at * gain_len, gain_len)[None]
    grad_centroids = lax.dynamic_slice_in_dim(
        rep_sums, width + rep_at * centre_len, centre_len
    )[None]
    attn_sums = lax.psum(grad_gain_a, ("rep", "exp"))
    attn_len = width // exp_size
    share_gain = lax.dynamic_slice_in_dim(attn_sums, exp_at * attn_len, attn_len)
    return (
        output,
        grad_tokens,
        full_qkv[0],
        full_qkv[1],
        full_qkv[2],
        full_o,
        share_gain,
        grad_w_inner,
        grad_w_outer,
        grad_expert_gain,
        grad_centroids,
    )


def solution(mesh):
    placed = (
        P(("rep", "exp"), None),
        P(("rep", "exp"), None),
        P(("rep", "exp"), None),
        P(("rep", "exp")),
        P("exp", None),
        P("exp", None),
        P("exp", None),
        P("exp", None),
        P("exp"),
        P("exp", "rep", None),
        P("exp", "rep", None),
        P("exp", "rep"),
        P("exp", "rep"),
    )
    return jax.shard_map(
        shards,
        mesh=mesh,
        in_specs=placed,
        out_specs=(
            P(("rep", "exp"), None),
            P(("rep", "exp"), None),
            P("exp", None),
            P("exp", None),
            P("exp", None),
            P("exp", None),
            P("exp"),
            P("exp", "rep", None),
            P("exp", "rep", None),
            P("exp", "rep"),
            P("exp", "rep"),
        ),
        check_vma=False,
    )
```

```python
import functools

import jax
import jax.numpy as jnp
from jax import lax
from jax.experimental import pallas as pl
from jax.experimental.pallas import tpu as pltpu
from jax.sharding import PartitionSpec as P

HEADS = 16
EPS = 1e-05
ROOT_HALF = 0.7071067811865476
INV_ROOT_TAU = 0.3989422804014327
CHUNKS = 2


def swap(shard, axis, mask):
    return lax.ppermute(shard, axis, [(i, i ^ mask) for i in range(lax.axis_size(axis))])


def plain_product(left_mat, right_mat):
    return jnp.dot(left_mat, right_mat, preferred_element_type=jnp.float32)


def tn_product(left_mat, right_mat):
    return lax.dot_general(
        left_mat, right_mat, (((0,), (0,)), ((), ())), preferred_element_type=jnp.float32
    )


def nt_product(left_mat, right_mat):
    return lax.dot_general(
        left_mat, right_mat, (((1,), (1,)), ((), ())), preferred_element_type=jnp.float32
    )


def xor_order(array, axis, index, count):
    bits = count.bit_length() - 1
    shape = array.shape
    array = array.reshape(shape[:axis] + (2,) * bits + (shape[axis] // count,) + shape[axis + 1 :])
    for at in range(bits):
        flag = (index >> (bits - 1 - at)) & 1
        if isinstance(flag, int):
            array = jnp.flip(array, axis + at) if flag else array
        else:
            array = jnp.where(flag == 1, jnp.flip(array, axis + at), array)
    return array.reshape(shape)


def norm_stats(rows):
    row_mean = jnp.mean(rows, axis=-1, keepdims=True)
    centered = rows - row_mean
    variance = jnp.mean(centered * centered, axis=-1, keepdims=True)
    inv_scale = lax.rsqrt(variance + EPS)
    return centered * inv_scale, inv_scale


def norm_back(grad_out, unit_rows, inv_scale, gain_row):
    grad_unit = grad_out * gain_row
    centred_grad = grad_unit - jnp.mean(grad_unit, axis=-1, keepdims=True)
    return (
        centred_grad - unit_rows * jnp.mean(grad_unit * unit_rows, axis=-1, keepdims=True)
    ) * inv_scale


MESH = pl.DeviceIdType.MESH
TILE = 256
ROWS = 64


def remote(src, dst, send_sem, recv_sem, device):
    return pltpu.make_async_remote_copy(
        src_ref=src,
        dst_ref=dst,
        send_sem=send_sem,
        recv_sem=recv_sem,
        device_id=device,
        device_id_type=MESH,
    )


def row_stats(rows):
    row_mean = jnp.mean(rows, axis=-1, keepdims=True)
    centered = rows - row_mean
    variance = jnp.mean(centered * centered, axis=-1, keepdims=True)
    inv_scale = lax.rsqrt(variance + EPS)
    return centered * inv_scale, inv_scale


def attend_kernel(
    exp_size,
    rep_size,
    slots,
    tokens,
    cotangent,
    doc,
    expert_of,
    w_query,
    w_key,
    w_value,
    w_output,
    gain_a,
    w_inner,
    w_outer,
    gain_e,
    cent,
    attn_w,
    inner_w,
    outer_w,
    arrived,
    counts_all,
    cents,
    gains_e,
    hidden,
    qkv,
    probs,
    normed_a,
    context,
    pick,
    weights,
    small_all,
    gain_row,
    gain_v,
    packed_x,
    packed_c,
    bias,
    counts_v,
    cent_v,
    own_s,
    line_s,
    line_r,
    side_s,
    side_r,
    core_s,
    core_r,
    weight_s,
    weight_r,
    disp_s,
    disp_r,
    count_s,
    count_r,
    cent_s,
    cent_r,
    gain_s,
    gain_r,
    out_s,
):
    low = jnp.bfloat16
    wide = jnp.float32
    rep_at = lax.axis_index("rep")
    exp_at = lax.axis_index("exp")
    core = rep_at % 2
    group = exp_at // 2
    side = exp_at % 2
    groups = exp_size // 2
    rows_n, width = tokens.shape
    half = width // 2
    block = w_query.shape[0]
    depth = w_inner.shape[0]
    ff_block = w_outer.shape[0]
    core_peer = (rep_at ^ 1, exp_at)
    side_peer = (rep_at, exp_at ^ 1)

    def block_rows(at):
        return pl.ds(pl.multiple_of(at * block, block), block)

    own_loads = []
    for at, source in enumerate((w_query, w_key, w_value, w_output)):
        own_loads.append(
            pltpu.make_async_copy(source, weights.at[at, block_rows(exp_at)], own_s.at[at])
        )
    for load in own_loads:
        load.start()

    barrier = pltpu.get_barrier_semaphore()
    for mask in range(1, rep_size):
        for flip in range(2):
            pl.semaphore_signal(
                barrier, inc=1, device_id=(rep_at ^ mask, exp_at ^ flip), device_id_type=MESH
            )

    @pl.loop(1, exp_size)
    def _(at):
        pl.semaphore_signal(barrier, inc=1, device_id=(rep_at, exp_at ^ at), device_id_type=MESH)

    pl.semaphore_wait(barrier, exp_size - 1 + 2 * (rep_size - 1))

    outer_copy = remote(
        w_outer, outer_w.at[ff_block:], weight_s.at[0], weight_r.at[0], (rep_at ^ 2, exp_at)
    )
    outer_copy.start()
    outer_own = pltpu.make_async_copy(w_outer, outer_w.at[:ff_block], own_s.at[5])
    outer_own.start()

    for load in own_loads:
        load.wait()

    picks = (slice(0, 3), slice(3, 4))
    own_half = pl.ds(pl.multiple_of(core * half, half), half)

    def view(kind, at):
        return weights.at[picks[kind], block_rows(at), own_half]

    def line_copy(kind, source, step):
        at = 2 * source + side
        return remote(
            view(kind, at),
            view(kind, at),
            line_s.at[kind, (1 + step) // 2, source],
            line_r.at[kind, source],
            (rep_at, exp_at + 2 * step),
        )

    def line_wait(kind, source):
        at = 2 * source + side
        remote(
            view(kind, at), view(kind, at), line_s.at[kind, 0, source], line_r.at[kind, source], side_peer
        ).wait_recv()

    def side_copy(kind, source):
        at = 2 * source + side
        return remote(
            view(kind, at), view(kind, at), side_s.at[kind, source], side_r.at[kind, source], side_peer
        )

    def side_wait(kind, source):
        at = 2 * source + 1 - side
        remote(
            view(kind, at), view(kind, at), side_s.at[kind, source], side_r.at[kind, source], side_peer
        ).wait_recv()

    def core_copy(kind, at):
        return remote(view(kind, at), view(kind, at), core_s.at[kind, at], core_r.at[kind, at], core_peer)

    def core_wait(kind, at):
        other = pl.ds(pl.multiple_of((1 - core) * half, half), half)
        there = weights.at[picks[kind], block_rows(at), other]
        remote(there, there, core_s.at[kind, at], core_r.at[kind, at], core_peer).wait_recv()

    def first_sends(kind):
        @pl.when(group + 1 < groups)
        def _():
            line_copy(kind, group, 1).start()

        @pl.when(group >= 1)
        def _():
            line_copy(kind, group, -1).start()

        side_copy(kind, group).start()

    def take_side(kind, source):
        side_wait(kind, source)
        core_copy(kind, 2 * source + 1 - side).start()

    def gather_step(kind, step):
        @pl.when(group - step >= 0)
        def _():
            source = group - step
            line_wait(kind, source)

            @pl.when(group + 1 < groups)
            def _():
                line_copy(kind, source, 1).start()

            side_copy(kind, source).start()
            core_copy(kind, 2 * source + side).start()

        @pl.when(group + step < groups)
        def _():
            source = group + step
            line_wait(kind, source)

            @pl.when(group >= 1)
            def _():
                line_copy(kind, source, -1).start()

            side_copy(kind, source).start()
            core_copy(kind, 2 * source + side).start()

        @pl.when(group - step + 1 >= 0)
        def _():
            take_side(kind, group - step + 1)

        @pl.when((step > 1) & (group + step - 1 < groups))
        def _():
            take_side(kind, group + step - 1)

    def gather_end(kind):
        last = groups - 1

        @pl.when(group - last >= 0)
        def _():
            take_side(kind, group - last)

        @pl.when((groups > 1) & (group + last < groups))
        def _():
            take_side(kind, group + last)

        @pl.loop(0, exp_size)
        def _(at):
            @pl.when(at != exp_at)
            def _():
                core_wait(kind, at)

    first_sends(0)
    first_sends(1)

    inner_rows = pl.ds(pl.multiple_of(rep_at * depth, depth), depth)

    def ff_cols(at):
        return pl.ds(pl.multiple_of(at * ff_block, ff_block), ff_block)

    def inner_copies(mask):
        dest = rep_at ^ mask
        found = []
        for part in range(2):
            source = w_inner.at[:, ff_cols(dest ^ (2 * part))]
            target = inner_w.at[inner_rows, part * ff_block : (part + 1) * ff_block]
            if mask == 0:
                found.append(pltpu.make_async_copy(source, target, weight_s.at[1 + part]))
            else:
                found.append(
                    remote(
                        source,
                        target,
                        weight_s.at[1 + 2 * mask + part],
                        weight_r.at[1 + 2 * mask + part],
                        (dest, exp_at),
                    )
                )
        return found

    for mask in range(rep_size):
        for copy in inner_copies(mask):
            copy.start()

    lanes = counts_v.shape[1]
    expert_row = expert_of[...]
    onehot = (
        lax.broadcasted_iota(jnp.int32, (lanes, rows_n), 0) == expert_row
    ).astype(wide)
    before = (
        lax.broadcasted_iota(jnp.int32, (rows_n, rows_n), 0)
        < lax.broadcasted_iota(jnp.int32, (rows_n, rows_n), 1)
    ).astype(low)
    earlier = jnp.dot(onehot.astype(low), before, preferred_element_type=wide)
    rank = jnp.sum(earlier * onehot, axis=0, keepdims=True).astype(jnp.int32)
    position = expert_row * slots + rank
    pick[...] = (
        lax.broadcasted_iota(jnp.int32, pick.shape, 0) == position
    ).astype(wide).astype(low)
    counts_v[:8, :] = lax.dot_general(
        jnp.ones((8, rows_n), low),
        onehot.astype(low),
        (((1,), (1,)), ((), ())),
        preferred_element_type=wide,
    )
    counts_v[8:, :block] = jnp.broadcast_to(gain_a[...].astype(wide), (8, block))
    cent_v[...] = jnp.broadcast_to(cent[...].astype(wide), cent_v.shape)
    gain_v[...] = jnp.broadcast_to(gain_e[...].astype(wide), gain_v.shape)

    def eight(at):
        return pl.ds(pl.multiple_of(at * 8, 8), 8)

    def sixteen(at):
        return pl.ds(pl.multiple_of(at * 16, 16), 16)

    def count_copy(dest):
        return remote(
            counts_v, small_all.at[sixteen(exp_at)], count_s.at[dest], count_r.at[exp_at], (rep_at, dest)
        )

    count_own = pltpu.make_async_copy(counts_v, small_all.at[sixteen(exp_at)], count_s.at[exp_at])
    count_own.start()

    @pl.loop(1, exp_size)
    def _(at):
        count_copy(exp_at ^ at).start()

    cent_at = side * rep_size + rep_at

    def cent_copy(mask, flip):
        return remote(
            cent_v,
            cents.at[eight(cent_at)],
            cent_s.at[flip * rep_size + mask],
            cent_r.at[flip * rep_size + mask],
            (rep_at ^ mask, exp_at ^ flip),
        )

    cent_own = pltpu.make_async_copy(cent_v, cents.at[eight(cent_at)], cent_s.at[0])
    cent_own.start()
    cent_pairs = [(m, f) for m in range(rep_size) for f in range(2) if m or f]
    for mask, flip in cent_pairs:
        cent_copy(mask, flip).start()

    def gain_copy(mask):
        return remote(
            gain_v, gains_e.at[eight(rep_at)], gain_s.at[mask], gain_r.at[mask], (rep_at ^ mask, exp_at)
        )

    gain_own = pltpu.make_async_copy(gain_v, gains_e.at[eight(rep_at)], gain_s.at[0])
    gain_own.start()
    for mask in range(1, rep_size):
        gain_copy(mask).start()

    count_own.wait()

    @pl.loop(1, exp_size)
    def _(at):
        source = exp_at ^ at
        remote(
            counts_v, small_all.at[sixteen(source)], count_s.at[source], count_r.at[source], (rep_at, source)
        ).wait()

    small_store = pltpu.make_async_copy(small_all, counts_all, out_s.at[1])
    small_store.start()

    tiled = jnp.dot(
        small_all[...].astype(low),
        (
            lax.broadcasted_iota(jnp.int32, (lanes, width), 1) % block
            == lax.broadcasted_iota(jnp.int32, (lanes, width), 0)
        ).astype(wide).astype(low),
        preferred_element_type=wide,
    )
    chosen_row = lax.broadcasted_iota(jnp.int32, (16 * exp_size, width), 0) == (
        16 * (lax.broadcasted_iota(jnp.int32, (16 * exp_size, width), 1) // block) + 8
    )
    gain_row[...] = jnp.sum(jnp.where(chosen_row, tiled, 0.0), axis=0, keepdims=True)

    @pl.loop(0, rows_n // ROWS)
    def _(step):
        here = pl.ds(pl.multiple_of(step * ROWS, ROWS), ROWS)
        unit, _ = row_stats(tokens[here, :].astype(wide))
        normed_a[here, :] = (unit * gain_row[...]).astype(low)

    down = lax.broadcasted_iota(jnp.int32, (rows_n, rows_n), 0)
    along = lax.broadcasted_iota(jnp.int32, (rows_n, rows_n), 1)
    end = jnp.int32(0)
    seg_down = jnp.zeros((rows_n, rows_n), jnp.int32)
    seg_along = jnp.zeros((rows_n, rows_n), jnp.int32)
    for at in range(doc.shape[1]):
        end = end + doc[0, at]
        seg_down = seg_down + (down >= end).astype(jnp.int32)
        seg_along = seg_along + (along >= end).astype(jnp.int32)
    bias[...] = jnp.where((seg_down == seg_along) & (down >= along), 0.0, -1e30)

    @pl.loop(1, groups)
    def _(step):
        gather_step(0, step)

    gather_end(0)

    def slot_rows(at):
        return pl.ds(pl.multiple_of(at * slots, slots), slots)

    def disp_copy(source, dest):
        return remote(
            source.at[slot_rows(dest // 2)],
            arrived.at[slot_rows(exp_at)],
            disp_s.at[dest],
            disp_r.at[exp_at],
            (rep_at, dest),
        )

    def dispatch(source, flip):
        @pl.loop(0, groups)
        def _(at):
            dest = 2 * (group ^ at) + flip

            @pl.when(dest != exp_at)
            def _():
                disp_copy(source, dest).start()

            @pl.when(dest == exp_at)
            def _():
                pltpu.make_async_copy(
                    source.at[slot_rows(group)], arrived.at[slot_rows(exp_at)], disp_s.at[exp_at]
                ).start()

    @pl.loop(0, width // TILE)
    def _(step):
        cols = pl.ds(pl.multiple_of(step * TILE, TILE), TILE)
        packed_c[:, cols] = jnp.dot(
            pick[...], cotangent[:, cols], preferred_element_type=wide
        ).astype(low)

    dispatch(packed_c, 1)

    for at in range(3):

        @pl.loop(0, width // TILE)
        def _(step):
            cols = pl.ds(pl.multiple_of(step * TILE, TILE), TILE)
            qkv[at, :, cols] = jnp.dot(
                normed_a[...], weights[at, :, cols], preferred_element_type=wide
            ).astype(low)

    head_dim = width // HEADS
    pair = 2 * head_dim
    factor = head_dim ** (-0.5)
    lane = lax.broadcasted_iota(jnp.int32, (rows_n, pair), 1)
    pairs = HEADS // 2
    parts = 4
    for part in range(parts):
        low_step = 1 + part * (groups - 1) // parts
        high_step = 1 + (part + 1) * (groups - 1) // parts

        @pl.loop(low_step, high_step)
        def _(step):
            gather_step(1, step)

        @pl.loop(part * pairs // parts, (part + 1) * pairs // parts)
        def _(at):
            cols = pl.ds(pl.multiple_of(at * pair, pair), pair)
            q_pair = qkv[0, :, cols]
            k_pair = qkv[1, :, cols]
            v_pair = qkv[2, :, cols]
            found = []
            for which in range(2):
                chosen = (lane >= head_dim) if which else (lane < head_dim)
                q_one = jnp.where(chosen, q_pair, jnp.zeros_like(q_pair))
                scores = (
                    lax.dot_general(
                        q_one, k_pair, (((1,), (1,)), ((), ())), preferred_element_type=wide
                    )
                    * factor
                    + bias[...]
                )
                top = jnp.max(scores, axis=1, keepdims=True)
                raised = jnp.exp(scores - top)
                total = jnp.sum(raised, axis=1, keepdims=True)
                prob = (raised * (1.0 / total)).astype(low)
                probs[pl.ds(pl.multiple_of((2 * at + which) * rows_n, rows_n), rows_n), :] = prob
                found.append(jnp.dot(prob, v_pair, preferred_element_type=wide))
            context[:, cols] = jnp.where(lane < head_dim, found[0], found[1]).astype(low)

    gather_end(1)
    store = pltpu.make_async_copy(weights, attn_w, out_s.at[0])
    store.start()

    @pl.loop(0, width // TILE)
    def _(step):
        cols = pl.ds(pl.multiple_of(step * TILE, TILE), TILE)
        sum_here = tokens[:, cols].astype(wide) + jnp.dot(
            context[...], weights[3, :, cols], preferred_element_type=wide
        )
        hidden[:, cols] = sum_here
        packed_x[:, cols] = jnp.dot(
            pick[...], sum_here.astype(low), preferred_element_type=wide
        ).astype(low)

    dispatch(packed_x, 0)

    store.wait()
    outer_copy.wait()
    outer_own.wait()
    for mask in range(rep_size):
        for copy in inner_copies(mask):
            copy.wait()
    for kind in range(2):
        side_copy(kind, group).wait_send()

        @pl.loop(0, groups)
        def _(source):
            @pl.when(source != group)
            def _():
                side_copy(kind, source).wait_send()

            @pl.when((source <= group) & (group + 1 < groups))
            def _():
                line_copy(kind, source, 1).wait_send()

            @pl.when((source >= group) & (group >= 1))
            def _():
                line_copy(kind, source, -1).wait_send()

        @pl.loop(0, exp_size)
        def _(at):
            @pl.when(at != exp_at)
            def _():
                core_copy(kind, at).wait_send()

    small_store.wait()
    cent_own.wait()
    gain_own.wait()
    for mask in range(1, rep_size):
        gain_copy(mask).wait()
    for mask, flip in cent_pairs:
        cent_copy(mask, flip).wait()

    @pl.loop(1, exp_size)
    def _(at):
        source = exp_at ^ at
        remote(
            packed_c.at[slot_rows(source // 2)],
            arrived.at[slot_rows(source)],
            disp_s.at[source],
            disp_r.at[source],
            (rep_at, source),
        ).wait()

    pltpu.make_async_copy(
        packed_c.at[slot_rows(group)], arrived.at[slot_rows(exp_at)], disp_s.at[exp_at]
    ).wait()


def run_attend(exp_size, rep_size, slots, tokens, cotangent, doc, expert_of, attn, gain_a, w_inner, w_outer, gain_e, cent):
    rows_n, width = tokens.shape
    low = jnp.bfloat16
    wide = jnp.float32
    groups = exp_size // 2
    depth = w_inner.shape[0]
    ff_block = w_outer.shape[0]
    anyplace = pl.BlockSpec(memory_space=pl.ANY)
    inside = pl.BlockSpec(memory_space=pltpu.VMEM)
    dma = pltpu.SemaphoreType.DMA
    shape = jax.ShapeDtypeStruct
    return pl.pallas_call(
        functools.partial(attend_kernel, exp_size, rep_size, slots),
        out_shape=(
            shape((4, width, width), low),
            shape((width, 2 * ff_block), low),
            shape((2 * ff_block, width), low),
            shape((exp_size * slots, width), low),
            shape((exp_size * 16, 128), wide),
            shape((2 * rep_size * 8, cent.shape[1]), wide),
            shape((rep_size * 8, depth), wide),
            shape((rows_n, width), wide),
            shape((3, rows_n, width), low),
            shape((HEADS * rows_n, rows_n), low),
            shape((rows_n, width), low),
            shape((rows_n, width), low),
            shape((groups * slots, rows_n), low),
        ),
        in_specs=[inside, inside, pl.BlockSpec(memory_space=pltpu.SMEM), inside]
        + [anyplace] * 4
        + [inside, anyplace, anyplace, inside, inside],
        out_specs=(anyplace,) * 7 + (inside,) * 6,
        scratch_shapes=[
            pltpu.VMEM((4, width, width), low),
            pltpu.VMEM((exp_size * 16, 128), wide),
            pltpu.VMEM((1, width), wide),
            pltpu.VMEM((8, depth), wide),
            pltpu.VMEM((groups * slots, width), low),
            pltpu.VMEM((groups * slots, width), low),
            pltpu.VMEM((rows_n, rows_n), wide),
            pltpu.VMEM((16, 128), wide),
            pltpu.VMEM((8, cent.shape[1]), wide),
            dma((6,)),
            dma((2, 2, groups)),
            dma((2, groups)),
            dma((2, groups)),
            dma((2, groups)),
            dma((2, exp_size)),
            dma((2, exp_size)),
            dma((1 + 2 * rep_size,)),
            dma((1 + 2 * rep_size,)),
            dma((exp_size,)),
            dma((exp_size,)),
            dma((exp_size,)),
            dma((exp_size,)),
            dma((2 * rep_size,)),
            dma((2 * rep_size,)),
            dma((rep_size,)),
            dma((rep_size,)),
            dma((2,)),
        ],
        compiler_params=pltpu.CompilerParams(
            collective_id=1, has_side_effects=True, vmem_limit_bytes=56 << 20
        ),
        cost_estimate=pl.CostEstimate(
            flops=10 * rows_n * width * width,
            bytes_accessed=40 << 20,
            transcendentals=HEADS * rows_n * rows_n,
        ),
        name="attend",
    )(tokens, cotangent, doc, expert_of, *attn, gain_a, w_inner, w_outer, gain_e, cent)


def expert_kernel(
    exp_size,
    rep_size,
    slots,
    arrived_h,
    inner_h,
    outer_h,
    counts_all,
    cents,
    gains_e,
    home,
    outer_keep,
    outer_send,
    inner_keep,
    inner_send,
    centre_parts,
    arrived,
    spread_m,
    offsets,
    cent_b,
    gain,
    centre_grad,
    centre_v,
    inner_w,
    outer_w,
    own_x,
    own_cot,
    normed,
    active,
    slope,
    states,
    fwd_send,
    fwd_recv,
    bwd_send,
    bwd_recv,
    hop,
    back,
    spread,
    acc,
    gates,
    gate_grads,
    outer_keep_v,
    outer_send_v,
    inner_keep_v,
    inner_send_v,
    load_sem,
    centre_s,
    centre_r,
    norm_s,
    norm_r,
    state_s,
    state_r,
    fwd_s,
    fwd_r,
    bwd_s,
    bwd_r,
    hop_s,
    hop_r,
    gate_s,
    gate_r,
    ret_s,
    ret_r,
    out_sem,
):
    low = jnp.bfloat16
    wide = jnp.float32
    rep_at = lax.axis_index("rep")
    exp_at = lax.axis_index("exp")
    first = exp_at % 2 == 0
    second = exp_at % 2 == 1
    core_peer = (rep_at ^ 1, exp_at)
    side_peer = (rep_at, exp_at ^ 1)
    width = own_x.shape[1]
    own_rows = own_x.shape[0]
    part = own_rows // CHUNKS
    wide_ff = inner_w.shape[1]
    block = wide_ff // 2
    depth = width // rep_size

    def slot_rows(at):
        return pl.ds(pl.multiple_of(at * slots, slots), slots)

    def inner_rows(mask):
        return pl.ds(pl.multiple_of((rep_at ^ mask) * depth, depth), depth)

    loads = [
        pltpu.make_async_copy(arrived_h, arrived, load_sem.at[0]),
        pltpu.make_async_copy(inner_h, inner_w, load_sem.at[1]),
        pltpu.make_async_copy(outer_h, outer_w, load_sem.at[2]),
    ]
    for load in loads:
        load.start()

    barrier = pltpu.get_barrier_semaphore()
    for mask in range(1, rep_size):
        for flip in range(2):
            pl.semaphore_signal(
                barrier, inc=1, device_id=(rep_at ^ mask, exp_at ^ flip), device_id_type=MESH
            )

    @pl.loop(1, exp_size)
    def _(at):
        pl.semaphore_signal(barrier, inc=1, device_id=(rep_at, exp_at ^ at), device_id_type=MESH)

    counted = counts_all.shape[0]
    group = exp_at // 2
    lane = lax.broadcasted_iota(jnp.int32, (counted, 128), 1)
    mine = jnp.sum(
        jnp.where(lane == group, counts_all[...], 0.0), axis=1, keepdims=True
    )
    mine = jnp.broadcast_to(mine, (counted, 128))
    down = lax.broadcasted_iota(jnp.int32, (counted, counted), 0)
    along = lax.broadcasted_iota(jnp.int32, (counted, counted), 1)
    ahead = ((along // 16 < down // 16) & (along % 16 == 0)).astype(wide).astype(low)
    offsets[0] = jnp.dot(ahead, mine.astype(low), preferred_element_type=wide)
    offsets[1] = mine
    slot_iota = lax.broadcasted_iota(jnp.int32, (slots, own_rows), 0)
    row_iota = lax.broadcasted_iota(jnp.int32, (slots, own_rows), 1)

    @pl.loop(0, exp_size)
    def _(at):
        eight = pl.ds(pl.multiple_of(at * 16, 16), 8)
        start = offsets[0, eight, :][:1, :1].astype(jnp.int32)
        limit = offsets[1, eight, :][:1, :1].astype(jnp.int32)
        spread_m[slot_rows(at), :] = (
            ((slot_iota + start) == row_iota) & (slot_iota < limit)
        ).astype(wide).astype(low)

    piece = cents.shape[1]
    for at in range(width // piece):
        cent_b[:, at * piece : (at + 1) * piece] = jnp.broadcast_to(
            cents[at * 8 : at * 8 + 1, :], (cent_b.shape[0], piece)
        ).astype(low)
    for at in range(rep_size):
        gain[:, at * depth : (at + 1) * depth] = gains_e[at * 8 : at * 8 + 1, :]
    loads[0].wait()

    for at in range(width // TILE):
        cols = slice(at * TILE, (at + 1) * TILE)
        rows_low = lax.dot_general(
            spread_m[...],
            arrived[:, cols],
            (((0,), (0,)), ((), ())),
            preferred_element_type=wide,
        ).astype(low)

        @pl.when(first)
        def _():
            own_x[:, cols] = rows_low

        @pl.when(second)
        def _():
            own_cot[:, cols] = rows_low

    pl.semaphore_wait(barrier, exp_size - 1 + 2 * (rep_size - 1))

    gate_copy = remote(gates, gates, gate_s.at[0], gate_r.at[0], side_peer)
    grad_copy = remote(gate_grads, gate_grads, gate_s.at[1], gate_r.at[1], side_peer)

    @pl.when(first)
    def _():
        logit = lax.dot_general(
            own_x[...], cent_b[...], (((1,), (1,)), ((), ())), preferred_element_type=wide
        )
        gates[...] = jax.nn.sigmoid(logit)
        gate_copy.start()

    def hop_forward(at):
        rows = pl.ds(at * part, part)
        return remote(hop.at[rows], own_x.at[rows], hop_s.at[at], hop_r.at[at], side_peer)

    def own_slice(at):
        return pl.ds(at * 2 * part + part, part)

    def other_slice(at):
        return pl.ds(at * 2 * part, part)

    def hop_backward(at):
        rows = pl.ds(at * part, part)
        return remote(
            hop.at[rows], states.at[own_slice(at)], hop_s.at[at], hop_r.at[at], side_peer
        )

    for load in loads[1:]:
        load.wait()

    def forward(at):
        base = at * part

        @pl.when(second)
        def _():
            hop_forward(at).wait_recv()

        @pl.loop(0, part // ROWS)
        def _(step):
            off = pl.multiple_of(step * ROWS, ROWS)
            unit, _ = row_stats(own_x[pl.ds(base + off, ROWS), :].astype(wide))
            normed[pl.ds(at * 2 * part + part + off, ROWS), :] = (unit * gain[...]).astype(low)

        norm_copy = remote(
            normed.at[own_slice(at)], normed.at[other_slice(at)], norm_s.at[at], norm_r.at[at], core_peer
        )
        norm_copy.start()
        norm_copy.wait_recv()

        @pl.loop(0, wide_ff // TILE)
        def _(step):
            cols = pl.ds(pl.multiple_of(step * TILE, TILE), TILE)
            inner = jnp.dot(
                normed[pl.ds(at * 2 * part, 2 * part), :],
                inner_w[:, cols],
                preferred_element_type=wide,
            )
            normal = 0.5 * (1.0 + lax.erf(inner * ROOT_HALF))
            active[pl.ds(at * 2 * part, 2 * part), cols] = (inner * normal).astype(low)
            slope[pl.ds(at * 2 * part, 2 * part), cols] = (
                normal + inner * jnp.exp(-0.5 * inner * inner) * INV_ROOT_TAU
            ).astype(low)

        @pl.loop(0, width // TILE)
        def _(step):
            cols = pl.ds(pl.multiple_of(step * TILE, TILE), TILE)
            fwd_send[pl.ds(base, part), cols] = jnp.dot(
                active[other_slice(at), :], outer_w[:, cols], preferred_element_type=wide
            ).astype(low)

        rows = pl.ds(base, part)
        copy = remote(fwd_send.at[rows], fwd_recv.at[rows], fwd_s.at[at], fwd_r.at[at], core_peer)
        copy.start()

        @pl.loop(0, width // TILE)
        def _(step):
            cols = pl.ds(pl.multiple_of(step * TILE, TILE), TILE)
            acc[:, cols] = jnp.dot(
                active[own_slice(at), :], outer_w[:, cols], preferred_element_type=wide
            )

        copy.wait_recv()

        @pl.when(first)
        def _():
            @pl.loop(0, part // ROWS)
            def _(step):
                off = pl.multiple_of(step * ROWS, ROWS)
                here = pl.ds(base + off, ROWS)
                result = (
                    own_x[here, :].astype(wide)
                    + acc[pl.ds(off, ROWS), :]
                    + fwd_recv[here, :].astype(wide)
                )
                hop[here, :] = result.astype(low)

            hop_forward(at).start()

        @pl.when(second)
        def _():
            if at == 0:
                gate_copy.wait_recv()

            @pl.loop(0, part // ROWS)
            def _(step):
                off = pl.multiple_of(step * ROWS, ROWS)
                here = pl.ds(base + off, ROWS)
                result = (
                    own_x[here, :].astype(wide)
                    + acc[pl.ds(off, ROWS), :]
                    + fwd_recv[here, :].astype(wide)
                )
                cot = own_cot[here, :].astype(wide)
                gate = gates[here, :][:, :1]
                back[here, :] = (gate * result).astype(low)
                gate_grads[here, :] = jnp.broadcast_to(
                    jnp.sum(cot * result, axis=1, keepdims=True), (ROWS, gate_grads.shape[1])
                )
                states[pl.ds(at * 2 * part + part + off, ROWS), :] = (gate * cot).astype(low)

    for at in range(CHUNKS):
        forward(at)

    def home_rows(at):
        return slot_rows((at % 2) * (exp_size // 2) + at // 2)

    def ret_copy(dest):
        return remote(
            spread.at[slot_rows(dest)],
            home.at[home_rows(exp_at)],
            ret_s.at[dest],
            ret_r.at[exp_at],
            (rep_at, dest),
        )

    ret_own = pltpu.make_async_copy(
        spread.at[slot_rows(exp_at)], home.at[home_rows(exp_at)], ret_s.at[exp_at]
    )

    def send_back():
        @pl.loop(0, width // TILE)
        def _(step):
            cols = pl.ds(pl.multiple_of(step * TILE, TILE), TILE)
            spread[:, cols] = jnp.dot(
                spread_m[...], back[:, cols], preferred_element_type=wide
            ).astype(low)

        @pl.loop(1, exp_size)
        def _(step):
            ret_copy(exp_at ^ step).start()

        ret_own.start()

    @pl.when(second)
    def _():
        grad_copy.start()
        send_back()

    centre_grad[...] = jnp.zeros_like(centre_grad)

    def backward(at):
        base = at * part

        @pl.when(first)
        def _():
            hop_backward(at).wait_recv()

        copy = remote(
            states.at[own_slice(at)], states.at[other_slice(at)], state_s.at[at], state_r.at[at], core_peer
        )
        copy.start()
        copy.wait_recv()

        @pl.loop(0, wide_ff // TILE)
        def _(step):
            rows = pl.ds(pl.multiple_of(step * TILE, TILE), TILE)
            grad_active = lax.dot_general(
                states[pl.ds(at * 2 * part, 2 * part), :],
                outer_w[rows, :],
                (((1,), (1,)), ((), ())),
                preferred_element_type=wide,
            )
            here = pl.ds(at * 2 * part, 2 * part)
            slope[here, rows] = (grad_active * slope[here, rows].astype(wide)).astype(low)

        @pl.loop(0, width // TILE)
        def _(step):
            cols = pl.ds(pl.multiple_of(step * TILE, TILE), TILE)
            bwd_send[pl.ds(base, part), cols] = lax.dot_general(
                slope[other_slice(at), :],
                inner_w[cols, :],
                (((1,), (1,)), ((), ())),
                preferred_element_type=wide,
            ).astype(low)

        rows = pl.ds(base, part)
        back_copy = remote(
            bwd_send.at[rows], bwd_recv.at[rows], bwd_s.at[at], bwd_r.at[at], core_peer
        )
        back_copy.start()

        @pl.loop(0, width // TILE)
        def _(step):
            cols = pl.ds(pl.multiple_of(step * TILE, TILE), TILE)
            acc[:, cols] = lax.dot_general(
                slope[own_slice(at), :],
                inner_w[cols, :],
                (((1,), (1,)), ((), ())),
                preferred_element_type=wide,
            )

        back_copy.wait_recv()
        if at == 0:

            @pl.when(first)
            def _():
                grad_copy.wait_recv()

        @pl.when(first)
        def _():
            hop_forward(at).wait_send()

        @pl.loop(0, part // ROWS)
        def _(step):
            off = pl.multiple_of(step * ROWS, ROWS)
            here = pl.ds(base + off, ROWS)
            rows_in = own_x[here, :].astype(wide)
            unit, inv_scale = row_stats(rows_in)
            grad_unit = (acc[pl.ds(off, ROWS), :] + bwd_recv[here, :].astype(wide)) * gain[...]
            grad_in = (
                grad_unit
                - jnp.mean(grad_unit, axis=-1, keepdims=True)
                - unit * jnp.mean(grad_unit * unit, axis=-1, keepdims=True)
            ) * inv_scale
            gate = gates[here, :][:, :1]

            @pl.when(second)
            def _():
                state = gate * own_cot[here, :].astype(wide) + grad_in
                hop[here, :] = state.astype(low)

            @pl.when(first)
            def _():
                state = states[pl.ds(at * 2 * part + part + off, ROWS), :].astype(wide) + grad_in
                grad_logit = gate_grads[here, :][:, :1] * gate * (1.0 - gate)
                back[here, :] = (state + grad_logit * cent_b[:1, :].astype(wide)).astype(low)
                centre_grad[...] += jnp.sum(grad_logit * rows_in, axis=0, keepdims=True)

        @pl.when(second)
        def _():
            hop_backward(at).start()

    for at in range(CHUNKS):
        backward(at)

    def eight_rows(at):
        return pl.ds(pl.multiple_of(at * 8, 8), 8)

    def centre_copy(mask, flip):
        dest = rep_at ^ mask
        return remote(
            centre_v.at[eight_rows(flip * rep_size + dest)],
            centre_parts.at[eight_rows(rep_at)],
            centre_s.at[flip * rep_size + mask],
            centre_r.at[mask],
            (dest, exp_at ^ flip),
        )

    centre_own = pltpu.make_async_copy(
        centre_v.at[eight_rows(rep_at)], centre_parts.at[eight_rows(rep_at)], centre_s.at[0]
    )
    centre_pairs = [(m, f) for m in range(rep_size) for f in range(2) if m or f]

    @pl.when(first)
    def _():
        send_back()
        for at in range(width // piece):
            centre_v[at * 8 : (at + 1) * 8, :] = jnp.broadcast_to(
                centre_grad[:, at * piece : (at + 1) * piece], (8, piece)
            )
        centre_own.start()
        for mask, flip in centre_pairs:
            centre_copy(mask, flip).start()

    outs = []
    for at in range(2 * block // TILE):
        rows = slice(at * TILE, (at + 1) * TILE)
        grad = lax.dot_general(
            active[:, rows], states[...], (((0,), (0,)), ((), ())), preferred_element_type=wide
        )
        if (at + 1) * TILE <= block:
            outer_keep_v[rows, :] = grad
            outs.append((outer_keep_v.at[rows], outer_keep.at[rows]))
        else:
            rows = slice(at * TILE - block, (at + 1) * TILE - block)
            outer_send_v[rows, :] = grad.astype(low)
            outs.append((outer_send_v.at[rows], outer_send.at[rows]))
        pltpu.make_async_copy(outs[-1][0], outs[-1][1], out_sem.at[len(outs) - 1]).start()
    for mask in range(rep_size):
        for side in range(2):
            cols = slice(side * block, (side + 1) * block)
            grad = lax.dot_general(
                normed[:, inner_rows(mask)],
                slope[:, cols],
                (((0,), (0,)), ((), ())),
                preferred_element_type=wide,
            )
            if mask == 0:
                inner_keep_v[:, cols] = grad
                outs.append((inner_keep_v.at[:, cols], inner_keep.at[:, cols]))
            else:
                rows = slice((mask - 1) * depth, mask * depth)
                inner_send_v[rows, cols] = grad.astype(low)
                outs.append((inner_send_v.at[rows, cols], inner_send.at[mask - 1, :, cols]))
            pltpu.make_async_copy(outs[-1][0], outs[-1][1], out_sem.at[len(outs) - 1]).start()

    for at, (source, target) in enumerate(outs):
        pltpu.make_async_copy(source, target, out_sem.at[at]).wait()
    for at in range(CHUNKS):
        rows = pl.ds(at * part, part)
        remote(
            normed.at[own_slice(at)], normed.at[other_slice(at)], norm_s.at[at], norm_r.at[at], core_peer
        ).wait_send()
        remote(
            states.at[own_slice(at)], states.at[other_slice(at)], state_s.at[at], state_r.at[at], core_peer
        ).wait_send()
        remote(
            fwd_send.at[rows], fwd_recv.at[rows], fwd_s.at[at], fwd_r.at[at], core_peer
        ).wait_send()
        remote(
            bwd_send.at[rows], bwd_recv.at[rows], bwd_s.at[at], bwd_r.at[at], core_peer
        ).wait_send()

        @pl.when(second)
        def _():
            hop_backward(at).wait_send()

    @pl.when(first)
    def _():
        gate_copy.wait_send()

    @pl.when(second)
    def _():
        grad_copy.wait_send()

    @pl.when(first)
    def _():
        centre_own.wait()
        for mask, flip in centre_pairs:
            centre_copy(mask, flip).wait_send()
        for mask in range(1, rep_size):
            centre_copy(mask, 0).wait_recv()

    @pl.when(second)
    def _():
        for mask in range(rep_size):
            centre_copy(mask, 1).wait_recv()

    ret_own.wait()

    @pl.loop(1, exp_size)
    def _(step):
        source = exp_at ^ step
        remote(
            spread.at[slot_rows(source)],
            home.at[home_rows(source)],
            ret_s.at[source],
            ret_r.at[source],
            (rep_at, source),
        ).wait()


def run_experts(
    exp_size, rep_size, slots, own_rows, arrived, inner_w, outer_w, counts_all, cents, gains_e
):
    width = arrived.shape[1]
    depth = width // rep_size
    block = outer_w.shape[0] // 2
    low = jnp.bfloat16
    wide = jnp.float32
    total = exp_size * slots
    all_rows = 2 * own_rows
    part = own_rows // CHUNKS
    piece = cents.shape[1]
    anyplace = pl.BlockSpec(memory_space=pl.ANY)
    inside = pl.BlockSpec(memory_space=pltpu.VMEM)
    dma = pltpu.SemaphoreType.DMA
    n_out = 2 * block // TILE + 2 * rep_size
    scratch = [
        pltpu.VMEM((total, width), low),
        pltpu.VMEM((total, own_rows), low),
        pltpu.VMEM((2, exp_size * 16, 128), wide),
        pltpu.VMEM((128, width), low),
        pltpu.VMEM((1, width), wide),
        pltpu.VMEM((1, width), wide),
        pltpu.VMEM((2 * rep_size * 8, piece), wide),
        pltpu.VMEM((width, 2 * block), low),
        pltpu.VMEM((2 * block, width), low),
        pltpu.VMEM((own_rows, width), low),
        pltpu.VMEM((own_rows, width), low),
        pltpu.VMEM((all_rows, width), low),
        pltpu.VMEM((all_rows, 2 * block), low),
        pltpu.VMEM((all_rows, 2 * block), low),
        pltpu.VMEM((all_rows, width), low),
        pltpu.VMEM((own_rows, width), low),
        pltpu.VMEM((own_rows, width), low),
        pltpu.VMEM((own_rows, width), low),
        pltpu.VMEM((own_rows, width), low),
        pltpu.VMEM((own_rows, width), low),
        pltpu.VMEM((own_rows, width), low),
        pltpu.VMEM((total, width), low),
        pltpu.VMEM((part, width), wide),
        pltpu.VMEM((own_rows, 128), wide),
        pltpu.VMEM((own_rows, 128), wide),
        pltpu.VMEM((block, width), wide),
        pltpu.VMEM((block, width), low),
        pltpu.VMEM((depth, 2 * block), wide),
        pltpu.VMEM(((rep_size - 1) * depth, 2 * block), low),
        dma((3,)),
        dma((2 * rep_size,)),
        dma((rep_size,)),
    ]
    scratch += [dma((CHUNKS,)) for _ in range(10)]
    scratch += [dma((2,)), dma((2,)), dma((exp_size,)), dma((exp_size,)), dma((n_out,))]
    flops = 2 * all_rows * width * 2 * block * 6
    return pl.pallas_call(
        functools.partial(expert_kernel, exp_size, rep_size, slots),
        out_shape=(
            jax.ShapeDtypeStruct((total, width), low),
            jax.ShapeDtypeStruct((block, width), wide),
            jax.ShapeDtypeStruct((block, width), low),
            jax.ShapeDtypeStruct((depth, 2 * block), wide),
            jax.ShapeDtypeStruct((rep_size - 1, depth, 2 * block), low),
            jax.ShapeDtypeStruct((rep_size * 8, piece), wide),
        ),
        in_specs=[anyplace] * 3 + [inside] * 3,
        out_specs=(anyplace,) * 6,
        scratch_shapes=scratch,
        compiler_params=pltpu.CompilerParams(
            collective_id=0, has_side_effects=True, vmem_limit_bytes=62 << 20
        ),
        cost_estimate=pl.CostEstimate(
            flops=flops, bytes_accessed=40 << 20, transcendentals=2 * all_rows * 2 * block
        ),
        name="experts",
    )(arrived, inner_w, outer_w, counts_all, cents, gains_e)


def reduce_weights(grads, exp_bits):
    count, rows, cols = grads.shape
    half = cols // 2
    total = grads[:, :, :half] + swap(grads[:, :, half:].astype(jnp.bfloat16), "rep", 1).astype(
        jnp.float32
    )
    total = total.reshape(count, -1, 2, rows >> exp_bits, half)
    total = total[:, :, 0] + swap(total[:, :, 1].astype(jnp.bfloat16), "exp", 1).astype(
        jnp.float32
    )
    for bit in range(exp_bits - 1, 0, -1):
        keep = total.shape[1] // 2
        total = total[:, :keep] + swap(
            total[:, keep:].astype(jnp.bfloat16), "exp", 1 << bit
        ).astype(jnp.float32)
    total = total[:, 0]
    total = total + swap(total.astype(jnp.bfloat16), "rep", 2).astype(jnp.float32)
    other = swap(total.astype(jnp.bfloat16), "rep", 1).astype(jnp.float32)
    return total, other


def shards(
    tokens,
    cotangent,
    doc_lengths,
    expert_of_token,
    w_query,
    w_key,
    w_value,
    w_output,
    attn_gain,
    w_inner,
    w_outer,
    expert_gain,
    centroids,
):
    exp_size = lax.axis_size("exp")
    rep_size = lax.axis_size("rep")
    exp_bits = exp_size.bit_length() - 1
    experts = exp_size // 2
    rep_at = lax.axis_index("rep")
    exp_at = lax.axis_index("exp")
    core = rep_at % 2
    row_count, width = tokens.shape
    head_dim = width // HEADS
    factor = head_dim ** (-0.5)
    low = jnp.bfloat16
    wide = jnp.float32

    slots = -(-3 * row_count // exp_size // 16) * 16
    (
        attn_w,
        inner_w,
        outer_w,
        arrived,
        counts_all,
        cents,
        gains_e,
        hidden,
        qkv,
        probs,
        normed_a,
        context,
        pick,
    ) = run_attend(
        exp_size,
        rep_size,
        slots,
        tokens,
        cotangent,
        doc_lengths,
        expert_of_token[None],
        (w_query, w_key, w_value, w_output),
        attn_gain[None],
        w_inner[0],
        w_outer[0],
        expert_gain,
        centroids,
    )
    home, outer_keep, outer_send, inner_keep, inner_send, centre_parts = run_experts(
        exp_size,
        rep_size,
        slots,
        2 * row_count,
        arrived,
        inner_w,
        outer_w,
        counts_all,
        cents,
        gains_e,
    )
    all_slots = experts * slots
    grad_home = tn_product(pick, home[:all_slots])
    branch_home = tn_product(pick, home[all_slots:])
    output = (hidden + branch_home).astype(low)
    grad_centroids = jnp.sum(centre_parts.reshape(rep_size, 8, -1)[:, 0], axis=0)[None]

    block = outer_keep.shape[0]
    grad_w_outer = (outer_keep + swap(outer_send, "rep", 2).astype(wide))[None]
    mine = inner_keep.reshape(width // rep_size, 2, block)
    got = [
        swap(inner_send[mask - 1], "rep", mask).astype(wide).reshape(mine.shape)
        for mask in range(1, rep_size)
    ]
    ordered = jnp.stack(
        [
            mine[:, 0] + got[1][:, 1],
            got[0][:, 0] + got[2][:, 1],
            mine[:, 1] + got[1][:, 0],
            got[0][:, 1] + got[2][:, 0],
        ],
        axis=1,
    )
    summed = xor_order(ordered.reshape(width // rep_size, -1), 1, rep_at, rep_size)
    grad_w_inner = summed[None]
    grad_expert_gain = jnp.sum(summed * w_inner[0].astype(wide), axis=1)[None] / expert_gain.astype(
        wide
    )

    grad_hidden = cotangent.astype(wide) + grad_home
    grad_attn = grad_hidden.astype(low)
    context_x = xor_order(context, 1, exp_at, exp_size)
    grad_w_o = tn_product(context_x, xor_order(grad_attn, 1, core, 2))
    share_o = reduce_weights(grad_w_o[None], exp_bits)
    grad_context3 = nt_product(grad_attn, attn_w[3]).astype(low).reshape(
        row_count, HEADS, head_dim
    )
    queries3, keys3, values3 = [qkv[i].reshape(row_count, HEADS, head_dim) for i in range(3)]
    attn_probs = probs.reshape(HEADS, row_count, row_count)
    grad_probs = jnp.einsum("qhe,khe->hqk", grad_context3, values3, preferred_element_type=wide)
    wide_probs = attn_probs.astype(wide)
    inner_sum = jnp.sum(wide_probs * grad_probs, axis=-1, keepdims=True)
    grad_scores = (wide_probs * (grad_probs - inner_sum)).astype(low)
    grad_query = (
        jnp.einsum("hqk,khe->qhe", grad_scores, keys3, preferred_element_type=wide) * factor
    ).astype(low)
    grad_key = (
        jnp.einsum("hqk,qhe->khe", grad_scores, queries3, preferred_element_type=wide) * factor
    ).astype(low)
    grad_value = jnp.einsum(
        "hqk,qhe->khe", attn_probs, grad_context3, preferred_element_type=wide
    ).astype(low)
    grads3 = [g.reshape(row_count, width) for g in (grad_query, grad_key, grad_value)]
    unit_x = xor_order(normed_a, 1, exp_at, exp_size)
    grad_w_qkv = jnp.stack([tn_product(unit_x, xor_order(g, 1, core, 2)) for g in grads3])
    share_qkv = reduce_weights(grad_w_qkv, exp_bits)
    grad_unit = sum(nt_product(g, attn_w[i]) for i, g in enumerate(grads3))
    unit_w, scale_a = row_stats(tokens.astype(wide))
    gain_all = lax.all_gather(attn_gain, "exp", axis=0, tiled=True).astype(wide)
    grad_unit = grad_unit * gain_all
    grad_tokens = (
        grad_hidden
        + (
            grad_unit
            - jnp.mean(grad_unit, axis=-1, keepdims=True)
            - unit_w * jnp.mean(grad_unit * unit_w, axis=-1, keepdims=True)
        )
        * scale_a
    )

    def true_halves(pair):
        mine_half, other_half = pair
        return xor_order(jnp.concatenate([mine_half, other_half], axis=-1), 2, core, 2)

    full_o = true_halves(share_o)[0]
    full_qkv = true_halves(share_qkv)
    share_gain = sum(
        jnp.sum(full_qkv[i] * w.astype(wide), axis=1)
        for i, w in enumerate((w_query, w_key, w_value))
    ) / attn_gain.astype(wide)
    return (
        output,
        grad_tokens,
        full_qkv[0],
        full_qkv[1],
        full_qkv[2],
        full_o,
        share_gain,
        grad_w_inner,
        grad_w_outer,
        grad_expert_gain,
        grad_centroids,
    )


def solution(mesh):
    placed = (
        P(("rep", "exp"), None),
        P(("rep", "exp"), None),
        P(("rep", "exp"), None),
        P(("rep", "exp")),
        P("exp", None),
        P("exp", None),
        P("exp", None),
        P("exp", None),
        P("exp"),
        P("exp", "rep", None),
        P("exp", "rep", None),
        P("exp", "rep"),
        P("exp", "rep"),
    )
    return jax.shard_map(
        shards,
        mesh=mesh,
        in_specs=placed,
        out_specs=(
            P(("rep", "exp"), None),
            P(("rep", "exp"), None),
            P("exp", None),
            P("exp", None),
            P("exp", None),
            P("exp", None),
            P("exp"),
            P("exp", "rep", None),
            P("exp", "rep", None),
            P("exp", "rep"),
            P("exp", "rep"),
        ),
        check_vma=False,
    )
```

```python
import functools

import jax
import jax.numpy as jnp
from jax import lax
from jax.experimental import pallas as pl
from jax.experimental.pallas import tpu as pltpu
from jax.sharding import PartitionSpec as P

HEADS = 16
EPS = 1e-05
ROOT_HALF = 0.7071067811865476
INV_ROOT_TAU = 0.3989422804014327
CHUNKS = 2


MESH = pl.DeviceIdType.MESH
TILE = 256
ROWS = 64


def remote(src, dst, send_sem, recv_sem, device):
    return pltpu.make_async_remote_copy(
        src_ref=src,
        dst_ref=dst,
        send_sem=send_sem,
        recv_sem=recv_sem,
        device_id=device,
        device_id_type=MESH,
    )


def row_stats(rows):
    row_mean = jnp.mean(rows, axis=-1, keepdims=True)
    centered = rows - row_mean
    variance = jnp.mean(centered * centered, axis=-1, keepdims=True)
    inv_scale = lax.rsqrt(variance + EPS)
    return centered * inv_scale, inv_scale


def attend_kernel(
    exp_size,
    rep_size,
    slots,
    tokens,
    cotangent,
    doc,
    expert_of,
    w_query,
    w_key,
    w_value,
    w_output,
    gain_a,
    w_inner,
    w_outer,
    gain_e,
    cent,
    attn_w,
    inner_w,
    outer_w,
    arrived,
    counts_all,
    cents,
    gains_e,
    hidden,
    qkv,
    probs,
    normed_a,
    context,
    pick,
    gain_row,
    weights,
    small_all,
    gain_v,
    packed_x,
    packed_c,
    bias,
    counts_v,
    cent_v,
    own_s,
    line_s,
    line_r,
    side_s,
    side_r,
    core_s,
    core_r,
    weight_s,
    weight_r,
    disp_s,
    disp_r,
    count_s,
    count_r,
    cent_s,
    cent_r,
    gain_s,
    gain_r,
    out_s,
):
    low = jnp.bfloat16
    wide = jnp.float32
    rep_at = lax.axis_index("rep")
    exp_at = lax.axis_index("exp")
    core = rep_at % 2
    group = exp_at // 2
    side = exp_at % 2
    groups = exp_size // 2
    rows_n, width = tokens.shape
    half = width // 2
    block = w_query.shape[0]
    depth = w_inner.shape[0]
    ff_block = w_outer.shape[0]
    core_peer = (rep_at ^ 1, exp_at)
    side_peer = (rep_at, exp_at ^ 1)

    def block_rows(at):
        return pl.ds(pl.multiple_of(at * block, block), block)

    own_loads = []
    for at, source in enumerate((w_query, w_key, w_value, w_output)):
        own_loads.append(
            pltpu.make_async_copy(source, weights.at[at, block_rows(exp_at)], own_s.at[at])
        )
    for load in own_loads:
        load.start()

    barrier = pltpu.get_barrier_semaphore()
    for mask in range(1, rep_size):
        for flip in range(2):
            pl.semaphore_signal(
                barrier, inc=1, device_id=(rep_at ^ mask, exp_at ^ flip), device_id_type=MESH
            )

    @pl.loop(1, exp_size)
    def _(at):
        pl.semaphore_signal(barrier, inc=1, device_id=(rep_at, exp_at ^ at), device_id_type=MESH)

    pl.semaphore_wait(barrier, exp_size - 1 + 2 * (rep_size - 1))

    outer_copy = remote(
        w_outer, outer_w.at[ff_block:], weight_s.at[0], weight_r.at[0], (rep_at ^ 2, exp_at)
    )
    outer_copy.start()
    outer_own = pltpu.make_async_copy(w_outer, outer_w.at[:ff_block], own_s.at[5])
    outer_own.start()

    for load in own_loads:
        load.wait()

    picks = (slice(0, 3), slice(3, 4))
    own_half = pl.ds(pl.multiple_of(core * half, half), half)

    def view(kind, at):
        return weights.at[picks[kind], block_rows(at), own_half]

    def line_copy(kind, source, step):
        at = 2 * source + side
        return remote(
            view(kind, at),
            view(kind, at),
            line_s.at[kind, (1 + step) // 2, source],
            line_r.at[kind, source],
            (rep_at, exp_at + 2 * step),
        )

    def line_wait(kind, source):
        at = 2 * source + side
        remote(
            view(kind, at), view(kind, at), line_s.at[kind, 0, source], line_r.at[kind, source], side_peer
        ).wait_recv()

    def side_copy(kind, source):
        at = 2 * source + side
        return remote(
            view(kind, at), view(kind, at), side_s.at[kind, source], side_r.at[kind, source], side_peer
        )

    def side_wait(kind, source):
        at = 2 * source + 1 - side
        remote(
            view(kind, at), view(kind, at), side_s.at[kind, source], side_r.at[kind, source], side_peer
        ).wait_recv()

    def core_copy(kind, at):
        return remote(view(kind, at), view(kind, at), core_s.at[kind, at], core_r.at[kind, at], core_peer)

    def core_wait(kind, at):
        other = pl.ds(pl.multiple_of((1 - core) * half, half), half)
        there = weights.at[picks[kind], block_rows(at), other]
        remote(there, there, core_s.at[kind, at], core_r.at[kind, at], core_peer).wait_recv()

    def first_sends(kind):
        @pl.when(group + 1 < groups)
        def _():
            line_copy(kind, group, 1).start()

        @pl.when(group >= 1)
        def _():
            line_copy(kind, group, -1).start()

        side_copy(kind, group).start()

    def take_side(kind, source):
        side_wait(kind, source)
        core_copy(kind, 2 * source + 1 - side).start()

    def gather_step(kind, step):
        @pl.when(group - step >= 0)
        def _():
            source = group - step
            line_wait(kind, source)

            @pl.when(group + 1 < groups)
            def _():
                line_copy(kind, source, 1).start()

            side_copy(kind, source).start()
            core_copy(kind, 2 * source + side).start()

        @pl.when(group + step < groups)
        def _():
            source = group + step
            line_wait(kind, source)

            @pl.when(group >= 1)
            def _():
                line_copy(kind, source, -1).start()

            side_copy(kind, source).start()
            core_copy(kind, 2 * source + side).start()

        @pl.when(group - step + 1 >= 0)
        def _():
            take_side(kind, group - step + 1)

        @pl.when((step > 1) & (group + step - 1 < groups))
        def _():
            take_side(kind, group + step - 1)

    def gather_end(kind):
        last = groups - 1

        @pl.when(group - last >= 0)
        def _():
            take_side(kind, group - last)

        @pl.when((groups > 1) & (group + last < groups))
        def _():
            take_side(kind, group + last)

        @pl.loop(0, exp_size)
        def _(at):
            @pl.when(at != exp_at)
            def _():
                core_wait(kind, at)

    first_sends(0)
    first_sends(1)

    inner_rows = pl.ds(pl.multiple_of(rep_at * depth, depth), depth)

    def ff_cols(at):
        return pl.ds(pl.multiple_of(at * ff_block, ff_block), ff_block)

    def inner_copies(mask):
        dest = rep_at ^ mask
        found = []
        for part in range(2):
            source = w_inner.at[:, ff_cols(dest ^ (2 * part))]
            target = inner_w.at[inner_rows, part * ff_block : (part + 1) * ff_block]
            if mask == 0:
                found.append(pltpu.make_async_copy(source, target, weight_s.at[1 + part]))
            else:
                found.append(
                    remote(
                        source,
                        target,
                        weight_s.at[1 + 2 * mask + part],
                        weight_r.at[1 + 2 * mask + part],
                        (dest, exp_at),
                    )
                )
        return found

    for mask in range(rep_size):
        for copy in inner_copies(mask):
            copy.start()

    lanes = counts_v.shape[1]
    expert_row = expert_of[...]
    onehot = (
        lax.broadcasted_iota(jnp.int32, (lanes, rows_n), 0) == expert_row
    ).astype(wide)
    before = (
        lax.broadcasted_iota(jnp.int32, (rows_n, rows_n), 0)
        < lax.broadcasted_iota(jnp.int32, (rows_n, rows_n), 1)
    ).astype(low)
    earlier = jnp.dot(onehot.astype(low), before, preferred_element_type=wide)
    rank = jnp.sum(earlier * onehot, axis=0, keepdims=True).astype(jnp.int32)
    position = expert_row * slots + rank
    pick[...] = (
        lax.broadcasted_iota(jnp.int32, pick.shape, 0) == position
    ).astype(wide).astype(low)
    counts_v[:8, :] = lax.dot_general(
        jnp.ones((8, rows_n), low),
        onehot.astype(low),
        (((1,), (1,)), ((), ())),
        preferred_element_type=wide,
    )
    counts_v[8:, :block] = jnp.broadcast_to(gain_a[...].astype(wide), (8, block))
    cent_v[...] = jnp.broadcast_to(cent[...].astype(wide), cent_v.shape)
    gain_v[...] = jnp.broadcast_to(gain_e[...].astype(wide), gain_v.shape)

    def eight(at):
        return pl.ds(pl.multiple_of(at * 8, 8), 8)

    def sixteen(at):
        return pl.ds(pl.multiple_of(at * 16, 16), 16)

    def count_copy(dest):
        return remote(
            counts_v, small_all.at[sixteen(exp_at)], count_s.at[dest], count_r.at[exp_at], (rep_at, dest)
        )

    count_own = pltpu.make_async_copy(counts_v, small_all.at[sixteen(exp_at)], count_s.at[exp_at])
    count_own.start()

    @pl.loop(1, exp_size)
    def _(at):
        count_copy(exp_at ^ at).start()

    cent_at = side * rep_size + rep_at

    def cent_copy(mask, flip):
        return remote(
            cent_v,
            cents.at[eight(cent_at)],
            cent_s.at[flip * rep_size + mask],
            cent_r.at[flip * rep_size + mask],
            (rep_at ^ mask, exp_at ^ flip),
        )

    cent_own = pltpu.make_async_copy(cent_v, cents.at[eight(cent_at)], cent_s.at[0])
    cent_own.start()
    cent_pairs = [(m, f) for m in range(rep_size) for f in range(2) if m or f]
    for mask, flip in cent_pairs:
        cent_copy(mask, flip).start()

    def gain_copy(mask):
        return remote(
            gain_v, gains_e.at[eight(rep_at)], gain_s.at[mask], gain_r.at[mask], (rep_at ^ mask, exp_at)
        )

    gain_own = pltpu.make_async_copy(gain_v, gains_e.at[eight(rep_at)], gain_s.at[0])
    gain_own.start()
    for mask in range(1, rep_size):
        gain_copy(mask).start()

    count_own.wait()

    @pl.loop(1, exp_size)
    def _(at):
        source = exp_at ^ at
        remote(
            counts_v, small_all.at[sixteen(source)], count_s.at[source], count_r.at[source], (rep_at, source)
        ).wait()

    small_store = pltpu.make_async_copy(small_all, counts_all, out_s.at[1])
    small_store.start()

    tiled = jnp.dot(
        small_all[...].astype(low),
        (
            lax.broadcasted_iota(jnp.int32, (lanes, width), 1) % block
            == lax.broadcasted_iota(jnp.int32, (lanes, width), 0)
        ).astype(wide).astype(low),
        preferred_element_type=wide,
    )
    chosen_row = lax.broadcasted_iota(jnp.int32, (16 * exp_size, width), 0) == (
        16 * (lax.broadcasted_iota(jnp.int32, (16 * exp_size, width), 1) // block) + 8
    )
    gain_row[...] = jnp.sum(jnp.where(chosen_row, tiled, 0.0), axis=0, keepdims=True)

    @pl.loop(0, rows_n // ROWS)
    def _(step):
        here = pl.ds(pl.multiple_of(step * ROWS, ROWS), ROWS)
        unit, _ = row_stats(tokens[here, :].astype(wide))
        normed_a[here, :] = (unit * gain_row[...]).astype(low)

    down = lax.broadcasted_iota(jnp.int32, (rows_n, rows_n), 0)
    along = lax.broadcasted_iota(jnp.int32, (rows_n, rows_n), 1)
    end = jnp.int32(0)
    seg_down = jnp.zeros((rows_n, rows_n), jnp.int32)
    seg_along = jnp.zeros((rows_n, rows_n), jnp.int32)
    for at in range(doc.shape[1]):
        end = end + doc[0, at]
        seg_down = seg_down + (down >= end).astype(jnp.int32)
        seg_along = seg_along + (along >= end).astype(jnp.int32)
    bias[...] = jnp.where((seg_down == seg_along) & (down >= along), 0.0, -1e30)

    @pl.loop(1, groups)
    def _(step):
        gather_step(0, step)

    gather_end(0)

    def slot_rows(at):
        return pl.ds(pl.multiple_of(at * slots, slots), slots)

    def disp_copy(source, dest):
        return remote(
            source.at[slot_rows(dest // 2)],
            arrived.at[slot_rows(exp_at)],
            disp_s.at[dest],
            disp_r.at[exp_at],
            (rep_at, dest),
        )

    def dispatch(source, flip):
        @pl.loop(0, groups)
        def _(at):
            dest = 2 * (group ^ at) + flip

            @pl.when(dest != exp_at)
            def _():
                disp_copy(source, dest).start()

            @pl.when(dest == exp_at)
            def _():
                pltpu.make_async_copy(
                    source.at[slot_rows(group)], arrived.at[slot_rows(exp_at)], disp_s.at[exp_at]
                ).start()

    @pl.loop(0, width // TILE)
    def _(step):
        cols = pl.ds(pl.multiple_of(step * TILE, TILE), TILE)
        packed_c[:, cols] = jnp.dot(
            pick[...], cotangent[:, cols], preferred_element_type=wide
        ).astype(low)

    dispatch(packed_c, 1)

    for at in range(3):

        @pl.loop(0, width // TILE)
        def _(step):
            cols = pl.ds(pl.multiple_of(step * TILE, TILE), TILE)
            qkv[at, :, cols] = jnp.dot(
                normed_a[...], weights[at, :, cols], preferred_element_type=wide
            ).astype(low)

    head_dim = width // HEADS
    pair = 2 * head_dim
    factor = head_dim ** (-0.5)
    lane = lax.broadcasted_iota(jnp.int32, (rows_n, pair), 1)
    pairs = HEADS // 2
    parts = 4
    for part in range(parts):
        low_step = 1 + part * (groups - 1) // parts
        high_step = 1 + (part + 1) * (groups - 1) // parts

        @pl.loop(low_step, high_step)
        def _(step):
            gather_step(1, step)

        @pl.loop(part * pairs // parts, (part + 1) * pairs // parts)
        def _(at):
            cols = pl.ds(pl.multiple_of(at * pair, pair), pair)
            q_pair = qkv[0, :, cols]
            k_pair = qkv[1, :, cols]
            v_pair = qkv[2, :, cols]
            found = []
            for which in range(2):
                chosen = (lane >= head_dim) if which else (lane < head_dim)
                q_one = jnp.where(chosen, q_pair, jnp.zeros_like(q_pair))
                scores = (
                    lax.dot_general(
                        q_one, k_pair, (((1,), (1,)), ((), ())), preferred_element_type=wide
                    )
                    * factor
                    + bias[...]
                )
                top = jnp.max(scores, axis=1, keepdims=True)
                raised = jnp.exp(scores - top)
                total = jnp.sum(raised, axis=1, keepdims=True)
                prob = (raised * (1.0 / total)).astype(low)
                probs[pl.ds(pl.multiple_of((2 * at + which) * rows_n, rows_n), rows_n), :] = prob
                found.append(jnp.dot(prob, v_pair, preferred_element_type=wide))
            context[:, cols] = jnp.where(lane < head_dim, found[0], found[1]).astype(low)

    gather_end(1)
    store = pltpu.make_async_copy(weights, attn_w, out_s.at[0])
    store.start()

    @pl.loop(0, width // TILE)
    def _(step):
        cols = pl.ds(pl.multiple_of(step * TILE, TILE), TILE)
        sum_here = tokens[:, cols].astype(wide) + jnp.dot(
            context[...], weights[3, :, cols], preferred_element_type=wide
        )
        hidden[:, cols] = sum_here
        packed_x[:, cols] = jnp.dot(
            pick[...], sum_here.astype(low), preferred_element_type=wide
        ).astype(low)

    dispatch(packed_x, 0)

    store.wait()
    outer_copy.wait()
    outer_own.wait()
    for mask in range(rep_size):
        for copy in inner_copies(mask):
            copy.wait()
    for kind in range(2):
        side_copy(kind, group).wait_send()

        @pl.loop(0, groups)
        def _(source):
            @pl.when(source != group)
            def _():
                side_copy(kind, source).wait_send()

            @pl.when((source <= group) & (group + 1 < groups))
            def _():
                line_copy(kind, source, 1).wait_send()

            @pl.when((source >= group) & (group >= 1))
            def _():
                line_copy(kind, source, -1).wait_send()

        @pl.loop(0, exp_size)
        def _(at):
            @pl.when(at != exp_at)
            def _():
                core_copy(kind, at).wait_send()

    small_store.wait()
    cent_own.wait()
    gain_own.wait()
    for mask in range(1, rep_size):
        gain_copy(mask).wait()
    for mask, flip in cent_pairs:
        cent_copy(mask, flip).wait()

    @pl.loop(1, exp_size)
    def _(at):
        source = exp_at ^ at
        remote(
            packed_c.at[slot_rows(source // 2)],
            arrived.at[slot_rows(source)],
            disp_s.at[source],
            disp_r.at[source],
            (rep_at, source),
        ).wait()

    pltpu.make_async_copy(
        packed_c.at[slot_rows(group)], arrived.at[slot_rows(exp_at)], disp_s.at[exp_at]
    ).wait()


def run_attend(exp_size, rep_size, slots, tokens, cotangent, doc, expert_of, attn, gain_a, w_inner, w_outer, gain_e, cent):
    rows_n, width = tokens.shape
    low = jnp.bfloat16
    wide = jnp.float32
    groups = exp_size // 2
    depth = w_inner.shape[0]
    ff_block = w_outer.shape[0]
    anyplace = pl.BlockSpec(memory_space=pl.ANY)
    inside = pl.BlockSpec(memory_space=pltpu.VMEM)
    dma = pltpu.SemaphoreType.DMA
    shape = jax.ShapeDtypeStruct
    return pl.pallas_call(
        functools.partial(attend_kernel, exp_size, rep_size, slots),
        out_shape=(
            shape((4, width, width), low),
            shape((width, 2 * ff_block), low),
            shape((2 * ff_block, width), low),
            shape((exp_size * slots, width), low),
            shape((exp_size * 16, 128), wide),
            shape((2 * rep_size * 8, cent.shape[1]), wide),
            shape((rep_size * 8, depth), wide),
            shape((rows_n, width), wide),
            shape((3, rows_n, width), low),
            shape((HEADS * rows_n, rows_n), low),
            shape((rows_n, width), low),
            shape((rows_n, width), low),
            shape((groups * slots, rows_n), low),
            shape((1, width), wide),
        ),
        in_specs=[inside, inside, pl.BlockSpec(memory_space=pltpu.SMEM), inside]
        + [anyplace] * 4
        + [inside, anyplace, anyplace, inside, inside],
        out_specs=(anyplace,) * 7 + (inside,) * 7,
        scratch_shapes=[
            pltpu.VMEM((4, width, width), low),
            pltpu.VMEM((exp_size * 16, 128), wide),
            pltpu.VMEM((8, depth), wide),
            pltpu.VMEM((groups * slots, width), low),
            pltpu.VMEM((groups * slots, width), low),
            pltpu.VMEM((rows_n, rows_n), wide),
            pltpu.VMEM((16, 128), wide),
            pltpu.VMEM((8, cent.shape[1]), wide),
            dma((6,)),
            dma((2, 2, groups)),
            dma((2, groups)),
            dma((2, groups)),
            dma((2, groups)),
            dma((2, exp_size)),
            dma((2, exp_size)),
            dma((1 + 2 * rep_size,)),
            dma((1 + 2 * rep_size,)),
            dma((exp_size,)),
            dma((exp_size,)),
            dma((exp_size,)),
            dma((exp_size,)),
            dma((2 * rep_size,)),
            dma((2 * rep_size,)),
            dma((rep_size,)),
            dma((rep_size,)),
            dma((2,)),
        ],
        compiler_params=pltpu.CompilerParams(
            collective_id=1, has_side_effects=True, vmem_limit_bytes=56 << 20
        ),
        cost_estimate=pl.CostEstimate(
            flops=10 * rows_n * width * width,
            bytes_accessed=40 << 20,
            transcendentals=HEADS * rows_n * rows_n,
        ),
        name="attend",
    )(tokens, cotangent, doc, expert_of, *attn, gain_a, w_inner, w_outer, gain_e, cent)


def expert_kernel(
    exp_size,
    rep_size,
    slots,
    arrived_h,
    inner_h,
    outer_h,
    counts_all,
    cents,
    gains_e,
    home,
    outer_keep,
    outer_send,
    inner_send,
    centre_parts,
    arrived,
    spread_m,
    offsets,
    cent_b,
    gain,
    centre_grad,
    centre_v,
    inner_w,
    outer_w,
    own_x,
    own_cot,
    normed,
    active,
    slope,
    states,
    fwd_send,
    fwd_recv,
    bwd_send,
    bwd_recv,
    hop,
    back,
    spread,
    acc,
    gates,
    gate_grads,
    outer_keep_v,
    outer_send_v,
    inner_send_v,
    load_sem,
    centre_s,
    centre_r,
    norm_s,
    norm_r,
    state_s,
    state_r,
    fwd_s,
    fwd_r,
    bwd_s,
    bwd_r,
    hop_s,
    hop_r,
    gate_s,
    gate_r,
    ret_s,
    ret_r,
    out_sem,
):
    low = jnp.bfloat16
    wide = jnp.float32
    rep_at = lax.axis_index("rep")
    exp_at = lax.axis_index("exp")
    first = exp_at % 2 == 0
    second = exp_at % 2 == 1
    core_peer = (rep_at ^ 1, exp_at)
    side_peer = (rep_at, exp_at ^ 1)
    width = own_x.shape[1]
    own_rows = own_x.shape[0]
    part = own_rows // CHUNKS
    wide_ff = inner_w.shape[1]
    block = wide_ff // 2
    depth = width // rep_size

    def slot_rows(at):
        return pl.ds(pl.multiple_of(at * slots, slots), slots)

    def inner_rows(mask):
        return pl.ds(pl.multiple_of((rep_at ^ mask) * depth, depth), depth)

    loads = [
        pltpu.make_async_copy(arrived_h, arrived, load_sem.at[0]),
        pltpu.make_async_copy(inner_h, inner_w, load_sem.at[1]),
        pltpu.make_async_copy(outer_h, outer_w, load_sem.at[2]),
    ]
    for load in loads:
        load.start()

    barrier = pltpu.get_barrier_semaphore()
    for mask in range(1, rep_size):
        for flip in range(2):
            pl.semaphore_signal(
                barrier, inc=1, device_id=(rep_at ^ mask, exp_at ^ flip), device_id_type=MESH
            )

    @pl.loop(1, exp_size)
    def _(at):
        pl.semaphore_signal(barrier, inc=1, device_id=(rep_at, exp_at ^ at), device_id_type=MESH)

    counted = counts_all.shape[0]
    group = exp_at // 2
    lane = lax.broadcasted_iota(jnp.int32, (counted, 128), 1)
    mine = jnp.sum(
        jnp.where(lane == group, counts_all[...], 0.0), axis=1, keepdims=True
    )
    mine = jnp.broadcast_to(mine, (counted, 128))
    down = lax.broadcasted_iota(jnp.int32, (counted, counted), 0)
    along = lax.broadcasted_iota(jnp.int32, (counted, counted), 1)
    ahead = ((along // 16 < down // 16) & (along % 16 == 0)).astype(wide).astype(low)
    offsets[0] = jnp.dot(ahead, mine.astype(low), preferred_element_type=wide)
    offsets[1] = mine
    slot_iota = lax.broadcasted_iota(jnp.int32, (slots, own_rows), 0)
    row_iota = lax.broadcasted_iota(jnp.int32, (slots, own_rows), 1)

    @pl.loop(0, exp_size)
    def _(at):
        eight = pl.ds(pl.multiple_of(at * 16, 16), 8)
        start = offsets[0, eight, :][:1, :1].astype(jnp.int32)
        limit = offsets[1, eight, :][:1, :1].astype(jnp.int32)
        spread_m[slot_rows(at), :] = (
            ((slot_iota + start) == row_iota) & (slot_iota < limit)
        ).astype(wide).astype(low)

    piece = cents.shape[1]
    for at in range(width // piece):
        cent_b[:, at * piece : (at + 1) * piece] = jnp.broadcast_to(
            cents[at * 8 : at * 8 + 1, :], (cent_b.shape[0], piece)
        ).astype(low)
    for at in range(rep_size):
        gain[:, at * depth : (at + 1) * depth] = gains_e[at * 8 : at * 8 + 1, :]
    loads[0].wait()

    for at in range(width // TILE):
        cols = slice(at * TILE, (at + 1) * TILE)
        rows_low = lax.dot_general(
            spread_m[...],
            arrived[:, cols],
            (((0,), (0,)), ((), ())),
            preferred_element_type=wide,
        ).astype(low)

        @pl.when(first)
        def _():
            own_x[:, cols] = rows_low

        @pl.when(second)
        def _():
            own_cot[:, cols] = rows_low

    pl.semaphore_wait(barrier, exp_size - 1 + 2 * (rep_size - 1))

    gate_copy = remote(gates, gates, gate_s.at[0], gate_r.at[0], side_peer)
    grad_copy = remote(gate_grads, gate_grads, gate_s.at[1], gate_r.at[1], side_peer)

    @pl.when(first)
    def _():
        logit = lax.dot_general(
            own_x[...], cent_b[...], (((1,), (1,)), ((), ())), preferred_element_type=wide
        )
        gates[...] = jax.nn.sigmoid(logit)
        gate_copy.start()

    def hop_forward(at):
        rows = pl.ds(at * part, part)
        return remote(hop.at[rows], own_x.at[rows], hop_s.at[at], hop_r.at[at], side_peer)

    def own_slice(at):
        return pl.ds(at * 2 * part + part, part)

    def other_slice(at):
        return pl.ds(at * 2 * part, part)

    def hop_backward(at):
        rows = pl.ds(at * part, part)
        return remote(
            hop.at[rows], states.at[own_slice(at)], hop_s.at[at], hop_r.at[at], side_peer
        )

    for load in loads[1:]:
        load.wait()

    def forward(at):
        base = at * part

        @pl.when(second)
        def _():
            hop_forward(at).wait_recv()

        @pl.loop(0, part // ROWS)
        def _(step):
            off = pl.multiple_of(step * ROWS, ROWS)
            unit, _ = row_stats(own_x[pl.ds(base + off, ROWS), :].astype(wide))
            normed[pl.ds(at * 2 * part + part + off, ROWS), :] = (unit * gain[...]).astype(low)

        norm_copy = remote(
            normed.at[own_slice(at)], normed.at[other_slice(at)], norm_s.at[at], norm_r.at[at], core_peer
        )
        norm_copy.start()
        norm_copy.wait_recv()

        @pl.loop(0, wide_ff // TILE)
        def _(step):
            cols = pl.ds(pl.multiple_of(step * TILE, TILE), TILE)
            inner = jnp.dot(
                normed[pl.ds(at * 2 * part, 2 * part), :],
                inner_w[:, cols],
                preferred_element_type=wide,
            )
            normal = 0.5 * (1.0 + lax.erf(inner * ROOT_HALF))
            active[pl.ds(at * 2 * part, 2 * part), cols] = (inner * normal).astype(low)
            slope[pl.ds(at * 2 * part, 2 * part), cols] = (
                normal + inner * jnp.exp(-0.5 * inner * inner) * INV_ROOT_TAU
            ).astype(low)

        @pl.loop(0, width // TILE)
        def _(step):
            cols = pl.ds(pl.multiple_of(step * TILE, TILE), TILE)
            fwd_send[pl.ds(base, part), cols] = jnp.dot(
                active[other_slice(at), :], outer_w[:, cols], preferred_element_type=wide
            ).astype(low)

        rows = pl.ds(base, part)
        copy = remote(fwd_send.at[rows], fwd_recv.at[rows], fwd_s.at[at], fwd_r.at[at], core_peer)
        copy.start()

        @pl.loop(0, width // TILE)
        def _(step):
            cols = pl.ds(pl.multiple_of(step * TILE, TILE), TILE)
            acc[:, cols] = jnp.dot(
                active[own_slice(at), :], outer_w[:, cols], preferred_element_type=wide
            )

        copy.wait_recv()

        @pl.when(first)
        def _():
            @pl.loop(0, part // ROWS)
            def _(step):
                off = pl.multiple_of(step * ROWS, ROWS)
                here = pl.ds(base + off, ROWS)
                result = (
                    own_x[here, :].astype(wide)
                    + acc[pl.ds(off, ROWS), :]
                    + fwd_recv[here, :].astype(wide)
                )
                hop[here, :] = result.astype(low)

            hop_forward(at).start()

        @pl.when(second)
        def _():
            if at == 0:
                gate_copy.wait_recv()

            @pl.loop(0, part // ROWS)
            def _(step):
                off = pl.multiple_of(step * ROWS, ROWS)
                here = pl.ds(base + off, ROWS)
                result = (
                    own_x[here, :].astype(wide)
                    + acc[pl.ds(off, ROWS), :]
                    + fwd_recv[here, :].astype(wide)
                )
                cot = own_cot[here, :].astype(wide)
                gate = gates[here, :][:, :1]
                back[here, :] = (gate * result).astype(low)
                gate_grads[here, :] = jnp.broadcast_to(
                    jnp.sum(cot * result, axis=1, keepdims=True), (ROWS, gate_grads.shape[1])
                )
                states[pl.ds(at * 2 * part + part + off, ROWS), :] = (gate * cot).astype(low)

    for at in range(CHUNKS):
        forward(at)

    def home_rows(at):
        return slot_rows((at % 2) * (exp_size // 2) + at // 2)

    def ret_copy(dest):
        return remote(
            spread.at[slot_rows(dest)],
            home.at[home_rows(exp_at)],
            ret_s.at[dest],
            ret_r.at[exp_at],
            (rep_at, dest),
        )

    ret_own = pltpu.make_async_copy(
        spread.at[slot_rows(exp_at)], home.at[home_rows(exp_at)], ret_s.at[exp_at]
    )

    def send_back():
        @pl.loop(0, width // TILE)
        def _(step):
            cols = pl.ds(pl.multiple_of(step * TILE, TILE), TILE)
            spread[:, cols] = jnp.dot(
                spread_m[...], back[:, cols], preferred_element_type=wide
            ).astype(low)

        @pl.loop(1, exp_size)
        def _(step):
            ret_copy(exp_at ^ step).start()

        ret_own.start()

    @pl.when(second)
    def _():
        grad_copy.start()
        send_back()

    centre_grad[...] = jnp.zeros_like(centre_grad)

    def backward(at):
        base = at * part

        @pl.when(first)
        def _():
            hop_backward(at).wait_recv()

        copy = remote(
            states.at[own_slice(at)], states.at[other_slice(at)], state_s.at[at], state_r.at[at], core_peer
        )
        copy.start()
        copy.wait_recv()

        @pl.loop(0, wide_ff // TILE)
        def _(step):
            rows = pl.ds(pl.multiple_of(step * TILE, TILE), TILE)
            grad_active = lax.dot_general(
                states[pl.ds(at * 2 * part, 2 * part), :],
                outer_w[rows, :],
                (((1,), (1,)), ((), ())),
                preferred_element_type=wide,
            )
            here = pl.ds(at * 2 * part, 2 * part)
            slope[here, rows] = (grad_active * slope[here, rows].astype(wide)).astype(low)

        @pl.loop(0, width // TILE)
        def _(step):
            cols = pl.ds(pl.multiple_of(step * TILE, TILE), TILE)
            bwd_send[pl.ds(base, part), cols] = lax.dot_general(
                slope[other_slice(at), :],
                inner_w[cols, :],
                (((1,), (1,)), ((), ())),
                preferred_element_type=wide,
            ).astype(low)

        rows = pl.ds(base, part)
        back_copy = remote(
            bwd_send.at[rows], bwd_recv.at[rows], bwd_s.at[at], bwd_r.at[at], core_peer
        )
        back_copy.start()

        @pl.loop(0, width // TILE)
        def _(step):
            cols = pl.ds(pl.multiple_of(step * TILE, TILE), TILE)
            acc[:, cols] = lax.dot_general(
                slope[own_slice(at), :],
                inner_w[cols, :],
                (((1,), (1,)), ((), ())),
                preferred_element_type=wide,
            )

        back_copy.wait_recv()
        if at == 0:

            @pl.when(first)
            def _():
                grad_copy.wait_recv()

        @pl.when(first)
        def _():
            hop_forward(at).wait_send()

        @pl.loop(0, part // ROWS)
        def _(step):
            off = pl.multiple_of(step * ROWS, ROWS)
            here = pl.ds(base + off, ROWS)
            rows_in = own_x[here, :].astype(wide)
            unit, inv_scale = row_stats(rows_in)
            grad_unit = (acc[pl.ds(off, ROWS), :] + bwd_recv[here, :].astype(wide)) * gain[...]
            grad_in = (
                grad_unit
                - jnp.mean(grad_unit, axis=-1, keepdims=True)
                - unit * jnp.mean(grad_unit * unit, axis=-1, keepdims=True)
            ) * inv_scale
            gate = gates[here, :][:, :1]

            @pl.when(second)
            def _():
                state = gate * own_cot[here, :].astype(wide) + grad_in
                hop[here, :] = state.astype(low)

            @pl.when(first)
            def _():
                state = states[pl.ds(at * 2 * part + part + off, ROWS), :].astype(wide) + grad_in
                grad_logit = gate_grads[here, :][:, :1] * gate * (1.0 - gate)
                back[here, :] = (state + grad_logit * cent_b[:1, :].astype(wide)).astype(low)
                centre_grad[...] += jnp.sum(grad_logit * rows_in, axis=0, keepdims=True)

        @pl.when(second)
        def _():
            hop_backward(at).start()

    for at in range(CHUNKS):
        backward(at)

    def eight_rows(at):
        return pl.ds(pl.multiple_of(at * 8, 8), 8)

    def centre_copy(mask, flip):
        dest = rep_at ^ mask
        return remote(
            centre_v.at[eight_rows(flip * rep_size + dest)],
            centre_parts.at[eight_rows(rep_at)],
            centre_s.at[flip * rep_size + mask],
            centre_r.at[mask],
            (dest, exp_at ^ flip),
        )

    centre_own = pltpu.make_async_copy(
        centre_v.at[eight_rows(rep_at)], centre_parts.at[eight_rows(rep_at)], centre_s.at[0]
    )
    centre_pairs = [(m, f) for m in range(rep_size) for f in range(2) if m or f]

    @pl.when(first)
    def _():
        send_back()
        for at in range(width // piece):
            centre_v[at * 8 : (at + 1) * 8, :] = jnp.broadcast_to(
                centre_grad[:, at * piece : (at + 1) * piece], (8, piece)
            )
        centre_own.start()
        for mask, flip in centre_pairs:
            centre_copy(mask, flip).start()

    outs = []
    for at in range(2 * block // TILE):
        rows = slice(at * TILE, (at + 1) * TILE)
        grad = lax.dot_general(
            active[:, rows], states[...], (((0,), (0,)), ((), ())), preferred_element_type=wide
        )
        if (at + 1) * TILE <= block:
            outer_keep_v[rows, :] = grad
            outs.append((outer_keep_v.at[rows], outer_keep.at[rows]))
        else:
            rows = slice(at * TILE - block, (at + 1) * TILE - block)
            outer_send_v[rows, :] = grad.astype(low)
            outs.append((outer_send_v.at[rows], outer_send.at[rows]))
        pltpu.make_async_copy(outs[-1][0], outs[-1][1], out_sem.at[len(outs) - 1]).start()
    for mask in range(rep_size):
        for side in range(2):
            cols = slice(side * block, (side + 1) * block)
            grad = lax.dot_general(
                normed[:, inner_rows(mask)],
                slope[:, cols],
                (((0,), (0,)), ((), ())),
                preferred_element_type=wide,
            )
            inner_send_v[mask, side] = grad.astype(low)
            outs.append((inner_send_v.at[mask, side], inner_send.at[mask, side]))
            pltpu.make_async_copy(outs[-1][0], outs[-1][1], out_sem.at[len(outs) - 1]).start()

    for at, (source, target) in enumerate(outs):
        pltpu.make_async_copy(source, target, out_sem.at[at]).wait()
    for at in range(CHUNKS):
        rows = pl.ds(at * part, part)
        remote(
            normed.at[own_slice(at)], normed.at[other_slice(at)], norm_s.at[at], norm_r.at[at], core_peer
        ).wait_send()
        remote(
            states.at[own_slice(at)], states.at[other_slice(at)], state_s.at[at], state_r.at[at], core_peer
        ).wait_send()
        remote(
            fwd_send.at[rows], fwd_recv.at[rows], fwd_s.at[at], fwd_r.at[at], core_peer
        ).wait_send()
        remote(
            bwd_send.at[rows], bwd_recv.at[rows], bwd_s.at[at], bwd_r.at[at], core_peer
        ).wait_send()

        @pl.when(second)
        def _():
            hop_backward(at).wait_send()

    @pl.when(first)
    def _():
        gate_copy.wait_send()

    @pl.when(second)
    def _():
        grad_copy.wait_send()

    @pl.when(first)
    def _():
        centre_own.wait()
        for mask, flip in centre_pairs:
            centre_copy(mask, flip).wait_send()
        for mask in range(1, rep_size):
            centre_copy(mask, 0).wait_recv()

    @pl.when(second)
    def _():
        for mask in range(rep_size):
            centre_copy(mask, 1).wait_recv()

    ret_own.wait()

    @pl.loop(1, exp_size)
    def _(step):
        source = exp_at ^ step
        remote(
            spread.at[slot_rows(source)],
            home.at[home_rows(source)],
            ret_s.at[source],
            ret_r.at[source],
            (rep_at, source),
        ).wait()


def run_experts(
    exp_size, rep_size, slots, own_rows, arrived, inner_w, outer_w, counts_all, cents, gains_e
):
    width = arrived.shape[1]
    depth = width // rep_size
    block = outer_w.shape[0] // 2
    low = jnp.bfloat16
    wide = jnp.float32
    total = exp_size * slots
    all_rows = 2 * own_rows
    part = own_rows // CHUNKS
    piece = cents.shape[1]
    anyplace = pl.BlockSpec(memory_space=pl.ANY)
    inside = pl.BlockSpec(memory_space=pltpu.VMEM)
    dma = pltpu.SemaphoreType.DMA
    n_out = 2 * block // TILE + 2 * rep_size
    scratch = [
        pltpu.VMEM((total, width), low),
        pltpu.VMEM((total, own_rows), low),
        pltpu.VMEM((2, exp_size * 16, 128), wide),
        pltpu.VMEM((128, width), low),
        pltpu.VMEM((1, width), wide),
        pltpu.VMEM((1, width), wide),
        pltpu.VMEM((2 * rep_size * 8, piece), wide),
        pltpu.VMEM((width, 2 * block), low),
        pltpu.VMEM((2 * block, width), low),
        pltpu.VMEM((own_rows, width), low),
        pltpu.VMEM((own_rows, width), low),
        pltpu.VMEM((all_rows, width), low),
        pltpu.VMEM((all_rows, 2 * block), low),
        pltpu.VMEM((all_rows, 2 * block), low),
        pltpu.VMEM((all_rows, width), low),
        pltpu.VMEM((own_rows, width), low),
        pltpu.VMEM((own_rows, width), low),
        pltpu.VMEM((own_rows, width), low),
        pltpu.VMEM((own_rows, width), low),
        pltpu.VMEM((own_rows, width), low),
        pltpu.VMEM((own_rows, width), low),
        pltpu.VMEM((total, width), low),
        pltpu.VMEM((part, width), wide),
        pltpu.VMEM((own_rows, 128), wide),
        pltpu.VMEM((own_rows, 128), wide),
        pltpu.VMEM((block, width), wide),
        pltpu.VMEM((block, width), low),
        pltpu.VMEM((rep_size, 2, depth, block), low),
        dma((3,)),
        dma((2 * rep_size,)),
        dma((rep_size,)),
    ]
    scratch += [dma((CHUNKS,)) for _ in range(10)]
    scratch += [dma((2,)), dma((2,)), dma((exp_size,)), dma((exp_size,)), dma((n_out,))]
    flops = 2 * all_rows * width * 2 * block * 6
    return pl.pallas_call(
        functools.partial(expert_kernel, exp_size, rep_size, slots),
        out_shape=(
            jax.ShapeDtypeStruct((total, width), low),
            jax.ShapeDtypeStruct((block, width), wide),
            jax.ShapeDtypeStruct((block, width), low),
            jax.ShapeDtypeStruct((rep_size, 2, depth, block), low),
            jax.ShapeDtypeStruct((rep_size * 8, piece), wide),
        ),
        in_specs=[anyplace] * 3 + [inside] * 3,
        out_specs=(anyplace,) * 5,
        scratch_shapes=scratch,
        compiler_params=pltpu.CompilerParams(
            collective_id=0, has_side_effects=True, vmem_limit_bytes=62 << 20
        ),
        cost_estimate=pl.CostEstimate(
            flops=flops, bytes_accessed=40 << 20, transcendentals=2 * all_rows * 2 * block
        ),
        name="experts",
    )(arrived, inner_w, outer_w, counts_all, cents, gains_e)


def finish_kernel(
    exp_size,
    rep_size,
    home,
    pick,
    hidden,
    cotangent,
    tokens,
    gain_row,
    qkv,
    probs,
    normed_a,
    context,
    attn_w,
    outer_send,
    inner_send,
    output,
    grad_tokens,
    shares,
    outer_recv,
    inner_zero,
    inner_one,
    weights,
    grad_hidden,
    grad_attn,
    grad_context,
    grads3,
    keep,
    core_out,
    core_in,
    side_out,
    side_in,
    line_out,
    line_in,
    total,
    row_out,
    row_in,
    half_out,
    half_in,
    load_s,
    expert_s,
    expert_r,
    core_s,
    core_r,
    side_s,
    side_r,
    line_s,
    line_r,
    row_s,
    row_r,
    half_s,
    half_r,
):
    low = jnp.bfloat16
    wide = jnp.float32
    rep_at = lax.axis_index("rep")
    exp_at = lax.axis_index("exp")
    core = rep_at % 2
    group = exp_at // 2
    side = exp_at % 2
    groups = exp_size // 2
    rows_n, width = tokens.shape
    half = width // 2
    block = width // exp_size
    ff_block = inner_zero.shape[1] // rep_size
    core_peer = (rep_at ^ 1, exp_at)
    side_peer = (rep_at, exp_at ^ 1)
    row_peer = (rep_at ^ 2, exp_at)

    load = pltpu.make_async_copy(attn_w, weights, load_s.at[0])
    load.start()

    barrier = pltpu.get_barrier_semaphore()
    for mask in range(1, rep_size):
        pl.semaphore_signal(
            barrier, inc=1, device_id=(rep_at ^ mask, exp_at), device_id_type=MESH
        )

    @pl.loop(1, exp_size)
    def _(at):
        pl.semaphore_signal(barrier, inc=1, device_id=(rep_at, exp_at ^ at), device_id_type=MESH)

    pl.semaphore_wait(barrier, exp_size - 1 + rep_size - 1)

    outer_copy = remote(outer_send, outer_recv, expert_s.at[0], expert_r.at[0], row_peer)

    def inner_copies(mask):
        found = []
        for part, target in enumerate((inner_zero, inner_one)):
            at = rep_at ^ (2 * part)
            cols = pl.ds(pl.multiple_of(at * ff_block, ff_block), ff_block)
            source = inner_send.at[mask, part]
            if mask == 0:
                found.append(
                    pltpu.make_async_copy(source, target.at[:, cols], expert_s.at[1 + part])
                )
            else:
                found.append(
                    remote(
                        source,
                        target.at[:, cols],
                        expert_s.at[1 + 2 * mask + part],
                        expert_r.at[1 + 2 * mask + part],
                        (rep_at ^ mask, exp_at),
                    )
                )
        return found

    for mask in (2, 3, 1, 0):
        for copy in inner_copies(mask):
            copy.start()
    outer_copy.start()

    all_slots = pick.shape[0]

    @pl.loop(0, width // TILE)
    def _(step):
        cols = pl.ds(pl.multiple_of(step * TILE, TILE), TILE)
        back = lax.dot_general(
            pick[...], home[:all_slots, cols], (((0,), (0,)), ((), ())), preferred_element_type=wide
        )
        grad = cotangent[:, cols].astype(wide) + back
        grad_hidden[:, cols] = grad
        grad_attn[:, cols] = grad.astype(low)
        branch = lax.dot_general(
            pick[...], home[all_slots:, cols], (((0,), (0,)), ((), ())), preferred_element_type=wide
        )
        output[:, cols] = (hidden[:, cols] + branch).astype(low)

    own_half = pl.ds(pl.multiple_of(core * half, half), half)
    other_half = pl.ds(pl.multiple_of((1 - core) * half, half), half)

    def core_copy(at):
        return remote(core_out.at[at], core_in.at[at], core_s.at[at], core_r.at[at], core_peer)

    def product(at, left, right, cols, target, kind):
        @pl.loop(0, width // TILE)
        def _(step):
            rows = pl.ds(pl.multiple_of(step * TILE, TILE), TILE)
            target[at, rows, :] = lax.dot_general(
                left[:, rows], right[:, cols], (((0,), (0,)), ((), ())), preferred_element_type=wide
            ).astype(kind)

    def share_start(at, left, right):
        product(at, left, right, other_half, core_out, low)
        core_copy(at).start()
        product(at, left, right, own_half, keep, wide)

    def block_rows(at):
        return pl.ds(pl.multiple_of(at * block, block), block)

    def side_copy(at):
        return remote(side_out.at[at], side_in.at[at], side_s.at[at], side_r.at[at], side_peer)

    def share_side(at):
        core_copy(at).wait_recv()

        @pl.loop(0, groups)
        def _(which):
            rows = block_rows(2 * which + 1 - side)
            side_out[at, block_rows(which), :] = (
                keep[at, rows, :] + core_in[at, rows, :].astype(wide)
            ).astype(low)

        side_copy(at).start()

        @pl.loop(0, groups)
        def _(which):
            rows = block_rows(2 * which + side)
            keep[at, rows, :] = keep[at, rows, :] + core_in[at, rows, :].astype(wide)

    def line_copy(at, mask):
        dest = group ^ mask
        return remote(
            line_out.at[at, block_rows(dest)],
            line_in.at[at, block_rows(group)],
            line_s.at[at, mask],
            line_r.at[at, mask],
            (rep_at, 2 * dest + side),
        )

    def share_line(at):
        side_copy(at).wait_recv()

        @pl.loop(1, groups)
        def _(mask):
            dest = group ^ mask
            line_out[at, block_rows(dest), :] = (
                keep[at, block_rows(2 * dest + side), :] + side_in[at, block_rows(dest), :].astype(wide)
            ).astype(low)
            line_copy(at, mask).start()

        total[at] = keep[at, block_rows(exp_at), :] + side_in[at, block_rows(group), :].astype(wide)

    def row_copy(at):
        return remote(row_out.at[at], row_in.at[at], row_s.at[at], row_r.at[at], row_peer)

    def share_row(at):
        @pl.loop(1, groups)
        def _(mask):
            line_copy(at, mask).wait_recv()
            total[at] = total[at] + line_in[at, block_rows(group ^ mask), :].astype(wide)

        row_out[at] = total[at].astype(low)
        row_copy(at).start()

    def half_copy(at):
        return remote(half_out.at[at], half_in.at[at], half_s.at[at], half_r.at[at], core_peer)

    def share_half(at):
        row_copy(at).wait_recv()
        summed = row_out[at].astype(wide) + row_in[at].astype(wide)
        half_out[at] = summed
        half_copy(at).start()
        shares[at, :, own_half] = summed

    def share_end(at):
        half_copy(at).wait_recv()
        shares[at, :, other_half] = half_in[at]

    share_start(3, context, grad_attn)
    load.wait()

    @pl.loop(0, width // TILE)
    def _(step):
        rows = pl.ds(pl.multiple_of(step * TILE, TILE), TILE)
        grad_context[:, rows] = lax.dot_general(
            grad_attn[...], weights[3, rows, :], (((1,), (1,)), ((), ())), preferred_element_type=wide
        ).astype(low)

    share_side(3)

    head_dim = width // HEADS
    pair = 2 * head_dim
    factor = head_dim ** (-0.5)
    lane = lax.broadcasted_iota(jnp.int32, (rows_n, pair), 1)

    def heads(start, stop):
        @pl.loop(start, stop)
        def _(at):
            cols = pl.ds(pl.multiple_of(at * pair, pair), pair)
            q_pair = qkv[0, :, cols]
            k_pair = qkv[1, :, cols]
            v_pair = qkv[2, :, cols]
            c_pair = grad_context[:, cols]
            found = []
            for which in range(2):
                chosen = (lane >= head_dim) if which else (lane < head_dim)
                c_one = jnp.where(chosen, c_pair, jnp.zeros_like(c_pair))
                prob = probs[pl.ds(pl.multiple_of((2 * at + which) * rows_n, rows_n), rows_n), :]
                grad_prob = lax.dot_general(
                    c_one, v_pair, (((1,), (1,)), ((), ())), preferred_element_type=wide
                )
                weighted = prob.astype(wide) * grad_prob
                row_sum = jnp.sum(weighted, axis=1, keepdims=True)
                grad_score = (weighted - prob.astype(wide) * row_sum).astype(low)
                found.append(
                    (
                        jnp.dot(grad_score, k_pair, preferred_element_type=wide) * factor,
                        lax.dot_general(
                            grad_score,
                            q_pair,
                            (((0,), (0,)), ((), ())),
                            preferred_element_type=wide,
                        )
                        * factor,
                        lax.dot_general(
                            prob, c_pair, (((0,), (0,)), ((), ())), preferred_element_type=wide
                        ),
                    )
                )
            for which in range(3):
                grads3[which, :, cols] = jnp.where(
                    lane < head_dim, found[0][which], found[1][which]
                ).astype(low)

    heads(0, HEADS // 4)
    share_line(3)
    heads(HEADS // 4, HEADS // 2)
    for at in range(3):
        share_start(at, normed_a, grads3.at[at])
    for at in range(3):
        share_side(at)
    share_row(3)

    @pl.loop(0, width // TILE)
    def _(step):
        rows = pl.ds(pl.multiple_of(step * TILE, TILE), TILE)
        grad_normed = jnp.zeros((rows_n, TILE), wide)
        for at in range(3):
            grad_normed = grad_normed + lax.dot_general(
                grads3[at], weights[at, rows, :], (((1,), (1,)), ((), ())), preferred_element_type=wide
            )
        grad_tokens[:, rows] = grad_normed

    share_half(3)

    @pl.loop(0, rows_n // ROWS)
    def _(step):
        here = pl.ds(pl.multiple_of(step * ROWS, ROWS), ROWS)
        unit, inv_scale = row_stats(tokens[here, :].astype(wide))
        grad_unit = grad_tokens[here, :] * gain_row[...]
        grad_in = (
            grad_unit
            - jnp.mean(grad_unit, axis=-1, keepdims=True)
            - unit * jnp.mean(grad_unit * unit, axis=-1, keepdims=True)
        ) * inv_scale
        grad_tokens[here, :] = grad_hidden[here, :] + grad_in

    for at in range(3):
        share_line(at)
    share_end(3)
    for at in range(3):
        share_row(at)
    for at in range(3):
        share_half(at)
    for at in range(3):
        share_end(at)

    for at in range(4):
        core_copy(at).wait_send()
        side_copy(at).wait_send()
        row_copy(at).wait_send()
        half_copy(at).wait_send()

        @pl.loop(1, groups)
        def _(mask):
            line_copy(at, mask).wait_send()

    for mask in range(rep_size):
        for copy in inner_copies(mask):
            copy.wait()
    outer_copy.wait()


def run_finish(exp_size, rep_size, home, pick, hidden, cotangent, tokens, gain_row, qkv, probs, normed_a, context, attn_w, outer_send, inner_send):
    rows_n, width = tokens.shape
    low = jnp.bfloat16
    wide = jnp.float32
    half = width // 2
    groups = exp_size // 2
    block = width // exp_size
    depth, ff_block = inner_send.shape[2:]
    anyplace = pl.BlockSpec(memory_space=pl.ANY)
    inside = pl.BlockSpec(memory_space=pltpu.VMEM)
    dma = pltpu.SemaphoreType.DMA
    shape = jax.ShapeDtypeStruct
    return pl.pallas_call(
        functools.partial(finish_kernel, exp_size, rep_size),
        out_shape=(
            shape((rows_n, width), low),
            shape((rows_n, width), wide),
            shape((4, block, width), wide),
            shape(outer_send.shape, low),
            shape((depth, rep_size * ff_block), low),
            shape((depth, rep_size * ff_block), low),
        ),
        in_specs=[inside] * 10 + [anyplace] * 3,
        out_specs=(inside,) * 3 + (anyplace,) * 3,
        scratch_shapes=[
            pltpu.VMEM((4, width, width), low),
            pltpu.VMEM((rows_n, width), wide),
            pltpu.VMEM((rows_n, width), low),
            pltpu.VMEM((rows_n, width), low),
            pltpu.VMEM((3, rows_n, width), low),
            pltpu.VMEM((4, width, half), wide),
            pltpu.VMEM((4, width, half), low),
            pltpu.VMEM((4, width, half), low),
            pltpu.VMEM((4, width // 2, half), low),
            pltpu.VMEM((4, width // 2, half), low),
            pltpu.VMEM((4, width // 2, half), low),
            pltpu.VMEM((4, width // 2, half), low),
            pltpu.VMEM((4, block, half), wide),
            pltpu.VMEM((4, block, half), low),
            pltpu.VMEM((4, block, half), low),
            pltpu.VMEM((4, block, half), wide),
            pltpu.VMEM((4, block, half), wide),
            dma((1,)),
            dma((1 + 2 * rep_size,)),
            dma((1 + 2 * rep_size,)),
            dma((4,)),
            dma((4,)),
            dma((4,)),
            dma((4,)),
            dma((4, groups)),
            dma((4, groups)),
            dma((4,)),
            dma((4,)),
            dma((4,)),
            dma((4,)),
        ],
        compiler_params=pltpu.CompilerParams(
            collective_id=2, has_side_effects=True, vmem_limit_bytes=60 << 20
        ),
        cost_estimate=pl.CostEstimate(
            flops=20 * rows_n * width * width, bytes_accessed=60 << 20, transcendentals=0
        ),
        name="finish",
    )(
        home,
        pick,
        hidden,
        cotangent,
        tokens,
        gain_row,
        qkv,
        probs,
        normed_a,
        context,
        attn_w,
        outer_send,
        inner_send,
    )


def shards(
    tokens,
    cotangent,
    doc_lengths,
    expert_of_token,
    w_query,
    w_key,
    w_value,
    w_output,
    attn_gain,
    w_inner,
    w_outer,
    expert_gain,
    centroids,
):
    exp_size = lax.axis_size("exp")
    rep_size = lax.axis_size("rep")
    row_count = tokens.shape[0]
    wide = jnp.float32

    slots = -(-3 * row_count // exp_size // 16) * 16
    (
        attn_w,
        inner_w,
        outer_w,
        arrived,
        counts_all,
        cents,
        gains_e,
        hidden,
        qkv,
        probs,
        normed_a,
        context,
        pick,
        gain_row,
    ) = run_attend(
        exp_size,
        rep_size,
        slots,
        tokens,
        cotangent,
        doc_lengths,
        expert_of_token[None],
        (w_query, w_key, w_value, w_output),
        attn_gain[None],
        w_inner[0],
        w_outer[0],
        expert_gain,
        centroids,
    )
    home, outer_keep, outer_send, inner_send, centre_parts = run_experts(
        exp_size,
        rep_size,
        slots,
        2 * row_count,
        arrived,
        inner_w,
        outer_w,
        counts_all,
        cents,
        gains_e,
    )
    output, grad_tokens, shares, outer_recv, inner_zero, inner_one = run_finish(
        exp_size,
        rep_size,
        home,
        pick,
        hidden,
        cotangent,
        tokens,
        gain_row,
        qkv,
        probs,
        normed_a,
        context,
        attn_w,
        outer_send,
        inner_send,
    )
    grad_centroids = jnp.sum(centre_parts.reshape(rep_size, 8, -1)[:, 0], axis=0)[None]
    grad_w_outer = (outer_keep + outer_recv.astype(wide))[None]
    summed = inner_zero.astype(wide) + inner_one.astype(wide)
    grad_w_inner = summed[None]
    grad_expert_gain = jnp.sum(summed * w_inner[0].astype(wide), axis=1)[None] / expert_gain.astype(
        wide
    )
    share_gain = sum(
        jnp.sum(shares[i] * w.astype(wide), axis=1) for i, w in enumerate((w_query, w_key, w_value))
    ) / attn_gain.astype(wide)
    return (
        output,
        grad_tokens,
        shares[0],
        shares[1],
        shares[2],
        shares[3],
        share_gain,
        grad_w_inner,
        grad_w_outer,
        grad_expert_gain,
        grad_centroids,
    )


def solution(mesh):
    placed = (
        P(("rep", "exp"), None),
        P(("rep", "exp"), None),
        P(("rep", "exp"), None),
        P(("rep", "exp")),
        P("exp", None),
        P("exp", None),
        P("exp", None),
        P("exp", None),
        P("exp"),
        P("exp", "rep", None),
        P("exp", "rep", None),
        P("exp", "rep"),
        P("exp", "rep"),
    )
    return jax.shard_map(
        shards,
        mesh=mesh,
        in_specs=placed,
        out_specs=(
            P(("rep", "exp"), None),
            P(("rep", "exp"), None),
            P("exp", None),
            P("exp", None),
            P("exp", None),
            P("exp", None),
            P("exp"),
            P("exp", "rep", None),
            P("exp", "rep", None),
            P("exp", "rep"),
            P("exp", "rep"),
        ),
        check_vma=False,
    )
```

```python
import functools

import jax
import jax.numpy as jnp
from jax import lax
from jax.experimental import pallas as pl
from jax.experimental.pallas import tpu as pltpu
from jax.sharding import PartitionSpec as P

HEADS = 16
EPS = 1e-05
ROOT_HALF = 0.7071067811865476
INV_ROOT_TAU = 0.3989422804014327
CHUNKS = 4
DEFER = 256
EARLY = 512


MESH = pl.DeviceIdType.MESH
TILE = 256
ROWS = 64
BIG = 512


def remote(src, dst, send_sem, recv_sem, device):
    return pltpu.make_async_remote_copy(
        src_ref=src,
        dst_ref=dst,
        send_sem=send_sem,
        recv_sem=recv_sem,
        device_id=device,
        device_id_type=MESH,
    )


def row_stats(rows):
    row_mean = jnp.mean(rows, axis=-1, keepdims=True)
    centered = rows - row_mean
    variance = jnp.mean(centered * centered, axis=-1, keepdims=True)
    inv_scale = lax.rsqrt(variance + EPS)
    return centered * inv_scale, inv_scale


def attend_kernel(
    exp_size,
    rep_size,
    slots,
    tokens,
    cotangent,
    doc,
    expert_of,
    w_query,
    w_key,
    w_value,
    w_output,
    gain_a,
    w_inner,
    w_outer,
    gain_e,
    cent,
    attn_w,
    inner_w,
    outer_w,
    arrived,
    counts_all,
    cents,
    gains_e,
    hidden,
    qkv,
    probs,
    normed_a,
    context,
    pick,
    gain_row,
    weights,
    staging,
    small_all,
    gain_v,
    packed_x,
    packed_c,
    bias,
    counts_v,
    cent_v,
    own_s,
    line_s,
    line_r,
    side_s,
    side_r,
    core_s,
    core_r,
    weight_s,
    weight_r,
    disp_s,
    disp_r,
    count_s,
    count_r,
    cent_s,
    cent_r,
    gain_s,
    gain_r,
    out_s,
):
    low = jnp.bfloat16
    wide = jnp.float32
    rep_at = lax.axis_index("rep")
    exp_at = lax.axis_index("exp")
    core = rep_at % 2
    group = exp_at // 2
    side = exp_at % 2
    groups = exp_size // 2
    rows_n, width = tokens.shape
    half = width // 2
    block = w_query.shape[0]
    depth = w_inner.shape[0]
    ff_block = w_outer.shape[0]
    core_peer = (rep_at ^ 1, exp_at)
    side_peer = (rep_at, exp_at ^ 1)

    def block_rows(at):
        return pl.ds(pl.multiple_of(at * block, block), block)

    own_loads = []
    for at, source in enumerate((w_query, w_key, w_value, w_output)):
        own_loads.append(
            pltpu.make_async_copy(source, weights.at[at, block_rows(exp_at)], own_s.at[at])
        )
    for load in own_loads:
        load.start()

    barrier = pltpu.get_barrier_semaphore()
    for mask in range(1, rep_size):
        for flip in range(2):
            pl.semaphore_signal(
                barrier, inc=1, device_id=(rep_at ^ mask, exp_at ^ flip), device_id_type=MESH
            )

    @pl.loop(1, exp_size)
    def _(at):
        pl.semaphore_signal(barrier, inc=1, device_id=(rep_at, exp_at ^ at), device_id_type=MESH)

    pl.semaphore_wait(barrier, exp_size - 1 + 2 * (rep_size - 1))

    outer_copy = remote(
        w_outer.at[: ff_block - DEFER],
        outer_w.at[ff_block:],
        weight_s.at[0],
        weight_r.at[0],
        (rep_at ^ 2, exp_at),
    )
    outer_own = pltpu.make_async_copy(w_outer, outer_w.at[:ff_block], own_s.at[5])
    outer_own.start()

    for load in own_loads:
        load.wait()

    picks = (slice(0, 3), slice(3, 4))
    own_half = pl.ds(pl.multiple_of(core * half, half), half)

    def view(kind, at):
        return weights.at[picks[kind], block_rows(at), own_half]

    def line_copy(kind, source, step):
        at = 2 * source + side
        return remote(
            view(kind, at),
            view(kind, at),
            line_s.at[kind, (1 + step) // 2, source],
            line_r.at[kind, source],
            (rep_at, exp_at + 2 * step),
        )

    def line_wait(kind, source):
        at = 2 * source + side
        remote(
            view(kind, at), view(kind, at), line_s.at[kind, 0, source], line_r.at[kind, source], side_peer
        ).wait_recv()

    def side_copy(kind, source):
        at = 2 * source + side
        return remote(
            view(kind, at), view(kind, at), side_s.at[kind, source], side_r.at[kind, source], side_peer
        )

    def side_wait(kind, source):
        at = 2 * source + 1 - side
        remote(
            view(kind, at), view(kind, at), side_s.at[kind, source], side_r.at[kind, source], side_peer
        ).wait_recv()

    def core_copy(kind, at):
        return remote(view(kind, at), view(kind, at), core_s.at[kind, at], core_r.at[kind, at], core_peer)

    def core_wait(kind, at):
        other = pl.ds(pl.multiple_of((1 - core) * half, half), half)
        there = weights.at[picks[kind], block_rows(at), other]
        remote(there, there, core_s.at[kind, at], core_r.at[kind, at], core_peer).wait_recv()

    def first_sends(kind):
        @pl.when(group + 1 < groups)
        def _():
            line_copy(kind, group, 1).start()

        @pl.when(group >= 1)
        def _():
            line_copy(kind, group, -1).start()

        side_copy(kind, group).start()

    def take_side(kind, source):
        side_wait(kind, source)
        core_copy(kind, 2 * source + 1 - side).start()

    def gather_step(kind, step):
        @pl.when(group - step >= 0)
        def _():
            source = group - step
            line_wait(kind, source)

            @pl.when(group + 1 < groups)
            def _():
                line_copy(kind, source, 1).start()

            side_copy(kind, source).start()
            core_copy(kind, 2 * source + side).start()

        @pl.when(group + step < groups)
        def _():
            source = group + step
            line_wait(kind, source)

            @pl.when(group >= 1)
            def _():
                line_copy(kind, source, -1).start()

            side_copy(kind, source).start()
            core_copy(kind, 2 * source + side).start()

        @pl.when(group - step + 1 >= 0)
        def _():
            take_side(kind, group - step + 1)

        @pl.when((step > 1) & (group + step - 1 < groups))
        def _():
            take_side(kind, group + step - 1)

    def gather_end(kind):
        last = groups - 1

        @pl.when(group - last >= 0)
        def _():
            take_side(kind, group - last)

        @pl.when((groups > 1) & (group + last < groups))
        def _():
            take_side(kind, group + last)

        @pl.loop(0, exp_size)
        def _(at):
            @pl.when(at != exp_at)
            def _():
                core_wait(kind, at)

    first_sends(0)
    first_sends(1)

    inner_rows = pl.ds(pl.multiple_of(rep_at * depth, depth), depth)

    def ff_cols(at):
        return pl.ds(pl.multiple_of(at * ff_block, ff_block), ff_block)

    def inner_copies(mask):
        dest = rep_at ^ mask
        found = []
        for part in range(2):
            source = w_inner.at[:, ff_cols(dest ^ (2 * part))]
            cols = slice(part * ff_block, (part + 1) * ff_block)
            at = 1 + 2 * mask + part
            if mask == 0:
                found.append(
                    pltpu.make_async_copy(source, inner_w.at[inner_rows, cols], weight_s.at[at])
                )
            elif mask == 3:
                found.append(
                    remote(
                        source,
                        staging.at[:, cols],
                        weight_s.at[at],
                        weight_r.at[at],
                        (rep_at ^ 2, exp_at),
                    )
                )
            else:
                found.append(
                    remote(
                        source,
                        inner_w.at[inner_rows, cols],
                        weight_s.at[at],
                        weight_r.at[at],
                        (dest, exp_at),
                    )
                )
        return found

    far_rows = pl.ds(pl.multiple_of((rep_at ^ 2) * depth, depth), depth)
    forward_copy = remote(
        staging,
        inner_w.at[far_rows],
        weight_s.at[1 + 2 * rep_size],
        weight_r.at[1 + 2 * rep_size],
        core_peer,
    )

    for mask in (3, 2, 1, 0):
        for copy in inner_copies(mask):
            copy.start()
    outer_copy.start()

    lanes = counts_v.shape[1]
    expert_row = expert_of[...]
    onehot = (
        lax.broadcasted_iota(jnp.int32, (lanes, rows_n), 0) == expert_row
    ).astype(wide)
    before = (
        lax.broadcasted_iota(jnp.int32, (rows_n, rows_n), 0)
        < lax.broadcasted_iota(jnp.int32, (rows_n, rows_n), 1)
    ).astype(low)
    earlier = jnp.dot(onehot.astype(low), before, preferred_element_type=wide)
    rank = jnp.sum(earlier * onehot, axis=0, keepdims=True).astype(jnp.int32)
    position = expert_row * slots + rank
    pick[...] = (
        lax.broadcasted_iota(jnp.int32, pick.shape, 0) == position
    ).astype(wide).astype(low)
    counts_v[:8, :] = lax.dot_general(
        jnp.ones((8, rows_n), low),
        onehot.astype(low),
        (((1,), (1,)), ((), ())),
        preferred_element_type=wide,
    )
    counts_v[8:, :block] = jnp.broadcast_to(gain_a[...].astype(wide), (8, block))
    cent_v[...] = jnp.broadcast_to(cent[...].astype(wide), cent_v.shape)
    gain_v[...] = jnp.broadcast_to(gain_e[...].astype(wide), gain_v.shape)

    def eight(at):
        return pl.ds(pl.multiple_of(at * 8, 8), 8)

    def sixteen(at):
        return pl.ds(pl.multiple_of(at * 16, 16), 16)

    def count_copy(dest):
        return remote(
            counts_v, small_all.at[sixteen(exp_at)], count_s.at[dest], count_r.at[exp_at], (rep_at, dest)
        )

    count_own = pltpu.make_async_copy(counts_v, small_all.at[sixteen(exp_at)], count_s.at[exp_at])
    count_own.start()

    @pl.loop(1, exp_size)
    def _(at):
        count_copy(exp_at ^ at).start()

    cent_at = side * rep_size + rep_at

    def cent_copy(mask, flip):
        return remote(
            cent_v,
            cents.at[eight(cent_at)],
            cent_s.at[flip * rep_size + mask],
            cent_r.at[flip * rep_size + mask],
            (rep_at ^ mask, exp_at ^ flip),
        )

    cent_own = pltpu.make_async_copy(cent_v, cents.at[eight(cent_at)], cent_s.at[0])
    cent_own.start()
    cent_pairs = [(m, f) for m in range(rep_size) for f in range(2) if m or f]
    for mask, flip in cent_pairs:
        cent_copy(mask, flip).start()

    def gain_copy(mask):
        return remote(
            gain_v, gains_e.at[eight(rep_at)], gain_s.at[mask], gain_r.at[mask], (rep_at ^ mask, exp_at)
        )

    gain_own = pltpu.make_async_copy(gain_v, gains_e.at[eight(rep_at)], gain_s.at[0])
    gain_own.start()
    for mask in range(1, rep_size):
        gain_copy(mask).start()

    count_own.wait()

    @pl.loop(1, exp_size)
    def _(at):
        source = exp_at ^ at
        remote(
            counts_v, small_all.at[sixteen(source)], count_s.at[source], count_r.at[source], (rep_at, source)
        ).wait()

    small_store = pltpu.make_async_copy(small_all, counts_all, out_s.at[1])
    small_store.start()

    tiled = jnp.dot(
        small_all[...].astype(low),
        (
            lax.broadcasted_iota(jnp.int32, (lanes, width), 1) % block
            == lax.broadcasted_iota(jnp.int32, (lanes, width), 0)
        ).astype(wide).astype(low),
        preferred_element_type=wide,
    )
    chosen_row = lax.broadcasted_iota(jnp.int32, (16 * exp_size, width), 0) == (
        16 * (lax.broadcasted_iota(jnp.int32, (16 * exp_size, width), 1) // block) + 8
    )
    gain_row[...] = jnp.sum(jnp.where(chosen_row, tiled, 0.0), axis=0, keepdims=True)

    @pl.loop(0, rows_n // ROWS)
    def _(step):
        here = pl.ds(pl.multiple_of(step * ROWS, ROWS), ROWS)
        unit, _ = row_stats(tokens[here, :].astype(wide))
        normed_a[here, :] = (unit * gain_row[...]).astype(low)

    down = lax.broadcasted_iota(jnp.int32, (rows_n, rows_n), 0)
    along = lax.broadcasted_iota(jnp.int32, (rows_n, rows_n), 1)
    end = jnp.int32(0)
    seg_down = jnp.zeros((rows_n, rows_n), jnp.int32)
    seg_along = jnp.zeros((rows_n, rows_n), jnp.int32)
    for at in range(doc.shape[1]):
        end = end + doc[0, at]
        seg_down = seg_down + (down >= end).astype(jnp.int32)
        seg_along = seg_along + (along >= end).astype(jnp.int32)
    bias[...] = jnp.where((seg_down == seg_along) & (down >= along), 0.0, -1e30)

    @pl.loop(1, groups)
    def _(step):
        gather_step(0, step)

    gather_end(0)
    for copy in inner_copies(3):
        copy.wait_recv()
    forward_copy.start()

    def slot_rows(at):
        return pl.ds(pl.multiple_of(at * slots, slots), slots)

    def disp_copy(source, dest):
        return remote(
            source.at[slot_rows(dest // 2)],
            arrived.at[slot_rows(exp_at)],
            disp_s.at[dest],
            disp_r.at[exp_at],
            (rep_at, dest),
        )

    def dispatch(source, flip):
        @pl.loop(0, groups)
        def _(at):
            dest = 2 * (group ^ at) + flip

            @pl.when(dest != exp_at)
            def _():
                disp_copy(source, dest).start()

            @pl.when(dest == exp_at)
            def _():
                pltpu.make_async_copy(
                    source.at[slot_rows(group)], arrived.at[slot_rows(exp_at)], disp_s.at[exp_at]
                ).start()

    @pl.loop(1, 1 + (groups - 1 + 2) // 3)
    def _(step):
        gather_step(1, step)

    for at in range(3):

        @pl.loop(0, width // TILE)
        def _(step):
            cols = pl.ds(pl.multiple_of(step * TILE, TILE), TILE)
            qkv[at, :, cols] = jnp.dot(
                normed_a[...], weights[at, :, cols], preferred_element_type=wide
            ).astype(low)

    head_dim = width // HEADS
    pair = 2 * head_dim
    factor = head_dim ** (-0.5)
    lane = lax.broadcasted_iota(jnp.int32, (rows_n, pair), 1)
    pairs = HEADS // 2
    parts = 2
    begun = (groups - 1 + 2) // 3
    for part in range(parts):
        low_step = 1 + begun + part * (groups - 1 - begun) // parts
        high_step = 1 + begun + (part + 1) * (groups - 1 - begun) // parts

        @pl.loop(low_step, high_step)
        def _(step):
            gather_step(1, step)

        @pl.loop(part * pairs // parts, (part + 1) * pairs // parts)
        def _(at):
            cols = pl.ds(pl.multiple_of(at * pair, pair), pair)
            q_pair = qkv[0, :, cols]
            k_pair = qkv[1, :, cols]
            v_pair = qkv[2, :, cols]
            found = []
            for which in range(2):
                chosen = (lane >= head_dim) if which else (lane < head_dim)
                q_one = jnp.where(chosen, q_pair, jnp.zeros_like(q_pair))
                scores = (
                    lax.dot_general(
                        q_one, k_pair, (((1,), (1,)), ((), ())), preferred_element_type=wide
                    )
                    * factor
                    + bias[...]
                )
                top = jnp.max(scores, axis=1, keepdims=True)
                raised = jnp.exp(scores - top)
                total = jnp.sum(raised, axis=1, keepdims=True)
                prob = (raised * (1.0 / total)).astype(low)
                probs[pl.ds(pl.multiple_of((2 * at + which) * rows_n, rows_n), rows_n), :] = prob
                found.append(jnp.dot(prob, v_pair, preferred_element_type=wide))
            context[:, cols] = jnp.where(lane < head_dim, found[0], found[1]).astype(low)

    @pl.loop(0, width // TILE)
    def _(step):
        cols = pl.ds(pl.multiple_of(step * TILE, TILE), TILE)
        packed_c[:, cols] = jnp.dot(
            pick[...], cotangent[:, cols], preferred_element_type=wide
        ).astype(low)

    dispatch(packed_c, 1)

    gather_end(1)
    store = pltpu.make_async_copy(weights, attn_w, out_s.at[0])
    store.start()

    @pl.loop(0, width // TILE)
    def _(step):
        cols = pl.ds(pl.multiple_of(step * TILE, TILE), TILE)
        sum_here = tokens[:, cols].astype(wide) + jnp.dot(
            context[...], weights[3, :, cols], preferred_element_type=wide
        )
        hidden[:, cols] = sum_here
        packed_x[:, cols] = jnp.dot(
            pick[...], sum_here.astype(low), preferred_element_type=wide
        ).astype(low)

    dispatch(packed_x, 0)

    store.wait()
    outer_copy.wait()
    outer_own.wait()
    forward_copy.wait()
    for mask in range(rep_size):
        for copy in inner_copies(mask):
            if mask == 3:
                copy.wait_send()
            else:
                copy.wait()
    for kind in range(2):
        side_copy(kind, group).wait_send()

        @pl.loop(0, groups)
        def _(source):
            @pl.when(source != group)
            def _():
                side_copy(kind, source).wait_send()

            @pl.when((source <= group) & (group + 1 < groups))
            def _():
                line_copy(kind, source, 1).wait_send()

            @pl.when((source >= group) & (group >= 1))
            def _():
                line_copy(kind, source, -1).wait_send()

        @pl.loop(0, exp_size)
        def _(at):
            @pl.when(at != exp_at)
            def _():
                core_copy(kind, at).wait_send()

    small_store.wait()
    cent_own.wait()
    gain_own.wait()
    for mask in range(1, rep_size):
        gain_copy(mask).wait()
    for mask, flip in cent_pairs:
        cent_copy(mask, flip).wait()

    @pl.loop(1, exp_size)
    def _(at):
        source = exp_at ^ at
        remote(
            packed_c.at[slot_rows(source // 2)],
            arrived.at[slot_rows(source)],
            disp_s.at[source],
            disp_r.at[source],
            (rep_at, source),
        ).wait()

    pltpu.make_async_copy(
        packed_c.at[slot_rows(group)], arrived.at[slot_rows(exp_at)], disp_s.at[exp_at]
    ).wait()


def run_attend(exp_size, rep_size, slots, tokens, cotangent, doc, expert_of, attn, gain_a, w_inner, w_outer, gain_e, cent):
    rows_n, width = tokens.shape
    low = jnp.bfloat16
    wide = jnp.float32
    groups = exp_size // 2
    depth = w_inner.shape[0]
    ff_block = w_outer.shape[0]
    anyplace = pl.BlockSpec(memory_space=pl.ANY)
    inside = pl.BlockSpec(memory_space=pltpu.VMEM)
    dma = pltpu.SemaphoreType.DMA
    shape = jax.ShapeDtypeStruct
    return pl.pallas_call(
        functools.partial(attend_kernel, exp_size, rep_size, slots),
        out_shape=(
            shape((4, width, width), low),
            shape((width, 2 * ff_block), low),
            shape((2 * ff_block - DEFER, width), low),
            shape((exp_size * slots, width), low),
            shape((exp_size * 16, 128), wide),
            shape((2 * rep_size * 8, cent.shape[1]), wide),
            shape((rep_size * 8, depth), wide),
            shape((rows_n, width), wide),
            shape((3, rows_n, width), low),
            shape((HEADS * rows_n, rows_n), low),
            shape((rows_n, width), low),
            shape((rows_n, width), low),
            shape((groups * slots, rows_n), low),
            shape((1, width), wide),
        ),
        in_specs=[inside, inside, pl.BlockSpec(memory_space=pltpu.SMEM), inside]
        + [anyplace] * 4
        + [inside, anyplace, anyplace, inside, inside],
        out_specs=(anyplace,) * 7 + (inside,) * 7,
        scratch_shapes=[
            pltpu.VMEM((4, width, width), low),
            pltpu.VMEM((depth, 2 * ff_block), low),
            pltpu.VMEM((exp_size * 16, 128), wide),
            pltpu.VMEM((8, depth), wide),
            pltpu.VMEM((groups * slots, width), low),
            pltpu.VMEM((groups * slots, width), low),
            pltpu.VMEM((rows_n, rows_n), wide),
            pltpu.VMEM((16, 128), wide),
            pltpu.VMEM((8, cent.shape[1]), wide),
            dma((6,)),
            dma((2, 2, groups)),
            dma((2, groups)),
            dma((2, groups)),
            dma((2, groups)),
            dma((2, exp_size)),
            dma((2, exp_size)),
            dma((2 + 2 * rep_size,)),
            dma((2 + 2 * rep_size,)),
            dma((exp_size,)),
            dma((exp_size,)),
            dma((exp_size,)),
            dma((exp_size,)),
            dma((2 * rep_size,)),
            dma((2 * rep_size,)),
            dma((rep_size,)),
            dma((rep_size,)),
            dma((2,)),
        ],
        compiler_params=pltpu.CompilerParams(
            collective_id=1, has_side_effects=True, vmem_limit_bytes=56 << 20
        ),
        cost_estimate=pl.CostEstimate(
            flops=10 * rows_n * width * width,
            bytes_accessed=40 << 20,
            transcendentals=HEADS * rows_n * rows_n,
        ),
        name="attend",
    )(tokens, cotangent, doc, expert_of, *attn, gain_a, w_inner, w_outer, gain_e, cent)


def expert_kernel(
    exp_size,
    rep_size,
    slots,
    arrived_h,
    inner_h,
    outer_h,
    w_outer,
    counts_all,
    cents,
    gains_e,
    home,
    branch,
    outer_keep,
    outer_send,
    outer_got,
    inner_sum,
    centre_parts,
    arrived,
    spread_m,
    offsets,
    cent_b,
    gain,
    centre_grad,
    centre_v,
    inner_w,
    outer_w,
    own_x,
    own_cot,
    normed,
    active,
    slope,
    states,
    fwd_send,
    fwd_recv,
    bwd_send,
    bwd_recv,
    hop,
    back,
    spread,
    relay,
    acc,
    gates,
    gate_grads,
    outer_keep_v,
    outer_send_v,
    inner_send_v,
    load_sem,
    centre_s,
    centre_r,
    norm_s,
    norm_r,
    state_s,
    state_r,
    fwd_s,
    fwd_r,
    bwd_s,
    bwd_r,
    hop_s,
    hop_r,
    gate_s,
    gate_r,
    ret_s,
    ret_r,
    relay_s,
    relay_r,
    early_s,
    early_r,
    out_sem,
    inner_s,
    out_r,
):
    low = jnp.bfloat16
    wide = jnp.float32
    rep_at = lax.axis_index("rep")
    exp_at = lax.axis_index("exp")
    first = exp_at % 2 == 0
    second = exp_at % 2 == 1
    core_peer = (rep_at ^ 1, exp_at)
    side_peer = (rep_at, exp_at ^ 1)
    width = own_x.shape[1]
    own_rows = own_x.shape[0]
    part = own_rows // CHUNKS
    wide_ff = inner_w.shape[1]
    block = wide_ff // 2
    depth = width // rep_size

    def slot_rows(at):
        return pl.ds(pl.multiple_of(at * slots, slots), slots)

    def inner_rows(mask):
        return pl.ds(pl.multiple_of((rep_at ^ mask) * depth, depth), depth)

    loads = [
        pltpu.make_async_copy(arrived_h, arrived, load_sem.at[0]),
        pltpu.make_async_copy(inner_h, inner_w, load_sem.at[1]),
        pltpu.make_async_copy(
            outer_h, outer_w.at[: outer_h.shape[0]], load_sem.at[2]
        ),
    ]
    for load in loads:
        load.start()

    barrier = pltpu.get_barrier_semaphore()
    for mask in range(1, rep_size):
        for flip in range(2):
            pl.semaphore_signal(
                barrier, inc=1, device_id=(rep_at ^ mask, exp_at ^ flip), device_id_type=MESH
            )

    @pl.loop(1, exp_size)
    def _(at):
        pl.semaphore_signal(barrier, inc=1, device_id=(rep_at, exp_at ^ at), device_id_type=MESH)

    counted = counts_all.shape[0]
    group = exp_at // 2
    lane = lax.broadcasted_iota(jnp.int32, (counted, 128), 1)
    mine = jnp.sum(
        jnp.where(lane == group, counts_all[...], 0.0), axis=1, keepdims=True
    )
    mine = jnp.broadcast_to(mine, (counted, 128))
    down = lax.broadcasted_iota(jnp.int32, (counted, counted), 0)
    along = lax.broadcasted_iota(jnp.int32, (counted, counted), 1)
    ahead = ((along // 16 < down // 16) & (along % 16 == 0)).astype(wide).astype(low)
    offsets[0] = jnp.dot(ahead, mine.astype(low), preferred_element_type=wide)
    offsets[1] = mine
    slot_iota = lax.broadcasted_iota(jnp.int32, (slots, own_rows), 0)
    row_iota = lax.broadcasted_iota(jnp.int32, (slots, own_rows), 1)

    @pl.loop(0, exp_size)
    def _(at):
        eight = pl.ds(pl.multiple_of(at * 16, 16), 8)
        start = offsets[0, eight, :][:1, :1].astype(jnp.int32)
        limit = offsets[1, eight, :][:1, :1].astype(jnp.int32)
        spread_m[slot_rows(at), :] = (
            ((slot_iota + start) == row_iota) & (slot_iota < limit)
        ).astype(wide).astype(low)

    piece = cents.shape[1]
    for at in range(width // piece):
        cent_b[:, at * piece : (at + 1) * piece] = jnp.broadcast_to(
            cents[at * 8 : at * 8 + 1, :], (cent_b.shape[0], piece)
        ).astype(low)
    for at in range(rep_size):
        gain[:, at * depth : (at + 1) * depth] = gains_e[at * 8 : at * 8 + 1, :]
    loads[0].wait()

    for at in range(width // TILE):
        cols = slice(at * TILE, (at + 1) * TILE)
        rows_low = lax.dot_general(
            spread_m[...],
            arrived[:, cols],
            (((0,), (0,)), ((), ())),
            preferred_element_type=wide,
        ).astype(low)

        @pl.when(first)
        def _():
            own_x[:, cols] = rows_low

        @pl.when(second)
        def _():
            own_cot[:, cols] = rows_low

    pl.semaphore_wait(barrier, exp_size - 1 + 2 * (rep_size - 1))
    row_peer = (rep_at ^ 2, exp_at)
    late_copy = remote(
        w_outer.at[block - DEFER :],
        outer_w.at[2 * block - DEFER :],
        early_s.at[0],
        early_r.at[0],
        row_peer,
    )
    late_copy.start()

    gate_copy = remote(gates, gates, gate_s.at[0], gate_r.at[0], side_peer)
    grad_copy = remote(gate_grads, gate_grads, gate_s.at[1], gate_r.at[1], side_peer)

    @pl.when(first)
    def _():
        logit = lax.dot_general(
            own_x[...], cent_b[...], (((1,), (1,)), ((), ())), preferred_element_type=wide
        )
        gates[...] = jax.nn.sigmoid(logit)
        gate_copy.start()

    def hop_forward(at):
        rows = pl.ds(at * part, part)
        return remote(hop.at[rows], own_x.at[rows], hop_s.at[at], hop_r.at[at], side_peer)

    def own_slice(at):
        return pl.ds(at * 2 * part + part, part)

    def other_slice(at):
        return pl.ds(at * 2 * part, part)

    def hop_backward(at):
        rows = pl.ds(at * part, part)
        return remote(
            hop.at[rows], states.at[own_slice(at)], hop_s.at[at], hop_r.at[at], side_peer
        )

    for load in loads[1:]:
        load.wait()

    def forward(at):
        base = at * part

        @pl.when(second)
        def _():
            hop_forward(at).wait_recv()

        @pl.loop(0, part // ROWS)
        def _(step):
            off = pl.multiple_of(step * ROWS, ROWS)
            unit, _ = row_stats(own_x[pl.ds(base + off, ROWS), :].astype(wide))
            normed[pl.ds(at * 2 * part + part + off, ROWS), :] = (unit * gain[...]).astype(low)

        norm_copy = remote(
            normed.at[own_slice(at)], normed.at[other_slice(at)], norm_s.at[at], norm_r.at[at], core_peer
        )
        norm_copy.start()
        norm_copy.wait_recv()
        if at == 0:
            late_copy.wait_recv()

        @pl.loop(0, wide_ff // BIG)
        def _(step):
            cols = pl.ds(pl.multiple_of(step * BIG, BIG), BIG)
            inner = jnp.dot(
                normed[pl.ds(at * 2 * part, 2 * part), :],
                inner_w[:, cols],
                preferred_element_type=wide,
            )
            normal = 0.5 * (1.0 + lax.erf(inner * ROOT_HALF))
            active[pl.ds(at * 2 * part, 2 * part), cols] = (inner * normal).astype(low)
            slope[pl.ds(at * 2 * part, 2 * part), cols] = (
                normal + inner * jnp.exp(-0.5 * inner * inner) * INV_ROOT_TAU
            ).astype(low)

        @pl.loop(0, width // BIG)
        def _(step):
            cols = pl.ds(pl.multiple_of(step * BIG, BIG), BIG)
            both = jnp.dot(
                active[pl.ds(at * 2 * part, 2 * part), :], outer_w[:, cols], preferred_element_type=wide
            )
            fwd_send[pl.ds(base, part), cols] = both[:part].astype(low)
            acc[:, cols] = both[part:]

        rows = pl.ds(base, part)
        copy = remote(fwd_send.at[rows], fwd_recv.at[rows], fwd_s.at[at], fwd_r.at[at], core_peer)
        copy.start()

        copy.wait_recv()

        @pl.when(first)
        def _():
            @pl.loop(0, part // ROWS)
            def _(step):
                off = pl.multiple_of(step * ROWS, ROWS)
                here = pl.ds(base + off, ROWS)
                result = (
                    own_x[here, :].astype(wide)
                    + acc[pl.ds(off, ROWS), :]
                    + fwd_recv[here, :].astype(wide)
                )
                hop[here, :] = result.astype(low)

            hop_forward(at).start()

        @pl.when(second)
        def _():
            if at == 0:
                gate_copy.wait_recv()

            @pl.loop(0, part // ROWS)
            def _(step):
                off = pl.multiple_of(step * ROWS, ROWS)
                here = pl.ds(base + off, ROWS)
                result = (
                    own_x[here, :].astype(wide)
                    + acc[pl.ds(off, ROWS), :]
                    + fwd_recv[here, :].astype(wide)
                )
                cot = own_cot[here, :].astype(wide)
                gate = gates[here, :][:, :1]
                back[here, :] = (gate * result).astype(low)
                gate_grads[here, :] = jnp.broadcast_to(
                    jnp.sum(cot * result, axis=1, keepdims=True), (ROWS, gate_grads.shape[1])
                )
                states[pl.ds(at * 2 * part + part + off, ROWS), :] = (gate * cot).astype(low)

    for at in range(CHUNKS):
        forward(at)

    groups = exp_size // 2

    def ret_copy(source, dest):
        return remote(
            source,
            home.at[slot_rows(group)],
            ret_s.at[dest],
            ret_r.at[group],
            (rep_at, dest),
        )

    def relay_copy(which):
        return remote(
            spread.at[slot_rows(2 * which + 1)],
            relay.at[slot_rows(which)],
            relay_s.at[which],
            relay_r.at[which],
            side_peer,
        )

    ret_own = pltpu.make_async_copy(
        spread.at[slot_rows(exp_at)], home.at[slot_rows(group)], ret_s.at[exp_at]
    )

    def make_spread():
        @pl.loop(0, width // TILE)
        def _(step):
            cols = pl.ds(pl.multiple_of(step * TILE, TILE), TILE)
            spread[:, cols] = jnp.dot(
                spread_m[...], back[:, cols], preferred_element_type=wide
            ).astype(low)

    def send_back():
        @pl.loop(1, groups)
        def _(step):
            relay_copy(group ^ (groups - step)).start()

        @pl.loop(1, groups)
        def _(step):
            dest = 2 * (group ^ (groups - step))
            ret_copy(spread.at[slot_rows(dest)], dest).start()

        ret_copy(spread.at[slot_rows(exp_at + 1)], exp_at + 1).start()
        ret_own.start()

    @pl.when(second)
    def _():
        grad_copy.start()

    centre_grad[...] = jnp.zeros_like(centre_grad)

    def backward(at):
        base = at * part

        @pl.when(first)
        def _():
            hop_backward(at).wait_recv()

        copy = remote(
            states.at[own_slice(at)], states.at[other_slice(at)], state_s.at[at], state_r.at[at], core_peer
        )
        copy.start()
        copy.wait_recv()

        @pl.loop(0, wide_ff // BIG)
        def _(step):
            rows = pl.ds(pl.multiple_of(step * BIG, BIG), BIG)
            grad_active = lax.dot_general(
                states[pl.ds(at * 2 * part, 2 * part), :],
                outer_w[rows, :],
                (((1,), (1,)), ((), ())),
                preferred_element_type=wide,
            )
            here = pl.ds(at * 2 * part, 2 * part)
            slope[here, rows] = (grad_active * slope[here, rows].astype(wide)).astype(low)

        @pl.loop(0, width // BIG)
        def _(step):
            cols = pl.ds(pl.multiple_of(step * BIG, BIG), BIG)
            both = lax.dot_general(
                slope[pl.ds(at * 2 * part, 2 * part), :],
                inner_w[cols, :],
                (((1,), (1,)), ((), ())),
                preferred_element_type=wide,
            )
            bwd_send[pl.ds(base, part), cols] = both[:part].astype(low)
            acc[:, cols] = both[part:]

        rows = pl.ds(base, part)
        back_copy = remote(
            bwd_send.at[rows], bwd_recv.at[rows], bwd_s.at[at], bwd_r.at[at], core_peer
        )
        back_copy.start()

        back_copy.wait_recv()
        if at == 0:

            @pl.when(first)
            def _():
                grad_copy.wait_recv()

        @pl.when(first)
        def _():
            hop_forward(at).wait_send()

        @pl.loop(0, part // ROWS)
        def _(step):
            off = pl.multiple_of(step * ROWS, ROWS)
            here = pl.ds(base + off, ROWS)
            rows_in = own_x[here, :].astype(wide)
            unit, inv_scale = row_stats(rows_in)
            grad_unit = (acc[pl.ds(off, ROWS), :] + bwd_recv[here, :].astype(wide)) * gain[...]
            grad_in = (
                grad_unit
                - jnp.mean(grad_unit, axis=-1, keepdims=True)
                - unit * jnp.mean(grad_unit * unit, axis=-1, keepdims=True)
            ) * inv_scale
            gate = gates[here, :][:, :1]

            @pl.when(second)
            def _():
                state = gate * own_cot[here, :].astype(wide) + grad_in
                hop[here, :] = state.astype(low)

            @pl.when(first)
            def _():
                state = states[pl.ds(at * 2 * part + part + off, ROWS), :].astype(wide) + grad_in
                grad_logit = gate_grads[here, :][:, :1] * gate * (1.0 - gate)
                back[here, :] = (state + grad_logit * cent_b[:1, :].astype(wide)).astype(low)
                centre_grad[...] += jnp.sum(grad_logit * rows_in, axis=0, keepdims=True)

        @pl.when(second)
        def _():
            hop_backward(at).start()

    for at in range(CHUNKS):
        backward(at)

    def eight_rows(at):
        return pl.ds(pl.multiple_of(at * 8, 8), 8)

    def centre_copy(mask, flip):
        dest = rep_at ^ mask
        return remote(
            centre_v.at[eight_rows(flip * rep_size + dest)],
            centre_parts.at[eight_rows(rep_at)],
            centre_s.at[flip * rep_size + mask],
            centre_r.at[mask],
            (dest, exp_at ^ flip),
        )

    centre_own = pltpu.make_async_copy(
        centre_v.at[eight_rows(rep_at)], centre_parts.at[eight_rows(rep_at)], centre_s.at[0]
    )
    centre_pairs = [(m, f) for m in range(rep_size) for f in range(2) if m or f]

    make_spread()

    @pl.when(first)
    def _():
        send_back()
        for at in range(width // piece):
            centre_v[at * 8 : (at + 1) * 8, :] = jnp.broadcast_to(
                centre_grad[:, at * piece : (at + 1) * piece], (8, piece)
            )
        centre_own.start()
        for mask, flip in centre_pairs:
            centre_copy(mask, flip).start()

    outs = []
    tiles = block // TILE
    early_copy = remote(
        outer_send_v.at[:EARLY], outer_got, early_s.at[1], early_r.at[1], row_peer
    )
    for at in list(range(tiles, 2 * tiles)) + list(range(tiles)):
        rows = slice(at * TILE, (at + 1) * TILE)
        grad = lax.dot_general(
            active[:, rows], states[...], (((0,), (0,)), ((), ())), preferred_element_type=wide
        )
        if at < tiles:
            outer_keep_v[rows, :] = grad
            outs.append((outer_keep_v.at[rows], outer_keep.at[rows]))
        else:
            top = at * TILE - block
            outer_send_v[top : top + TILE, :] = grad.astype(low)
            if top + TILE == EARLY:
                early_copy.start()
            if top < EARLY:
                continue
            outs.append(
                (outer_send_v.at[top : top + TILE], outer_send.at[top - EARLY : top - EARLY + TILE])
            )
        pltpu.make_async_copy(outs[-1][0], outs[-1][1], out_sem.at[len(outs) - 1]).start()
    outs.append((spread, branch))
    pltpu.make_async_copy(spread, branch, out_sem.at[len(outs) - 1]).start()

    def inner_copy(mask, side):
        at = rep_at ^ (2 * side)
        cols = pl.ds(pl.multiple_of(at * block, block), block)
        target = inner_sum.at[mask // 2, :, cols]
        source = inner_send_v.at[mask, side]
        count = 2 * mask + side
        if mask % 2 == 0:
            return pltpu.make_async_copy(source, target, inner_s.at[count])
        return remote(source, target, inner_s.at[count], out_r.at[count], core_peer)

    inner_order = [(m, f) for m in (3, 1, 2, 0) for f in range(2)]
    for mask, side in inner_order:
        cols = slice(side * block, (side + 1) * block)
        grad = lax.dot_general(
            normed[:, inner_rows(mask)],
            slope[:, cols],
            (((0,), (0,)), ((), ())),
            preferred_element_type=wide,
        )
        inner_send_v[mask, side] = grad.astype(low)
        inner_copy(mask, side).start()

    @pl.when(second)
    def _():
        @pl.loop(1, groups)
        def _(step):
            which = group ^ (groups - step)
            relay_copy(which).wait_recv()
            ret_copy(relay.at[slot_rows(which)], 2 * which + 1).start()

    late_copy.wait_send()
    early_copy.wait()
    for at, (source, target) in enumerate(outs):
        pltpu.make_async_copy(source, target, out_sem.at[at]).wait()
    for mask, side in inner_order:
        inner_copy(mask, side).wait()
    for at in range(CHUNKS):
        rows = pl.ds(at * part, part)
        remote(
            normed.at[own_slice(at)], normed.at[other_slice(at)], norm_s.at[at], norm_r.at[at], core_peer
        ).wait_send()
        remote(
            states.at[own_slice(at)], states.at[other_slice(at)], state_s.at[at], state_r.at[at], core_peer
        ).wait_send()
        remote(
            fwd_send.at[rows], fwd_recv.at[rows], fwd_s.at[at], fwd_r.at[at], core_peer
        ).wait_send()
        remote(
            bwd_send.at[rows], bwd_recv.at[rows], bwd_s.at[at], bwd_r.at[at], core_peer
        ).wait_send()

        @pl.when(second)
        def _():
            hop_backward(at).wait_send()

    @pl.when(first)
    def _():
        gate_copy.wait_send()

    @pl.when(second)
    def _():
        grad_copy.wait_send()

    @pl.when(first)
    def _():
        centre_own.wait()
        for mask, flip in centre_pairs:
            centre_copy(mask, flip).wait_send()
        for mask in range(1, rep_size):
            centre_copy(mask, 0).wait_recv()

    @pl.when(second)
    def _():
        for mask in range(rep_size):
            centre_copy(mask, 1).wait_recv()

    @pl.when(first)
    def _():
        ret_own.wait()
        ret_copy(spread.at[slot_rows(exp_at + 1)], exp_at + 1).wait_send()

        @pl.loop(1, groups)
        def _(step):
            which = group ^ step
            relay_copy(which).wait_send()
            ret_copy(spread.at[slot_rows(2 * which)], 2 * which).wait_send()

    @pl.when(second)
    def _():
        @pl.loop(1, groups)
        def _(step):
            which = group ^ step
            ret_copy(relay.at[slot_rows(which)], 2 * which + 1).wait_send()

        remote(
            relay.at[slot_rows(group)],
            home.at[slot_rows(group)],
            relay_s.at[group],
            ret_r.at[group],
            side_peer,
        ).wait_recv()

    @pl.loop(1, groups)
    def _(step):
        source = group ^ step
        remote(
            relay.at[slot_rows(source)],
            home.at[slot_rows(source)],
            relay_s.at[source],
            ret_r.at[source],
            side_peer,
        ).wait_recv()


def run_experts(
    exp_size, rep_size, slots, own_rows, arrived, inner_w, outer_w, w_outer, counts_all, cents, gains_e
):
    width = arrived.shape[1]
    depth = width // rep_size
    block = w_outer.shape[0]
    low = jnp.bfloat16
    wide = jnp.float32
    total = exp_size * slots
    all_rows = 2 * own_rows
    part = own_rows // CHUNKS
    piece = cents.shape[1]
    anyplace = pl.BlockSpec(memory_space=pl.ANY)
    inside = pl.BlockSpec(memory_space=pltpu.VMEM)
    dma = pltpu.SemaphoreType.DMA
    n_out = (2 * block - EARLY) // TILE + 1
    scratch = [
        pltpu.VMEM((total, width), low),
        pltpu.VMEM((total, own_rows), low),
        pltpu.VMEM((2, exp_size * 16, 128), wide),
        pltpu.VMEM((128, width), low),
        pltpu.VMEM((1, width), wide),
        pltpu.VMEM((1, width), wide),
        pltpu.VMEM((2 * rep_size * 8, piece), wide),
        pltpu.VMEM((width, 2 * block), low),
        pltpu.VMEM((2 * block, width), low),
        pltpu.VMEM((own_rows, width), low),
        pltpu.VMEM((own_rows, width), low),
        pltpu.VMEM((all_rows, width), low),
        pltpu.VMEM((all_rows, 2 * block), low),
        pltpu.VMEM((all_rows, 2 * block), low),
        pltpu.VMEM((all_rows, width), low),
        pltpu.VMEM((own_rows, width), low),
        pltpu.VMEM((own_rows, width), low),
        pltpu.VMEM((own_rows, width), low),
        pltpu.VMEM((own_rows, width), low),
        pltpu.VMEM((own_rows, width), low),
        pltpu.VMEM((own_rows, width), low),
        pltpu.VMEM((total, width), low),
        pltpu.VMEM((total // 2, width), low),
        pltpu.VMEM((part, width), wide),
        pltpu.VMEM((own_rows, 128), wide),
        pltpu.VMEM((own_rows, 128), wide),
        pltpu.VMEM((block, width), wide),
        pltpu.VMEM((block, width), low),
        pltpu.VMEM((rep_size, 2, depth, block), low),
        dma((3,)),
        dma((2 * rep_size,)),
        dma((rep_size,)),
    ]
    scratch += [dma((CHUNKS,)) for _ in range(10)]
    scratch += [dma((2,)), dma((2,)), dma((exp_size,)), dma((exp_size // 2,))]
    scratch += [dma((exp_size // 2,)), dma((exp_size // 2,)), dma((2,)), dma((2,)), dma((n_out,))]
    scratch += [dma((2 * rep_size,)), dma((2 * rep_size,))]
    flops = 2 * all_rows * width * 2 * block * 6
    return pl.pallas_call(
        functools.partial(expert_kernel, exp_size, rep_size, slots),
        out_shape=(
            jax.ShapeDtypeStruct((total // 2, width), low),
            jax.ShapeDtypeStruct((total, width), low),
            jax.ShapeDtypeStruct((block, width), wide),
            jax.ShapeDtypeStruct((block - EARLY, width), low),
            jax.ShapeDtypeStruct((EARLY, width), low),
            jax.ShapeDtypeStruct((2, depth, rep_size * block), low),
            jax.ShapeDtypeStruct((rep_size * 8, piece), wide),
        ),
        in_specs=[anyplace] * 4 + [inside] * 3,
        out_specs=(anyplace,) * 7,
        scratch_shapes=scratch,
        compiler_params=pltpu.CompilerParams(
            collective_id=0, has_side_effects=True, vmem_limit_bytes=62 << 20
        ),
        cost_estimate=pl.CostEstimate(
            flops=flops, bytes_accessed=40 << 20, transcendentals=2 * all_rows * 2 * block
        ),
        name="experts",
    )(arrived, inner_w, outer_w, w_outer, counts_all, cents, gains_e)


def finish_kernel(
    exp_size,
    rep_size,
    home,
    branch,
    pick,
    hidden,
    cotangent,
    tokens,
    gain_row,
    qkv,
    probs,
    normed_a,
    context,
    attn_w,
    outer_send,
    inner_sum,
    output,
    grad_tokens,
    shares,
    outer_recv,
    inner_recv,
    branch_in,
    weights,
    grad_hidden,
    grad_attn,
    grad_context,
    grads3,
    keep,
    core_out,
    core_in,
    side_out,
    side_in,
    line_out,
    line_in,
    total,
    row_out,
    row_in,
    half_out,
    half_in,
    load_s,
    branch_s,
    branch_r,
    expert_s,
    expert_r,
    core_s,
    core_r,
    side_s,
    side_r,
    line_s,
    line_r,
    row_s,
    row_r,
    half_s,
    half_r,
):
    low = jnp.bfloat16
    wide = jnp.float32
    rep_at = lax.axis_index("rep")
    exp_at = lax.axis_index("exp")
    core = rep_at % 2
    group = exp_at // 2
    side = exp_at % 2
    groups = exp_size // 2
    rows_n, width = tokens.shape
    half = width // 2
    block = width // exp_size
    core_peer = (rep_at ^ 1, exp_at)
    side_peer = (rep_at, exp_at ^ 1)
    row_peer = (rep_at ^ 2, exp_at)

    load = pltpu.make_async_copy(attn_w, weights, load_s.at[0])
    load.start()

    barrier = pltpu.get_barrier_semaphore()
    for mask in range(1, 3):
        pl.semaphore_signal(
            barrier, inc=1, device_id=(rep_at ^ mask, exp_at), device_id_type=MESH
        )

    @pl.loop(1, exp_size)
    def _(at):
        pl.semaphore_signal(barrier, inc=1, device_id=(rep_at, exp_at ^ at), device_id_type=MESH)

    pl.semaphore_wait(barrier, exp_size + 1)

    outer_copy = remote(outer_send, outer_recv, expert_s.at[0], expert_r.at[0], row_peer)

    inner_copy = remote(inner_sum.at[1], inner_recv, expert_s.at[1], expert_r.at[1], row_peer)
    inner_copy.start()
    outer_copy.start()

    slots = pick.shape[0] // groups

    def slot_rows(at):
        return pl.ds(pl.multiple_of(at * slots, slots), slots)

    def branch_copy(dest):
        return remote(
            branch.at[slot_rows(dest)],
            branch_in.at[slot_rows(group)],
            branch_s.at[dest],
            branch_r.at[group],
            (rep_at, dest),
        )

    branch_own = pltpu.make_async_copy(
        branch.at[slot_rows(exp_at)], branch_in.at[slot_rows(group)], branch_s.at[exp_at]
    )

    @pl.when(side == 1)
    def _():
        branch_own.start()

        @pl.loop(1, exp_size)
        def _(at):
            branch_copy(exp_at ^ at).start()

    @pl.loop(0, width // TILE)
    def _(step):
        cols = pl.ds(pl.multiple_of(step * TILE, TILE), TILE)
        back = lax.dot_general(
            pick[...], home[:, cols], (((0,), (0,)), ((), ())), preferred_element_type=wide
        )
        grad = cotangent[:, cols].astype(wide) + back
        grad_hidden[:, cols] = grad
        grad_attn[:, cols] = grad.astype(low)

    own_half = pl.ds(pl.multiple_of(core * half, half), half)
    other_half = pl.ds(pl.multiple_of((1 - core) * half, half), half)

    def core_copy(at):
        return remote(core_out.at[at], core_in.at[at], core_s.at[at], core_r.at[at], core_peer)

    def product(at, left, right, cols, target, kind):
        @pl.loop(0, width // TILE)
        def _(step):
            rows = pl.ds(pl.multiple_of(step * TILE, TILE), TILE)
            target[at, rows, :] = lax.dot_general(
                left[:, rows], right[:, cols], (((0,), (0,)), ((), ())), preferred_element_type=wide
            ).astype(kind)

    def share_start(at, left, right):
        product(at, left, right, other_half, core_out, low)
        core_copy(at).start()
        product(at, left, right, own_half, keep, wide)

    def block_rows(at):
        return pl.ds(pl.multiple_of(at * block, block), block)

    def side_copy(at):
        return remote(side_out.at[at], side_in.at[at], side_s.at[at], side_r.at[at], side_peer)

    def share_side(at):
        core_copy(at).wait_recv()

        @pl.loop(0, groups)
        def _(which):
            rows = block_rows(2 * which + 1 - side)
            side_out[at, block_rows(which), :] = (
                keep[at, rows, :] + core_in[at, rows, :].astype(wide)
            ).astype(low)

        side_copy(at).start()

        @pl.loop(0, groups)
        def _(which):
            rows = block_rows(2 * which + side)
            keep[at, rows, :] = keep[at, rows, :] + core_in[at, rows, :].astype(wide)

    def line_copy(at, mask):
        dest = group ^ mask
        return remote(
            line_out.at[at, block_rows(dest)],
            line_in.at[at, block_rows(group)],
            line_s.at[at, mask],
            line_r.at[at, mask],
            (rep_at, 2 * dest + side),
        )

    def share_line(at):
        side_copy(at).wait_recv()

        @pl.loop(1, groups)
        def _(mask):
            dest = group ^ mask
            line_out[at, block_rows(dest), :] = (
                keep[at, block_rows(2 * dest + side), :] + side_in[at, block_rows(dest), :].astype(wide)
            ).astype(low)
            line_copy(at, mask).start()

        total[at] = keep[at, block_rows(exp_at), :] + side_in[at, block_rows(group), :].astype(wide)

    def row_copy(at):
        return remote(row_out.at[at], row_in.at[at], row_s.at[at], row_r.at[at], row_peer)

    def share_row(at):
        @pl.loop(1, groups)
        def _(mask):
            line_copy(at, mask).wait_recv()
            total[at] = total[at] + line_in[at, block_rows(group ^ mask), :].astype(wide)

        row_out[at] = total[at].astype(low)
        row_copy(at).start()

    def half_copy(at):
        return remote(half_out.at[at], half_in.at[at], half_s.at[at], half_r.at[at], core_peer)

    def share_half(at):
        row_copy(at).wait_recv()
        summed = row_out[at].astype(wide) + row_in[at].astype(wide)
        half_out[at] = summed
        half_copy(at).start()
        shares[at, :, own_half] = summed

    def share_end(at):
        half_copy(at).wait_recv()
        shares[at, :, other_half] = half_in[at]

    share_start(3, context, grad_attn)
    load.wait()

    @pl.loop(0, width // TILE)
    def _(step):
        rows = pl.ds(pl.multiple_of(step * TILE, TILE), TILE)
        grad_context[:, rows] = lax.dot_general(
            grad_attn[...], weights[3, rows, :], (((1,), (1,)), ((), ())), preferred_element_type=wide
        ).astype(low)

    share_side(3)

    head_dim = width // HEADS
    pair = 2 * head_dim
    factor = head_dim ** (-0.5)
    lane = lax.broadcasted_iota(jnp.int32, (rows_n, pair), 1)

    def heads(start, stop):
        @pl.loop(start, stop)
        def _(at):
            cols = pl.ds(pl.multiple_of(at * pair, pair), pair)
            q_pair = qkv[0, :, cols]
            k_pair = qkv[1, :, cols]
            v_pair = qkv[2, :, cols]
            c_pair = grad_context[:, cols]
            found = []
            for which in range(2):
                chosen = (lane >= head_dim) if which else (lane < head_dim)
                c_one = jnp.where(chosen, c_pair, jnp.zeros_like(c_pair))
                prob = probs[pl.ds(pl.multiple_of((2 * at + which) * rows_n, rows_n), rows_n), :]
                grad_prob = lax.dot_general(
                    c_one, v_pair, (((1,), (1,)), ((), ())), preferred_element_type=wide
                )
                weighted = prob.astype(wide) * grad_prob
                row_sum = jnp.sum(weighted, axis=1, keepdims=True)
                grad_score = (weighted - prob.astype(wide) * row_sum).astype(low)
                found.append(
                    (
                        jnp.dot(grad_score, k_pair, preferred_element_type=wide) * factor,
                        lax.dot_general(
                            grad_score,
                            q_pair,
                            (((0,), (0,)), ((), ())),
                            preferred_element_type=wide,
                        )
                        * factor,
                        lax.dot_general(
                            prob, c_pair, (((0,), (0,)), ((), ())), preferred_element_type=wide
                        ),
                    )
                )
            for which in range(3):
                grads3[which, :, cols] = jnp.where(
                    lane < head_dim, found[0][which], found[1][which]
                ).astype(low)

    heads(0, HEADS // 4)
    share_line(3)
    heads(HEADS // 4, HEADS // 2)
    for at in range(3):
        share_start(at, normed_a, grads3.at[at])
    for at in range(3):
        share_side(at)

    @pl.loop(0, width // TILE)
    def _(step):
        rows = pl.ds(pl.multiple_of(step * TILE, TILE), TILE)
        grad_normed = jnp.zeros((rows_n, TILE), wide)
        for at in range(3):
            grad_normed = grad_normed + lax.dot_general(
                grads3[at], weights[at, rows, :], (((1,), (1,)), ((), ())), preferred_element_type=wide
            )
        grad_tokens[:, rows] = grad_normed

    @pl.loop(0, rows_n // ROWS)
    def _(step):
        here = pl.ds(pl.multiple_of(step * ROWS, ROWS), ROWS)
        unit, inv_scale = row_stats(tokens[here, :].astype(wide))
        grad_unit = grad_tokens[here, :] * gain_row[...]
        grad_in = (
            grad_unit
            - jnp.mean(grad_unit, axis=-1, keepdims=True)
            - unit * jnp.mean(grad_unit * unit, axis=-1, keepdims=True)
        ) * inv_scale
        grad_tokens[here, :] = grad_hidden[here, :] + grad_in

    share_row(3)
    for at in range(3):
        share_line(at)

    def branch_wait(which):
        remote(
            branch.at[slot_rows(which)],
            branch_in.at[slot_rows(which)],
            branch_s.at[which],
            branch_r.at[which],
            side_peer,
        ).wait_recv()

    @pl.when(side == 0)
    def _():
        branch_wait(group)

    @pl.when(side == 1)
    def _():
        branch_own.wait()

    @pl.loop(1, groups)
    def _(at):
        branch_wait(group ^ at)

    @pl.loop(0, width // TILE)
    def _(step):
        cols = pl.ds(pl.multiple_of(step * TILE, TILE), TILE)
        rows = lax.dot_general(
            pick[...], branch_in[:, cols], (((0,), (0,)), ((), ())), preferred_element_type=wide
        )
        output[:, cols] = (hidden[:, cols] + rows).astype(low)

    for at in range(3):
        share_row(at)
    for at in (3, 0, 1, 2):
        share_half(at)
    for at in (3, 0, 1, 2):
        share_end(at)

    @pl.when(side == 1)
    def _():
        @pl.loop(1, exp_size)
        def _(at):
            branch_copy(exp_at ^ at).wait_send()

    for at in range(4):
        core_copy(at).wait_send()
        side_copy(at).wait_send()
        row_copy(at).wait_send()
        half_copy(at).wait_send()

        @pl.loop(1, groups)
        def _(mask):
            line_copy(at, mask).wait_send()

    inner_copy.wait()
    outer_copy.wait()


def run_finish(exp_size, rep_size, home, branch, pick, hidden, cotangent, tokens, gain_row, qkv, probs, normed_a, context, attn_w, outer_send, inner_sum):
    rows_n, width = tokens.shape
    low = jnp.bfloat16
    wide = jnp.float32
    half = width // 2
    groups = exp_size // 2
    block = width // exp_size
    anyplace = pl.BlockSpec(memory_space=pl.ANY)
    inside = pl.BlockSpec(memory_space=pltpu.VMEM)
    dma = pltpu.SemaphoreType.DMA
    shape = jax.ShapeDtypeStruct
    return pl.pallas_call(
        functools.partial(finish_kernel, exp_size, rep_size),
        out_shape=(
            shape((rows_n, width), low),
            shape((rows_n, width), wide),
            shape((4, block, width), wide),
            shape(outer_send.shape, low),
            shape(inner_sum.shape[1:], low),
        ),
        in_specs=[inside, anyplace] + [inside] * 9 + [anyplace] * 3,
        out_specs=(inside,) * 3 + (anyplace,) * 2,
        scratch_shapes=[
            pltpu.VMEM(pick.shape[:1] + (width,), low),
            pltpu.VMEM((4, width, width), low),
            pltpu.VMEM((rows_n, width), wide),
            pltpu.VMEM((rows_n, width), low),
            pltpu.VMEM((rows_n, width), low),
            pltpu.VMEM((3, rows_n, width), low),
            pltpu.VMEM((4, width, half), wide),
            pltpu.VMEM((4, width, half), low),
            pltpu.VMEM((4, width, half), low),
            pltpu.VMEM((4, width // 2, half), low),
            pltpu.VMEM((4, width // 2, half), low),
            pltpu.VMEM((4, width // 2, half), low),
            pltpu.VMEM((4, width // 2, half), low),
            pltpu.VMEM((4, block, half), wide),
            pltpu.VMEM((4, block, half), low),
            pltpu.VMEM((4, block, half), low),
            pltpu.VMEM((4, block, half), wide),
            pltpu.VMEM((4, block, half), wide),
            dma((1,)),
            dma((exp_size,)),
            dma((groups,)),
            dma((2,)),
            dma((2,)),
            dma((4,)),
            dma((4,)),
            dma((4,)),
            dma((4,)),
            dma((4, groups)),
            dma((4, groups)),
            dma((4,)),
            dma((4,)),
            dma((4,)),
            dma((4,)),
        ],
        compiler_params=pltpu.CompilerParams(
            collective_id=2, has_side_effects=True, vmem_limit_bytes=60 << 20
        ),
        cost_estimate=pl.CostEstimate(
            flops=20 * rows_n * width * width, bytes_accessed=60 << 20, transcendentals=0
        ),
        name="finish",
    )(
        home,
        branch,
        pick,
        hidden,
        cotangent,
        tokens,
        gain_row,
        qkv,
        probs,
        normed_a,
        context,
        attn_w,
        outer_send,
        inner_sum,
    )


def shards(
    tokens,
    cotangent,
    doc_lengths,
    expert_of_token,
    w_query,
    w_key,
    w_value,
    w_output,
    attn_gain,
    w_inner,
    w_outer,
    expert_gain,
    centroids,
):
    exp_size = lax.axis_size("exp")
    rep_size = lax.axis_size("rep")
    row_count = tokens.shape[0]
    wide = jnp.float32

    slots = -(-3 * row_count // exp_size // 16) * 16
    (
        attn_w,
        inner_w,
        outer_w,
        arrived,
        counts_all,
        cents,
        gains_e,
        hidden,
        qkv,
        probs,
        normed_a,
        context,
        pick,
        gain_row,
    ) = run_attend(
        exp_size,
        rep_size,
        slots,
        tokens,
        cotangent,
        doc_lengths,
        expert_of_token[None],
        (w_query, w_key, w_value, w_output),
        attn_gain[None],
        w_inner[0],
        w_outer[0],
        expert_gain,
        centroids,
    )
    home, branch, outer_keep, outer_send, outer_got, inner_sum, centre_parts = run_experts(
        exp_size,
        rep_size,
        slots,
        2 * row_count,
        arrived,
        inner_w,
        outer_w,
        w_outer[0],
        counts_all,
        cents,
        gains_e,
    )
    output, grad_tokens, shares, outer_recv, inner_recv = run_finish(
        exp_size,
        rep_size,
        home,
        branch,
        pick,
        hidden,
        cotangent,
        tokens,
        gain_row,
        qkv,
        probs,
        normed_a,
        context,
        attn_w,
        outer_send,
        inner_sum,
    )
    grad_centroids = jnp.sum(centre_parts.reshape(rep_size, 8, -1)[:, 0], axis=0)[None]
    grad_w_outer = (
        outer_keep + jnp.concatenate([outer_got, outer_recv], axis=0).astype(wide)
    )[None]
    summed = inner_sum[0].astype(wide) + inner_recv.astype(wide)
    grad_w_inner = summed[None]
    grad_expert_gain = jnp.sum(summed * w_inner[0].astype(wide), axis=1)[None] / expert_gain.astype(
        wide
    )
    share_gain = sum(
        jnp.sum(shares[i] * w.astype(wide), axis=1) for i, w in enumerate((w_query, w_key, w_value))
    ) / attn_gain.astype(wide)
    return (
        output,
        grad_tokens,
        shares[0],
        shares[1],
        shares[2],
        shares[3],
        share_gain,
        grad_w_inner,
        grad_w_outer,
        grad_expert_gain,
        grad_centroids,
    )


def solution(mesh):
    placed = (
        P(("rep", "exp"), None),
        P(("rep", "exp"), None),
        P(("rep", "exp"), None),
        P(("rep", "exp")),
        P("exp", None),
        P("exp", None),
        P("exp", None),
        P("exp", None),
        P("exp"),
        P("exp", "rep", None),
        P("exp", "rep", None),
        P("exp", "rep"),
        P("exp", "rep"),
    )
    return jax.shard_map(
        shards,
        mesh=mesh,
        in_specs=placed,
        out_specs=(
            P(("rep", "exp"), None),
            P(("rep", "exp"), None),
            P("exp", None),
            P("exp", None),
            P("exp", None),
            P("exp", None),
            P("exp"),
            P("exp", "rep", None),
            P("exp", "rep", None),
            P("exp", "rep"),
            P("exp", "rep"),
        ),
        check_vma=False,
    )
```

```python
import functools

import jax
import jax.numpy as jnp
from jax import lax
from jax.experimental import pallas as pl
from jax.experimental.pallas import tpu as pltpu
from jax.sharding import PartitionSpec as P

HEADS = 16
EPS = 1e-05
ROOT_HALF = 0.7071067811865476
INV_ROOT_TAU = 0.3989422804014327
CHUNKS = 4
DEFER = 256
EARLY = 512


MESH = pl.DeviceIdType.MESH
TILE = 256
ROWS = 64
BIG = 1024


def remote(src, dst, send_sem, recv_sem, device):
    return pltpu.make_async_remote_copy(
        src_ref=src,
        dst_ref=dst,
        send_sem=send_sem,
        recv_sem=recv_sem,
        device_id=device,
        device_id_type=MESH,
    )


def row_stats(rows):
    row_mean = jnp.mean(rows, axis=-1, keepdims=True)
    centered = rows - row_mean
    variance = jnp.mean(centered * centered, axis=-1, keepdims=True)
    inv_scale = lax.rsqrt(variance + EPS)
    return centered * inv_scale, inv_scale


def attend_kernel(
    exp_size,
    rep_size,
    slots,
    tokens,
    cotangent,
    doc,
    expert_of,
    w_query,
    w_key,
    w_value,
    w_output,
    gain_a,
    w_inner,
    w_outer,
    gain_e,
    cent,
    attn_w,
    inner_w,
    outer_w,
    arrived,
    counts_all,
    cents,
    gains_e,
    hidden,
    qkv,
    probs,
    normed_a,
    context,
    pick,
    gain_row,
    weights,
    staging,
    small_all,
    gain_v,
    packed_x,
    packed_c,
    bias,
    counts_v,
    cent_v,
    own_s,
    line_s,
    line_r,
    side_s,
    side_r,
    core_s,
    core_r,
    weight_s,
    weight_r,
    disp_s,
    disp_r,
    count_s,
    count_r,
    cent_s,
    cent_r,
    gain_s,
    gain_r,
    out_s,
):
    low = jnp.bfloat16
    wide = jnp.float32
    rep_at = lax.axis_index("rep")
    exp_at = lax.axis_index("exp")
    core = rep_at % 2
    group = exp_at // 2
    side = exp_at % 2
    groups = exp_size // 2
    rows_n, width = tokens.shape
    half = width // 2
    block = w_query.shape[0]
    depth = w_inner.shape[0]
    ff_block = w_outer.shape[0]
    core_peer = (rep_at ^ 1, exp_at)
    side_peer = (rep_at, exp_at ^ 1)

    def block_rows(at):
        return pl.ds(pl.multiple_of(at * block, block), block)

    own_loads = []
    for at, source in enumerate((w_query, w_key, w_value, w_output)):
        own_loads.append(
            pltpu.make_async_copy(source, weights.at[at, block_rows(exp_at)], own_s.at[at])
        )
    for load in own_loads:
        load.start()

    barrier = pltpu.get_barrier_semaphore()
    for mask in range(1, rep_size):
        for flip in range(2):
            pl.semaphore_signal(
                barrier, inc=1, device_id=(rep_at ^ mask, exp_at ^ flip), device_id_type=MESH
            )

    @pl.loop(1, exp_size)
    def _(at):
        pl.semaphore_signal(barrier, inc=1, device_id=(rep_at, exp_at ^ at), device_id_type=MESH)

    pl.semaphore_wait(barrier, exp_size - 1 + 2 * (rep_size - 1))

    outer_copy = remote(
        w_outer.at[: ff_block - DEFER],
        outer_w,
        weight_s.at[0],
        weight_r.at[0],
        (rep_at ^ 2, exp_at),
    )

    for load in own_loads:
        load.wait()

    picks = (slice(0, 3), slice(3, 4))
    own_half = pl.ds(pl.multiple_of(core * half, half), half)

    def view(kind, at):
        return weights.at[picks[kind], block_rows(at), own_half]

    def line_copy(kind, source, step):
        at = 2 * source + side
        return remote(
            view(kind, at),
            view(kind, at),
            line_s.at[kind, (1 + step) // 2, source],
            line_r.at[kind, source],
            (rep_at, exp_at + 2 * step),
        )

    def line_wait(kind, source):
        at = 2 * source + side
        remote(
            view(kind, at), view(kind, at), line_s.at[kind, 0, source], line_r.at[kind, source], side_peer
        ).wait_recv()

    def side_copy(kind, source):
        at = 2 * source + side
        return remote(
            view(kind, at), view(kind, at), side_s.at[kind, source], side_r.at[kind, source], side_peer
        )

    def side_wait(kind, source):
        at = 2 * source + 1 - side
        remote(
            view(kind, at), view(kind, at), side_s.at[kind, source], side_r.at[kind, source], side_peer
        ).wait_recv()

    def core_copy(kind, at):
        return remote(view(kind, at), view(kind, at), core_s.at[kind, at], core_r.at[kind, at], core_peer)

    def core_wait(kind, at):
        other = pl.ds(pl.multiple_of((1 - core) * half, half), half)
        there = weights.at[picks[kind], block_rows(at), other]
        remote(there, there, core_s.at[kind, at], core_r.at[kind, at], core_peer).wait_recv()

    def first_sends(kind):
        @pl.when(group + 1 < groups)
        def _():
            line_copy(kind, group, 1).start()

        @pl.when(group >= 1)
        def _():
            line_copy(kind, group, -1).start()

        side_copy(kind, group).start()

    def take_side(kind, source):
        side_wait(kind, source)
        core_copy(kind, 2 * source + 1 - side).start()

    def gather_step(kind, step):
        @pl.when(group - step >= 0)
        def _():
            source = group - step
            line_wait(kind, source)

            @pl.when(group + 1 < groups)
            def _():
                line_copy(kind, source, 1).start()

            side_copy(kind, source).start()
            core_copy(kind, 2 * source + side).start()

        @pl.when(group + step < groups)
        def _():
            source = group + step
            line_wait(kind, source)

            @pl.when(group >= 1)
            def _():
                line_copy(kind, source, -1).start()

            side_copy(kind, source).start()
            core_copy(kind, 2 * source + side).start()

        @pl.when(group - step + 1 >= 0)
        def _():
            take_side(kind, group - step + 1)

        @pl.when((step > 1) & (group + step - 1 < groups))
        def _():
            take_side(kind, group + step - 1)

    def gather_end(kind):
        last = groups - 1

        @pl.when(group - last >= 0)
        def _():
            take_side(kind, group - last)

        @pl.when((groups > 1) & (group + last < groups))
        def _():
            take_side(kind, group + last)

        @pl.loop(0, exp_size)
        def _(at):
            @pl.when(at != exp_at)
            def _():
                core_wait(kind, at)

    first_sends(0)
    first_sends(1)

    inner_rows = pl.ds(pl.multiple_of(rep_at * depth, depth), depth)

    def ff_cols(at):
        return pl.ds(pl.multiple_of(at * ff_block, ff_block), ff_block)

    def inner_copies(mask):
        dest = rep_at ^ mask
        found = []
        for part in range(2):
            source = w_inner.at[:, ff_cols(dest ^ (2 * part))]
            cols = slice(part * ff_block, (part + 1) * ff_block)
            at = 1 + 2 * mask + part
            if mask == 3:
                found.append(
                    remote(
                        source,
                        staging.at[:, cols],
                        weight_s.at[at],
                        weight_r.at[at],
                        (rep_at ^ 2, exp_at),
                    )
                )
            else:
                found.append(
                    remote(
                        source,
                        inner_w.at[inner_rows, cols],
                        weight_s.at[at],
                        weight_r.at[at],
                        (dest, exp_at),
                    )
                )
        return found

    far_rows = pl.ds(pl.multiple_of((rep_at ^ 2) * depth, depth), depth)
    forward_copy = remote(
        staging,
        inner_w.at[far_rows],
        weight_s.at[1 + 2 * rep_size],
        weight_r.at[1 + 2 * rep_size],
        core_peer,
    )

    for mask in (3, 2, 1):
        for copy in inner_copies(mask):
            copy.start()
    outer_copy.start()

    lanes = counts_v.shape[1]
    expert_row = expert_of[...]
    onehot = (
        lax.broadcasted_iota(jnp.int32, (lanes, rows_n), 0) == expert_row
    ).astype(wide)
    before = (
        lax.broadcasted_iota(jnp.int32, (rows_n, rows_n), 0)
        < lax.broadcasted_iota(jnp.int32, (rows_n, rows_n), 1)
    ).astype(low)
    earlier = jnp.dot(onehot.astype(low), before, preferred_element_type=wide)
    rank = jnp.sum(earlier * onehot, axis=0, keepdims=True).astype(jnp.int32)
    position = expert_row * slots + rank
    pick[...] = (
        lax.broadcasted_iota(jnp.int32, pick.shape, 0) == position
    ).astype(wide).astype(low)
    counts_v[:8, :] = lax.dot_general(
        jnp.ones((8, rows_n), low),
        onehot.astype(low),
        (((1,), (1,)), ((), ())),
        preferred_element_type=wide,
    )
    counts_v[8:, :block] = jnp.broadcast_to(gain_a[...].astype(wide), (8, block))
    cent_v[...] = jnp.broadcast_to(cent[...].astype(wide), cent_v.shape)
    gain_v[...] = jnp.broadcast_to(gain_e[...].astype(wide), gain_v.shape)

    def eight(at):
        return pl.ds(pl.multiple_of(at * 8, 8), 8)

    def sixteen(at):
        return pl.ds(pl.multiple_of(at * 16, 16), 16)

    def count_copy(dest):
        return remote(
            counts_v, small_all.at[sixteen(exp_at)], count_s.at[dest], count_r.at[exp_at], (rep_at, dest)
        )

    count_own = pltpu.make_async_copy(counts_v, small_all.at[sixteen(exp_at)], count_s.at[exp_at])
    count_own.start()

    @pl.loop(1, exp_size)
    def _(at):
        count_copy(exp_at ^ at).start()

    cent_at = side * rep_size + rep_at

    def cent_copy(mask, flip):
        return remote(
            cent_v,
            cents.at[eight(cent_at)],
            cent_s.at[flip * rep_size + mask],
            cent_r.at[flip * rep_size + mask],
            (rep_at ^ mask, exp_at ^ flip),
        )

    cent_own = pltpu.make_async_copy(cent_v, cents.at[eight(cent_at)], cent_s.at[0])
    cent_own.start()
    cent_pairs = [(m, f) for m in range(rep_size) for f in range(2) if m or f]
    for mask, flip in cent_pairs:
        cent_copy(mask, flip).start()

    def gain_copy(mask):
        return remote(
            gain_v, gains_e.at[eight(rep_at)], gain_s.at[mask], gain_r.at[mask], (rep_at ^ mask, exp_at)
        )

    gain_own = pltpu.make_async_copy(gain_v, gains_e.at[eight(rep_at)], gain_s.at[0])
    gain_own.start()
    for mask in range(1, rep_size):
        gain_copy(mask).start()

    count_own.wait()

    @pl.loop(1, exp_size)
    def _(at):
        source = exp_at ^ at
        remote(
            counts_v, small_all.at[sixteen(source)], count_s.at[source], count_r.at[source], (rep_at, source)
        ).wait()

    small_store = pltpu.make_async_copy(small_all, counts_all, out_s.at[1])
    small_store.start()

    tiled = jnp.dot(
        small_all[...].astype(low),
        (
            lax.broadcasted_iota(jnp.int32, (lanes, width), 1) % block
            == lax.broadcasted_iota(jnp.int32, (lanes, width), 0)
        ).astype(wide).astype(low),
        preferred_element_type=wide,
    )
    chosen_row = lax.broadcasted_iota(jnp.int32, (16 * exp_size, width), 0) == (
        16 * (lax.broadcasted_iota(jnp.int32, (16 * exp_size, width), 1) // block) + 8
    )
    gain_row[...] = jnp.sum(jnp.where(chosen_row, tiled, 0.0), axis=0, keepdims=True)

    @pl.loop(0, rows_n // ROWS)
    def _(step):
        here = pl.ds(pl.multiple_of(step * ROWS, ROWS), ROWS)
        unit, _ = row_stats(tokens[here, :].astype(wide))
        normed_a[here, :] = (unit * gain_row[...]).astype(low)

    down = lax.broadcasted_iota(jnp.int32, (rows_n, rows_n), 0)
    along = lax.broadcasted_iota(jnp.int32, (rows_n, rows_n), 1)
    end = jnp.int32(0)
    seg_down = jnp.zeros((rows_n, rows_n), jnp.int32)
    seg_along = jnp.zeros((rows_n, rows_n), jnp.int32)
    for at in range(doc.shape[1]):
        end = end + doc[0, at]
        seg_down = seg_down + (down >= end).astype(jnp.int32)
        seg_along = seg_along + (along >= end).astype(jnp.int32)
    bias[...] = jnp.where((seg_down == seg_along) & (down >= along), 0.0, -1e30)

    @pl.loop(1, groups)
    def _(step):
        gather_step(0, step)

    gather_end(0)

    def slot_rows(at):
        return pl.ds(pl.multiple_of(at * slots, slots), slots)

    def disp_copy(source, dest):
        return remote(
            source.at[slot_rows(dest // 2)],
            arrived.at[slot_rows(exp_at)],
            disp_s.at[dest],
            disp_r.at[exp_at],
            (rep_at, dest),
        )

    def dispatch(source, flip):
        @pl.loop(0, groups)
        def _(at):
            dest = 2 * (group ^ at) + flip

            @pl.when(dest != exp_at)
            def _():
                disp_copy(source, dest).start()

            @pl.when(dest == exp_at)
            def _():
                pltpu.make_async_copy(
                    source.at[slot_rows(group)], arrived.at[slot_rows(exp_at)], disp_s.at[exp_at]
                ).start()

    @pl.loop(1, 1 + (groups - 1 + 2) // 3)
    def _(step):
        gather_step(1, step)

    for at in range(3):

        @pl.loop(0, width // TILE)
        def _(step):
            cols = pl.ds(pl.multiple_of(step * TILE, TILE), TILE)
            qkv[at, :, cols] = jnp.dot(
                normed_a[...], weights[at, :, cols], preferred_element_type=wide
            ).astype(low)

    head_dim = width // HEADS
    pair = 2 * head_dim
    factor = head_dim ** (-0.5)
    lane = lax.broadcasted_iota(jnp.int32, (rows_n, pair), 1)
    pairs = HEADS // 2
    parts = 2
    begun = (groups - 1 + 2) // 3
    for part in range(parts):
        low_step = 1 + begun + part * (groups - 1 - begun) // parts
        high_step = 1 + begun + (part + 1) * (groups - 1 - begun) // parts

        @pl.loop(low_step, high_step)
        def _(step):
            gather_step(1, step)

        @pl.loop(part * pairs // parts, (part + 1) * pairs // parts)
        def _(at):
            cols = pl.ds(pl.multiple_of(at * pair, pair), pair)
            q_pair = qkv[0, :, cols]
            k_pair = qkv[1, :, cols]
            v_pair = qkv[2, :, cols]
            found = []
            for which in range(2):
                chosen = (lane >= head_dim) if which else (lane < head_dim)
                q_one = jnp.where(chosen, q_pair, jnp.zeros_like(q_pair))
                scores = (
                    lax.dot_general(
                        q_one, k_pair, (((1,), (1,)), ((), ())), preferred_element_type=wide
                    )
                    * factor
                    + bias[...]
                )
                top = jnp.max(scores, axis=1, keepdims=True)
                raised = jnp.exp(scores - top)
                total = jnp.sum(raised, axis=1, keepdims=True)
                prob = (raised * (1.0 / total)).astype(low)
                probs[pl.ds(pl.multiple_of((2 * at + which) * rows_n, rows_n), rows_n), :] = prob
                found.append(jnp.dot(prob, v_pair, preferred_element_type=wide))
            context[:, cols] = jnp.where(lane < head_dim, found[0], found[1]).astype(low)

    @pl.loop(0, width // TILE)
    def _(step):
        cols = pl.ds(pl.multiple_of(step * TILE, TILE), TILE)
        packed_c[:, cols] = jnp.dot(
            pick[...], cotangent[:, cols], preferred_element_type=wide
        ).astype(low)

    dispatch(packed_c, 1)

    gather_end(1)
    store = pltpu.make_async_copy(weights, attn_w, out_s.at[0])
    store.start()

    @pl.loop(0, width // TILE)
    def _(step):
        cols = pl.ds(pl.multiple_of(step * TILE, TILE), TILE)
        sum_here = tokens[:, cols].astype(wide) + jnp.dot(
            context[...], weights[3, :, cols], preferred_element_type=wide
        )
        hidden[:, cols] = sum_here
        packed_x[:, cols] = jnp.dot(
            pick[...], sum_here.astype(low), preferred_element_type=wide
        ).astype(low)

    dispatch(packed_x, 0)
    for copy in inner_copies(3):
        copy.wait_recv()
    forward_copy.start()

    store.wait()
    outer_copy.wait()
    forward_copy.wait()
    for mask in range(1, rep_size):
        for copy in inner_copies(mask):
            if mask == 3:
                copy.wait_send()
            else:
                copy.wait()
    for kind in range(2):
        side_copy(kind, group).wait_send()

        @pl.loop(0, groups)
        def _(source):
            @pl.when(source != group)
            def _():
                side_copy(kind, source).wait_send()

            @pl.when((source <= group) & (group + 1 < groups))
            def _():
                line_copy(kind, source, 1).wait_send()

            @pl.when((source >= group) & (group >= 1))
            def _():
                line_copy(kind, source, -1).wait_send()

        @pl.loop(0, exp_size)
        def _(at):
            @pl.when(at != exp_at)
            def _():
                core_copy(kind, at).wait_send()

    small_store.wait()
    cent_own.wait()
    gain_own.wait()
    for mask in range(1, rep_size):
        gain_copy(mask).wait()
    for mask, flip in cent_pairs:
        cent_copy(mask, flip).wait()

    @pl.loop(1, exp_size)
    def _(at):
        source = exp_at ^ at
        remote(
            packed_c.at[slot_rows(source // 2)],
            arrived.at[slot_rows(source)],
            disp_s.at[source],
            disp_r.at[source],
            (rep_at, source),
        ).wait()

    pltpu.make_async_copy(
        packed_c.at[slot_rows(group)], arrived.at[slot_rows(exp_at)], disp_s.at[exp_at]
    ).wait()


def run_attend(exp_size, rep_size, slots, tokens, cotangent, doc, expert_of, attn, gain_a, w_inner, w_outer, gain_e, cent):
    rows_n, width = tokens.shape
    low = jnp.bfloat16
    wide = jnp.float32
    groups = exp_size // 2
    depth = w_inner.shape[0]
    ff_block = w_outer.shape[0]
    anyplace = pl.BlockSpec(memory_space=pl.ANY)
    inside = pl.BlockSpec(memory_space=pltpu.VMEM)
    dma = pltpu.SemaphoreType.DMA
    shape = jax.ShapeDtypeStruct
    return pl.pallas_call(
        functools.partial(attend_kernel, exp_size, rep_size, slots),
        out_shape=(
            shape((4, width, width), low),
            shape((width, 2 * ff_block), low),
            shape((ff_block - DEFER, width), low),
            shape((exp_size * slots, width), low),
            shape((exp_size * 16, 128), wide),
            shape((2 * rep_size * 8, cent.shape[1]), wide),
            shape((rep_size * 8, depth), wide),
            shape((rows_n, width), wide),
            shape((3, rows_n, width), low),
            shape((HEADS * rows_n, rows_n), low),
            shape((rows_n, width), low),
            shape((rows_n, width), low),
            shape((groups * slots, rows_n), low),
            shape((1, width), wide),
        ),
        in_specs=[inside, inside, pl.BlockSpec(memory_space=pltpu.SMEM), inside]
        + [anyplace] * 4
        + [inside, anyplace, anyplace, inside, inside],
        out_specs=(anyplace,) * 7 + (inside,) * 7,
        scratch_shapes=[
            pltpu.VMEM((4, width, width), low),
            pltpu.VMEM((depth, 2 * ff_block), low),
            pltpu.VMEM((exp_size * 16, 128), wide),
            pltpu.VMEM((8, depth), wide),
            pltpu.VMEM((groups * slots, width), low),
            pltpu.VMEM((groups * slots, width), low),
            pltpu.VMEM((rows_n, rows_n), wide),
            pltpu.VMEM((16, 128), wide),
            pltpu.VMEM((8, cent.shape[1]), wide),
            dma((6,)),
            dma((2, 2, groups)),
            dma((2, groups)),
            dma((2, groups)),
            dma((2, groups)),
            dma((2, exp_size)),
            dma((2, exp_size)),
            dma((2 + 2 * rep_size,)),
            dma((2 + 2 * rep_size,)),
            dma((exp_size,)),
            dma((exp_size,)),
            dma((exp_size,)),
            dma((exp_size,)),
            dma((2 * rep_size,)),
            dma((2 * rep_size,)),
            dma((rep_size,)),
            dma((rep_size,)),
            dma((2,)),
        ],
        compiler_params=pltpu.CompilerParams(
            collective_id=1, has_side_effects=True, vmem_limit_bytes=56 << 20
        ),
        cost_estimate=pl.CostEstimate(
            flops=10 * rows_n * width * width,
            bytes_accessed=40 << 20,
            transcendentals=HEADS * rows_n * rows_n,
        ),
        name="attend",
    )(tokens, cotangent, doc, expert_of, *attn, gain_a, w_inner, w_outer, gain_e, cent)


def expert_kernel(
    exp_size,
    rep_size,
    slots,
    arrived_h,
    inner_h,
    outer_h,
    w_inner,
    w_outer,
    counts_all,
    cents,
    gains_e,
    home,
    branch,
    outer_keep,
    outer_send,
    outer_got,
    inner_sum,
    centre_parts,
    arrived,
    spread_m,
    offsets,
    cent_b,
    gain,
    centre_grad,
    centre_v,
    inner_w,
    outer_w,
    own_x,
    own_cot,
    normed,
    active,
    slope,
    states,
    part_send,
    part_recv,
    hop,
    back,
    spread,
    relay,
    acc,
    gates,
    gate_grads,
    outer_keep_v,
    outer_send_v,
    inner_send_v,
    load_sem,
    centre_s,
    centre_r,
    norm_s,
    norm_r,
    state_s,
    state_r,
    part_s,
    part_r,
    grad_s,
    grad_r,
    hop_s,
    hop_r,
    gate_s,
    gate_r,
    ret_s,
    ret_r,
    relay_s,
    relay_r,
    early_s,
    early_r,
    out_sem,
    inner_s,
    out_r,
):
    low = jnp.bfloat16
    wide = jnp.float32
    rep_at = lax.axis_index("rep")
    exp_at = lax.axis_index("exp")
    first = exp_at % 2 == 0
    second = exp_at % 2 == 1
    core_peer = (rep_at ^ 1, exp_at)
    side_peer = (rep_at, exp_at ^ 1)
    width = own_x.shape[1]
    own_rows = own_x.shape[0]
    part = own_rows // CHUNKS
    wide_ff = inner_w.shape[1]
    block = wide_ff // 2
    depth = width // rep_size

    def slot_rows(at):
        return pl.ds(pl.multiple_of(at * slots, slots), slots)

    def inner_rows(mask):
        return pl.ds(pl.multiple_of((rep_at ^ mask) * depth, depth), depth)

    loads = [
        pltpu.make_async_copy(arrived_h, arrived, load_sem.at[0]),
        pltpu.make_async_copy(w_outer, outer_w.at[:block], load_sem.at[1]),
        pltpu.make_async_copy(outer_h, outer_w.at[block : 2 * block - DEFER], load_sem.at[2]),
    ]
    for side in range(2):
        at = rep_at ^ (2 * side)
        loads.append(
            pltpu.make_async_copy(
                w_inner.at[:, pl.ds(pl.multiple_of(at * block, block), block)],
                inner_w.at[inner_rows(0), side * block : (side + 1) * block],
                load_sem.at[3 + side],
            )
        )
    for mask in range(1, rep_size):
        loads.append(
            pltpu.make_async_copy(
                inner_h.at[inner_rows(mask)], inner_w.at[inner_rows(mask)], load_sem.at[4 + mask]
            )
        )
    for load in loads:
        load.start()

    barrier = pltpu.get_barrier_semaphore()
    for mask in range(1, rep_size):
        for flip in range(2):
            pl.semaphore_signal(
                barrier, inc=1, device_id=(rep_at ^ mask, exp_at ^ flip), device_id_type=MESH
            )

    @pl.loop(1, exp_size)
    def _(at):
        pl.semaphore_signal(barrier, inc=1, device_id=(rep_at, exp_at ^ at), device_id_type=MESH)

    counted = counts_all.shape[0]
    group = exp_at // 2
    lane = lax.broadcasted_iota(jnp.int32, (counted, 128), 1)
    mine = jnp.sum(
        jnp.where(lane == group, counts_all[...], 0.0), axis=1, keepdims=True
    )
    mine = jnp.broadcast_to(mine, (counted, 128))
    down = lax.broadcasted_iota(jnp.int32, (counted, counted), 0)
    along = lax.broadcasted_iota(jnp.int32, (counted, counted), 1)
    ahead = ((along // 16 < down // 16) & (along % 16 == 0)).astype(wide).astype(low)
    offsets[0] = jnp.dot(ahead, mine.astype(low), preferred_element_type=wide)
    offsets[1] = mine
    slot_iota = lax.broadcasted_iota(jnp.int32, (slots, own_rows), 0)
    row_iota = lax.broadcasted_iota(jnp.int32, (slots, own_rows), 1)

    @pl.loop(0, exp_size)
    def _(at):
        eight = pl.ds(pl.multiple_of(at * 16, 16), 8)
        start = offsets[0, eight, :][:1, :1].astype(jnp.int32)
        limit = offsets[1, eight, :][:1, :1].astype(jnp.int32)
        spread_m[slot_rows(at), :] = (
            ((slot_iota + start) == row_iota) & (slot_iota < limit)
        ).astype(wide).astype(low)

    piece = cents.shape[1]
    for at in range(width // piece):
        cent_b[:, at * piece : (at + 1) * piece] = jnp.broadcast_to(
            cents[at * 8 : at * 8 + 1, :], (cent_b.shape[0], piece)
        ).astype(low)
    for at in range(rep_size):
        gain[:, at * depth : (at + 1) * depth] = gains_e[at * 8 : at * 8 + 1, :]
    loads[0].wait()

    for at in range(width // TILE):
        cols = slice(at * TILE, (at + 1) * TILE)
        rows_low = lax.dot_general(
            spread_m[...],
            arrived[:, cols],
            (((0,), (0,)), ((), ())),
            preferred_element_type=wide,
        ).astype(low)

        @pl.when(first)
        def _():
            own_x[:, cols] = rows_low

        @pl.when(second)
        def _():
            own_cot[:, cols] = rows_low

    pl.semaphore_wait(barrier, exp_size - 1 + 2 * (rep_size - 1))
    row_peer = (rep_at ^ 2, exp_at)
    late_copy = remote(
        w_outer.at[block - DEFER :],
        outer_w.at[2 * block - DEFER :],
        early_s.at[0],
        early_r.at[0],
        row_peer,
    )
    late_copy.start()

    gate_copy = remote(gates, gates, gate_s.at[0], gate_r.at[0], side_peer)

    def part_rows(at):
        return pl.ds(pl.multiple_of(at * part, part), part)

    def both_rows(at):
        return pl.ds(pl.multiple_of(at * 2 * part, 2 * part), 2 * part)

    def own_slice(at):
        return pl.ds(pl.multiple_of(at * 2 * part + part, part), part)

    def other_slice(at):
        return pl.ds(pl.multiple_of(at * 2 * part, part), part)

    def grad_copy(at):
        rows = part_rows(at)
        return remote(
            gate_grads.at[rows], gate_grads.at[rows], grad_s.at[at], grad_r.at[at], side_peer
        )

    def hop_forward(at):
        rows = part_rows(at)
        return remote(hop.at[rows], own_x.at[rows], hop_s.at[at], hop_r.at[at], side_peer)

    def hop_backward(at):
        return remote(
            hop.at[part_rows(at)], states.at[own_slice(at)], hop_s.at[at], hop_r.at[at], side_peer
        )

    def norm_copy(at):
        return remote(
            normed.at[own_slice(at)], normed.at[other_slice(at)], norm_s.at[at], norm_r.at[at], core_peer
        )

    def state_copy(at):
        return remote(
            states.at[own_slice(at)], states.at[other_slice(at)], state_s.at[at], state_r.at[at], core_peer
        )

    def part_copy(kind, at):
        count = kind * CHUNKS + at
        rows = part_rows(count)
        return remote(
            part_send.at[rows], part_recv.at[rows], part_s.at[count], part_r.at[count], core_peer
        )

    def norm_rows(at):
        @pl.loop(0, part // ROWS)
        def _(step):
            off = pl.multiple_of(step * ROWS, ROWS)
            unit, _ = row_stats(own_x[pl.ds(at * part + off, ROWS), :].astype(wide))
            normed[pl.ds(at * 2 * part + part + off, ROWS), :] = (unit * gain[...]).astype(low)

        norm_copy(at).start()

    steps = 2 * CHUNKS

    def is_forward(step):
        early = step < CHUNKS
        mixed = (step == 0) | ((step % 2 == 1) & (step < steps - 1))
        return (first & early) | (second & mixed)

    def chunk_at(step):
        of_first = jnp.where(step < CHUNKS, step, step - CHUNKS)
        mixed = (step == 0) | ((step % 2 == 1) & (step < steps - 1))
        of_second = jnp.where(
            mixed,
            (step + 1) // 2,
            jnp.where(step == steps - 1, CHUNKS - 1, (step - 2) // 2),
        )
        return jnp.where(first, of_first, of_second)

    @pl.when(first)
    def _():
        logit = lax.dot_general(
            own_x[...], cent_b[...], (((1,), (1,)), ((), ())), preferred_element_type=wide
        )
        gates[...] = jax.nn.sigmoid(logit)
        gate_copy.start()

        @pl.loop(0, CHUNKS)
        def _(at):
            norm_rows(at)

    @pl.when(second)
    def _():
        gate_copy.wait_recv()

        @pl.loop(0, CHUNKS)
        def _(at):
            @pl.loop(0, part // ROWS)
            def _(step):
                off = pl.multiple_of(step * ROWS, ROWS)
                here = pl.ds(at * part + off, ROWS)
                states[pl.ds(at * 2 * part + part + off, ROWS), :] = (
                    gates[here, :][:, :1] * own_cot[here, :].astype(wide)
                ).astype(low)

            state_copy(at).start()

        hop_forward(0).wait_recv()
        norm_rows(0)

    for load in loads[1:]:
        load.wait()
    late_copy.wait_recv()
    centre_grad[...] = jnp.zeros_like(centre_grad)

    def finish_forward(step, at):
        part_copy(0, at).wait_recv()

        @pl.loop(0, part // ROWS)
        def _(tile):
            off = pl.multiple_of(tile * ROWS, ROWS)
            here = pl.ds(at * part + off, ROWS)
            result = (
                own_x[here, :].astype(wide)
                + acc[step % 2, pl.ds(off, ROWS), :]
                + part_recv[here, :].astype(wide)
            )

            @pl.when(first)
            def _():
                hop[here, :] = result.astype(low)

            @pl.when(second)
            def _():
                cot = own_cot[here, :].astype(wide)
                back[here, :] = (gates[here, :][:, :1] * result).astype(low)
                gate_grads[here, :] = jnp.broadcast_to(
                    jnp.sum(cot * result, axis=1, keepdims=True), (ROWS, gate_grads.shape[1])
                )

        @pl.when(first)
        def _():
            hop_forward(at).start()

        @pl.when(second)
        def _():
            grad_copy(at).start()

    def finish_backward(step, at):
        part_copy(1, at).wait_recv()

        @pl.when(first)
        def _():
            grad_copy(at).wait_recv()

        @pl.loop(0, part // ROWS)
        def _(tile):
            off = pl.multiple_of(tile * ROWS, ROWS)
            here = pl.ds(at * part + off, ROWS)
            rows_in = own_x[here, :].astype(wide)
            unit, inv_scale = row_stats(rows_in)
            grad_unit = (
                acc[step % 2, pl.ds(off, ROWS), :]
                + part_recv[pl.ds((CHUNKS + at) * part + off, ROWS), :].astype(wide)
            ) * gain[...]
            grad_in = (
                grad_unit
                - jnp.mean(grad_unit, axis=-1, keepdims=True)
                - unit * jnp.mean(grad_unit * unit, axis=-1, keepdims=True)
            ) * inv_scale
            gate = gates[here, :][:, :1]

            @pl.when(second)
            def _():
                state = gate * own_cot[here, :].astype(wide) + grad_in
                hop[here, :] = state.astype(low)

            @pl.when(first)
            def _():
                state = states[pl.ds(at * 2 * part + part + off, ROWS), :].astype(wide) + grad_in
                grad_logit = gate_grads[here, :][:, :1] * gate * (1.0 - gate)
                back[here, :] = (state + grad_logit * cent_b[:1, :].astype(wide)).astype(low)
                centre_grad[...] += jnp.sum(grad_logit * rows_in, axis=0, keepdims=True)

        @pl.when(second)
        def _():
            hop_backward(at).start()

    def finish(step):
        at = chunk_at(step)
        forward = is_forward(step)

        @pl.when(forward)
        def _():
            finish_forward(step, at)

        @pl.when(jnp.logical_not(forward))
        def _():
            finish_backward(step, at)

    @pl.loop(0, steps)
    def _(step):
        at = chunk_at(step)
        forward = is_forward(step)
        rows = both_rows(at)

        @pl.when(forward)
        def _():
            norm_copy(at).wait_recv()

            @pl.loop(0, wide_ff // BIG)
            def _(tile):
                cols = pl.ds(pl.multiple_of(tile * BIG, BIG), BIG)
                inner = jnp.dot(normed[rows, :], inner_w[:, cols], preferred_element_type=wide)
                normal = 0.5 * (1.0 + lax.erf(inner * ROOT_HALF))
                active[rows, cols] = (inner * normal).astype(low)
                slope[rows, cols] = (
                    normal + inner * jnp.exp(-0.5 * inner * inner) * INV_ROOT_TAU
                ).astype(low)

        @pl.when(jnp.logical_not(forward))
        def _():
            state_copy(at).wait_recv()

            @pl.loop(0, wide_ff // BIG)
            def _(tile):
                cols = pl.ds(pl.multiple_of(tile * BIG, BIG), BIG)
                grad_active = lax.dot_general(
                    states[rows, :],
                    outer_w[cols, :],
                    (((1,), (1,)), ((), ())),
                    preferred_element_type=wide,
                )
                slope[rows, cols] = (grad_active * slope[rows, cols].astype(wide)).astype(low)

        @pl.when((step > 0) & jnp.logical_not(first & (step == CHUNKS)))
        def _():
            finish(step - 1)

        @pl.when(forward)
        def _():
            both = jnp.dot(active[rows, :], outer_w[...], preferred_element_type=wide)
            part_send[part_rows(at), :] = both[:part].astype(low)
            acc[step % 2] = both[part:]
            part_copy(0, at).start()

        @pl.when(jnp.logical_not(forward))
        def _():
            both = lax.dot_general(
                slope[rows, :],
                inner_w[...],
                (((1,), (1,)), ((), ())),
                preferred_element_type=wide,
            )
            part_send[part_rows(CHUNKS + at), :] = both[:part].astype(low)
            acc[step % 2] = both[part:]
            part_copy(1, at).start()

        @pl.when(first & (step == CHUNKS - 1))
        def _():
            finish(step)

        after = step + 1
        after_at = chunk_at(after)

        @pl.when(first & (after >= CHUNKS) & (after < steps))
        def _():
            hop_backward(after_at).wait_recv()
            state_copy(after_at).start()

        @pl.when(second & is_forward(after) & (after < steps))
        def _():
            hop_forward(after_at).wait_recv()
            norm_rows(after_at)

    finish(steps - 1)

    groups = exp_size // 2

    def ret_copy(source, dest):
        return remote(
            source,
            home.at[slot_rows(group)],
            ret_s.at[dest],
            ret_r.at[group],
            (rep_at, dest),
        )

    def relay_copy(which):
        return remote(
            spread.at[slot_rows(2 * which + 1)],
            relay.at[slot_rows(which)],
            relay_s.at[which],
            relay_r.at[which],
            side_peer,
        )

    ret_own = pltpu.make_async_copy(
        spread.at[slot_rows(exp_at)], home.at[slot_rows(group)], ret_s.at[exp_at]
    )

    def make_spread():
        @pl.loop(0, width // TILE)
        def _(step):
            cols = pl.ds(pl.multiple_of(step * TILE, TILE), TILE)
            spread[:, cols] = jnp.dot(
                spread_m[...], back[:, cols], preferred_element_type=wide
            ).astype(low)

    def send_back():
        @pl.loop(1, groups)
        def _(step):
            relay_copy(group ^ (groups - step)).start()

        @pl.loop(1, groups)
        def _(step):
            dest = 2 * (group ^ (groups - step))
            ret_copy(spread.at[slot_rows(dest)], dest).start()

        ret_copy(spread.at[slot_rows(exp_at + 1)], exp_at + 1).start()
        ret_own.start()

    def eight_rows(at):
        return pl.ds(pl.multiple_of(at * 8, 8), 8)

    def centre_copy(mask, flip):
        dest = rep_at ^ mask
        return remote(
            centre_v.at[eight_rows(flip * rep_size + dest)],
            centre_parts.at[eight_rows(rep_at)],
            centre_s.at[flip * rep_size + mask],
            centre_r.at[mask],
            (dest, exp_at ^ flip),
        )

    centre_own = pltpu.make_async_copy(
        centre_v.at[eight_rows(rep_at)], centre_parts.at[eight_rows(rep_at)], centre_s.at[0]
    )
    centre_pairs = [(m, f) for m in range(rep_size) for f in range(2) if m or f]

    make_spread()

    @pl.when(first)
    def _():
        send_back()
        for at in range(width // piece):
            centre_v[at * 8 : (at + 1) * 8, :] = jnp.broadcast_to(
                centre_grad[:, at * piece : (at + 1) * piece], (8, piece)
            )
        centre_own.start()
        for mask, flip in centre_pairs:
            centre_copy(mask, flip).start()

    outs = []
    tiles = block // TILE
    early_copy = remote(
        outer_send_v.at[:EARLY], outer_got, early_s.at[1], early_r.at[1], row_peer
    )
    for at in list(range(tiles, 2 * tiles)) + list(range(tiles)):
        rows = slice(at * TILE, (at + 1) * TILE)
        grad = lax.dot_general(
            active[:, rows], states[...], (((0,), (0,)), ((), ())), preferred_element_type=wide
        )
        if at < tiles:
            outer_keep_v[rows, :] = grad
            outs.append((outer_keep_v.at[rows], outer_keep.at[rows]))
        else:
            top = at * TILE - block
            outer_send_v[top : top + TILE, :] = grad.astype(low)
            if top + TILE == EARLY:
                early_copy.start()
            if top < EARLY:
                continue
            outs.append(
                (outer_send_v.at[top : top + TILE], outer_send.at[top - EARLY : top - EARLY + TILE])
            )
        pltpu.make_async_copy(outs[-1][0], outs[-1][1], out_sem.at[len(outs) - 1]).start()
    outs.append((spread, branch))
    pltpu.make_async_copy(spread, branch, out_sem.at[len(outs) - 1]).start()

    def inner_copy(mask, side):
        at = rep_at ^ (2 * side)
        cols = pl.ds(pl.multiple_of(at * block, block), block)
        target = inner_sum.at[mask // 2, :, cols]
        source = inner_send_v.at[mask, side]
        count = 2 * mask + side
        if mask % 2 == 0:
            return pltpu.make_async_copy(source, target, inner_s.at[count])
        return remote(source, target, inner_s.at[count], out_r.at[count], core_peer)

    inner_order = [(m, f) for m in (3, 1, 2, 0) for f in range(2)]
    for mask, side in inner_order:
        cols = slice(side * block, (side + 1) * block)
        grad = lax.dot_general(
            normed[:, inner_rows(mask)],
            slope[:, cols],
            (((0,), (0,)), ((), ())),
            preferred_element_type=wide,
        )
        inner_send_v[mask, side] = grad.astype(low)
        inner_copy(mask, side).start()

    @pl.when(second)
    def _():
        @pl.loop(1, groups)
        def _(step):
            which = group ^ (groups - step)
            relay_copy(which).wait_recv()
            ret_copy(relay.at[slot_rows(which)], 2 * which + 1).start()

    late_copy.wait_send()
    early_copy.wait()
    for at, (source, target) in enumerate(outs):
        pltpu.make_async_copy(source, target, out_sem.at[at]).wait()
    for mask, side in inner_order:
        inner_copy(mask, side).wait()
    for at in range(CHUNKS):
        norm_copy(at).wait_send()
        state_copy(at).wait_send()
        part_copy(0, at).wait_send()
        part_copy(1, at).wait_send()

        @pl.when(first)
        def _():
            hop_forward(at).wait_send()

        @pl.when(second)
        def _():
            hop_backward(at).wait_send()
            grad_copy(at).wait_send()

    @pl.when(first)
    def _():
        gate_copy.wait_send()

    @pl.when(first)
    def _():
        centre_own.wait()
        for mask, flip in centre_pairs:
            centre_copy(mask, flip).wait_send()
        for mask in range(1, rep_size):
            centre_copy(mask, 0).wait_recv()

    @pl.when(second)
    def _():
        for mask in range(rep_size):
            centre_copy(mask, 1).wait_recv()

    @pl.when(first)
    def _():
        ret_own.wait()
        ret_copy(spread.at[slot_rows(exp_at + 1)], exp_at + 1).wait_send()

        @pl.loop(1, groups)
        def _(step):
            which = group ^ step
            relay_copy(which).wait_send()
            ret_copy(spread.at[slot_rows(2 * which)], 2 * which).wait_send()

    @pl.when(second)
    def _():
        @pl.loop(1, groups)
        def _(step):
            which = group ^ step
            ret_copy(relay.at[slot_rows(which)], 2 * which + 1).wait_send()

        remote(
            relay.at[slot_rows(group)],
            home.at[slot_rows(group)],
            relay_s.at[group],
            ret_r.at[group],
            side_peer,
        ).wait_recv()

    @pl.loop(1, groups)
    def _(step):
        source = group ^ step
        remote(
            relay.at[slot_rows(source)],
            home.at[slot_rows(source)],
            relay_s.at[source],
            ret_r.at[source],
            side_peer,
        ).wait_recv()


def run_experts(
    exp_size, rep_size, slots, own_rows, arrived, inner_w, outer_w, w_inner, w_outer, counts_all, cents, gains_e
):
    width = arrived.shape[1]
    depth = width // rep_size
    block = w_outer.shape[0]
    low = jnp.bfloat16
    wide = jnp.float32
    total = exp_size * slots
    all_rows = 2 * own_rows
    part = own_rows // CHUNKS
    piece = cents.shape[1]
    anyplace = pl.BlockSpec(memory_space=pl.ANY)
    inside = pl.BlockSpec(memory_space=pltpu.VMEM)
    dma = pltpu.SemaphoreType.DMA
    n_out = (2 * block - EARLY) // TILE + 1
    scratch = [
        pltpu.VMEM((total, width), low),
        pltpu.VMEM((total, own_rows), low),
        pltpu.VMEM((2, exp_size * 16, 128), wide),
        pltpu.VMEM((128, width), low),
        pltpu.VMEM((1, width), wide),
        pltpu.VMEM((1, width), wide),
        pltpu.VMEM((2 * rep_size * 8, piece), wide),
        pltpu.VMEM((width, 2 * block), low),
        pltpu.VMEM((2 * block, width), low),
        pltpu.VMEM((own_rows, width), low),
        pltpu.VMEM((own_rows, width), low),
        pltpu.VMEM((all_rows, width), low),
        pltpu.VMEM((all_rows, 2 * block), low),
        pltpu.VMEM((all_rows, 2 * block), low),
        pltpu.VMEM((all_rows, width), low),
        pltpu.VMEM((2 * own_rows, width), low),
        pltpu.VMEM((2 * own_rows, width), low),
        pltpu.VMEM((own_rows, width), low),
        pltpu.VMEM((own_rows, width), low),
        pltpu.VMEM((total, width), low),
        pltpu.VMEM((total // 2, width), low),
        pltpu.VMEM((2, part, width), wide),
        pltpu.VMEM((own_rows, 128), wide),
        pltpu.VMEM((own_rows, 128), wide),
        pltpu.VMEM((block, width), wide),
        pltpu.VMEM((block, width), low),
        pltpu.VMEM((rep_size, 2, depth, block), low),
        dma((8,)),
        dma((2 * rep_size,)),
        dma((rep_size,)),
    ]
    scratch += [dma((CHUNKS,)) for _ in range(4)]
    scratch += [dma((2 * CHUNKS,)), dma((2 * CHUNKS,))]
    scratch += [dma((CHUNKS,)) for _ in range(4)]
    scratch += [dma((1,)), dma((1,)), dma((exp_size,)), dma((exp_size // 2,))]
    scratch += [dma((exp_size // 2,)), dma((exp_size // 2,)), dma((2,)), dma((2,)), dma((n_out,))]
    scratch += [dma((2 * rep_size,)), dma((2 * rep_size,))]
    flops = 2 * all_rows * width * 2 * block * 6
    return pl.pallas_call(
        functools.partial(expert_kernel, exp_size, rep_size, slots),
        out_shape=(
            jax.ShapeDtypeStruct((total // 2, width), low),
            jax.ShapeDtypeStruct((total, width), low),
            jax.ShapeDtypeStruct((block, width), wide),
            jax.ShapeDtypeStruct((block - EARLY, width), low),
            jax.ShapeDtypeStruct((EARLY, width), low),
            jax.ShapeDtypeStruct((2, depth, rep_size * block), low),
            jax.ShapeDtypeStruct((rep_size * 8, piece), wide),
        ),
        in_specs=[anyplace] * 5 + [inside] * 3,
        out_specs=(anyplace,) * 7,
        scratch_shapes=scratch,
        compiler_params=pltpu.CompilerParams(
            collective_id=0, has_side_effects=True, vmem_limit_bytes=62 << 20
        ),
        cost_estimate=pl.CostEstimate(
            flops=flops, bytes_accessed=40 << 20, transcendentals=2 * all_rows * 2 * block
        ),
        name="experts",
    )(arrived, inner_w, outer_w, w_inner, w_outer, counts_all, cents, gains_e)


def finish_kernel(
    exp_size,
    rep_size,
    home,
    branch,
    pick,
    hidden,
    cotangent,
    tokens,
    gain_row,
    qkv,
    probs,
    normed_a,
    context,
    attn_w,
    outer_send,
    inner_sum,
    output,
    grad_tokens,
    shares,
    outer_recv,
    inner_recv,
    branch_in,
    weights,
    grad_hidden,
    grad_attn,
    grad_context,
    grads3,
    keep,
    core_out,
    core_in,
    side_out,
    side_in,
    line_out,
    line_in,
    total,
    row_out,
    row_in,
    half_out,
    half_in,
    load_s,
    branch_s,
    branch_r,
    expert_s,
    expert_r,
    core_s,
    core_r,
    side_s,
    side_r,
    line_s,
    line_r,
    row_s,
    row_r,
    half_s,
    half_r,
):
    low = jnp.bfloat16
    wide = jnp.float32
    rep_at = lax.axis_index("rep")
    exp_at = lax.axis_index("exp")
    core = rep_at % 2
    group = exp_at // 2
    side = exp_at % 2
    groups = exp_size // 2
    rows_n, width = tokens.shape
    half = width // 2
    block = width // exp_size
    core_peer = (rep_at ^ 1, exp_at)
    side_peer = (rep_at, exp_at ^ 1)
    row_peer = (rep_at ^ 2, exp_at)

    load = pltpu.make_async_copy(attn_w, weights, load_s.at[0])
    load.start()

    barrier = pltpu.get_barrier_semaphore()
    for mask in range(1, 3):
        pl.semaphore_signal(
            barrier, inc=1, device_id=(rep_at ^ mask, exp_at), device_id_type=MESH
        )

    @pl.loop(1, exp_size)
    def _(at):
        pl.semaphore_signal(barrier, inc=1, device_id=(rep_at, exp_at ^ at), device_id_type=MESH)

    pl.semaphore_wait(barrier, exp_size + 1)

    outer_copy = remote(outer_send, outer_recv, expert_s.at[0], expert_r.at[0], row_peer)

    inner_copy = remote(inner_sum.at[1], inner_recv, expert_s.at[1], expert_r.at[1], row_peer)
    inner_copy.start()
    outer_copy.start()

    slots = pick.shape[0] // groups

    def slot_rows(at):
        return pl.ds(pl.multiple_of(at * slots, slots), slots)

    def branch_copy(dest):
        return remote(
            branch.at[slot_rows(dest)],
            branch_in.at[slot_rows(group)],
            branch_s.at[dest],
            branch_r.at[group],
            (rep_at, dest),
        )

    branch_own = pltpu.make_async_copy(
        branch.at[slot_rows(exp_at)], branch_in.at[slot_rows(group)], branch_s.at[exp_at]
    )

    @pl.when(side == 1)
    def _():
        branch_own.start()

        @pl.loop(1, exp_size)
        def _(at):
            branch_copy(exp_at ^ at).start()

    @pl.loop(0, width // TILE)
    def _(step):
        cols = pl.ds(pl.multiple_of(step * TILE, TILE), TILE)
        back = lax.dot_general(
            pick[...], home[:, cols], (((0,), (0,)), ((), ())), preferred_element_type=wide
        )
        grad = cotangent[:, cols].astype(wide) + back
        grad_hidden[:, cols] = grad
        grad_attn[:, cols] = grad.astype(low)

    own_half = pl.ds(pl.multiple_of(core * half, half), half)
    other_half = pl.ds(pl.multiple_of((1 - core) * half, half), half)

    def core_copy(at):
        return remote(core_out.at[at], core_in.at[at], core_s.at[at], core_r.at[at], core_peer)

    def product(at, left, right, cols, target, kind):
        @pl.loop(0, width // TILE)
        def _(step):
            rows = pl.ds(pl.multiple_of(step * TILE, TILE), TILE)
            target[at, rows, :] = lax.dot_general(
                left[:, rows], right[:, cols], (((0,), (0,)), ((), ())), preferred_element_type=wide
            ).astype(kind)

    def share_start(at, left, right):
        product(at, left, right, other_half, core_out, low)
        core_copy(at).start()
        product(at, left, right, own_half, keep, wide)

    def block_rows(at):
        return pl.ds(pl.multiple_of(at * block, block), block)

    def side_copy(at):
        return remote(side_out.at[at], side_in.at[at], side_s.at[at], side_r.at[at], side_peer)

    def share_side(at):
        core_copy(at).wait_recv()

        @pl.loop(0, groups)
        def _(which):
            rows = block_rows(2 * which + 1 - side)
            side_out[at, block_rows(which), :] = (
                keep[at, rows, :] + core_in[at, rows, :].astype(wide)
            ).astype(low)

        side_copy(at).start()

        @pl.loop(0, groups)
        def _(which):
            rows = block_rows(2 * which + side)
            keep[at, rows, :] = keep[at, rows, :] + core_in[at, rows, :].astype(wide)

    def line_copy(at, mask):
        dest = group ^ mask
        return remote(
            line_out.at[at, block_rows(dest)],
            line_in.at[at, block_rows(group)],
            line_s.at[at, mask],
            line_r.at[at, mask],
            (rep_at, 2 * dest + side),
        )

    def share_line(at):
        side_copy(at).wait_recv()

        @pl.loop(1, groups)
        def _(mask):
            dest = group ^ mask
            line_out[at, block_rows(dest), :] = (
                keep[at, block_rows(2 * dest + side), :] + side_in[at, block_rows(dest), :].astype(wide)
            ).astype(low)
            line_copy(at, mask).start()

        total[at] = keep[at, block_rows(exp_at), :] + side_in[at, block_rows(group), :].astype(wide)

    def row_copy(at):
        return remote(row_out.at[at], row_in.at[at], row_s.at[at], row_r.at[at], row_peer)

    def share_row(at):
        @pl.loop(1, groups)
        def _(mask):
            line_copy(at, mask).wait_recv()
            total[at] = total[at] + line_in[at, block_rows(group ^ mask), :].astype(wide)

        row_out[at] = total[at].astype(low)
        row_copy(at).start()

    def half_copy(at):
        return remote(half_out.at[at], half_in.at[at], half_s.at[at], half_r.at[at], core_peer)

    def share_half(at):
        row_copy(at).wait_recv()
        summed = row_out[at].astype(wide) + row_in[at].astype(wide)
        half_out[at] = summed
        half_copy(at).start()
        shares[at, :, own_half] = summed

    def share_end(at):
        half_copy(at).wait_recv()
        shares[at, :, other_half] = half_in[at]

    share_start(3, context, grad_attn)
    load.wait()

    @pl.loop(0, width // TILE)
    def _(step):
        rows = pl.ds(pl.multiple_of(step * TILE, TILE), TILE)
        grad_context[:, rows] = lax.dot_general(
            grad_attn[...], weights[3, rows, :], (((1,), (1,)), ((), ())), preferred_element_type=wide
        ).astype(low)

    share_side(3)

    head_dim = width // HEADS
    pair = 2 * head_dim
    factor = head_dim ** (-0.5)
    lane = lax.broadcasted_iota(jnp.int32, (rows_n, pair), 1)

    def heads(start, stop):
        @pl.loop(start, stop)
        def _(at):
            cols = pl.ds(pl.multiple_of(at * pair, pair), pair)
            q_pair = qkv[0, :, cols]
            k_pair = qkv[1, :, cols]
            v_pair = qkv[2, :, cols]
            c_pair = grad_context[:, cols]
            found = []
            for which in range(2):
                chosen = (lane >= head_dim) if which else (lane < head_dim)
                c_one = jnp.where(chosen, c_pair, jnp.zeros_like(c_pair))
                prob = probs[pl.ds(pl.multiple_of((2 * at + which) * rows_n, rows_n), rows_n), :]
                grad_prob = lax.dot_general(
                    c_one, v_pair, (((1,), (1,)), ((), ())), preferred_element_type=wide
                )
                weighted = prob.astype(wide) * grad_prob
                row_sum = jnp.sum(weighted, axis=1, keepdims=True)
                grad_score = (weighted - prob.astype(wide) * row_sum).astype(low)
                found.append(
                    (
                        jnp.dot(grad_score, k_pair, preferred_element_type=wide) * factor,
                        lax.dot_general(
                            grad_score,
                            q_pair,
                            (((0,), (0,)), ((), ())),
                            preferred_element_type=wide,
                        )
                        * factor,
                        lax.dot_general(
                            prob, c_pair, (((0,), (0,)), ((), ())), preferred_element_type=wide
                        ),
                    )
                )
            for which in range(3):
                grads3[which, :, cols] = jnp.where(
                    lane < head_dim, found[0][which], found[1][which]
                ).astype(low)

    heads(0, HEADS // 4)
    share_line(3)
    heads(HEADS // 4, HEADS // 2)
    for at in range(3):
        share_start(at, normed_a, grads3.at[at])
    for at in range(3):
        share_side(at)

    @pl.loop(0, width // TILE)
    def _(step):
        rows = pl.ds(pl.multiple_of(step * TILE, TILE), TILE)
        grad_normed = jnp.zeros((rows_n, TILE), wide)
        for at in range(3):
            grad_normed = grad_normed + lax.dot_general(
                grads3[at], weights[at, rows, :], (((1,), (1,)), ((), ())), preferred_element_type=wide
            )
        grad_tokens[:, rows] = grad_normed

    @pl.loop(0, rows_n // ROWS)
    def _(step):
        here = pl.ds(pl.multiple_of(step * ROWS, ROWS), ROWS)
        unit, inv_scale = row_stats(tokens[here, :].astype(wide))
        grad_unit = grad_tokens[here, :] * gain_row[...]
        grad_in = (
            grad_unit
            - jnp.mean(grad_unit, axis=-1, keepdims=True)
            - unit * jnp.mean(grad_unit * unit, axis=-1, keepdims=True)
        ) * inv_scale
        grad_tokens[here, :] = grad_hidden[here, :] + grad_in

    share_row(3)
    for at in range(3):
        share_line(at)

    def branch_wait(which):
        remote(
            branch.at[slot_rows(which)],
            branch_in.at[slot_rows(which)],
            branch_s.at[which],
            branch_r.at[which],
            side_peer,
        ).wait_recv()

    @pl.when(side == 0)
    def _():
        branch_wait(group)

    @pl.when(side == 1)
    def _():
        branch_own.wait()

    @pl.loop(1, groups)
    def _(at):
        branch_wait(group ^ at)

    @pl.loop(0, width // TILE)
    def _(step):
        cols = pl.ds(pl.multiple_of(step * TILE, TILE), TILE)
        rows = lax.dot_general(
            pick[...], branch_in[:, cols], (((0,), (0,)), ((), ())), preferred_element_type=wide
        )
        output[:, cols] = (hidden[:, cols] + rows).astype(low)

    for at in range(3):
        share_row(at)
    for at in (3, 0, 1, 2):
        share_half(at)
    for at in (3, 0, 1, 2):
        share_end(at)

    @pl.when(side == 1)
    def _():
        @pl.loop(1, exp_size)
        def _(at):
            branch_copy(exp_at ^ at).wait_send()

    for at in range(4):
        core_copy(at).wait_send()
        side_copy(at).wait_send()
        row_copy(at).wait_send()
        half_copy(at).wait_send()

        @pl.loop(1, groups)
        def _(mask):
            line_copy(at, mask).wait_send()

    inner_copy.wait()
    outer_copy.wait()


def run_finish(exp_size, rep_size, home, branch, pick, hidden, cotangent, tokens, gain_row, qkv, probs, normed_a, context, attn_w, outer_send, inner_sum):
    rows_n, width = tokens.shape
    low = jnp.bfloat16
    wide = jnp.float32
    half = width // 2
    groups = exp_size // 2
    block = width // exp_size
    anyplace = pl.BlockSpec(memory_space=pl.ANY)
    inside = pl.BlockSpec(memory_space=pltpu.VMEM)
    dma = pltpu.SemaphoreType.DMA
    shape = jax.ShapeDtypeStruct
    return pl.pallas_call(
        functools.partial(finish_kernel, exp_size, rep_size),
        out_shape=(
            shape((rows_n, width), low),
            shape((rows_n, width), wide),
            shape((4, block, width), wide),
            shape(outer_send.shape, low),
            shape(inner_sum.shape[1:], low),
        ),
        in_specs=[inside, anyplace] + [inside] * 9 + [anyplace] * 3,
        out_specs=(inside,) * 3 + (anyplace,) * 2,
        scratch_shapes=[
            pltpu.VMEM(pick.shape[:1] + (width,), low),
            pltpu.VMEM((4, width, width), low),
            pltpu.VMEM((rows_n, width), wide),
            pltpu.VMEM((rows_n, width), low),
            pltpu.VMEM((rows_n, width), low),
            pltpu.VMEM((3, rows_n, width), low),
            pltpu.VMEM((4, width, half), wide),
            pltpu.VMEM((4, width, half), low),
            pltpu.VMEM((4, width, half), low),
            pltpu.VMEM((4, width // 2, half), low),
            pltpu.VMEM((4, width // 2, half), low),
            pltpu.VMEM((4, width // 2, half), low),
            pltpu.VMEM((4, width // 2, half), low),
            pltpu.VMEM((4, block, half), wide),
            pltpu.VMEM((4, block, half), low),
            pltpu.VMEM((4, block, half), low),
            pltpu.VMEM((4, block, half), wide),
            pltpu.VMEM((4, block, half), wide),
            dma((1,)),
            dma((exp_size,)),
            dma((groups,)),
            dma((2,)),
            dma((2,)),
            dma((4,)),
            dma((4,)),
            dma((4,)),
            dma((4,)),
            dma((4, groups)),
            dma((4, groups)),
            dma((4,)),
            dma((4,)),
            dma((4,)),
            dma((4,)),
        ],
        compiler_params=pltpu.CompilerParams(
            collective_id=2, has_side_effects=True, vmem_limit_bytes=60 << 20
        ),
        cost_estimate=pl.CostEstimate(
            flops=20 * rows_n * width * width, bytes_accessed=60 << 20, transcendentals=0
        ),
        name="finish",
    )(
        home,
        branch,
        pick,
        hidden,
        cotangent,
        tokens,
        gain_row,
        qkv,
        probs,
        normed_a,
        context,
        attn_w,
        outer_send,
        inner_sum,
    )


def shards(
    tokens,
    cotangent,
    doc_lengths,
    expert_of_token,
    w_query,
    w_key,
    w_value,
    w_output,
    attn_gain,
    w_inner,
    w_outer,
    expert_gain,
    centroids,
):
    exp_size = lax.axis_size("exp")
    rep_size = lax.axis_size("rep")
    row_count = tokens.shape[0]
    wide = jnp.float32

    slots = -(-3 * row_count // exp_size // 16) * 16
    (
        attn_w,
        inner_w,
        outer_w,
        arrived,
        counts_all,
        cents,
        gains_e,
        hidden,
        qkv,
        probs,
        normed_a,
        context,
        pick,
        gain_row,
    ) = run_attend(
        exp_size,
        rep_size,
        slots,
        tokens,
        cotangent,
        doc_lengths,
        expert_of_token[None],
        (w_query, w_key, w_value, w_output),
        attn_gain[None],
        w_inner[0],
        w_outer[0],
        expert_gain,
        centroids,
    )
    home, branch, outer_keep, outer_send, outer_got, inner_sum, centre_parts = run_experts(
        exp_size,
        rep_size,
        slots,
        2 * row_count,
        arrived,
        inner_w,
        outer_w,
        w_inner[0],
        w_outer[0],
        counts_all,
        cents,
        gains_e,
    )
    output, grad_tokens, shares, outer_recv, inner_recv = run_finish(
        exp_size,
        rep_size,
        home,
        branch,
        pick,
        hidden,
        cotangent,
        tokens,
        gain_row,
        qkv,
        probs,
        normed_a,
        context,
        attn_w,
        outer_send,
        inner_sum,
    )
    grad_centroids = jnp.sum(centre_parts.reshape(rep_size, 8, -1)[:, 0], axis=0)[None]
    grad_w_outer = (
        outer_keep + jnp.concatenate([outer_got, outer_recv], axis=0).astype(wide)
    )[None]
    summed = inner_sum[0].astype(wide) + inner_recv.astype(wide)
    grad_w_inner = summed[None]
    grad_expert_gain = jnp.sum(summed * w_inner[0].astype(wide), axis=1)[None] / expert_gain.astype(
        wide
    )
    share_gain = sum(
        jnp.sum(shares[i] * w.astype(wide), axis=1) for i, w in enumerate((w_query, w_key, w_value))
    ) / attn_gain.astype(wide)
    return (
        output,
        grad_tokens,
        shares[0],
        shares[1],
        shares[2],
        shares[3],
        share_gain,
        grad_w_inner,
        grad_w_outer,
        grad_expert_gain,
        grad_centroids,
    )


def solution(mesh):
    placed = (
        P(("rep", "exp"), None),
        P(("rep", "exp"), None),
        P(("rep", "exp"), None),
        P(("rep", "exp")),
        P("exp", None),
        P("exp", None),
        P("exp", None),
        P("exp", None),
        P("exp"),
        P("exp", "rep", None),
        P("exp", "rep", None),
        P("exp", "rep"),
        P("exp", "rep"),
    )
    return jax.shard_map(
        shards,
        mesh=mesh,
        in_specs=placed,
        out_specs=(
            P(("rep", "exp"), None),
            P(("rep", "exp"), None),
            P("exp", None),
            P("exp", None),
            P("exp", None),
            P("exp", None),
            P("exp"),
            P("exp", "rep", None),
            P("exp", "rep", None),
            P("exp", "rep"),
            P("exp", "rep"),
        ),
        check_vma=False,
    )
```

```python
import functools

import jax
import jax.numpy as jnp
from jax import lax
from jax.experimental import pallas as pl
from jax.experimental.pallas import tpu as pltpu
from jax.sharding import PartitionSpec as P

HEADS = 16
EPS = 1e-05
ROOT_HALF = 0.7071067811865476
INV_ROOT_TAU = 0.3989422804014327
CHUNKS = 4
DEFER = 256
EARLY = 512


MESH = pl.DeviceIdType.MESH
TILE = 256
ROWS = 64
BIG = 1024


def remote(src, dst, send_sem, recv_sem, device):
    return pltpu.make_async_remote_copy(
        src_ref=src,
        dst_ref=dst,
        send_sem=send_sem,
        recv_sem=recv_sem,
        device_id=device,
        device_id_type=MESH,
    )


def row_stats(rows):
    row_mean = jnp.mean(rows, axis=-1, keepdims=True)
    centered = rows - row_mean
    variance = jnp.mean(centered * centered, axis=-1, keepdims=True)
    inv_scale = lax.rsqrt(variance + EPS)
    return centered * inv_scale, inv_scale


def attend_kernel(
    exp_size,
    rep_size,
    slots,
    tokens,
    cotangent,
    doc,
    expert_of,
    w_query,
    w_key,
    w_value,
    w_output,
    gain_a,
    w_inner,
    w_outer,
    gain_e,
    cent,
    attn_w,
    inner_w,
    outer_w,
    arrived,
    counts_all,
    cents,
    gains_e,
    packed_h,
    hidden_h,
    qkv_h,
    probs_h,
    normed_h,
    context_h,
    pick,
    gain_row,
    hidden,
    qkv,
    probs,
    normed_a,
    context,
    weights,
    staging,
    small_all,
    gain_v,
    packed_x,
    packed_c,
    bias,
    counts_v,
    cent_v,
    own_s,
    line_s,
    line_r,
    side_s,
    side_r,
    core_s,
    core_r,
    weight_s,
    weight_r,
    disp_s,
    disp_r,
    count_s,
    count_r,
    cent_s,
    cent_r,
    gain_s,
    gain_r,
    out_s,
):
    low = jnp.bfloat16
    wide = jnp.float32
    rep_at = lax.axis_index("rep")
    exp_at = lax.axis_index("exp")
    core = rep_at % 2
    group = exp_at // 2
    side = exp_at % 2
    groups = exp_size // 2
    rows_n, width = tokens.shape
    half = width // 2
    block = w_query.shape[0]
    depth = w_inner.shape[0]
    ff_block = w_outer.shape[0]
    core_peer = (rep_at ^ 1, exp_at)
    side_peer = (rep_at, exp_at ^ 1)

    def block_rows(at):
        return pl.ds(pl.multiple_of(at * block, block), block)

    own_loads = []
    for at, source in enumerate((w_query, w_key, w_value, w_output)):
        own_loads.append(
            pltpu.make_async_copy(source, weights.at[at, block_rows(exp_at)], own_s.at[at])
        )
    for load in own_loads:
        load.start()

    barrier = pltpu.get_barrier_semaphore()
    for mask in range(1, rep_size):
        for flip in range(2):
            pl.semaphore_signal(
                barrier, inc=1, device_id=(rep_at ^ mask, exp_at ^ flip), device_id_type=MESH
            )

    @pl.loop(1, exp_size)
    def _(at):
        pl.semaphore_signal(barrier, inc=1, device_id=(rep_at, exp_at ^ at), device_id_type=MESH)

    pl.semaphore_wait(barrier, exp_size - 1 + 2 * (rep_size - 1))

    outer_copy = remote(
        w_outer.at[: ff_block - DEFER],
        outer_w,
        weight_s.at[0],
        weight_r.at[0],
        (rep_at ^ 2, exp_at),
    )

    for load in own_loads:
        load.wait()

    picks = (slice(0, 3), slice(3, 4))
    own_half = pl.ds(pl.multiple_of(core * half, half), half)

    def view(kind, at):
        return weights.at[picks[kind], block_rows(at), own_half]

    def line_copy(kind, source, step):
        at = 2 * source + side
        return remote(
            view(kind, at),
            view(kind, at),
            line_s.at[kind, (1 + step) // 2, source],
            line_r.at[kind, source],
            (rep_at, exp_at + 2 * step),
        )

    def line_wait(kind, source):
        at = 2 * source + side
        remote(
            view(kind, at), view(kind, at), line_s.at[kind, 0, source], line_r.at[kind, source], side_peer
        ).wait_recv()

    def side_copy(kind, source):
        at = 2 * source + side
        return remote(
            view(kind, at), view(kind, at), side_s.at[kind, source], side_r.at[kind, source], side_peer
        )

    def side_wait(kind, source):
        at = 2 * source + 1 - side
        remote(
            view(kind, at), view(kind, at), side_s.at[kind, source], side_r.at[kind, source], side_peer
        ).wait_recv()

    def core_copy(kind, at):
        return remote(view(kind, at), view(kind, at), core_s.at[kind, at], core_r.at[kind, at], core_peer)

    def core_wait(kind, at):
        other = pl.ds(pl.multiple_of((1 - core) * half, half), half)
        there = weights.at[picks[kind], block_rows(at), other]
        remote(there, there, core_s.at[kind, at], core_r.at[kind, at], core_peer).wait_recv()

    def first_sends(kind):
        @pl.when(group + 1 < groups)
        def _():
            line_copy(kind, group, 1).start()

        @pl.when(group >= 1)
        def _():
            line_copy(kind, group, -1).start()

        side_copy(kind, group).start()

    def take_side(kind, source):
        side_wait(kind, source)
        core_copy(kind, 2 * source + 1 - side).start()

    def gather_step(kind, step):
        @pl.when(group - step >= 0)
        def _():
            source = group - step
            line_wait(kind, source)

            @pl.when(group + 1 < groups)
            def _():
                line_copy(kind, source, 1).start()

            side_copy(kind, source).start()
            core_copy(kind, 2 * source + side).start()

        @pl.when(group + step < groups)
        def _():
            source = group + step
            line_wait(kind, source)

            @pl.when(group >= 1)
            def _():
                line_copy(kind, source, -1).start()

            side_copy(kind, source).start()
            core_copy(kind, 2 * source + side).start()

        @pl.when(group - step + 1 >= 0)
        def _():
            take_side(kind, group - step + 1)

        @pl.when((step > 1) & (group + step - 1 < groups))
        def _():
            take_side(kind, group + step - 1)

    def gather_end(kind):
        last = groups - 1

        @pl.when(group - last >= 0)
        def _():
            take_side(kind, group - last)

        @pl.when((groups > 1) & (group + last < groups))
        def _():
            take_side(kind, group + last)

        @pl.loop(0, exp_size)
        def _(at):
            @pl.when(at != exp_at)
            def _():
                core_wait(kind, at)

    first_sends(0)
    first_sends(1)

    inner_rows = pl.ds(pl.multiple_of(rep_at * depth, depth), depth)

    def ff_cols(at):
        return pl.ds(pl.multiple_of(at * ff_block, ff_block), ff_block)

    def inner_copies(mask):
        dest = rep_at ^ mask
        found = []
        for part in range(2):
            source = w_inner.at[:, ff_cols(dest ^ (2 * part))]
            cols = slice(part * ff_block, (part + 1) * ff_block)
            at = 1 + 2 * mask + part
            if mask == 3:
                found.append(
                    remote(
                        source,
                        staging.at[:, cols],
                        weight_s.at[at],
                        weight_r.at[at],
                        (rep_at ^ 2, exp_at),
                    )
                )
            else:
                found.append(
                    remote(
                        source,
                        inner_w.at[inner_rows, cols],
                        weight_s.at[at],
                        weight_r.at[at],
                        (dest, exp_at),
                    )
                )
        return found

    far_rows = pl.ds(pl.multiple_of((rep_at ^ 2) * depth, depth), depth)
    forward_copy = remote(
        staging,
        inner_w.at[far_rows],
        weight_s.at[1 + 2 * rep_size],
        weight_r.at[1 + 2 * rep_size],
        core_peer,
    )

    for mask in (3, 2, 1):
        for copy in inner_copies(mask):
            copy.start()
    outer_copy.start()

    lanes = counts_v.shape[1]
    expert_row = expert_of[...]
    onehot = (
        lax.broadcasted_iota(jnp.int32, (lanes, rows_n), 0) == expert_row
    ).astype(wide)
    before = (
        lax.broadcasted_iota(jnp.int32, (rows_n, rows_n), 0)
        < lax.broadcasted_iota(jnp.int32, (rows_n, rows_n), 1)
    ).astype(low)
    earlier = jnp.dot(onehot.astype(low), before, preferred_element_type=wide)
    rank = jnp.sum(earlier * onehot, axis=0, keepdims=True).astype(jnp.int32)
    position = expert_row * slots + rank
    pick[...] = (
        lax.broadcasted_iota(jnp.int32, pick.shape, 0) == position
    ).astype(wide).astype(low)
    counts_v[:8, :] = lax.dot_general(
        jnp.ones((8, rows_n), low),
        onehot.astype(low),
        (((1,), (1,)), ((), ())),
        preferred_element_type=wide,
    )
    counts_v[8:, :block] = jnp.broadcast_to(gain_a[...].astype(wide), (8, block))
    cent_v[...] = jnp.broadcast_to(cent[...].astype(wide), cent_v.shape)
    gain_v[...] = jnp.broadcast_to(gain_e[...].astype(wide), gain_v.shape)

    def eight(at):
        return pl.ds(pl.multiple_of(at * 8, 8), 8)

    def sixteen(at):
        return pl.ds(pl.multiple_of(at * 16, 16), 16)

    def count_copy(dest):
        return remote(
            counts_v, small_all.at[sixteen(exp_at)], count_s.at[dest], count_r.at[exp_at], (rep_at, dest)
        )

    count_own = pltpu.make_async_copy(counts_v, small_all.at[sixteen(exp_at)], count_s.at[exp_at])
    count_own.start()

    @pl.loop(1, exp_size)
    def _(at):
        count_copy(exp_at ^ at).start()

    cent_at = side * rep_size + rep_at

    def cent_copy(mask, flip):
        return remote(
            cent_v,
            cents.at[eight(cent_at)],
            cent_s.at[flip * rep_size + mask],
            cent_r.at[flip * rep_size + mask],
            (rep_at ^ mask, exp_at ^ flip),
        )

    cent_own = pltpu.make_async_copy(cent_v, cents.at[eight(cent_at)], cent_s.at[0])
    cent_own.start()
    cent_pairs = [(m, f) for m in range(rep_size) for f in range(2) if m or f]
    for mask, flip in cent_pairs:
        cent_copy(mask, flip).start()

    def gain_copy(mask):
        return remote(
            gain_v, gains_e.at[eight(rep_at)], gain_s.at[mask], gain_r.at[mask], (rep_at ^ mask, exp_at)
        )

    gain_own = pltpu.make_async_copy(gain_v, gains_e.at[eight(rep_at)], gain_s.at[0])
    gain_own.start()
    for mask in range(1, rep_size):
        gain_copy(mask).start()

    count_own.wait()

    @pl.loop(1, exp_size)
    def _(at):
        source = exp_at ^ at
        remote(
            counts_v, small_all.at[sixteen(source)], count_s.at[source], count_r.at[source], (rep_at, source)
        ).wait()

    small_store = pltpu.make_async_copy(small_all, counts_all, out_s.at[1])
    small_store.start()

    tiled = jnp.dot(
        small_all[...].astype(low),
        (
            lax.broadcasted_iota(jnp.int32, (lanes, width), 1) % block
            == lax.broadcasted_iota(jnp.int32, (lanes, width), 0)
        ).astype(wide).astype(low),
        preferred_element_type=wide,
    )
    chosen_row = lax.broadcasted_iota(jnp.int32, (16 * exp_size, width), 0) == (
        16 * (lax.broadcasted_iota(jnp.int32, (16 * exp_size, width), 1) // block) + 8
    )
    gain_row[...] = jnp.sum(jnp.where(chosen_row, tiled, 0.0), axis=0, keepdims=True)

    @pl.loop(0, rows_n // ROWS)
    def _(step):
        here = pl.ds(pl.multiple_of(step * ROWS, ROWS), ROWS)
        unit, _ = row_stats(tokens[here, :].astype(wide))
        normed_a[here, :] = (unit * gain_row[...]).astype(low)

    down = lax.broadcasted_iota(jnp.int32, (rows_n, rows_n), 0)
    along = lax.broadcasted_iota(jnp.int32, (rows_n, rows_n), 1)
    end = jnp.int32(0)
    seg_down = jnp.zeros((rows_n, rows_n), jnp.int32)
    seg_along = jnp.zeros((rows_n, rows_n), jnp.int32)
    for at in range(doc.shape[1]):
        end = end + doc[0, at]
        seg_down = seg_down + (down >= end).astype(jnp.int32)
        seg_along = seg_along + (along >= end).astype(jnp.int32)
    bias[...] = jnp.where((seg_down == seg_along) & (down >= along), 0.0, -1e30)

    @pl.loop(1, groups)
    def _(step):
        gather_step(0, step)

    gather_end(0)

    def slot_rows(at):
        return pl.ds(pl.multiple_of(at * slots, slots), slots)

    def disp_copy(source, dest):
        return remote(
            source.at[slot_rows(dest // 2)],
            arrived.at[slot_rows(exp_at)],
            disp_s.at[dest],
            disp_r.at[exp_at],
            (rep_at, dest),
        )

    def dispatch(source, flip):
        @pl.loop(0, groups)
        def _(at):
            dest = 2 * (group ^ at) + flip

            @pl.when(dest != exp_at)
            def _():
                disp_copy(source, dest).start()

            @pl.when(dest == exp_at)
            def _():
                pltpu.make_async_copy(
                    source.at[slot_rows(group)], arrived.at[slot_rows(exp_at)], disp_s.at[exp_at]
                ).start()

    @pl.loop(1, 1 + (groups - 1 + 2) // 3)
    def _(step):
        gather_step(1, step)

    for at in range(3):

        @pl.loop(0, width // TILE)
        def _(step):
            cols = pl.ds(pl.multiple_of(step * TILE, TILE), TILE)
            qkv[at, :, cols] = jnp.dot(
                normed_a[...], weights[at, :, cols], preferred_element_type=wide
            ).astype(low)

    head_dim = width // HEADS
    pair = 2 * head_dim
    factor = head_dim ** (-0.5)
    lane = lax.broadcasted_iota(jnp.int32, (rows_n, pair), 1)
    pairs = HEADS // 2
    parts = 2
    begun = (groups - 1 + 2) // 3
    for part in range(parts):
        low_step = 1 + begun + part * (groups - 1 - begun) // parts
        high_step = 1 + begun + (part + 1) * (groups - 1 - begun) // parts

        @pl.loop(low_step, high_step)
        def _(step):
            gather_step(1, step)

        @pl.loop(part * pairs // parts, (part + 1) * pairs // parts)
        def _(at):
            cols = pl.ds(pl.multiple_of(at * pair, pair), pair)
            q_pair = qkv[0, :, cols]
            k_pair = qkv[1, :, cols]
            v_pair = qkv[2, :, cols]
            found = []
            for which in range(2):
                chosen = (lane >= head_dim) if which else (lane < head_dim)
                q_one = jnp.where(chosen, q_pair, jnp.zeros_like(q_pair))
                scores = (
                    lax.dot_general(
                        q_one, k_pair, (((1,), (1,)), ((), ())), preferred_element_type=wide
                    )
                    * factor
                    + bias[...]
                )
                top = jnp.max(scores, axis=1, keepdims=True)
                raised = jnp.exp(scores - top)
                total = jnp.sum(raised, axis=1, keepdims=True)
                prob = (raised * (1.0 / total)).astype(low)
                probs[pl.ds(pl.multiple_of((2 * at + which) * rows_n, rows_n), rows_n), :] = prob
                found.append(jnp.dot(prob, v_pair, preferred_element_type=wide))
            context[:, cols] = jnp.where(lane < head_dim, found[0], found[1]).astype(low)

    @pl.loop(0, width // TILE)
    def _(step):
        cols = pl.ds(pl.multiple_of(step * TILE, TILE), TILE)
        packed_c[:, cols] = jnp.dot(
            pick[...], cotangent[:, cols], preferred_element_type=wide
        ).astype(low)

    gather_end(1)
    stores = [
        pltpu.make_async_copy(source, target, out_s.at[at])
        for at, (source, target) in (
            (0, (weights, attn_w)),
            (2, (qkv, qkv_h)),
            (3, (probs, probs_h)),
            (4, (normed_a, normed_h)),
            (5, (context, context_h)),
            (7, (packed_c, packed_h)),
            (6, (hidden, hidden_h)),
        )
    ]
    for store in stores[:-1]:
        store.start()

    @pl.loop(0, width // TILE)
    def _(step):
        cols = pl.ds(pl.multiple_of(step * TILE, TILE), TILE)
        sum_here = tokens[:, cols].astype(wide) + jnp.dot(
            context[...], weights[3, :, cols], preferred_element_type=wide
        )
        hidden[:, cols] = sum_here
        packed_x[:, cols] = jnp.dot(
            pick[...], sum_here.astype(low), preferred_element_type=wide
        ).astype(low)

    dispatch(packed_x, 0)
    stores[-1].start()
    for copy in inner_copies(3):
        copy.wait_recv()
    forward_copy.start()

    for store in stores:
        store.wait()
    outer_copy.wait()
    forward_copy.wait()
    for mask in range(1, rep_size):
        for copy in inner_copies(mask):
            if mask == 3:
                copy.wait_send()
            else:
                copy.wait()
    for kind in range(2):
        side_copy(kind, group).wait_send()

        @pl.loop(0, groups)
        def _(source):
            @pl.when(source != group)
            def _():
                side_copy(kind, source).wait_send()

            @pl.when((source <= group) & (group + 1 < groups))
            def _():
                line_copy(kind, source, 1).wait_send()

            @pl.when((source >= group) & (group >= 1))
            def _():
                line_copy(kind, source, -1).wait_send()

        @pl.loop(0, exp_size)
        def _(at):
            @pl.when(at != exp_at)
            def _():
                core_copy(kind, at).wait_send()

    small_store.wait()
    cent_own.wait()
    gain_own.wait()
    for mask in range(1, rep_size):
        gain_copy(mask).wait()
    for mask, flip in cent_pairs:
        cent_copy(mask, flip).wait()

    def disp_wait(source):
        return remote(
            packed_x.at[slot_rows(source // 2)],
            arrived.at[slot_rows(source)],
            disp_s.at[source],
            disp_r.at[source],
            (rep_at, source),
        )

    @pl.loop(0, groups)
    def _(at):
        @pl.when(2 * at != exp_at)
        def _():
            disp_wait(2 * at).wait_send()

    @pl.when(side == 0)
    def _():
        pltpu.make_async_copy(
            packed_x.at[slot_rows(group)], arrived.at[slot_rows(exp_at)], disp_s.at[exp_at]
        ).wait()

        @pl.loop(1, exp_size)
        def _(at):
            disp_wait(exp_at ^ at).wait_recv()


def run_attend(exp_size, rep_size, slots, tokens, cotangent, doc, expert_of, attn, gain_a, w_inner, w_outer, gain_e, cent):
    rows_n, width = tokens.shape
    low = jnp.bfloat16
    wide = jnp.float32
    groups = exp_size // 2
    depth = w_inner.shape[0]
    ff_block = w_outer.shape[0]
    anyplace = pl.BlockSpec(memory_space=pl.ANY)
    inside = pl.BlockSpec(memory_space=pltpu.VMEM)
    dma = pltpu.SemaphoreType.DMA
    shape = jax.ShapeDtypeStruct
    return pl.pallas_call(
        functools.partial(attend_kernel, exp_size, rep_size, slots),
        out_shape=(
            shape((4, width, width), low),
            shape((width, 2 * ff_block), low),
            shape((ff_block - DEFER, width), low),
            shape((exp_size * slots, width), low),
            shape((exp_size * 16, 128), wide),
            shape((2 * rep_size * 8, cent.shape[1]), wide),
            shape((rep_size * 8, depth), wide),
            shape((groups * slots, width), low),
            shape((rows_n, width), wide),
            shape((3, rows_n, width), low),
            shape((HEADS * rows_n, rows_n), low),
            shape((rows_n, width), low),
            shape((rows_n, width), low),
            shape((groups * slots, rows_n), low),
            shape((1, width), wide),
        ),
        in_specs=[inside, inside, pl.BlockSpec(memory_space=pltpu.SMEM), inside]
        + [anyplace] * 4
        + [inside, anyplace, anyplace, inside, inside],
        out_specs=(anyplace,) * 13 + (inside,) * 2,
        scratch_shapes=[
            pltpu.VMEM((rows_n, width), wide),
            pltpu.VMEM((3, rows_n, width), low),
            pltpu.VMEM((HEADS * rows_n, rows_n), low),
            pltpu.VMEM((rows_n, width), low),
            pltpu.VMEM((rows_n, width), low),
            pltpu.VMEM((4, width, width), low),
            pltpu.VMEM((depth, 2 * ff_block), low),
            pltpu.VMEM((exp_size * 16, 128), wide),
            pltpu.VMEM((8, depth), wide),
            pltpu.VMEM((groups * slots, width), low),
            pltpu.VMEM((groups * slots, width), low),
            pltpu.VMEM((rows_n, rows_n), wide),
            pltpu.VMEM((16, 128), wide),
            pltpu.VMEM((8, cent.shape[1]), wide),
            dma((6,)),
            dma((2, 2, groups)),
            dma((2, groups)),
            dma((2, groups)),
            dma((2, groups)),
            dma((2, exp_size)),
            dma((2, exp_size)),
            dma((2 + 2 * rep_size,)),
            dma((2 + 2 * rep_size,)),
            dma((exp_size,)),
            dma((exp_size,)),
            dma((exp_size,)),
            dma((exp_size,)),
            dma((2 * rep_size,)),
            dma((2 * rep_size,)),
            dma((rep_size,)),
            dma((rep_size,)),
            dma((8,)),
        ],
        compiler_params=pltpu.CompilerParams(
            collective_id=1, has_side_effects=True, vmem_limit_bytes=56 << 20
        ),
        cost_estimate=pl.CostEstimate(
            flops=10 * rows_n * width * width,
            bytes_accessed=40 << 20,
            transcendentals=HEADS * rows_n * rows_n,
        ),
        name="attend",
    )(tokens, cotangent, doc, expert_of, *attn, gain_a, w_inner, w_outer, gain_e, cent)


def expert_kernel(
    exp_size,
    rep_size,
    slots,
    arrived_h,
    packed_h,
    inner_h,
    outer_h,
    w_inner,
    w_outer,
    counts_all,
    cents,
    gains_e,
    home,
    branch,
    branch_got,
    outer_keep,
    outer_send,
    outer_got,
    inner_sum,
    centre_parts,
    arrived,
    spread_m,
    offsets,
    cent_b,
    gain,
    centre_grad,
    centre_v,
    inner_w,
    outer_w,
    own_x,
    own_cot,
    normed,
    active,
    slope,
    states,
    part_send,
    part_recv,
    hop,
    back,
    spread,
    relay,
    acc,
    gates,
    gate_grads,
    outer_keep_v,
    outer_send_v,
    inner_send_v,
    load_sem,
    disp_s,
    disp_r,
    bran_s,
    bran_r,
    centre_s,
    centre_r,
    norm_s,
    norm_r,
    state_s,
    state_r,
    part_s,
    part_r,
    grad_s,
    grad_r,
    hop_s,
    hop_r,
    gate_s,
    gate_r,
    ret_s,
    ret_r,
    relay_s,
    relay_r,
    early_s,
    early_r,
    out_sem,
    inner_s,
    out_r,
):
    low = jnp.bfloat16
    wide = jnp.float32
    rep_at = lax.axis_index("rep")
    exp_at = lax.axis_index("exp")
    first = exp_at % 2 == 0
    second = exp_at % 2 == 1
    core_peer = (rep_at ^ 1, exp_at)
    side_peer = (rep_at, exp_at ^ 1)
    width = own_x.shape[1]
    own_rows = own_x.shape[0]
    part = own_rows // CHUNKS
    wide_ff = inner_w.shape[1]
    block = wide_ff // 2
    depth = width // rep_size

    def slot_rows(at):
        return pl.ds(pl.multiple_of(at * slots, slots), slots)

    def inner_rows(mask):
        return pl.ds(pl.multiple_of((rep_at ^ mask) * depth, depth), depth)

    rows_load = pltpu.make_async_copy(arrived_h, arrived, load_sem.at[0])

    @pl.when(first)
    def _():
        rows_load.start()

    loads = [
        pltpu.make_async_copy(w_outer, outer_w.at[:block], load_sem.at[1]),
        pltpu.make_async_copy(outer_h, outer_w.at[block : 2 * block - DEFER], load_sem.at[2]),
    ]
    for side in range(2):
        at = rep_at ^ (2 * side)
        loads.append(
            pltpu.make_async_copy(
                w_inner.at[:, pl.ds(pl.multiple_of(at * block, block), block)],
                inner_w.at[inner_rows(0), side * block : (side + 1) * block],
                load_sem.at[3 + side],
            )
        )
    for mask in range(1, rep_size):
        loads.append(
            pltpu.make_async_copy(
                inner_h.at[inner_rows(mask)], inner_w.at[inner_rows(mask)], load_sem.at[4 + mask]
            )
        )
    for load in loads:
        load.start()

    barrier = pltpu.get_barrier_semaphore()
    for mask in range(1, rep_size):
        for flip in range(2):
            pl.semaphore_signal(
                barrier, inc=1, device_id=(rep_at ^ mask, exp_at ^ flip), device_id_type=MESH
            )

    @pl.loop(1, exp_size)
    def _(at):
        pl.semaphore_signal(barrier, inc=1, device_id=(rep_at, exp_at ^ at), device_id_type=MESH)

    counted = counts_all.shape[0]
    group = exp_at // 2
    lane = lax.broadcasted_iota(jnp.int32, (counted, 128), 1)
    mine = jnp.sum(
        jnp.where(lane == group, counts_all[...], 0.0), axis=1, keepdims=True
    )
    mine = jnp.broadcast_to(mine, (counted, 128))
    down = lax.broadcasted_iota(jnp.int32, (counted, counted), 0)
    along = lax.broadcasted_iota(jnp.int32, (counted, counted), 1)
    ahead = ((along // 16 < down // 16) & (along % 16 == 0)).astype(wide).astype(low)
    offsets[0] = jnp.dot(ahead, mine.astype(low), preferred_element_type=wide)
    offsets[1] = mine
    slot_iota = lax.broadcasted_iota(jnp.int32, (slots, own_rows), 0)
    row_iota = lax.broadcasted_iota(jnp.int32, (slots, own_rows), 1)

    @pl.loop(0, exp_size)
    def _(at):
        eight = pl.ds(pl.multiple_of(at * 16, 16), 8)
        start = offsets[0, eight, :][:1, :1].astype(jnp.int32)
        limit = offsets[1, eight, :][:1, :1].astype(jnp.int32)
        spread_m[slot_rows(at), :] = (
            ((slot_iota + start) == row_iota) & (slot_iota < limit)
        ).astype(wide).astype(low)

    piece = cents.shape[1]
    for at in range(width // piece):
        cent_b[:, at * piece : (at + 1) * piece] = jnp.broadcast_to(
            cents[at * 8 : at * 8 + 1, :], (cent_b.shape[0], piece)
        ).astype(low)
    for at in range(rep_size):
        gain[:, at * depth : (at + 1) * depth] = gains_e[at * 8 : at * 8 + 1, :]
    def compact_rows():
        return lax.dot_general(
            spread_m[...], arrived[...], (((0,), (0,)), ((), ())), preferred_element_type=wide
        ).astype(low)

    @pl.when(first)
    def _():
        rows_load.wait()
        own_x[...] = compact_rows()

    pl.semaphore_wait(barrier, exp_size - 1 + 2 * (rep_size - 1))

    def disp_copy(which):
        return remote(
            packed_h.at[slot_rows(which)],
            arrived.at[slot_rows(exp_at)],
            disp_s.at[which],
            disp_r.at[exp_at],
            (rep_at, 2 * which + 1),
        )

    disp_own = pltpu.make_async_copy(
        packed_h.at[slot_rows(group)], arrived.at[slot_rows(exp_at)], disp_s.at[group]
    )

    @pl.loop(0, exp_size // 2)
    def _(step):
        which = group ^ (exp_size // 2 - 1 - step)

        @pl.when(2 * which + 1 != exp_at)
        def _():
            disp_copy(which).start()

        @pl.when(2 * which + 1 == exp_at)
        def _():
            disp_own.start()

    row_peer = (rep_at ^ 2, exp_at)
    late_copy = remote(
        w_outer.at[block - DEFER :],
        outer_w.at[2 * block - DEFER :],
        early_s.at[0],
        early_r.at[0],
        row_peer,
    )
    late_copy.start()

    gate_copy = remote(gates, gates, gate_s.at[0], gate_r.at[0], side_peer)

    def part_rows(at):
        return pl.ds(pl.multiple_of(at * part, part), part)

    def both_rows(at):
        return pl.ds(pl.multiple_of(at * 2 * part, 2 * part), 2 * part)

    def own_slice(at):
        return pl.ds(pl.multiple_of(at * 2 * part + part, part), part)

    def other_slice(at):
        return pl.ds(pl.multiple_of(at * 2 * part, part), part)

    def grad_copy(at):
        rows = part_rows(at)
        return remote(
            gate_grads.at[rows], gate_grads.at[rows], grad_s.at[at], grad_r.at[at], side_peer
        )

    def hop_forward(at):
        rows = part_rows(at)
        return remote(hop.at[rows], own_x.at[rows], hop_s.at[at], hop_r.at[at], side_peer)

    def hop_backward(at):
        return remote(
            hop.at[part_rows(at)], states.at[own_slice(at)], hop_s.at[at], hop_r.at[at], side_peer
        )

    def norm_copy(at):
        return remote(
            normed.at[own_slice(at)], normed.at[other_slice(at)], norm_s.at[at], norm_r.at[at], core_peer
        )

    def state_copy(at):
        return remote(
            states.at[own_slice(at)], states.at[other_slice(at)], state_s.at[at], state_r.at[at], core_peer
        )

    def part_copy(kind, at):
        count = kind * CHUNKS + at
        rows = part_rows(count)
        return remote(
            part_send.at[rows], part_recv.at[rows], part_s.at[count], part_r.at[count], core_peer
        )

    def norm_rows(at):
        @pl.loop(0, part // ROWS)
        def _(step):
            off = pl.multiple_of(step * ROWS, ROWS)
            unit, _ = row_stats(own_x[pl.ds(at * part + off, ROWS), :].astype(wide))
            normed[pl.ds(at * 2 * part + part + off, ROWS), :] = (unit * gain[...]).astype(low)

        norm_copy(at).start()

    steps = 2 * CHUNKS

    def is_forward(step):
        early = step < CHUNKS
        mixed = (step == 0) | ((step % 2 == 1) & (step < steps - 1))
        return (first & early) | (second & mixed)

    def chunk_at(step):
        of_first = jnp.where(step < CHUNKS, step, step - CHUNKS)
        mixed = (step == 0) | ((step % 2 == 1) & (step < steps - 1))
        of_second = jnp.where(
            mixed,
            (step + 1) // 2,
            jnp.where(step == steps - 1, CHUNKS - 1, (step - 2) // 2),
        )
        return jnp.where(first, of_first, of_second)

    @pl.when(first)
    def _():
        logit = lax.dot_general(
            own_x[...], cent_b[...], (((1,), (1,)), ((), ())), preferred_element_type=wide
        )
        gates[...] = jax.nn.sigmoid(logit)
        gate_copy.start()

        @pl.loop(0, CHUNKS)
        def _(at):
            norm_rows(at)

    @pl.when(second)
    def _():
        hop_forward(0).wait_recv()
        norm_rows(0)

    def take_cotangent():
        disp_own.wait()

        @pl.loop(1, exp_size)
        def _(at):
            source = exp_at ^ at
            remote(
                packed_h.at[slot_rows(0)],
                arrived.at[slot_rows(source)],
                disp_s.at[0],
                disp_r.at[source],
                side_peer,
            ).wait_recv()

        own_cot[...] = compact_rows()
        gate_copy.wait_recv()

        @pl.loop(0, CHUNKS)
        def _(at):
            @pl.loop(0, part // ROWS)
            def _(step):
                off = pl.multiple_of(step * ROWS, ROWS)
                here = pl.ds(at * part + off, ROWS)
                states[pl.ds(at * 2 * part + part + off, ROWS), :] = (
                    gates[here, :][:, :1] * own_cot[here, :].astype(wide)
                ).astype(low)

            state_copy(at).start()

    for load in loads:
        load.wait()
    centre_grad[...] = jnp.zeros_like(centre_grad)

    def finish_forward(step, at):
        part_copy(0, at).wait_recv()

        @pl.loop(0, part // ROWS)
        def _(tile):
            off = pl.multiple_of(tile * ROWS, ROWS)
            here = pl.ds(at * part + off, ROWS)
            result = (
                own_x[here, :].astype(wide)
                + acc[step % 2, pl.ds(off, ROWS), :]
                + part_recv[here, :].astype(wide)
            )

            @pl.when(first)
            def _():
                hop[here, :] = result.astype(low)

            @pl.when(second)
            def _():
                cot = own_cot[here, :].astype(wide)
                back[here, :] = (gates[here, :][:, :1] * result).astype(low)
                gate_grads[here, :] = jnp.broadcast_to(
                    jnp.sum(cot * result, axis=1, keepdims=True), (ROWS, gate_grads.shape[1])
                )

        @pl.when(first)
        def _():
            hop_forward(at).start()

        @pl.when(second)
        def _():
            grad_copy(at).start()

    def finish_backward(step, at):
        part_copy(1, at).wait_recv()

        @pl.when(first)
        def _():
            grad_copy(at).wait_recv()

        @pl.loop(0, part // ROWS)
        def _(tile):
            off = pl.multiple_of(tile * ROWS, ROWS)
            here = pl.ds(at * part + off, ROWS)
            rows_in = own_x[here, :].astype(wide)
            unit, inv_scale = row_stats(rows_in)
            grad_unit = (
                acc[step % 2, pl.ds(off, ROWS), :]
                + part_recv[pl.ds((CHUNKS + at) * part + off, ROWS), :].astype(wide)
            ) * gain[...]
            grad_in = (
                grad_unit
                - jnp.mean(grad_unit, axis=-1, keepdims=True)
                - unit * jnp.mean(grad_unit * unit, axis=-1, keepdims=True)
            ) * inv_scale
            gate = gates[here, :][:, :1]

            @pl.when(second)
            def _():
                state = gate * own_cot[here, :].astype(wide) + grad_in
                hop[here, :] = state.astype(low)

            @pl.when(first)
            def _():
                state = states[pl.ds(at * 2 * part + part + off, ROWS), :].astype(wide) + grad_in
                grad_logit = gate_grads[here, :][:, :1] * gate * (1.0 - gate)
                back[here, :] = (state + grad_logit * cent_b[:1, :].astype(wide)).astype(low)
                centre_grad[...] += jnp.sum(grad_logit * rows_in, axis=0, keepdims=True)

        @pl.when(second)
        def _():
            hop_backward(at).start()

    def finish(step):
        at = chunk_at(step)
        forward = is_forward(step)

        @pl.when(forward)
        def _():
            finish_forward(step, at)

        @pl.when(jnp.logical_not(forward))
        def _():
            finish_backward(step, at)

    @pl.loop(0, steps)
    def _(step):
        at = chunk_at(step)
        forward = is_forward(step)
        rows = both_rows(at)

        @pl.when(forward)
        def _():
            norm_copy(at).wait_recv()

            @pl.loop(0, wide_ff // BIG)
            def _(tile):
                cols = pl.ds(pl.multiple_of(tile * BIG, BIG), BIG)
                inner = jnp.dot(normed[rows, :], inner_w[:, cols], preferred_element_type=wide)
                normal = 0.5 * (1.0 + lax.erf(inner * ROOT_HALF))
                active[rows, cols] = (inner * normal).astype(low)
                slope[rows, cols] = (
                    normal + inner * jnp.exp(-0.5 * inner * inner) * INV_ROOT_TAU
                ).astype(low)

        @pl.when(jnp.logical_not(forward))
        def _():
            state_copy(at).wait_recv()

            @pl.loop(0, wide_ff // BIG)
            def _(tile):
                cols = pl.ds(pl.multiple_of(tile * BIG, BIG), BIG)
                grad_active = lax.dot_general(
                    states[rows, :],
                    outer_w[cols, :],
                    (((1,), (1,)), ((), ())),
                    preferred_element_type=wide,
                )
                slope[rows, cols] = (grad_active * slope[rows, cols].astype(wide)).astype(low)

        @pl.when((step > 0) & jnp.logical_not(first & (step == CHUNKS)))
        def _():
            finish(step - 1)

        @pl.when(step == 0)
        def _():
            late_copy.wait_recv()

        @pl.when(forward)
        def _():
            both = jnp.dot(active[rows, :], outer_w[...], preferred_element_type=wide)
            part_send[part_rows(at), :] = both[:part].astype(low)
            acc[step % 2] = both[part:]
            part_copy(0, at).start()

        @pl.when(jnp.logical_not(forward))
        def _():
            both = lax.dot_general(
                slope[rows, :],
                inner_w[...],
                (((1,), (1,)), ((), ())),
                preferred_element_type=wide,
            )
            part_send[part_rows(CHUNKS + at), :] = both[:part].astype(low)
            acc[step % 2] = both[part:]
            part_copy(1, at).start()

        @pl.when(first & (step == CHUNKS - 1))
        def _():
            finish(step)

        @pl.when(second & (step == 0))
        def _():
            take_cotangent()

        after = step + 1
        after_at = chunk_at(after)

        @pl.when(first & (after >= CHUNKS) & (after < steps))
        def _():
            hop_backward(after_at).wait_recv()
            state_copy(after_at).start()

        @pl.when(second & is_forward(after) & (after < steps))
        def _():
            hop_forward(after_at).wait_recv()
            norm_rows(after_at)

    finish(steps - 1)

    groups = exp_size // 2

    def ret_copy(source, dest):
        return remote(
            source,
            home.at[slot_rows(group)],
            ret_s.at[dest],
            ret_r.at[group],
            (rep_at, dest),
        )

    def relay_copy(which):
        return remote(
            spread.at[slot_rows(2 * which + 1)],
            relay.at[slot_rows(which)],
            relay_s.at[which],
            relay_r.at[which],
            side_peer,
        )

    ret_own = pltpu.make_async_copy(
        spread.at[slot_rows(exp_at)], home.at[slot_rows(group)], ret_s.at[exp_at]
    )

    def make_spread():
        @pl.loop(0, width // TILE)
        def _(step):
            cols = pl.ds(pl.multiple_of(step * TILE, TILE), TILE)
            spread[:, cols] = jnp.dot(
                spread_m[...], back[:, cols], preferred_element_type=wide
            ).astype(low)

    def send_back():
        @pl.loop(1, groups)
        def _(step):
            relay_copy(group ^ (groups - step)).start()

        @pl.loop(1, groups)
        def _(step):
            dest = 2 * (group ^ (groups - step))
            ret_copy(spread.at[slot_rows(dest)], dest).start()

        ret_copy(spread.at[slot_rows(exp_at + 1)], exp_at + 1).start()
        ret_own.start()

    def eight_rows(at):
        return pl.ds(pl.multiple_of(at * 8, 8), 8)

    def centre_copy(mask, flip):
        dest = rep_at ^ mask
        return remote(
            centre_v.at[eight_rows(flip * rep_size + dest)],
            centre_parts.at[eight_rows(rep_at)],
            centre_s.at[flip * rep_size + mask],
            centre_r.at[mask],
            (dest, exp_at ^ flip),
        )

    centre_own = pltpu.make_async_copy(
        centre_v.at[eight_rows(rep_at)], centre_parts.at[eight_rows(rep_at)], centre_s.at[0]
    )
    centre_pairs = [(m, f) for m in range(rep_size) for f in range(2) if m or f]

    make_spread()

    def bran_copy(which):
        return remote(
            spread.at[slot_rows(2 * which + 1)],
            branch_got.at[slot_rows(group)],
            bran_s.at[which],
            bran_r.at[group],
            (rep_at, 2 * which + 1),
        )

    bran_own = pltpu.make_async_copy(
        spread.at[slot_rows(exp_at)], branch_got.at[slot_rows(group)], bran_s.at[group]
    )

    @pl.when(second)
    def _():
        bran_own.start()

        @pl.loop(1, groups)
        def _(step):
            bran_copy(group ^ (groups - step)).start()

    @pl.when(first)
    def _():
        send_back()
        for at in range(width // piece):
            centre_v[at * 8 : (at + 1) * 8, :] = jnp.broadcast_to(
                centre_grad[:, at * piece : (at + 1) * piece], (8, piece)
            )
        centre_own.start()
        for mask, flip in centre_pairs:
            centre_copy(mask, flip).start()

    outs = []
    tiles = block // TILE
    early_copy = remote(
        outer_send_v.at[:EARLY], outer_got, early_s.at[1], early_r.at[1], row_peer
    )
    for at in list(range(tiles, 2 * tiles)) + list(range(tiles)):
        rows = slice(at * TILE, (at + 1) * TILE)
        grad = lax.dot_general(
            active[:, rows], states[...], (((0,), (0,)), ((), ())), preferred_element_type=wide
        )
        if at < tiles:
            outer_keep_v[rows, :] = grad
            outs.append((outer_keep_v.at[rows], outer_keep.at[rows]))
        else:
            top = at * TILE - block
            outer_send_v[top : top + TILE, :] = grad.astype(low)
            if top + TILE == EARLY:
                early_copy.start()
            if top < EARLY:
                continue
            outs.append(
                (outer_send_v.at[top : top + TILE], outer_send.at[top - EARLY : top - EARLY + TILE])
            )
        pltpu.make_async_copy(outs[-1][0], outs[-1][1], out_sem.at[len(outs) - 1]).start()
    outs.append((spread, branch))
    pltpu.make_async_copy(spread, branch, out_sem.at[len(outs) - 1]).start()

    def inner_copy(mask, side):
        at = rep_at ^ (2 * side)
        cols = pl.ds(pl.multiple_of(at * block, block), block)
        target = inner_sum.at[mask // 2, :, cols]
        source = inner_send_v.at[mask, side]
        count = 2 * mask + side
        if mask % 2 == 0:
            return pltpu.make_async_copy(source, target, inner_s.at[count])
        return remote(source, target, inner_s.at[count], out_r.at[count], core_peer)

    inner_order = [(m, f) for m in (3, 1, 2, 0) for f in range(2)]
    for mask, side in inner_order:
        cols = slice(side * block, (side + 1) * block)
        grad = lax.dot_general(
            normed[:, inner_rows(mask)],
            slope[:, cols],
            (((0,), (0,)), ((), ())),
            preferred_element_type=wide,
        )
        inner_send_v[mask, side] = grad.astype(low)
        inner_copy(mask, side).start()

    @pl.when(second)
    def _():
        @pl.loop(1, groups)
        def _(step):
            which = group ^ (groups - step)
            relay_copy(which).wait_recv()
            ret_copy(relay.at[slot_rows(which)], 2 * which + 1).start()

    late_copy.wait_send()
    early_copy.wait()
    for at, (source, target) in enumerate(outs):
        pltpu.make_async_copy(source, target, out_sem.at[at]).wait()
    for mask, side in inner_order:
        inner_copy(mask, side).wait()
    for at in range(CHUNKS):
        norm_copy(at).wait_send()
        state_copy(at).wait_send()
        part_copy(0, at).wait_send()
        part_copy(1, at).wait_send()

        @pl.when(first)
        def _():
            hop_forward(at).wait_send()

        @pl.when(second)
        def _():
            hop_backward(at).wait_send()
            grad_copy(at).wait_send()

    @pl.loop(0, groups)
    def _(which):
        @pl.when(2 * which + 1 != exp_at)
        def _():
            disp_copy(which).wait_send()

    @pl.when(second)
    def _():
        bran_own.wait()

        @pl.loop(1, groups)
        def _(step):
            which = group ^ step
            bran_copy(which).wait_send()
            remote(
                spread.at[slot_rows(which)],
                branch_got.at[slot_rows(which)],
                bran_s.at[which],
                bran_r.at[which],
                side_peer,
            ).wait_recv()

    @pl.when(first)
    def _():
        gate_copy.wait_send()

    @pl.when(first)
    def _():
        centre_own.wait()
        for mask, flip in centre_pairs:
            centre_copy(mask, flip).wait_send()
        for mask in range(1, rep_size):
            centre_copy(mask, 0).wait_recv()

    @pl.when(second)
    def _():
        for mask in range(rep_size):
            centre_copy(mask, 1).wait_recv()

    @pl.when(first)
    def _():
        ret_own.wait()
        ret_copy(spread.at[slot_rows(exp_at + 1)], exp_at + 1).wait_send()

        @pl.loop(1, groups)
        def _(step):
            which = group ^ step
            relay_copy(which).wait_send()
            ret_copy(spread.at[slot_rows(2 * which)], 2 * which).wait_send()

    @pl.when(second)
    def _():
        @pl.loop(1, groups)
        def _(step):
            which = group ^ step
            ret_copy(relay.at[slot_rows(which)], 2 * which + 1).wait_send()

        remote(
            relay.at[slot_rows(group)],
            home.at[slot_rows(group)],
            relay_s.at[group],
            ret_r.at[group],
            side_peer,
        ).wait_recv()

    @pl.loop(1, groups)
    def _(step):
        source = group ^ step
        remote(
            relay.at[slot_rows(source)],
            home.at[slot_rows(source)],
            relay_s.at[source],
            ret_r.at[source],
            side_peer,
        ).wait_recv()


def run_experts(
    exp_size, rep_size, slots, own_rows, arrived, packed, inner_w, outer_w, w_inner, w_outer, counts_all, cents, gains_e
):
    width = arrived.shape[1]
    depth = width // rep_size
    block = w_outer.shape[0]
    low = jnp.bfloat16
    wide = jnp.float32
    total = exp_size * slots
    all_rows = 2 * own_rows
    part = own_rows // CHUNKS
    piece = cents.shape[1]
    anyplace = pl.BlockSpec(memory_space=pl.ANY)
    inside = pl.BlockSpec(memory_space=pltpu.VMEM)
    dma = pltpu.SemaphoreType.DMA
    n_out = (2 * block - EARLY) // TILE + 1
    scratch = [
        pltpu.VMEM((total, width), low),
        pltpu.VMEM((total, own_rows), low),
        pltpu.VMEM((2, exp_size * 16, 128), wide),
        pltpu.VMEM((128, width), low),
        pltpu.VMEM((1, width), wide),
        pltpu.VMEM((1, width), wide),
        pltpu.VMEM((2 * rep_size * 8, piece), wide),
        pltpu.VMEM((width, 2 * block), low),
        pltpu.VMEM((2 * block, width), low),
        pltpu.VMEM((own_rows, width), low),
        pltpu.VMEM((own_rows, width), low),
        pltpu.VMEM((all_rows, width), low),
        pltpu.VMEM((all_rows, 2 * block), low),
        pltpu.VMEM((all_rows, 2 * block), low),
        pltpu.VMEM((all_rows, width), low),
        pltpu.VMEM((2 * own_rows, width), low),
        pltpu.VMEM((2 * own_rows, width), low),
        pltpu.VMEM((own_rows, width), low),
        pltpu.VMEM((own_rows, width), low),
        pltpu.VMEM((total, width), low),
        pltpu.VMEM((total // 2, width), low),
        pltpu.VMEM((2, part, width), wide),
        pltpu.VMEM((own_rows, 128), wide),
        pltpu.VMEM((own_rows, 128), wide),
        pltpu.VMEM((block, width), wide),
        pltpu.VMEM((block, width), low),
        pltpu.VMEM((rep_size, 2, depth, block), low),
        dma((8,)),
        dma((exp_size // 2,)),
        dma((exp_size,)),
        dma((exp_size // 2,)),
        dma((exp_size // 2,)),
        dma((2 * rep_size,)),
        dma((rep_size,)),
    ]
    scratch += [dma((CHUNKS,)) for _ in range(4)]
    scratch += [dma((2 * CHUNKS,)), dma((2 * CHUNKS,))]
    scratch += [dma((CHUNKS,)) for _ in range(4)]
    scratch += [dma((1,)), dma((1,)), dma((exp_size,)), dma((exp_size // 2,))]
    scratch += [dma((exp_size // 2,)), dma((exp_size // 2,)), dma((2,)), dma((2,)), dma((n_out,))]
    scratch += [dma((2 * rep_size,)), dma((2 * rep_size,))]
    flops = 2 * all_rows * width * 2 * block * 6
    return pl.pallas_call(
        functools.partial(expert_kernel, exp_size, rep_size, slots),
        out_shape=(
            jax.ShapeDtypeStruct((total // 2, width), low),
            jax.ShapeDtypeStruct((total, width), low),
            jax.ShapeDtypeStruct((total // 2, width), low),
            jax.ShapeDtypeStruct((block, width), wide),
            jax.ShapeDtypeStruct((block - EARLY, width), low),
            jax.ShapeDtypeStruct((EARLY, width), low),
            jax.ShapeDtypeStruct((2, depth, rep_size * block), low),
            jax.ShapeDtypeStruct((rep_size * 8, piece), wide),
        ),
        in_specs=[anyplace] * 6 + [inside] * 3,
        out_specs=(anyplace,) * 8,
        scratch_shapes=scratch,
        compiler_params=pltpu.CompilerParams(
            collective_id=0, has_side_effects=True, vmem_limit_bytes=62 << 20
        ),
        cost_estimate=pl.CostEstimate(
            flops=flops, bytes_accessed=40 << 20, transcendentals=2 * all_rows * 2 * block
        ),
        name="experts",
    )(arrived, packed, inner_w, outer_w, w_inner, w_outer, counts_all, cents, gains_e)


def finish_kernel(
    exp_size,
    rep_size,
    home,
    branch,
    branch_got,
    pick,
    hidden_h,
    cotangent,
    tokens_h,
    gain_row,
    qkv_h,
    probs_h,
    normed_h,
    context_h,
    attn_w,
    outer_send,
    inner_sum,
    output,
    grad_tokens,
    shares,
    outer_recv,
    inner_recv,
    hidden,
    tokens,
    qkv,
    probs,
    normed_a,
    context,
    normed_t,
    context_t,
    branch_in,
    weights,
    grad_hidden,
    grad_attn,
    grad_context,
    grads3,
    keep,
    core_out,
    core_in,
    side_out,
    side_in,
    line_out,
    line_in,
    total,
    row_out,
    row_in,
    half_out,
    half_in,
    load_s,
    branch_s,
    branch_r,
    expert_s,
    expert_r,
    core_s,
    core_r,
    side_s,
    side_r,
    line_s,
    line_r,
    row_s,
    row_r,
    half_s,
    half_r,
):
    low = jnp.bfloat16
    wide = jnp.float32
    rep_at = lax.axis_index("rep")
    exp_at = lax.axis_index("exp")
    core = rep_at % 2
    group = exp_at // 2
    side = exp_at % 2
    groups = exp_size // 2
    rows_n, width = cotangent.shape
    half = width // 2
    block = width // exp_size
    core_peer = (rep_at ^ 1, exp_at)
    side_peer = (rep_at, exp_at ^ 1)
    row_peer = (rep_at ^ 2, exp_at)

    loads = [
        pltpu.make_async_copy(source, target, load_s.at[at])
        for at, (source, target) in enumerate(
            (
                (context_h, context),
                (attn_w, weights),
                (qkv_h, qkv),
                (probs_h, probs),
                (normed_h, normed_a),
                (tokens_h, tokens),
                (hidden_h, hidden),
            )
        )
    ]
    for load in loads:
        load.start()

    barrier = pltpu.get_barrier_semaphore()
    for mask in range(1, 3):
        pl.semaphore_signal(
            barrier, inc=1, device_id=(rep_at ^ mask, exp_at), device_id_type=MESH
        )

    @pl.loop(1, exp_size)
    def _(at):
        pl.semaphore_signal(barrier, inc=1, device_id=(rep_at, exp_at ^ at), device_id_type=MESH)

    pl.semaphore_wait(barrier, exp_size + 1)

    outer_copy = remote(outer_send, outer_recv, expert_s.at[0], expert_r.at[0], row_peer)

    inner_copy = remote(inner_sum.at[1], inner_recv, expert_s.at[1], expert_r.at[1], row_peer)
    inner_copy.start()
    outer_copy.start()

    slots = pick.shape[0] // groups

    def slot_rows(at):
        return pl.ds(pl.multiple_of(at * slots, slots), slots)

    def branch_copy(dest):
        return remote(
            branch.at[slot_rows(dest)],
            branch_in.at[slot_rows(group)],
            branch_s.at[dest],
            branch_r.at[group],
            (rep_at, dest),
        )

    branch_own = pltpu.make_async_copy(branch_got, branch_in, branch_s.at[exp_at])

    @pl.when(side == 1)
    def _():
        branch_own.start()

        @pl.loop(0, groups)
        def _(at):
            branch_copy(2 * (group ^ (groups - 1 - at))).start()

    back_rows = lax.dot_general(
        pick[...], home[...], (((0,), (0,)), ((), ())), preferred_element_type=wide
    )
    grad_hidden[...] = cotangent[...].astype(wide) + back_rows
    grad_attn[...] = grad_hidden[...].astype(low)
    loads[0].wait()
    context_t[...] = context[...].T

    own_half = pl.ds(pl.multiple_of(core * half, half), half)
    other_half = pl.ds(pl.multiple_of((1 - core) * half, half), half)

    def core_copy(at):
        return remote(core_out.at[at], core_in.at[at], core_s.at[at], core_r.at[at], core_peer)

    def product(at, left, right, cols, target, kind):
        @pl.loop(0, width // 512)
        def _(step):
            rows = pl.ds(pl.multiple_of(step * 512, 512), 512)
            target[at, rows, :] = jnp.dot(
                left[rows, :], right[:, cols], preferred_element_type=wide
            ).astype(kind)

    def share_start(at, left, right):
        product(at, left, right, other_half, core_out, low)
        core_copy(at).start()
        product(at, left, right, own_half, keep, wide)

    def block_rows(at):
        return pl.ds(pl.multiple_of(at * block, block), block)

    def side_copy(at):
        return remote(side_out.at[at], side_in.at[at], side_s.at[at], side_r.at[at], side_peer)

    def share_side(at):
        core_copy(at).wait_recv()

        @pl.loop(0, groups)
        def _(which):
            rows = block_rows(2 * which + 1 - side)
            side_out[at, block_rows(which), :] = (
                keep[at, rows, :] + core_in[at, rows, :].astype(wide)
            ).astype(low)

        side_copy(at).start()

        @pl.loop(0, groups)
        def _(which):
            rows = block_rows(2 * which + side)
            keep[at, rows, :] = keep[at, rows, :] + core_in[at, rows, :].astype(wide)

    def line_copy(at, mask):
        dest = group ^ mask
        return remote(
            line_out.at[at, block_rows(dest)],
            line_in.at[at, block_rows(group)],
            line_s.at[at, mask],
            line_r.at[at, mask],
            (rep_at, 2 * dest + side),
        )

    def share_line(at):
        side_copy(at).wait_recv()

        @pl.loop(1, groups)
        def _(mask):
            dest = group ^ mask
            line_out[at, block_rows(dest), :] = (
                keep[at, block_rows(2 * dest + side), :] + side_in[at, block_rows(dest), :].astype(wide)
            ).astype(low)
            line_copy(at, mask).start()

        total[at] = keep[at, block_rows(exp_at), :] + side_in[at, block_rows(group), :].astype(wide)

    def row_copy(at):
        return remote(row_out.at[at], row_in.at[at], row_s.at[at], row_r.at[at], row_peer)

    def share_row(at):
        @pl.loop(1, groups)
        def _(mask):
            line_copy(at, mask).wait_recv()
            total[at] = total[at] + line_in[at, block_rows(group ^ mask), :].astype(wide)

        row_out[at] = total[at].astype(low)
        row_copy(at).start()

    def half_copy(at):
        return remote(half_out.at[at], half_in.at[at], half_s.at[at], half_r.at[at], core_peer)

    def share_half(at):
        row_copy(at).wait_recv()
        summed = row_out[at].astype(wide) + row_in[at].astype(wide)
        half_out[at] = summed
        half_copy(at).start()
        shares[at, :, own_half] = summed

    def share_end(at):
        half_copy(at).wait_recv()
        shares[at, :, other_half] = half_in[at]

    share_start(3, context_t, grad_attn)
    loads[1].wait()

    @pl.loop(0, width // TILE)
    def _(step):
        rows = pl.ds(pl.multiple_of(step * TILE, TILE), TILE)
        grad_context[:, rows] = lax.dot_general(
            grad_attn[...], weights[3, rows, :], (((1,), (1,)), ((), ())), preferred_element_type=wide
        ).astype(low)

    share_side(3)

    head_dim = width // HEADS
    pair = 2 * head_dim
    factor = head_dim ** (-0.5)
    lane = lax.broadcasted_iota(jnp.int32, (rows_n, pair), 1)

    def heads(start, stop):
        @pl.loop(start, stop)
        def _(at):
            cols = pl.ds(pl.multiple_of(at * pair, pair), pair)
            q_pair = qkv[0, :, cols]
            k_pair = qkv[1, :, cols]
            v_pair = qkv[2, :, cols]
            c_pair = grad_context[:, cols]
            found = []
            for which in range(2):
                chosen = (lane >= head_dim) if which else (lane < head_dim)
                c_one = jnp.where(chosen, c_pair, jnp.zeros_like(c_pair))
                prob = probs[pl.ds(pl.multiple_of((2 * at + which) * rows_n, rows_n), rows_n), :]
                grad_prob = lax.dot_general(
                    c_one, v_pair, (((1,), (1,)), ((), ())), preferred_element_type=wide
                )
                weighted = prob.astype(wide) * grad_prob
                row_sum = jnp.sum(weighted, axis=1, keepdims=True)
                grad_score = (weighted - prob.astype(wide) * row_sum).astype(low)
                found.append(
                    (
                        jnp.dot(grad_score, k_pair, preferred_element_type=wide) * factor,
                        lax.dot_general(
                            grad_score,
                            q_pair,
                            (((0,), (0,)), ((), ())),
                            preferred_element_type=wide,
                        )
                        * factor,
                        lax.dot_general(
                            prob, c_pair, (((0,), (0,)), ((), ())), preferred_element_type=wide
                        ),
                    )
                )
            for which in range(3):
                grads3[which, :, cols] = jnp.where(
                    lane < head_dim, found[0][which], found[1][which]
                ).astype(low)

    loads[2].wait()
    loads[3].wait()
    heads(0, HEADS // 4)
    share_line(3)
    heads(HEADS // 4, HEADS // 2)
    loads[4].wait()
    normed_t[...] = normed_a[...].T
    for at in range(3):
        share_start(at, normed_t, grads3.at[at])
    for at in range(3):
        share_side(at)

    loads[5].wait()
    @pl.loop(0, width // TILE)
    def _(step):
        rows = pl.ds(pl.multiple_of(step * TILE, TILE), TILE)
        grad_normed = jnp.zeros((rows_n, TILE), wide)
        for at in range(3):
            grad_normed = grad_normed + lax.dot_general(
                grads3[at], weights[at, rows, :], (((1,), (1,)), ((), ())), preferred_element_type=wide
            )
        grad_tokens[:, rows] = grad_normed

    @pl.loop(0, rows_n // ROWS)
    def _(step):
        here = pl.ds(pl.multiple_of(step * ROWS, ROWS), ROWS)
        unit, inv_scale = row_stats(tokens[here, :].astype(wide))
        grad_unit = grad_tokens[here, :] * gain_row[...]
        grad_in = (
            grad_unit
            - jnp.mean(grad_unit, axis=-1, keepdims=True)
            - unit * jnp.mean(grad_unit * unit, axis=-1, keepdims=True)
        ) * inv_scale
        grad_tokens[here, :] = grad_hidden[here, :] + grad_in

    share_row(3)
    for at in range(3):
        share_line(at)

    for at in range(3):
        share_row(at)
    def branch_wait(which):
        remote(
            branch.at[slot_rows(which)],
            branch_in.at[slot_rows(which)],
            branch_s.at[which],
            branch_r.at[which],
            side_peer,
        ).wait_recv()

    @pl.when(side == 0)
    def _():
        @pl.loop(0, groups)
        def _(at):
            branch_wait(at)

    @pl.when(side == 1)
    def _():
        branch_own.wait()

    loads[6].wait()
    rows = lax.dot_general(
        pick[...], branch_in[...], (((0,), (0,)), ((), ())), preferred_element_type=wide
    )
    output[...] = (hidden[...] + rows).astype(low)

    for at in (3, 0, 1, 2):
        share_half(at)
    for at in (3, 0, 1, 2):
        share_end(at)

    @pl.when(side == 1)
    def _():
        @pl.loop(0, groups)
        def _(at):
            branch_copy(2 * at).wait_send()

    for at in range(4):
        core_copy(at).wait_send()
        side_copy(at).wait_send()
        row_copy(at).wait_send()
        half_copy(at).wait_send()

        @pl.loop(1, groups)
        def _(mask):
            line_copy(at, mask).wait_send()

    inner_copy.wait()
    outer_copy.wait()


def run_finish(exp_size, rep_size, home, branch, branch_got, pick, hidden, cotangent, tokens, gain_row, qkv, probs, normed_a, context, attn_w, outer_send, inner_sum):
    rows_n, width = tokens.shape
    low = jnp.bfloat16
    wide = jnp.float32
    half = width // 2
    groups = exp_size // 2
    block = width // exp_size
    anyplace = pl.BlockSpec(memory_space=pl.ANY)
    inside = pl.BlockSpec(memory_space=pltpu.VMEM)
    dma = pltpu.SemaphoreType.DMA
    shape = jax.ShapeDtypeStruct
    return pl.pallas_call(
        functools.partial(finish_kernel, exp_size, rep_size),
        out_shape=(
            shape((rows_n, width), low),
            shape((rows_n, width), wide),
            shape((4, block, width), wide),
            shape(outer_send.shape, low),
            shape(inner_sum.shape[1:], low),
        ),
        in_specs=[inside, anyplace, anyplace, inside, anyplace, inside, anyplace, inside]
        + [anyplace] * 7,
        out_specs=(inside,) * 3 + (anyplace,) * 2,
        scratch_shapes=[
            pltpu.VMEM((rows_n, width), wide),
            pltpu.VMEM((rows_n, width), low),
            pltpu.VMEM(qkv.shape, low),
            pltpu.VMEM(probs.shape, low),
            pltpu.VMEM((rows_n, width), low),
            pltpu.VMEM((rows_n, width), low),
            pltpu.VMEM((width, rows_n), low),
            pltpu.VMEM((width, rows_n), low),
            pltpu.VMEM(pick.shape[:1] + (width,), low),
            pltpu.VMEM((4, width, width), low),
            pltpu.VMEM((rows_n, width), wide),
            pltpu.VMEM((rows_n, width), low),
            pltpu.VMEM((rows_n, width), low),
            pltpu.VMEM((3, rows_n, width), low),
            pltpu.VMEM((4, width, half), wide),
            pltpu.VMEM((4, width, half), low),
            pltpu.VMEM((4, width, half), low),
            pltpu.VMEM((4, width // 2, half), low),
            pltpu.VMEM((4, width // 2, half), low),
            pltpu.VMEM((4, width // 2, half), low),
            pltpu.VMEM((4, width // 2, half), low),
            pltpu.VMEM((4, block, half), wide),
            pltpu.VMEM((4, block, half), low),
            pltpu.VMEM((4, block, half), low),
            pltpu.VMEM((4, block, half), wide),
            pltpu.VMEM((4, block, half), wide),
            dma((7,)),
            dma((exp_size,)),
            dma((groups,)),
            dma((2,)),
            dma((2,)),
            dma((4,)),
            dma((4,)),
            dma((4,)),
            dma((4,)),
            dma((4, groups)),
            dma((4, groups)),
            dma((4,)),
            dma((4,)),
            dma((4,)),
            dma((4,)),
        ],
        compiler_params=pltpu.CompilerParams(
            collective_id=2, has_side_effects=True, vmem_limit_bytes=60 << 20
        ),
        cost_estimate=pl.CostEstimate(
            flops=20 * rows_n * width * width, bytes_accessed=60 << 20, transcendentals=0
        ),
        name="finish",
    )(
        home,
        branch,
        branch_got,
        pick,
        hidden,
        cotangent,
        tokens,
        gain_row,
        qkv,
        probs,
        normed_a,
        context,
        attn_w,
        outer_send,
        inner_sum,
    )


def shards(
    tokens,
    cotangent,
    doc_lengths,
    expert_of_token,
    w_query,
    w_key,
    w_value,
    w_output,
    attn_gain,
    w_inner,
    w_outer,
    expert_gain,
    centroids,
):
    exp_size = lax.axis_size("exp")
    rep_size = lax.axis_size("rep")
    row_count = tokens.shape[0]
    wide = jnp.float32

    slots = -(-3 * row_count // exp_size // 16) * 16
    (
        attn_w,
        inner_w,
        outer_w,
        arrived,
        counts_all,
        cents,
        gains_e,
        packed,
        hidden,
        qkv,
        probs,
        normed_a,
        context,
        pick,
        gain_row,
    ) = run_attend(
        exp_size,
        rep_size,
        slots,
        tokens,
        cotangent,
        doc_lengths,
        expert_of_token[None],
        (w_query, w_key, w_value, w_output),
        attn_gain[None],
        w_inner[0],
        w_outer[0],
        expert_gain,
        centroids,
    )
    home, branch, branch_got, outer_keep, outer_send, outer_got, inner_sum, centre_parts = run_experts(
        exp_size,
        rep_size,
        slots,
        2 * row_count,
        arrived,
        packed,
        inner_w,
        outer_w,
        w_inner[0],
        w_outer[0],
        counts_all,
        cents,
        gains_e,
    )
    output, grad_tokens, shares, outer_recv, inner_recv = run_finish(
        exp_size,
        rep_size,
        home,
        branch,
        branch_got,
        pick,
        hidden,
        cotangent,
        tokens,
        gain_row,
        qkv,
        probs,
        normed_a,
        context,
        attn_w,
        outer_send,
        inner_sum,
    )
    grad_centroids = jnp.sum(centre_parts.reshape(rep_size, 8, -1)[:, 0], axis=0)[None]
    grad_w_outer = (
        outer_keep + jnp.concatenate([outer_got, outer_recv], axis=0).astype(wide)
    )[None]
    summed = inner_sum[0].astype(wide) + inner_recv.astype(wide)
    grad_w_inner = summed[None]
    grad_expert_gain = jnp.sum(summed * w_inner[0].astype(wide), axis=1)[None] / expert_gain.astype(
        wide
    )
    share_gain = sum(
        jnp.sum(shares[i] * w.astype(wide), axis=1) for i, w in enumerate((w_query, w_key, w_value))
    ) / attn_gain.astype(wide)
    return (
        output,
        grad_tokens,
        shares[0],
        shares[1],
        shares[2],
        shares[3],
        share_gain,
        grad_w_inner,
        grad_w_outer,
        grad_expert_gain,
        grad_centroids,
    )


def solution(mesh):
    placed = (
        P(("rep", "exp"), None),
        P(("rep", "exp"), None),
        P(("rep", "exp"), None),
        P(("rep", "exp")),
        P("exp", None),
        P("exp", None),
        P("exp", None),
        P("exp", None),
        P("exp"),
        P("exp", "rep", None),
        P("exp", "rep", None),
        P("exp", "rep"),
        P("exp", "rep"),
    )
    return jax.shard_map(
        shards,
        mesh=mesh,
        in_specs=placed,
        out_specs=(
            P(("rep", "exp"), None),
            P(("rep", "exp"), None),
            P("exp", None),
            P("exp", None),
            P("exp", None),
            P("exp", None),
            P("exp"),
            P("exp", "rep", None),
            P("exp", "rep", None),
            P("exp", "rep"),
            P("exp", "rep"),
        ),
        check_vma=False,
    )
```

```python
import functools

import jax
import jax.numpy as jnp
from jax import lax
from jax.experimental import pallas as pl
from jax.experimental.pallas import tpu as pltpu
from jax.sharding import PartitionSpec as P

HEADS = 16
EPS = 1e-05
ROOT_HALF = 0.7071067811865476
INV_ROOT_TAU = 0.3989422804014327
CHUNKS = 4
DEFER = 256
EARLY = 512


MESH = pl.DeviceIdType.MESH
TILE = 256
ROWS = 128
BIG = 2048


def remote(src, dst, send_sem, recv_sem, device):
    return pltpu.make_async_remote_copy(
        src_ref=src,
        dst_ref=dst,
        send_sem=send_sem,
        recv_sem=recv_sem,
        device_id=device,
        device_id_type=MESH,
    )


def row_stats(rows):
    row_mean = jnp.mean(rows, axis=-1, keepdims=True)
    centered = rows - row_mean
    variance = jnp.mean(centered * centered, axis=-1, keepdims=True)
    inv_scale = lax.rsqrt(variance + EPS)
    return centered * inv_scale, inv_scale


def attend_kernel(
    exp_size,
    rep_size,
    slots,
    tokens,
    cotangent,
    doc,
    expert_of,
    w_query,
    w_key,
    w_value,
    w_output,
    gain_a,
    w_inner,
    w_outer,
    gain_e,
    cent,
    attn_w,
    inner_w,
    outer_w,
    arrived,
    counts_all,
    cents,
    gains_e,
    packed_h,
    hidden_h,
    qkv_h,
    probs_h,
    normed_h,
    context_h,
    pick,
    gain_row,
    hidden,
    qkv,
    probs,
    normed_a,
    context,
    weights,
    staging,
    small_all,
    gain_v,
    packed_x,
    packed_c,
    bias,
    counts_v,
    cent_v,
    own_s,
    line_s,
    line_r,
    side_s,
    side_r,
    core_s,
    core_r,
    weight_s,
    weight_r,
    disp_s,
    disp_r,
    count_s,
    count_r,
    cent_s,
    cent_r,
    gain_s,
    gain_r,
    out_s,
):
    low = jnp.bfloat16
    wide = jnp.float32
    rep_at = lax.axis_index("rep")
    exp_at = lax.axis_index("exp")
    core = rep_at % 2
    group = exp_at // 2
    side = exp_at % 2
    groups = exp_size // 2
    rows_n, width = tokens.shape
    half = width // 2
    block = w_query.shape[0]
    depth = w_inner.shape[0]
    ff_block = w_outer.shape[0]
    core_peer = (rep_at ^ 1, exp_at)
    side_peer = (rep_at, exp_at ^ 1)

    def block_rows(at):
        return pl.ds(pl.multiple_of(at * block, block), block)

    own_loads = []
    for at, source in enumerate((w_query, w_key, w_value, w_output)):
        own_loads.append(
            pltpu.make_async_copy(source, weights.at[at, block_rows(exp_at)], own_s.at[at])
        )
    for load in own_loads:
        load.start()

    barrier = pltpu.get_barrier_semaphore()
    for mask in range(1, rep_size):
        for flip in range(2):
            pl.semaphore_signal(
                barrier, inc=1, device_id=(rep_at ^ mask, exp_at ^ flip), device_id_type=MESH
            )

    @pl.loop(1, exp_size)
    def _(at):
        pl.semaphore_signal(barrier, inc=1, device_id=(rep_at, exp_at ^ at), device_id_type=MESH)

    pl.semaphore_wait(barrier, exp_size - 1 + 2 * (rep_size - 1))

    outer_copy = remote(
        w_outer.at[: ff_block - DEFER],
        outer_w,
        weight_s.at[0],
        weight_r.at[0],
        (rep_at ^ 2, exp_at),
    )

    for load in own_loads:
        load.wait()

    picks = (slice(0, 3), slice(3, 4))
    own_half = pl.ds(pl.multiple_of(core * half, half), half)

    def view(kind, at):
        return weights.at[picks[kind], block_rows(at), own_half]

    def line_copy(kind, source, step):
        at = 2 * source + side
        return remote(
            view(kind, at),
            view(kind, at),
            line_s.at[kind, (1 + step) // 2, source],
            line_r.at[kind, source],
            (rep_at, exp_at + 2 * step),
        )

    def line_wait(kind, source):
        at = 2 * source + side
        remote(
            view(kind, at), view(kind, at), line_s.at[kind, 0, source], line_r.at[kind, source], side_peer
        ).wait_recv()

    def side_copy(kind, source):
        at = 2 * source + side
        return remote(
            view(kind, at), view(kind, at), side_s.at[kind, source], side_r.at[kind, source], side_peer
        )

    def side_wait(kind, source):
        at = 2 * source + 1 - side
        remote(
            view(kind, at), view(kind, at), side_s.at[kind, source], side_r.at[kind, source], side_peer
        ).wait_recv()

    def core_copy(kind, at):
        return remote(view(kind, at), view(kind, at), core_s.at[kind, at], core_r.at[kind, at], core_peer)

    def core_wait(kind, at):
        other = pl.ds(pl.multiple_of((1 - core) * half, half), half)
        there = weights.at[picks[kind], block_rows(at), other]
        remote(there, there, core_s.at[kind, at], core_r.at[kind, at], core_peer).wait_recv()

    def first_sends(kind):
        @pl.when(group + 1 < groups)
        def _():
            line_copy(kind, group, 1).start()

        @pl.when(group >= 1)
        def _():
            line_copy(kind, group, -1).start()

        side_copy(kind, group).start()

    def take_side(kind, source):
        side_wait(kind, source)
        core_copy(kind, 2 * source + 1 - side).start()

    def gather_step(kind, step):
        @pl.when(group - step >= 0)
        def _():
            source = group - step
            line_wait(kind, source)

            @pl.when(group + 1 < groups)
            def _():
                line_copy(kind, source, 1).start()

            side_copy(kind, source).start()
            core_copy(kind, 2 * source + side).start()

        @pl.when(group + step < groups)
        def _():
            source = group + step
            line_wait(kind, source)

            @pl.when(group >= 1)
            def _():
                line_copy(kind, source, -1).start()

            side_copy(kind, source).start()
            core_copy(kind, 2 * source + side).start()

        @pl.when(group - step + 1 >= 0)
        def _():
            take_side(kind, group - step + 1)

        @pl.when((step > 1) & (group + step - 1 < groups))
        def _():
            take_side(kind, group + step - 1)

    def gather_end(kind):
        last = groups - 1

        @pl.when(group - last >= 0)
        def _():
            take_side(kind, group - last)

        @pl.when((groups > 1) & (group + last < groups))
        def _():
            take_side(kind, group + last)

        @pl.loop(0, exp_size)
        def _(at):
            @pl.when(at != exp_at)
            def _():
                core_wait(kind, at)

    first_sends(0)
    first_sends(1)

    inner_rows = pl.ds(pl.multiple_of(rep_at * depth, depth), depth)

    def ff_cols(at):
        return pl.ds(pl.multiple_of(at * ff_block, ff_block), ff_block)

    def inner_copies(mask):
        dest = rep_at ^ mask
        found = []
        for part in range(2):
            source = w_inner.at[:, ff_cols(dest ^ (2 * part))]
            cols = slice(part * ff_block, (part + 1) * ff_block)
            at = 1 + 2 * mask + part
            if mask == 3:
                found.append(
                    remote(
                        source,
                        staging.at[:, cols],
                        weight_s.at[at],
                        weight_r.at[at],
                        (rep_at ^ 2, exp_at),
                    )
                )
            else:
                found.append(
                    remote(
                        source,
                        inner_w.at[inner_rows, cols],
                        weight_s.at[at],
                        weight_r.at[at],
                        (dest, exp_at),
                    )
                )
        return found

    far_rows = pl.ds(pl.multiple_of((rep_at ^ 2) * depth, depth), depth)
    forward_copy = remote(
        staging,
        inner_w.at[far_rows],
        weight_s.at[1 + 2 * rep_size],
        weight_r.at[1 + 2 * rep_size],
        core_peer,
    )

    for mask in (3, 2, 1):
        for copy in inner_copies(mask):
            copy.start()
    outer_copy.start()

    lanes = counts_v.shape[1]
    expert_row = expert_of[...]
    onehot = (
        lax.broadcasted_iota(jnp.int32, (lanes, rows_n), 0) == expert_row
    ).astype(wide)
    before = (
        lax.broadcasted_iota(jnp.int32, (rows_n, rows_n), 0)
        < lax.broadcasted_iota(jnp.int32, (rows_n, rows_n), 1)
    ).astype(low)
    earlier = jnp.dot(onehot.astype(low), before, preferred_element_type=wide)
    rank = jnp.sum(earlier * onehot, axis=0, keepdims=True).astype(jnp.int32)
    position = expert_row * slots + rank
    pick[...] = (
        lax.broadcasted_iota(jnp.int32, pick.shape, 0) == position
    ).astype(wide).astype(low)
    counts_v[:8, :] = lax.dot_general(
        jnp.ones((8, rows_n), low),
        onehot.astype(low),
        (((1,), (1,)), ((), ())),
        preferred_element_type=wide,
    )
    counts_v[8:, :block] = jnp.broadcast_to(gain_a[...].astype(wide), (8, block))
    cent_v[...] = jnp.broadcast_to(cent[...].astype(wide), cent_v.shape)
    gain_v[...] = jnp.broadcast_to(gain_e[...].astype(wide), gain_v.shape)

    def eight(at):
        return pl.ds(pl.multiple_of(at * 8, 8), 8)

    def sixteen(at):
        return pl.ds(pl.multiple_of(at * 16, 16), 16)

    def count_copy(dest):
        return remote(
            counts_v, small_all.at[sixteen(exp_at)], count_s.at[dest], count_r.at[exp_at], (rep_at, dest)
        )

    count_own = pltpu.make_async_copy(counts_v, small_all.at[sixteen(exp_at)], count_s.at[exp_at])
    count_own.start()

    @pl.loop(1, exp_size)
    def _(at):
        count_copy(exp_at ^ at).start()

    cent_at = side * rep_size + rep_at

    def cent_copy(mask, flip):
        return remote(
            cent_v,
            cents.at[eight(cent_at)],
            cent_s.at[flip * rep_size + mask],
            cent_r.at[flip * rep_size + mask],
            (rep_at ^ mask, exp_at ^ flip),
        )

    cent_own = pltpu.make_async_copy(cent_v, cents.at[eight(cent_at)], cent_s.at[0])
    cent_own.start()
    cent_pairs = [(m, f) for m in range(rep_size) for f in range(2) if m or f]
    for mask, flip in cent_pairs:
        cent_copy(mask, flip).start()

    def gain_copy(mask):
        return remote(
            gain_v, gains_e.at[eight(rep_at)], gain_s.at[mask], gain_r.at[mask], (rep_at ^ mask, exp_at)
        )

    gain_own = pltpu.make_async_copy(gain_v, gains_e.at[eight(rep_at)], gain_s.at[0])
    gain_own.start()
    for mask in range(1, rep_size):
        gain_copy(mask).start()

    count_own.wait()

    @pl.loop(1, exp_size)
    def _(at):
        source = exp_at ^ at
        remote(
            counts_v, small_all.at[sixteen(source)], count_s.at[source], count_r.at[source], (rep_at, source)
        ).wait()

    small_store = pltpu.make_async_copy(small_all, counts_all, out_s.at[1])
    small_store.start()

    tiled = jnp.dot(
        small_all[...].astype(low),
        (
            lax.broadcasted_iota(jnp.int32, (lanes, width), 1) % block
            == lax.broadcasted_iota(jnp.int32, (lanes, width), 0)
        ).astype(wide).astype(low),
        preferred_element_type=wide,
    )
    chosen_row = lax.broadcasted_iota(jnp.int32, (16 * exp_size, width), 0) == (
        16 * (lax.broadcasted_iota(jnp.int32, (16 * exp_size, width), 1) // block) + 8
    )
    gain_row[...] = jnp.sum(jnp.where(chosen_row, tiled, 0.0), axis=0, keepdims=True)

    @pl.loop(0, rows_n // ROWS)
    def _(step):
        here = pl.ds(pl.multiple_of(step * ROWS, ROWS), ROWS)
        unit, _ = row_stats(tokens[here, :].astype(wide))
        normed_a[here, :] = (unit * gain_row[...]).astype(low)

    down = lax.broadcasted_iota(jnp.int32, (rows_n, rows_n), 0)
    along = lax.broadcasted_iota(jnp.int32, (rows_n, rows_n), 1)
    end = jnp.int32(0)
    seg_down = jnp.zeros((rows_n, rows_n), jnp.int32)
    seg_along = jnp.zeros((rows_n, rows_n), jnp.int32)
    for at in range(doc.shape[1]):
        end = end + doc[0, at]
        seg_down = seg_down + (down >= end).astype(jnp.int32)
        seg_along = seg_along + (along >= end).astype(jnp.int32)
    bias[...] = jnp.where((seg_down == seg_along) & (down >= along), 0.0, -1e30)

    @pl.loop(1, groups)
    def _(step):
        gather_step(0, step)

    gather_end(0)

    def slot_rows(at):
        return pl.ds(pl.multiple_of(at * slots, slots), slots)

    def disp_copy(source, dest):
        return remote(
            source.at[slot_rows(dest // 2)],
            arrived.at[slot_rows(exp_at)],
            disp_s.at[dest],
            disp_r.at[exp_at],
            (rep_at, dest),
        )

    def dispatch(source, flip):
        @pl.loop(0, groups)
        def _(at):
            dest = 2 * (group ^ at) + flip

            @pl.when(dest != exp_at)
            def _():
                disp_copy(source, dest).start()

            @pl.when(dest == exp_at)
            def _():
                pltpu.make_async_copy(
                    source.at[slot_rows(group)], arrived.at[slot_rows(exp_at)], disp_s.at[exp_at]
                ).start()

    @pl.loop(1, 1 + (groups - 1 + 2) // 3)
    def _(step):
        gather_step(1, step)

    for at in range(3):

        @pl.loop(0, width // TILE)
        def _(step):
            cols = pl.ds(pl.multiple_of(step * TILE, TILE), TILE)
            qkv[at, :, cols] = jnp.dot(
                normed_a[...], weights[at, :, cols], preferred_element_type=wide
            ).astype(low)

    head_dim = width // HEADS
    pair = 2 * head_dim
    factor = head_dim ** (-0.5)
    lane = lax.broadcasted_iota(jnp.int32, (rows_n, pair), 1)
    pairs = HEADS // 2
    parts = 2
    begun = (groups - 1 + 2) // 3
    for part in range(parts):
        low_step = 1 + begun + part * (groups - 1 - begun) // parts
        high_step = 1 + begun + (part + 1) * (groups - 1 - begun) // parts

        @pl.loop(low_step, high_step)
        def _(step):
            gather_step(1, step)

        @pl.loop(part * pairs // parts, (part + 1) * pairs // parts)
        def _(at):
            cols = pl.ds(pl.multiple_of(at * pair, pair), pair)
            q_pair = qkv[0, :, cols]
            k_pair = qkv[1, :, cols]
            v_pair = qkv[2, :, cols]
            found = []
            for which in range(2):
                chosen = (lane >= head_dim) if which else (lane < head_dim)
                q_one = jnp.where(chosen, q_pair, jnp.zeros_like(q_pair))
                scores = (
                    lax.dot_general(
                        q_one, k_pair, (((1,), (1,)), ((), ())), preferred_element_type=wide
                    )
                    * factor
                    + bias[...]
                )
                top = jnp.max(scores, axis=1, keepdims=True)
                raised = jnp.exp(scores - top)
                total = jnp.sum(raised, axis=1, keepdims=True)
                prob = (raised * (1.0 / total)).astype(low)
                probs[pl.ds(pl.multiple_of((2 * at + which) * rows_n, rows_n), rows_n), :] = prob
                found.append(jnp.dot(prob, v_pair, preferred_element_type=wide))
            context[:, cols] = jnp.where(lane < head_dim, found[0], found[1]).astype(low)

    @pl.loop(0, width // TILE)
    def _(step):
        cols = pl.ds(pl.multiple_of(step * TILE, TILE), TILE)
        packed_c[:, cols] = jnp.dot(
            pick[...], cotangent[:, cols], preferred_element_type=wide
        ).astype(low)

    gather_end(1)
    stores = [
        pltpu.make_async_copy(source, target, out_s.at[at])
        for at, (source, target) in (
            (0, (weights, attn_w)),
            (2, (qkv, qkv_h)),
            (3, (probs, probs_h)),
            (4, (normed_a, normed_h)),
            (5, (context, context_h)),
            (7, (packed_c, packed_h)),
            (6, (hidden, hidden_h)),
        )
    ]
    for store in stores[:-1]:
        store.start()

    @pl.loop(0, width // TILE)
    def _(step):
        cols = pl.ds(pl.multiple_of(step * TILE, TILE), TILE)
        sum_here = tokens[:, cols].astype(wide) + jnp.dot(
            context[...], weights[3, :, cols], preferred_element_type=wide
        )
        hidden[:, cols] = sum_here
        packed_x[:, cols] = jnp.dot(
            pick[...], sum_here.astype(low), preferred_element_type=wide
        ).astype(low)

    dispatch(packed_x, 0)
    stores[-1].start()
    for copy in inner_copies(3):
        copy.wait_recv()
    forward_copy.start()

    for store in stores:
        store.wait()
    outer_copy.wait()
    forward_copy.wait()
    for mask in range(1, rep_size):
        for copy in inner_copies(mask):
            if mask == 3:
                copy.wait_send()
            else:
                copy.wait()
    for kind in range(2):
        side_copy(kind, group).wait_send()

        @pl.loop(0, groups)
        def _(source):
            @pl.when(source != group)
            def _():
                side_copy(kind, source).wait_send()

            @pl.when((source <= group) & (group + 1 < groups))
            def _():
                line_copy(kind, source, 1).wait_send()

            @pl.when((source >= group) & (group >= 1))
            def _():
                line_copy(kind, source, -1).wait_send()

        @pl.loop(0, exp_size)
        def _(at):
            @pl.when(at != exp_at)
            def _():
                core_copy(kind, at).wait_send()

    small_store.wait()
    cent_own.wait()
    gain_own.wait()
    for mask in range(1, rep_size):
        gain_copy(mask).wait()
    for mask, flip in cent_pairs:
        cent_copy(mask, flip).wait()

    def disp_wait(source):
        return remote(
            packed_x.at[slot_rows(source // 2)],
            arrived.at[slot_rows(source)],
            disp_s.at[source],
            disp_r.at[source],
            (rep_at, source),
        )

    @pl.loop(0, groups)
    def _(at):
        @pl.when(2 * at != exp_at)
        def _():
            disp_wait(2 * at).wait_send()

    @pl.when(side == 0)
    def _():
        pltpu.make_async_copy(
            packed_x.at[slot_rows(group)], arrived.at[slot_rows(exp_at)], disp_s.at[exp_at]
        ).wait()

        @pl.loop(1, exp_size)
        def _(at):
            disp_wait(exp_at ^ at).wait_recv()


def run_attend(exp_size, rep_size, slots, tokens, cotangent, doc, expert_of, attn, gain_a, w_inner, w_outer, gain_e, cent):
    rows_n, width = tokens.shape
    low = jnp.bfloat16
    wide = jnp.float32
    groups = exp_size // 2
    depth = w_inner.shape[0]
    ff_block = w_outer.shape[0]
    anyplace = pl.BlockSpec(memory_space=pl.ANY)
    inside = pl.BlockSpec(memory_space=pltpu.VMEM)
    dma = pltpu.SemaphoreType.DMA
    shape = jax.ShapeDtypeStruct
    return pl.pallas_call(
        functools.partial(attend_kernel, exp_size, rep_size, slots),
        out_shape=(
            shape((4, width, width), low),
            shape((width, 2 * ff_block), low),
            shape((ff_block - DEFER, width), low),
            shape((exp_size * slots, width), low),
            shape((exp_size * 16, 128), wide),
            shape((2 * rep_size * 8, cent.shape[1]), wide),
            shape((rep_size * 8, depth), wide),
            shape((groups * slots, width), low),
            shape((rows_n, width), wide),
            shape((3, rows_n, width), low),
            shape((HEADS * rows_n, rows_n), low),
            shape((rows_n, width), low),
            shape((rows_n, width), low),
            shape((groups * slots, rows_n), low),
            shape((1, width), wide),
        ),
        in_specs=[inside, inside, pl.BlockSpec(memory_space=pltpu.SMEM), inside]
        + [anyplace] * 4
        + [inside, anyplace, anyplace, inside, inside],
        out_specs=(anyplace,) * 13 + (inside,) * 2,
        scratch_shapes=[
            pltpu.VMEM((rows_n, width), wide),
            pltpu.VMEM((3, rows_n, width), low),
            pltpu.VMEM((HEADS * rows_n, rows_n), low),
            pltpu.VMEM((rows_n, width), low),
            pltpu.VMEM((rows_n, width), low),
            pltpu.VMEM((4, width, width), low),
            pltpu.VMEM((depth, 2 * ff_block), low),
            pltpu.VMEM((exp_size * 16, 128), wide),
            pltpu.VMEM((8, depth), wide),
            pltpu.VMEM((groups * slots, width), low),
            pltpu.VMEM((groups * slots, width), low),
            pltpu.VMEM((rows_n, rows_n), wide),
            pltpu.VMEM((16, 128), wide),
            pltpu.VMEM((8, cent.shape[1]), wide),
            dma((6,)),
            dma((2, 2, groups)),
            dma((2, groups)),
            dma((2, groups)),
            dma((2, groups)),
            dma((2, exp_size)),
            dma((2, exp_size)),
            dma((2 + 2 * rep_size,)),
            dma((2 + 2 * rep_size,)),
            dma((exp_size,)),
            dma((exp_size,)),
            dma((exp_size,)),
            dma((exp_size,)),
            dma((2 * rep_size,)),
            dma((2 * rep_size,)),
            dma((rep_size,)),
            dma((rep_size,)),
            dma((8,)),
        ],
        compiler_params=pltpu.CompilerParams(
            collective_id=1, has_side_effects=True, vmem_limit_bytes=56 << 20
        ),
        cost_estimate=pl.CostEstimate(
            flops=10 * rows_n * width * width,
            bytes_accessed=40 << 20,
            transcendentals=HEADS * rows_n * rows_n,
        ),
        name="attend",
    )(tokens, cotangent, doc, expert_of, *attn, gain_a, w_inner, w_outer, gain_e, cent)


def expert_kernel(
    exp_size,
    rep_size,
    slots,
    arrived_h,
    packed_h,
    inner_h,
    outer_h,
    w_inner,
    w_outer,
    counts_all,
    cents,
    gains_e,
    home,
    branch,
    branch_got,
    outer_keep,
    outer_send,
    outer_got,
    inner_sum,
    centre_parts,
    arrived,
    spread_m,
    offsets,
    cent_b,
    gain,
    centre_grad,
    centre_v,
    inner_w,
    outer_w,
    own_x,
    own_cot,
    normed,
    active,
    slope,
    states,
    part_send,
    part_recv,
    hop,
    back,
    spread,
    relay,
    acc,
    gates,
    gate_grads,
    outer_keep_v,
    outer_send_v,
    inner_send_v,
    load_sem,
    disp_s,
    disp_r,
    bran_s,
    bran_r,
    centre_s,
    centre_r,
    norm_s,
    norm_r,
    state_s,
    state_r,
    part_s,
    part_r,
    grad_s,
    grad_r,
    hop_s,
    hop_r,
    gate_s,
    gate_r,
    ret_s,
    ret_r,
    relay_s,
    relay_r,
    early_s,
    early_r,
    out_sem,
    inner_s,
    out_r,
):
    low = jnp.bfloat16
    wide = jnp.float32
    rep_at = lax.axis_index("rep")
    exp_at = lax.axis_index("exp")
    first = exp_at % 2 == 0
    second = exp_at % 2 == 1
    core_peer = (rep_at ^ 1, exp_at)
    side_peer = (rep_at, exp_at ^ 1)
    width = own_x.shape[1]
    own_rows = own_x.shape[0]
    part = own_rows // CHUNKS
    wide_ff = inner_w.shape[1]
    block = wide_ff // 2
    depth = width // rep_size

    def slot_rows(at):
        return pl.ds(pl.multiple_of(at * slots, slots), slots)

    def inner_rows(mask):
        return pl.ds(pl.multiple_of((rep_at ^ mask) * depth, depth), depth)

    rows_load = pltpu.make_async_copy(arrived_h, arrived, load_sem.at[0])

    @pl.when(first)
    def _():
        rows_load.start()

    loads = [
        pltpu.make_async_copy(w_outer, outer_w.at[:block], load_sem.at[1]),
        pltpu.make_async_copy(outer_h, outer_w.at[block : 2 * block - DEFER], load_sem.at[2]),
    ]
    for side in range(2):
        at = rep_at ^ (2 * side)
        loads.append(
            pltpu.make_async_copy(
                w_inner.at[:, pl.ds(pl.multiple_of(at * block, block), block)],
                inner_w.at[inner_rows(0), side * block : (side + 1) * block],
                load_sem.at[3 + side],
            )
        )
    for mask in range(1, rep_size):
        loads.append(
            pltpu.make_async_copy(
                inner_h.at[inner_rows(mask)], inner_w.at[inner_rows(mask)], load_sem.at[4 + mask]
            )
        )
    for load in loads:
        load.start()

    barrier = pltpu.get_barrier_semaphore()
    for mask in range(1, rep_size):
        for flip in range(2):
            pl.semaphore_signal(
                barrier, inc=1, device_id=(rep_at ^ mask, exp_at ^ flip), device_id_type=MESH
            )

    @pl.loop(1, exp_size)
    def _(at):
        pl.semaphore_signal(barrier, inc=1, device_id=(rep_at, exp_at ^ at), device_id_type=MESH)

    counted = counts_all.shape[0]
    group = exp_at // 2
    lane = lax.broadcasted_iota(jnp.int32, (counted, 128), 1)
    mine = jnp.sum(
        jnp.where(lane == group, counts_all[...], 0.0), axis=1, keepdims=True
    )
    mine = jnp.broadcast_to(mine, (counted, 128))
    down = lax.broadcasted_iota(jnp.int32, (counted, counted), 0)
    along = lax.broadcasted_iota(jnp.int32, (counted, counted), 1)
    ahead = ((along // 16 < down // 16) & (along % 16 == 0)).astype(wide).astype(low)
    offsets[0] = jnp.dot(ahead, mine.astype(low), preferred_element_type=wide)
    offsets[1] = mine
    slot_iota = lax.broadcasted_iota(jnp.int32, (slots, own_rows), 0)
    row_iota = lax.broadcasted_iota(jnp.int32, (slots, own_rows), 1)

    @pl.loop(0, exp_size)
    def _(at):
        eight = pl.ds(pl.multiple_of(at * 16, 16), 8)
        start = offsets[0, eight, :][:1, :1].astype(jnp.int32)
        limit = offsets[1, eight, :][:1, :1].astype(jnp.int32)
        spread_m[slot_rows(at), :] = (
            ((slot_iota + start) == row_iota) & (slot_iota < limit)
        ).astype(wide).astype(low)

    piece = cents.shape[1]
    for at in range(width // piece):
        cent_b[:, at * piece : (at + 1) * piece] = jnp.broadcast_to(
            cents[at * 8 : at * 8 + 1, :], (cent_b.shape[0], piece)
        ).astype(low)
    for at in range(rep_size):
        gain[:, at * depth : (at + 1) * depth] = gains_e[at * 8 : at * 8 + 1, :]
    def compact_rows():
        return lax.dot_general(
            spread_m[...], arrived[...], (((0,), (0,)), ((), ())), preferred_element_type=wide
        ).astype(low)

    @pl.when(first)
    def _():
        rows_load.wait()
        own_x[...] = compact_rows()

    pl.semaphore_wait(barrier, exp_size - 1 + 2 * (rep_size - 1))

    def disp_copy(which):
        return remote(
            packed_h.at[slot_rows(which)],
            arrived.at[slot_rows(exp_at)],
            disp_s.at[which],
            disp_r.at[exp_at],
            (rep_at, 2 * which + 1),
        )

    disp_own = pltpu.make_async_copy(
        packed_h.at[slot_rows(group)], arrived.at[slot_rows(exp_at)], disp_s.at[group]
    )

    @pl.loop(0, exp_size // 2)
    def _(step):
        which = group ^ (exp_size // 2 - 1 - step)

        @pl.when(2 * which + 1 != exp_at)
        def _():
            disp_copy(which).start()

        @pl.when(2 * which + 1 == exp_at)
        def _():
            disp_own.start()

    row_peer = (rep_at ^ 2, exp_at)
    late_copy = remote(
        w_outer.at[block - DEFER :],
        outer_w.at[2 * block - DEFER :],
        early_s.at[0],
        early_r.at[0],
        row_peer,
    )
    late_copy.start()

    gate_copy = remote(gates, gates, gate_s.at[0], gate_r.at[0], side_peer)

    def part_rows(at):
        return pl.ds(pl.multiple_of(at * part, part), part)

    def both_rows(at):
        return pl.ds(pl.multiple_of(at * 2 * part, 2 * part), 2 * part)

    def own_slice(at):
        return pl.ds(pl.multiple_of(at * 2 * part + part, part), part)

    def other_slice(at):
        return pl.ds(pl.multiple_of(at * 2 * part, part), part)

    def grad_copy(at):
        rows = part_rows(at)
        return remote(
            gate_grads.at[rows], gate_grads.at[rows], grad_s.at[at], grad_r.at[at], side_peer
        )

    def hop_forward(at):
        rows = part_rows(at)
        return remote(hop.at[rows], own_x.at[rows], hop_s.at[at], hop_r.at[at], side_peer)

    def hop_backward(at):
        return remote(
            hop.at[part_rows(at)], states.at[own_slice(at)], hop_s.at[at], hop_r.at[at], side_peer
        )

    def norm_copy(at):
        return remote(
            normed.at[own_slice(at)], normed.at[other_slice(at)], norm_s.at[at], norm_r.at[at], core_peer
        )

    def state_copy(at):
        return remote(
            states.at[own_slice(at)], states.at[other_slice(at)], state_s.at[at], state_r.at[at], core_peer
        )

    def part_copy(kind, at):
        count = kind * CHUNKS + at
        rows = part_rows(count)
        return remote(
            part_send.at[rows], part_recv.at[rows], part_s.at[count], part_r.at[count], core_peer
        )

    def norm_rows(at):
        @pl.loop(0, part // ROWS)
        def _(step):
            off = pl.multiple_of(step * ROWS, ROWS)
            unit, _ = row_stats(own_x[pl.ds(at * part + off, ROWS), :].astype(wide))
            normed[pl.ds(at * 2 * part + part + off, ROWS), :] = (unit * gain[...]).astype(low)

        norm_copy(at).start()

    steps = 2 * CHUNKS

    def is_forward(step):
        early = step < CHUNKS
        mixed = (step == 0) | ((step % 2 == 1) & (step < steps - 1))
        return (first & early) | (second & mixed)

    def chunk_at(step):
        of_first = jnp.where(step < CHUNKS, step, step - CHUNKS)
        mixed = (step == 0) | ((step % 2 == 1) & (step < steps - 1))
        of_second = jnp.where(
            mixed,
            (step + 1) // 2,
            jnp.where(step == steps - 1, CHUNKS - 1, (step - 2) // 2),
        )
        return jnp.where(first, of_first, of_second)

    @pl.when(first)
    def _():
        logit = lax.dot_general(
            own_x[...], cent_b[...], (((1,), (1,)), ((), ())), preferred_element_type=wide
        )
        gates[...] = jax.nn.sigmoid(logit)
        gate_copy.start()

        @pl.loop(0, CHUNKS)
        def _(at):
            norm_rows(at)

    @pl.when(second)
    def _():
        hop_forward(0).wait_recv()
        norm_rows(0)

    def take_cotangent():
        disp_own.wait()

        @pl.loop(1, exp_size)
        def _(at):
            source = exp_at ^ at
            remote(
                packed_h.at[slot_rows(0)],
                arrived.at[slot_rows(source)],
                disp_s.at[0],
                disp_r.at[source],
                side_peer,
            ).wait_recv()

        own_cot[...] = compact_rows()
        gate_copy.wait_recv()

        @pl.loop(0, CHUNKS)
        def _(at):
            @pl.loop(0, part // ROWS)
            def _(step):
                off = pl.multiple_of(step * ROWS, ROWS)
                here = pl.ds(at * part + off, ROWS)
                states[pl.ds(at * 2 * part + part + off, ROWS), :] = (
                    gates[here, :][:, :1] * own_cot[here, :].astype(wide)
                ).astype(low)

            state_copy(at).start()

    for load in loads:
        load.wait()
    centre_grad[...] = jnp.zeros_like(centre_grad)

    def finish_forward(step, at):
        part_copy(0, at).wait_recv()

        @pl.loop(0, part // ROWS)
        def _(tile):
            off = pl.multiple_of(tile * ROWS, ROWS)
            here = pl.ds(at * part + off, ROWS)
            result = (
                own_x[here, :].astype(wide)
                + acc[step % 2, pl.ds(off, ROWS), :]
                + part_recv[here, :].astype(wide)
            )

            @pl.when(first)
            def _():
                hop[here, :] = result.astype(low)

            @pl.when(second)
            def _():
                cot = own_cot[here, :].astype(wide)
                back[here, :] = (gates[here, :][:, :1] * result).astype(low)
                gate_grads[here, :] = jnp.broadcast_to(
                    jnp.sum(cot * result, axis=1, keepdims=True), (ROWS, gate_grads.shape[1])
                )

        @pl.when(first)
        def _():
            hop_forward(at).start()

        @pl.when(second)
        def _():
            grad_copy(at).start()

    def finish_backward(step, at):
        part_copy(1, at).wait_recv()

        @pl.when(first)
        def _():
            grad_copy(at).wait_recv()

        @pl.loop(0, part // ROWS)
        def _(tile):
            off = pl.multiple_of(tile * ROWS, ROWS)
            here = pl.ds(at * part + off, ROWS)
            rows_in = own_x[here, :].astype(wide)
            unit, inv_scale = row_stats(rows_in)
            grad_unit = (
                acc[step % 2, pl.ds(off, ROWS), :]
                + part_recv[pl.ds((CHUNKS + at) * part + off, ROWS), :].astype(wide)
            ) * gain[...]
            grad_in = (
                grad_unit
                - jnp.mean(grad_unit, axis=-1, keepdims=True)
                - unit * jnp.mean(grad_unit * unit, axis=-1, keepdims=True)
            ) * inv_scale
            gate = gates[here, :][:, :1]

            @pl.when(second)
            def _():
                state = gate * own_cot[here, :].astype(wide) + grad_in
                hop[here, :] = state.astype(low)

            @pl.when(first)
            def _():
                state = states[pl.ds(at * 2 * part + part + off, ROWS), :].astype(wide) + grad_in
                grad_logit = gate_grads[here, :][:, :1] * gate * (1.0 - gate)
                back[here, :] = (state + grad_logit * cent_b[:1, :].astype(wide)).astype(low)
                centre_grad[...] += jnp.sum(grad_logit * rows_in, axis=0, keepdims=True)

        @pl.when(second)
        def _():
            hop_backward(at).start()

    def finish(step):
        at = chunk_at(step)
        forward = is_forward(step)

        @pl.when(forward)
        def _():
            finish_forward(step, at)

        @pl.when(jnp.logical_not(forward))
        def _():
            finish_backward(step, at)

    @pl.loop(0, steps)
    def _(step):
        at = chunk_at(step)
        forward = is_forward(step)
        rows = both_rows(at)

        @pl.when(forward)
        def _():
            norm_copy(at).wait_recv()

            @pl.loop(0, wide_ff // BIG)
            def _(tile):
                cols = pl.ds(pl.multiple_of(tile * BIG, BIG), BIG)
                inner = jnp.dot(normed[rows, :], inner_w[:, cols], preferred_element_type=wide)
                normal = 0.5 * (1.0 + lax.erf(inner * ROOT_HALF))
                active[rows, cols] = (inner * normal).astype(low)
                slope[rows, cols] = (
                    normal + inner * jnp.exp(-0.5 * inner * inner) * INV_ROOT_TAU
                ).astype(low)

        @pl.when(jnp.logical_not(forward))
        def _():
            state_copy(at).wait_recv()

            @pl.loop(0, wide_ff // BIG)
            def _(tile):
                cols = pl.ds(pl.multiple_of(tile * BIG, BIG), BIG)
                grad_active = lax.dot_general(
                    states[rows, :],
                    outer_w[cols, :],
                    (((1,), (1,)), ((), ())),
                    preferred_element_type=wide,
                )
                slope[rows, cols] = (grad_active * slope[rows, cols].astype(wide)).astype(low)

        @pl.when((step > 0) & jnp.logical_not(first & (step == CHUNKS)))
        def _():
            finish(step - 1)

        @pl.when(step == 0)
        def _():
            late_copy.wait_recv()

        @pl.when(forward)
        def _():
            both = jnp.dot(active[rows, :], outer_w[...], preferred_element_type=wide)
            part_send[part_rows(at), :] = both[:part].astype(low)
            acc[step % 2] = both[part:]
            part_copy(0, at).start()

        @pl.when(jnp.logical_not(forward))
        def _():
            both = lax.dot_general(
                slope[rows, :],
                inner_w[...],
                (((1,), (1,)), ((), ())),
                preferred_element_type=wide,
            )
            part_send[part_rows(CHUNKS + at), :] = both[:part].astype(low)
            acc[step % 2] = both[part:]
            part_copy(1, at).start()

        @pl.when(first & (step == CHUNKS - 1))
        def _():
            finish(step)

        @pl.when(second & (step == 0))
        def _():
            take_cotangent()

        after = step + 1
        after_at = chunk_at(after)

        @pl.when(first & (after >= CHUNKS) & (after < steps))
        def _():
            hop_backward(after_at).wait_recv()
            state_copy(after_at).start()

        @pl.when(second & is_forward(after) & (after < steps))
        def _():
            hop_forward(after_at).wait_recv()
            norm_rows(after_at)

    finish(steps - 1)

    groups = exp_size // 2

    def ret_copy(source, dest):
        return remote(
            source,
            home.at[slot_rows(group)],
            ret_s.at[dest],
            ret_r.at[group],
            (rep_at, dest),
        )

    def relay_copy(which):
        return remote(
            spread.at[slot_rows(2 * which + 1)],
            relay.at[slot_rows(which)],
            relay_s.at[which],
            relay_r.at[which],
            side_peer,
        )

    ret_own = pltpu.make_async_copy(
        spread.at[slot_rows(exp_at)], home.at[slot_rows(group)], ret_s.at[exp_at]
    )

    def make_spread():
        @pl.loop(0, width // TILE)
        def _(step):
            cols = pl.ds(pl.multiple_of(step * TILE, TILE), TILE)
            spread[:, cols] = jnp.dot(
                spread_m[...], back[:, cols], preferred_element_type=wide
            ).astype(low)

    def send_step(step):
        which = group ^ (groups - step)
        relay_copy(which).start()
        ret_copy(spread.at[slot_rows(2 * which)], 2 * which).start()

    def send_end():
        ret_copy(spread.at[slot_rows(exp_at + 1)], exp_at + 1).start()
        ret_own.start()

    def eight_rows(at):
        return pl.ds(pl.multiple_of(at * 8, 8), 8)

    def centre_copy(mask, flip):
        dest = rep_at ^ mask
        return remote(
            centre_v.at[eight_rows(flip * rep_size + dest)],
            centre_parts.at[eight_rows(rep_at)],
            centre_s.at[flip * rep_size + mask],
            centre_r.at[mask],
            (dest, exp_at ^ flip),
        )

    centre_own = pltpu.make_async_copy(
        centre_v.at[eight_rows(rep_at)], centre_parts.at[eight_rows(rep_at)], centre_s.at[0]
    )
    centre_pairs = [(m, f) for m in range(rep_size) for f in range(2) if m or f]

    make_spread()

    def bran_copy(which):
        return remote(
            spread.at[slot_rows(2 * which + 1)],
            branch_got.at[slot_rows(group)],
            bran_s.at[which],
            bran_r.at[group],
            (rep_at, 2 * which + 1),
        )

    bran_own = pltpu.make_async_copy(
        spread.at[slot_rows(exp_at)], branch_got.at[slot_rows(group)], bran_s.at[group]
    )

    @pl.when(second)
    def _():
        bran_own.start()

        @pl.loop(1, groups)
        def _(step):
            bran_copy(group ^ (groups - step)).start()

    spans = 4

    def send_span(span):
        @pl.when(first)
        def _():
            @pl.loop(1 + -(-span * (groups - 1) // spans), 1 + -(-(span + 1) * (groups - 1) // spans))
            def _(step):
                send_step(step)

    @pl.when(first)
    def _():
        for at in range(width // piece):
            centre_v[at * 8 : (at + 1) * 8, :] = jnp.broadcast_to(
                centre_grad[:, at * piece : (at + 1) * piece], (8, piece)
            )
        centre_own.start()
        for mask, flip in centre_pairs:
            centre_copy(mask, flip).start()

    outs = []
    tiles = block // TILE
    early_copy = remote(
        outer_send_v.at[:EARLY], outer_got, early_s.at[1], early_r.at[1], row_peer
    )
    for place, at in enumerate(list(range(tiles, 2 * tiles)) + list(range(tiles))):
        if place % 2 == 0 and place // 2 < spans:
            send_span(place // 2)
        rows = slice(at * TILE, (at + 1) * TILE)
        grad = lax.dot_general(
            active[:, rows], states[...], (((0,), (0,)), ((), ())), preferred_element_type=wide
        )
        if at < tiles:
            outer_keep_v[rows, :] = grad.astype(low)
            outs.append((outer_keep_v.at[rows], outer_keep.at[rows]))
        else:
            top = at * TILE - block
            outer_send_v[top : top + TILE, :] = grad.astype(low)
            if top + TILE == EARLY:
                early_copy.start()
            if top < EARLY:
                continue
            outs.append(
                (outer_send_v.at[top : top + TILE], outer_send.at[top - EARLY : top - EARLY + TILE])
            )
        pltpu.make_async_copy(outs[-1][0], outs[-1][1], out_sem.at[len(outs) - 1]).start()
    outs.append((spread, branch))
    pltpu.make_async_copy(spread, branch, out_sem.at[len(outs) - 1]).start()

    def inner_copy(mask, side):
        at = rep_at ^ (2 * side)
        cols = pl.ds(pl.multiple_of(at * block, block), block)
        target = inner_sum.at[mask // 2, :, cols]
        source = inner_send_v.at[mask, side]
        count = 2 * mask + side
        if mask % 2 == 0:
            return pltpu.make_async_copy(source, target, inner_s.at[count])
        return remote(source, target, inner_s.at[count], out_r.at[count], core_peer)

    inner_order = [(m, f) for m in (3, 1, 2, 0) for f in range(2)]
    @pl.when(first)
    def _():
        send_end()

    for mask, side in inner_order:
        cols = slice(side * block, (side + 1) * block)
        grad = lax.dot_general(
            normed[:, inner_rows(mask)],
            slope[:, cols],
            (((0,), (0,)), ((), ())),
            preferred_element_type=wide,
        )
        inner_send_v[mask, side] = grad.astype(low)
        inner_copy(mask, side).start()

    @pl.when(second)
    def _():
        @pl.loop(1, groups)
        def _(step):
            which = group ^ (groups - step)
            relay_copy(which).wait_recv()
            ret_copy(relay.at[slot_rows(which)], 2 * which + 1).start()

    late_copy.wait_send()
    early_copy.wait()
    for at, (source, target) in enumerate(outs):
        pltpu.make_async_copy(source, target, out_sem.at[at]).wait()
    for mask, side in inner_order:
        inner_copy(mask, side).wait()
    for at in range(CHUNKS):
        norm_copy(at).wait_send()
        state_copy(at).wait_send()
        part_copy(0, at).wait_send()
        part_copy(1, at).wait_send()

        @pl.when(first)
        def _():
            hop_forward(at).wait_send()

        @pl.when(second)
        def _():
            hop_backward(at).wait_send()
            grad_copy(at).wait_send()

    @pl.loop(0, groups)
    def _(which):
        @pl.when(2 * which + 1 != exp_at)
        def _():
            disp_copy(which).wait_send()

    @pl.when(second)
    def _():
        bran_own.wait()

        @pl.loop(1, groups)
        def _(step):
            which = group ^ step
            bran_copy(which).wait_send()
            remote(
                spread.at[slot_rows(which)],
                branch_got.at[slot_rows(which)],
                bran_s.at[which],
                bran_r.at[which],
                side_peer,
            ).wait_recv()

    @pl.when(first)
    def _():
        gate_copy.wait_send()

    @pl.when(first)
    def _():
        centre_own.wait()
        for mask, flip in centre_pairs:
            centre_copy(mask, flip).wait_send()
        for mask in range(1, rep_size):
            centre_copy(mask, 0).wait_recv()

    @pl.when(second)
    def _():
        for mask in range(rep_size):
            centre_copy(mask, 1).wait_recv()

    @pl.when(first)
    def _():
        ret_own.wait()
        ret_copy(spread.at[slot_rows(exp_at + 1)], exp_at + 1).wait_send()

        @pl.loop(1, groups)
        def _(step):
            which = group ^ step
            relay_copy(which).wait_send()
            ret_copy(spread.at[slot_rows(2 * which)], 2 * which).wait_send()

    @pl.when(second)
    def _():
        @pl.loop(1, groups)
        def _(step):
            which = group ^ step
            ret_copy(relay.at[slot_rows(which)], 2 * which + 1).wait_send()

        remote(
            relay.at[slot_rows(group)],
            home.at[slot_rows(group)],
            relay_s.at[group],
            ret_r.at[group],
            side_peer,
        ).wait_recv()

    @pl.loop(1, groups)
    def _(step):
        source = group ^ step
        remote(
            relay.at[slot_rows(source)],
            home.at[slot_rows(source)],
            relay_s.at[source],
            ret_r.at[source],
            side_peer,
        ).wait_recv()


def run_experts(
    exp_size, rep_size, slots, own_rows, arrived, packed, inner_w, outer_w, w_inner, w_outer, counts_all, cents, gains_e
):
    width = arrived.shape[1]
    depth = width // rep_size
    block = w_outer.shape[0]
    low = jnp.bfloat16
    wide = jnp.float32
    total = exp_size * slots
    all_rows = 2 * own_rows
    part = own_rows // CHUNKS
    piece = cents.shape[1]
    anyplace = pl.BlockSpec(memory_space=pl.ANY)
    inside = pl.BlockSpec(memory_space=pltpu.VMEM)
    dma = pltpu.SemaphoreType.DMA
    n_out = (2 * block - EARLY) // TILE + 1
    scratch = [
        pltpu.VMEM((total, width), low),
        pltpu.VMEM((total, own_rows), low),
        pltpu.VMEM((2, exp_size * 16, 128), wide),
        pltpu.VMEM((128, width), low),
        pltpu.VMEM((1, width), wide),
        pltpu.VMEM((1, width), wide),
        pltpu.VMEM((2 * rep_size * 8, piece), wide),
        pltpu.VMEM((width, 2 * block), low),
        pltpu.VMEM((2 * block, width), low),
        pltpu.VMEM((own_rows, width), low),
        pltpu.VMEM((own_rows, width), low),
        pltpu.VMEM((all_rows, width), low),
        pltpu.VMEM((all_rows, 2 * block), low),
        pltpu.VMEM((all_rows, 2 * block), low),
        pltpu.VMEM((all_rows, width), low),
        pltpu.VMEM((2 * own_rows, width), low),
        pltpu.VMEM((2 * own_rows, width), low),
        pltpu.VMEM((own_rows, width), low),
        pltpu.VMEM((own_rows, width), low),
        pltpu.VMEM((total, width), low),
        pltpu.VMEM((total // 2, width), low),
        pltpu.VMEM((2, part, width), wide),
        pltpu.VMEM((own_rows, 128), wide),
        pltpu.VMEM((own_rows, 128), wide),
        pltpu.VMEM((block, width), low),
        pltpu.VMEM((block, width), low),
        pltpu.VMEM((rep_size, 2, depth, block), low),
        dma((8,)),
        dma((exp_size // 2,)),
        dma((exp_size,)),
        dma((exp_size // 2,)),
        dma((exp_size // 2,)),
        dma((2 * rep_size,)),
        dma((rep_size,)),
    ]
    scratch += [dma((CHUNKS,)) for _ in range(4)]
    scratch += [dma((2 * CHUNKS,)), dma((2 * CHUNKS,))]
    scratch += [dma((CHUNKS,)) for _ in range(4)]
    scratch += [dma((1,)), dma((1,)), dma((exp_size,)), dma((exp_size // 2,))]
    scratch += [dma((exp_size // 2,)), dma((exp_size // 2,)), dma((2,)), dma((2,)), dma((n_out,))]
    scratch += [dma((2 * rep_size,)), dma((2 * rep_size,))]
    flops = 2 * all_rows * width * 2 * block * 6
    return pl.pallas_call(
        functools.partial(expert_kernel, exp_size, rep_size, slots),
        out_shape=(
            jax.ShapeDtypeStruct((total // 2, width), low),
            jax.ShapeDtypeStruct((total, width), low),
            jax.ShapeDtypeStruct((total // 2, width), low),
            jax.ShapeDtypeStruct((block, width), low),
            jax.ShapeDtypeStruct((block - EARLY, width), low),
            jax.ShapeDtypeStruct((EARLY, width), low),
            jax.ShapeDtypeStruct((2, depth, rep_size * block), low),
            jax.ShapeDtypeStruct((rep_size * 8, piece), wide),
        ),
        in_specs=[anyplace] * 6 + [inside] * 3,
        out_specs=(anyplace,) * 8,
        scratch_shapes=scratch,
        compiler_params=pltpu.CompilerParams(
            collective_id=0, has_side_effects=True, vmem_limit_bytes=62 << 20
        ),
        cost_estimate=pl.CostEstimate(
            flops=flops, bytes_accessed=40 << 20, transcendentals=2 * all_rows * 2 * block
        ),
        name="experts",
    )(arrived, packed, inner_w, outer_w, w_inner, w_outer, counts_all, cents, gains_e)


def finish_kernel(
    exp_size,
    rep_size,
    home,
    branch,
    branch_got,
    pick,
    hidden_h,
    cotangent,
    tokens_h,
    gain_row,
    qkv_h,
    probs_h,
    normed_h,
    context_h,
    attn_w,
    outer_send,
    outer_got,
    inner_sum,
    output,
    grad_tokens,
    shares,
    outer_recv,
    inner_recv,
    hidden,
    tokens,
    qkv,
    probs,
    normed_a,
    context,
    normed_t,
    context_t,
    branch_in,
    early_rows,
    weights,
    grad_hidden,
    grad_attn,
    grad_context,
    grads3,
    keep,
    core_out,
    core_in,
    side_out,
    side_in,
    line_out,
    line_in,
    total,
    row_out,
    row_in,
    half_out,
    half_in,
    load_s,
    branch_s,
    branch_r,
    expert_s,
    expert_r,
    core_s,
    core_r,
    side_s,
    side_r,
    line_s,
    line_r,
    row_s,
    row_r,
    half_s,
    half_r,
):
    low = jnp.bfloat16
    wide = jnp.float32
    rep_at = lax.axis_index("rep")
    exp_at = lax.axis_index("exp")
    core = rep_at % 2
    group = exp_at // 2
    side = exp_at % 2
    groups = exp_size // 2
    rows_n, width = cotangent.shape
    half = width // 2
    block = width // exp_size
    core_peer = (rep_at ^ 1, exp_at)
    side_peer = (rep_at, exp_at ^ 1)
    row_peer = (rep_at ^ 2, exp_at)

    loads = [
        pltpu.make_async_copy(source, target, load_s.at[at])
        for at, (source, target) in enumerate(
            (
                (context_h, context),
                (attn_w, weights),
                (qkv_h, qkv),
                (probs_h, probs),
                (normed_h, normed_a),
                (tokens_h, tokens),
                (hidden_h, hidden),
                (outer_got, early_rows),
            )
        )
    ]
    for load in loads:
        load.start()

    barrier = pltpu.get_barrier_semaphore()
    for mask in range(1, 3):
        pl.semaphore_signal(
            barrier, inc=1, device_id=(rep_at ^ mask, exp_at), device_id_type=MESH
        )

    @pl.loop(1, exp_size)
    def _(at):
        pl.semaphore_signal(barrier, inc=1, device_id=(rep_at, exp_at ^ at), device_id_type=MESH)

    pl.semaphore_wait(barrier, exp_size + 1)

    outer_copy = remote(
        outer_send, outer_recv.at[EARLY:], expert_s.at[0], expert_r.at[0], row_peer
    )
    early_store = pltpu.make_async_copy(early_rows, outer_recv.at[:EARLY], load_s.at[8])

    inner_copy = remote(inner_sum.at[1], inner_recv, expert_s.at[1], expert_r.at[1], row_peer)
    inner_copy.start()
    outer_copy.start()

    slots = pick.shape[0] // groups

    def slot_rows(at):
        return pl.ds(pl.multiple_of(at * slots, slots), slots)

    def branch_copy(dest):
        return remote(
            branch.at[slot_rows(dest)],
            branch_in.at[slot_rows(group)],
            branch_s.at[dest],
            branch_r.at[group],
            (rep_at, dest),
        )

    branch_own = pltpu.make_async_copy(branch_got, branch_in, branch_s.at[exp_at])

    @pl.when(side == 1)
    def _():
        branch_own.start()

        @pl.loop(0, groups)
        def _(at):
            branch_copy(2 * (group ^ (groups - 1 - at))).start()

    back_rows = lax.dot_general(
        pick[...], home[...], (((0,), (0,)), ((), ())), preferred_element_type=wide
    )
    grad_hidden[...] = cotangent[...].astype(wide) + back_rows
    grad_attn[...] = grad_hidden[...].astype(low)
    loads[0].wait()
    context_t[...] = context[...].T

    own_half = pl.ds(pl.multiple_of(core * half, half), half)
    other_half = pl.ds(pl.multiple_of((1 - core) * half, half), half)

    def core_copy(at):
        return remote(core_out.at[at], core_in.at[at], core_s.at[at], core_r.at[at], core_peer)

    def product(at, left, right, cols, target, kind):
        @pl.loop(0, width // 512)
        def _(step):
            rows = pl.ds(pl.multiple_of(step * 512, 512), 512)
            target[at, rows, :] = jnp.dot(
                left[rows, :], right[:, cols], preferred_element_type=wide
            ).astype(kind)

    def share_start(at, left, right):
        product(at, left, right, other_half, core_out, low)
        core_copy(at).start()
        product(at, left, right, own_half, keep, wide)

    def block_rows(at):
        return pl.ds(pl.multiple_of(at * block, block), block)

    def side_copy(at):
        return remote(side_out.at[at], side_in.at[at], side_s.at[at], side_r.at[at], side_peer)

    def share_side(at):
        core_copy(at).wait_recv()

        @pl.loop(0, groups)
        def _(which):
            rows = block_rows(2 * which + 1 - side)
            side_out[at, block_rows(which), :] = (
                keep[at, rows, :] + core_in[at, rows, :].astype(wide)
            ).astype(low)

        side_copy(at).start()

        @pl.loop(0, groups)
        def _(which):
            rows = block_rows(2 * which + side)
            keep[at, rows, :] = keep[at, rows, :] + core_in[at, rows, :].astype(wide)

    def line_copy(at, mask):
        dest = group ^ mask
        return remote(
            line_out.at[at, block_rows(dest)],
            line_in.at[at, block_rows(group)],
            line_s.at[at, mask],
            line_r.at[at, mask],
            (rep_at, 2 * dest + side),
        )

    def share_line(at):
        side_copy(at).wait_recv()

        @pl.loop(1, groups)
        def _(mask):
            dest = group ^ mask
            line_out[at, block_rows(dest), :] = (
                keep[at, block_rows(2 * dest + side), :] + side_in[at, block_rows(dest), :].astype(wide)
            ).astype(low)
            line_copy(at, mask).start()

        total[at] = keep[at, block_rows(exp_at), :] + side_in[at, block_rows(group), :].astype(wide)

    def row_copy(at):
        return remote(row_out.at[at], row_in.at[at], row_s.at[at], row_r.at[at], row_peer)

    def share_row(at):
        @pl.loop(1, groups)
        def _(mask):
            line_copy(at, mask).wait_recv()
            total[at] = total[at] + line_in[at, block_rows(group ^ mask), :].astype(wide)

        row_out[at] = total[at].astype(low)
        row_copy(at).start()

    def half_copy(at):
        return remote(half_out.at[at], half_in.at[at], half_s.at[at], half_r.at[at], core_peer)

    def share_half(at):
        row_copy(at).wait_recv()
        summed = row_out[at].astype(wide) + row_in[at].astype(wide)
        half_out[at] = summed
        half_copy(at).start()
        shares[at, :, own_half] = summed

    def share_end(at):
        half_copy(at).wait_recv()
        shares[at, :, other_half] = half_in[at]

    share_start(3, context_t, grad_attn)
    loads[1].wait()

    @pl.loop(0, width // TILE)
    def _(step):
        rows = pl.ds(pl.multiple_of(step * TILE, TILE), TILE)
        grad_context[:, rows] = lax.dot_general(
            grad_attn[...], weights[3, rows, :], (((1,), (1,)), ((), ())), preferred_element_type=wide
        ).astype(low)

    share_side(3)

    head_dim = width // HEADS
    pair = 2 * head_dim
    factor = head_dim ** (-0.5)
    lane = lax.broadcasted_iota(jnp.int32, (rows_n, pair), 1)

    def heads(which_half):
        @pl.loop(0, HEADS // 4)
        def _(step):
            at = which_half * (HEADS // 4) + step
            cols = pl.ds(pl.multiple_of(at * pair, pair), pair)
            q_pair = qkv[0, :, cols]
            k_pair = qkv[1, :, cols]
            v_pair = qkv[2, :, cols]
            c_pair = grad_context[:, cols]
            found = []
            for which in range(2):
                chosen = (lane >= head_dim) if which else (lane < head_dim)
                c_one = jnp.where(chosen, c_pair, jnp.zeros_like(c_pair))
                prob = probs[pl.ds(pl.multiple_of((2 * at + which) * rows_n, rows_n), rows_n), :]
                grad_prob = lax.dot_general(
                    c_one, v_pair, (((1,), (1,)), ((), ())), preferred_element_type=wide
                )
                weighted = prob.astype(wide) * grad_prob
                row_sum = jnp.sum(weighted, axis=1, keepdims=True)
                grad_score = (weighted - prob.astype(wide) * row_sum).astype(low)
                found.append(
                    (
                        jnp.dot(grad_score, k_pair, preferred_element_type=wide) * factor,
                        lax.dot_general(
                            grad_score,
                            q_pair,
                            (((0,), (0,)), ((), ())),
                            preferred_element_type=wide,
                        )
                        * factor,
                        lax.dot_general(
                            prob, c_pair, (((0,), (0,)), ((), ())), preferred_element_type=wide
                        ),
                    )
                )
            for which in range(3):
                grads3[which, :, cols] = jnp.where(
                    lane < head_dim, found[0][which], found[1][which]
                ).astype(low)

    loads[7].wait()
    early_store.start()
    loads[2].wait()
    loads[3].wait()
    heads(1 - core)
    loads[4].wait()
    normed_t[...] = normed_a[...].T
    for at in range(3):
        product(at, normed_t, grads3.at[at], other_half, core_out, low)
        core_copy(at).start()
    share_line(3)
    heads(core)
    for at in range(3):
        product(at, normed_t, grads3.at[at], own_half, keep, wide)
        share_side(at)
    loads[5].wait()
    @pl.loop(0, width // TILE)
    def _(step):
        rows = pl.ds(pl.multiple_of(step * TILE, TILE), TILE)
        grad_normed = jnp.zeros((rows_n, TILE), wide)
        for at in range(3):
            grad_normed = grad_normed + lax.dot_general(
                grads3[at], weights[at, rows, :], (((1,), (1,)), ((), ())), preferred_element_type=wide
            )
        grad_tokens[:, rows] = grad_normed

    @pl.loop(0, rows_n // ROWS)
    def _(step):
        here = pl.ds(pl.multiple_of(step * ROWS, ROWS), ROWS)
        unit, inv_scale = row_stats(tokens[here, :].astype(wide))
        grad_unit = grad_tokens[here, :] * gain_row[...]
        grad_in = (
            grad_unit
            - jnp.mean(grad_unit, axis=-1, keepdims=True)
            - unit * jnp.mean(grad_unit * unit, axis=-1, keepdims=True)
        ) * inv_scale
        grad_tokens[here, :] = grad_hidden[here, :] + grad_in

    share_row(3)
    for at in range(3):
        share_line(at)

    for at in range(3):
        share_row(at)
    def branch_wait(which):
        remote(
            branch.at[slot_rows(which)],
            branch_in.at[slot_rows(which)],
            branch_s.at[which],
            branch_r.at[which],
            side_peer,
        ).wait_recv()

    @pl.when(side == 0)
    def _():
        @pl.loop(0, groups)
        def _(at):
            branch_wait(at)

    @pl.when(side == 1)
    def _():
        branch_own.wait()

    loads[6].wait()
    rows = lax.dot_general(
        pick[...], branch_in[...], (((0,), (0,)), ((), ())), preferred_element_type=wide
    )
    output[...] = (hidden[...] + rows).astype(low)

    for at in (3, 0, 1, 2):
        share_half(at)
    for at in (3, 0, 1, 2):
        share_end(at)

    @pl.when(side == 1)
    def _():
        @pl.loop(0, groups)
        def _(at):
            branch_copy(2 * at).wait_send()

    for at in range(4):
        core_copy(at).wait_send()
        side_copy(at).wait_send()
        row_copy(at).wait_send()
        half_copy(at).wait_send()

        @pl.loop(1, groups)
        def _(mask):
            line_copy(at, mask).wait_send()

    inner_copy.wait()
    outer_copy.wait()
    early_store.wait()


def run_finish(exp_size, rep_size, home, branch, branch_got, pick, hidden, cotangent, tokens, gain_row, qkv, probs, normed_a, context, attn_w, outer_send, outer_got, inner_sum):
    rows_n, width = tokens.shape
    low = jnp.bfloat16
    wide = jnp.float32
    half = width // 2
    groups = exp_size // 2
    block = width // exp_size
    anyplace = pl.BlockSpec(memory_space=pl.ANY)
    inside = pl.BlockSpec(memory_space=pltpu.VMEM)
    dma = pltpu.SemaphoreType.DMA
    shape = jax.ShapeDtypeStruct
    return pl.pallas_call(
        functools.partial(finish_kernel, exp_size, rep_size),
        out_shape=(
            shape((rows_n, width), low),
            shape((rows_n, width), wide),
            shape((4, block, width), wide),
            shape((outer_send.shape[0] + EARLY, width), low),
            shape(inner_sum.shape[1:], low),
        ),
        in_specs=[inside, anyplace, anyplace, inside, anyplace, inside, anyplace, inside]
        + [anyplace] * 8,
        out_specs=(inside,) * 3 + (anyplace,) * 2,
        scratch_shapes=[
            pltpu.VMEM((rows_n, width), wide),
            pltpu.VMEM((rows_n, width), low),
            pltpu.VMEM(qkv.shape, low),
            pltpu.VMEM(probs.shape, low),
            pltpu.VMEM((rows_n, width), low),
            pltpu.VMEM((rows_n, width), low),
            pltpu.VMEM((width, rows_n), low),
            pltpu.VMEM((width, rows_n), low),
            pltpu.VMEM(pick.shape[:1] + (width,), low),
            pltpu.VMEM((EARLY, width), low),
            pltpu.VMEM((4, width, width), low),
            pltpu.VMEM((rows_n, width), wide),
            pltpu.VMEM((rows_n, width), low),
            pltpu.VMEM((rows_n, width), low),
            pltpu.VMEM((3, rows_n, width), low),
            pltpu.VMEM((4, width, half), wide),
            pltpu.VMEM((4, width, half), low),
            pltpu.VMEM((4, width, half), low),
            pltpu.VMEM((4, width // 2, half), low),
            pltpu.VMEM((4, width // 2, half), low),
            pltpu.VMEM((4, width // 2, half), low),
            pltpu.VMEM((4, width // 2, half), low),
            pltpu.VMEM((4, block, half), wide),
            pltpu.VMEM((4, block, half), low),
            pltpu.VMEM((4, block, half), low),
            pltpu.VMEM((4, block, half), wide),
            pltpu.VMEM((4, block, half), wide),
            dma((9,)),
            dma((exp_size,)),
            dma((groups,)),
            dma((2,)),
            dma((2,)),
            dma((4,)),
            dma((4,)),
            dma((4,)),
            dma((4,)),
            dma((4, groups)),
            dma((4, groups)),
            dma((4,)),
            dma((4,)),
            dma((4,)),
            dma((4,)),
        ],
        compiler_params=pltpu.CompilerParams(
            collective_id=2, has_side_effects=True, vmem_limit_bytes=60 << 20
        ),
        cost_estimate=pl.CostEstimate(
            flops=20 * rows_n * width * width, bytes_accessed=60 << 20, transcendentals=0
        ),
        name="finish",
    )(
        home,
        branch,
        branch_got,
        pick,
        hidden,
        cotangent,
        tokens,
        gain_row,
        qkv,
        probs,
        normed_a,
        context,
        attn_w,
        outer_send,
        outer_got,
        inner_sum,
    )


def shards(
    tokens,
    cotangent,
    doc_lengths,
    expert_of_token,
    w_query,
    w_key,
    w_value,
    w_output,
    attn_gain,
    w_inner,
    w_outer,
    expert_gain,
    centroids,
):
    exp_size = lax.axis_size("exp")
    rep_size = lax.axis_size("rep")
    row_count = tokens.shape[0]
    wide = jnp.float32

    slots = -(-3 * row_count // exp_size // 16) * 16
    (
        attn_w,
        inner_w,
        outer_w,
        arrived,
        counts_all,
        cents,
        gains_e,
        packed,
        hidden,
        qkv,
        probs,
        normed_a,
        context,
        pick,
        gain_row,
    ) = run_attend(
        exp_size,
        rep_size,
        slots,
        tokens,
        cotangent,
        doc_lengths,
        expert_of_token[None],
        (w_query, w_key, w_value, w_output),
        attn_gain[None],
        w_inner[0],
        w_outer[0],
        expert_gain,
        centroids,
    )
    home, branch, branch_got, outer_keep, outer_send, outer_got, inner_sum, centre_parts = run_experts(
        exp_size,
        rep_size,
        slots,
        2 * row_count,
        arrived,
        packed,
        inner_w,
        outer_w,
        w_inner[0],
        w_outer[0],
        counts_all,
        cents,
        gains_e,
    )
    output, grad_tokens, shares, outer_recv, inner_recv = run_finish(
        exp_size,
        rep_size,
        home,
        branch,
        branch_got,
        pick,
        hidden,
        cotangent,
        tokens,
        gain_row,
        qkv,
        probs,
        normed_a,
        context,
        attn_w,
        outer_send,
        outer_got,
        inner_sum,
    )
    grad_centroids = jnp.sum(centre_parts.reshape(rep_size, 8, -1)[:, 0], axis=0)[None]
    grad_w_outer = (outer_keep.astype(wide) + outer_recv.astype(wide))[None]
    summed = inner_sum[0].astype(wide) + inner_recv.astype(wide)
    grad_w_inner = summed[None]
    grad_expert_gain = jnp.sum(summed * w_inner[0].astype(wide), axis=1)[None] / expert_gain.astype(
        wide
    )
    share_gain = sum(
        jnp.sum(shares[i] * w.astype(wide), axis=1) for i, w in enumerate((w_query, w_key, w_value))
    ) / attn_gain.astype(wide)
    return (
        output,
        grad_tokens,
        shares[0],
        shares[1],
        shares[2],
        shares[3],
        share_gain,
        grad_w_inner,
        grad_w_outer,
        grad_expert_gain,
        grad_centroids,
    )


def solution(mesh):
    placed = (
        P(("rep", "exp"), None),
        P(("rep", "exp"), None),
        P(("rep", "exp"), None),
        P(("rep", "exp")),
        P("exp", None),
        P("exp", None),
        P("exp", None),
        P("exp", None),
        P("exp"),
        P("exp", "rep", None),
        P("exp", "rep", None),
        P("exp", "rep"),
        P("exp", "rep"),
    )
    return jax.shard_map(
        shards,
        mesh=mesh,
        in_specs=placed,
        out_specs=(
            P(("rep", "exp"), None),
            P(("rep", "exp"), None),
            P("exp", None),
            P("exp", None),
            P("exp", None),
            P("exp", None),
            P("exp"),
            P("exp", "rep", None),
            P("exp", "rep", None),
            P("exp", "rep"),
            P("exp", "rep"),
        ),
        check_vma=False,
    )
```

```python
import functools

import jax
import jax.numpy as jnp
from jax import lax
from jax.experimental import pallas as pl
from jax.experimental.pallas import tpu as pltpu
from jax.sharding import PartitionSpec as P

HEADS = 16
EPS = 1e-05
ROOT_HALF = 0.7071067811865476
INV_ROOT_TAU = 0.3989422804014327
CHUNKS = 4
DEFER = 384
EARLY = 512


MESH = pl.DeviceIdType.MESH
TILE = 256
ROWS = 128
BIG = 2048


def remote(src, dst, send_sem, recv_sem, device):
    return pltpu.make_async_remote_copy(
        src_ref=src,
        dst_ref=dst,
        send_sem=send_sem,
        recv_sem=recv_sem,
        device_id=device,
        device_id_type=MESH,
    )


def row_stats(rows):
    row_mean = jnp.mean(rows, axis=-1, keepdims=True)
    centered = rows - row_mean
    variance = jnp.mean(centered * centered, axis=-1, keepdims=True)
    inv_scale = lax.rsqrt(variance + EPS)
    return centered * inv_scale, inv_scale


def attend_kernel(
    exp_size,
    rep_size,
    slots,
    tokens,
    cotangent,
    doc,
    expert_of,
    w_query,
    w_key,
    w_value,
    w_output,
    gain_a,
    w_inner,
    w_outer,
    gain_e,
    cent,
    attn_w,
    inner_w,
    outer_w,
    arrived,
    spread_h,
    cents,
    gains_e,
    packed_h,
    hidden_h,
    qkv_h,
    probs_h,
    normed_h,
    context_h,
    pick,
    gain_row,
    hidden,
    qkv,
    probs,
    normed_a,
    context,
    weights,
    staging,
    spread_m,
    offsets,
    small_all,
    gain_v,
    packed_x,
    packed_c,
    bias,
    counts_v,
    cent_v,
    own_s,
    line_s,
    line_r,
    side_s,
    side_r,
    core_s,
    core_r,
    weight_s,
    weight_r,
    disp_s,
    disp_r,
    count_s,
    count_r,
    cent_s,
    cent_r,
    gain_s,
    gain_r,
    out_s,
):
    low = jnp.bfloat16
    wide = jnp.float32
    rep_at = lax.axis_index("rep")
    exp_at = lax.axis_index("exp")
    core = rep_at % 2
    group = exp_at // 2
    side = exp_at % 2
    groups = exp_size // 2
    rows_n, width = tokens.shape
    half = width // 2
    block = w_query.shape[0]
    depth = w_inner.shape[0]
    ff_block = w_outer.shape[0]
    core_peer = (rep_at ^ 1, exp_at)
    side_peer = (rep_at, exp_at ^ 1)

    def block_rows(at):
        return pl.ds(pl.multiple_of(at * block, block), block)

    own_loads = []
    for at, source in enumerate((w_query, w_key, w_value, w_output)):
        own_loads.append(
            pltpu.make_async_copy(source, weights.at[at, block_rows(exp_at)], own_s.at[at])
        )
    for load in own_loads:
        load.start()

    barrier = pltpu.get_barrier_semaphore()
    for mask in range(1, rep_size):
        for flip in range(2):
            pl.semaphore_signal(
                barrier, inc=1, device_id=(rep_at ^ mask, exp_at ^ flip), device_id_type=MESH
            )

    @pl.loop(1, exp_size)
    def _(at):
        pl.semaphore_signal(barrier, inc=1, device_id=(rep_at, exp_at ^ at), device_id_type=MESH)

    pl.semaphore_wait(barrier, exp_size - 1 + 2 * (rep_size - 1))

    outer_copy = remote(
        w_outer.at[: ff_block - DEFER],
        outer_w,
        weight_s.at[0],
        weight_r.at[0],
        (rep_at ^ 2, exp_at),
    )

    for load in own_loads:
        load.wait()

    picks = (slice(0, 3), slice(3, 4))
    own_half = pl.ds(pl.multiple_of(core * half, half), half)

    def view(kind, at):
        return weights.at[picks[kind], block_rows(at), own_half]

    def line_copy(kind, source, step):
        at = 2 * source + side
        return remote(
            view(kind, at),
            view(kind, at),
            line_s.at[kind, (1 + step) // 2, source],
            line_r.at[kind, source],
            (rep_at, exp_at + 2 * step),
        )

    def line_wait(kind, source):
        at = 2 * source + side
        remote(
            view(kind, at), view(kind, at), line_s.at[kind, 0, source], line_r.at[kind, source], side_peer
        ).wait_recv()

    def side_copy(kind, source):
        at = 2 * source + side
        return remote(
            view(kind, at), view(kind, at), side_s.at[kind, source], side_r.at[kind, source], side_peer
        )

    def side_wait(kind, source):
        at = 2 * source + 1 - side
        remote(
            view(kind, at), view(kind, at), side_s.at[kind, source], side_r.at[kind, source], side_peer
        ).wait_recv()

    def core_copy(kind, at):
        return remote(view(kind, at), view(kind, at), core_s.at[kind, at], core_r.at[kind, at], core_peer)

    def core_wait(kind, at):
        other = pl.ds(pl.multiple_of((1 - core) * half, half), half)
        there = weights.at[picks[kind], block_rows(at), other]
        remote(there, there, core_s.at[kind, at], core_r.at[kind, at], core_peer).wait_recv()

    def first_sends(kind):
        @pl.when(group + 1 < groups)
        def _():
            line_copy(kind, group, 1).start()

        @pl.when(group >= 1)
        def _():
            line_copy(kind, group, -1).start()

        side_copy(kind, group).start()

    def take_side(kind, source):
        side_wait(kind, source)
        core_copy(kind, 2 * source + 1 - side).start()

    def gather_step(kind, step):
        @pl.when(group - step >= 0)
        def _():
            source = group - step
            line_wait(kind, source)

            @pl.when(group + 1 < groups)
            def _():
                line_copy(kind, source, 1).start()

            side_copy(kind, source).start()
            core_copy(kind, 2 * source + side).start()

        @pl.when(group + step < groups)
        def _():
            source = group + step
            line_wait(kind, source)

            @pl.when(group >= 1)
            def _():
                line_copy(kind, source, -1).start()

            side_copy(kind, source).start()
            core_copy(kind, 2 * source + side).start()

        @pl.when(group - step + 1 >= 0)
        def _():
            take_side(kind, group - step + 1)

        @pl.when((step > 1) & (group + step - 1 < groups))
        def _():
            take_side(kind, group + step - 1)

    def gather_end(kind):
        last = groups - 1

        @pl.when(group - last >= 0)
        def _():
            take_side(kind, group - last)

        @pl.when((groups > 1) & (group + last < groups))
        def _():
            take_side(kind, group + last)

        @pl.loop(0, exp_size)
        def _(at):
            @pl.when(at != exp_at)
            def _():
                core_wait(kind, at)

    first_sends(0)
    first_sends(1)

    inner_rows = pl.ds(pl.multiple_of(rep_at * depth, depth), depth)

    def ff_cols(at):
        return pl.ds(pl.multiple_of(at * ff_block, ff_block), ff_block)

    def inner_copies(mask):
        dest = rep_at ^ mask
        found = []
        for part in range(2):
            source = w_inner.at[:, ff_cols(dest ^ (2 * part))]
            cols = slice(part * ff_block, (part + 1) * ff_block)
            at = 1 + 2 * mask + part
            if mask == 3:
                found.append(
                    remote(
                        source,
                        staging.at[:, cols],
                        weight_s.at[at],
                        weight_r.at[at],
                        (rep_at ^ 2, exp_at),
                    )
                )
            else:
                found.append(
                    remote(
                        source,
                        inner_w.at[inner_rows, cols],
                        weight_s.at[at],
                        weight_r.at[at],
                        (dest, exp_at),
                    )
                )
        return found

    far_rows = pl.ds(pl.multiple_of((rep_at ^ 2) * depth, depth), depth)
    forward_copy = remote(
        staging,
        inner_w.at[far_rows],
        weight_s.at[1 + 2 * rep_size],
        weight_r.at[1 + 2 * rep_size],
        core_peer,
    )

    for mask in (3, 2, 1):
        for copy in inner_copies(mask):
            copy.start()
    outer_copy.start()

    lanes = counts_v.shape[1]
    expert_row = expert_of[...]
    onehot = (
        lax.broadcasted_iota(jnp.int32, (lanes, rows_n), 0) == expert_row
    ).astype(wide)
    before = (
        lax.broadcasted_iota(jnp.int32, (rows_n, rows_n), 0)
        < lax.broadcasted_iota(jnp.int32, (rows_n, rows_n), 1)
    ).astype(low)
    earlier = jnp.dot(onehot.astype(low), before, preferred_element_type=wide)
    rank = jnp.sum(earlier * onehot, axis=0, keepdims=True).astype(jnp.int32)
    position = expert_row * slots + rank
    pick[...] = (
        lax.broadcasted_iota(jnp.int32, pick.shape, 0) == position
    ).astype(wide).astype(low)
    counts_v[:8, :] = lax.dot_general(
        jnp.ones((8, rows_n), low),
        onehot.astype(low),
        (((1,), (1,)), ((), ())),
        preferred_element_type=wide,
    )
    counts_v[8:, :block] = jnp.broadcast_to(gain_a[...].astype(wide), (8, block))
    cent_v[...] = jnp.broadcast_to(cent[...].astype(wide), cent_v.shape)
    gain_v[...] = jnp.broadcast_to(gain_e[...].astype(wide), gain_v.shape)

    def eight(at):
        return pl.ds(pl.multiple_of(at * 8, 8), 8)

    def sixteen(at):
        return pl.ds(pl.multiple_of(at * 16, 16), 16)

    def count_copy(dest):
        return remote(
            counts_v, small_all.at[sixteen(exp_at)], count_s.at[dest], count_r.at[exp_at], (rep_at, dest)
        )

    count_own = pltpu.make_async_copy(counts_v, small_all.at[sixteen(exp_at)], count_s.at[exp_at])
    count_own.start()

    @pl.loop(1, exp_size)
    def _(at):
        count_copy(exp_at ^ at).start()

    cent_at = side * rep_size + rep_at

    def cent_copy(mask, flip):
        return remote(
            cent_v,
            cents.at[eight(cent_at)],
            cent_s.at[flip * rep_size + mask],
            cent_r.at[flip * rep_size + mask],
            (rep_at ^ mask, exp_at ^ flip),
        )

    cent_own = pltpu.make_async_copy(cent_v, cents.at[eight(cent_at)], cent_s.at[0])
    cent_own.start()
    cent_pairs = [(m, f) for m in range(rep_size) for f in range(2) if m or f]
    for mask, flip in cent_pairs:
        cent_copy(mask, flip).start()

    def gain_copy(mask):
        return remote(
            gain_v, gains_e.at[eight(rep_at)], gain_s.at[mask], gain_r.at[mask], (rep_at ^ mask, exp_at)
        )

    gain_own = pltpu.make_async_copy(gain_v, gains_e.at[eight(rep_at)], gain_s.at[0])
    gain_own.start()
    for mask in range(1, rep_size):
        gain_copy(mask).start()

    count_own.wait()

    @pl.loop(1, exp_size)
    def _(at):
        source = exp_at ^ at
        remote(
            counts_v, small_all.at[sixteen(source)], count_s.at[source], count_r.at[source], (rep_at, source)
        ).wait()

    tiled = jnp.dot(
        small_all[...].astype(low),
        (
            lax.broadcasted_iota(jnp.int32, (lanes, width), 1) % block
            == lax.broadcasted_iota(jnp.int32, (lanes, width), 0)
        ).astype(wide).astype(low),
        preferred_element_type=wide,
    )
    chosen_row = lax.broadcasted_iota(jnp.int32, (16 * exp_size, width), 0) == (
        16 * (lax.broadcasted_iota(jnp.int32, (16 * exp_size, width), 1) // block) + 8
    )
    gain_row[...] = jnp.sum(jnp.where(chosen_row, tiled, 0.0), axis=0, keepdims=True)

    @pl.loop(0, rows_n // ROWS)
    def _(step):
        here = pl.ds(pl.multiple_of(step * ROWS, ROWS), ROWS)
        unit, _ = row_stats(tokens[here, :].astype(wide))
        normed_a[here, :] = (unit * gain_row[...]).astype(low)

    down = lax.broadcasted_iota(jnp.int32, (rows_n, rows_n), 0)
    along = lax.broadcasted_iota(jnp.int32, (rows_n, rows_n), 1)
    end = jnp.int32(0)
    seg_down = jnp.zeros((rows_n, rows_n), jnp.int32)
    seg_along = jnp.zeros((rows_n, rows_n), jnp.int32)
    for at in range(doc.shape[1]):
        end = end + doc[0, at]
        seg_down = seg_down + (down >= end).astype(jnp.int32)
        seg_along = seg_along + (along >= end).astype(jnp.int32)
    bias[...] = jnp.where((seg_down == seg_along) & (down >= along), 0.0, -1e30)

    @pl.loop(1, groups)
    def _(step):
        gather_step(0, step)

    gather_end(0)

    def slot_rows(at):
        return pl.ds(pl.multiple_of(at * slots, slots), slots)

    def disp_copy(source, dest):
        return remote(
            source.at[slot_rows(dest // 2)],
            arrived.at[slot_rows(exp_at)],
            disp_s.at[dest],
            disp_r.at[exp_at],
            (rep_at, dest),
        )

    def dispatch(source, flip):
        @pl.loop(0, groups)
        def _(at):
            dest = 2 * (group ^ at) + flip

            @pl.when(dest != exp_at)
            def _():
                disp_copy(source, dest).start()

            @pl.when(dest == exp_at)
            def _():
                pltpu.make_async_copy(
                    source.at[slot_rows(group)], arrived.at[slot_rows(exp_at)], disp_s.at[exp_at]
                ).start()

    @pl.loop(1, 1 + (groups - 1 + 2) // 3)
    def _(step):
        gather_step(1, step)

    for at in range(3):

        @pl.loop(0, width // TILE)
        def _(step):
            cols = pl.ds(pl.multiple_of(step * TILE, TILE), TILE)
            qkv[at, :, cols] = jnp.dot(
                normed_a[...], weights[at, :, cols], preferred_element_type=wide
            ).astype(low)

    head_dim = width // HEADS
    pair = 2 * head_dim
    factor = head_dim ** (-0.5)
    lane = lax.broadcasted_iota(jnp.int32, (rows_n, pair), 1)
    pairs = HEADS // 2
    parts = 2
    begun = (groups - 1 + 2) // 3
    for part in range(parts):
        low_step = 1 + begun + part * (groups - 1 - begun) // parts
        high_step = 1 + begun + (part + 1) * (groups - 1 - begun) // parts

        @pl.loop(low_step, high_step)
        def _(step):
            gather_step(1, step)

        @pl.loop(part * pairs // parts, (part + 1) * pairs // parts)
        def _(at):
            cols = pl.ds(pl.multiple_of(at * pair, pair), pair)
            q_pair = qkv[0, :, cols]
            k_pair = qkv[1, :, cols]
            v_pair = qkv[2, :, cols]
            found = []
            for which in range(2):
                chosen = (lane >= head_dim) if which else (lane < head_dim)
                q_one = jnp.where(chosen, q_pair, jnp.zeros_like(q_pair))
                scores = (
                    lax.dot_general(
                        q_one, k_pair, (((1,), (1,)), ((), ())), preferred_element_type=wide
                    )
                    * factor
                    + bias[...]
                )
                top = jnp.max(scores, axis=1, keepdims=True)
                raised = jnp.exp(scores - top)
                total = jnp.sum(raised, axis=1, keepdims=True)
                prob = (raised * (1.0 / total)).astype(low)
                probs[pl.ds(pl.multiple_of((2 * at + which) * rows_n, rows_n), rows_n), :] = prob
                found.append(jnp.dot(prob, v_pair, preferred_element_type=wide))
            context[:, cols] = jnp.where(lane < head_dim, found[0], found[1]).astype(low)

    @pl.loop(0, width // TILE)
    def _(step):
        cols = pl.ds(pl.multiple_of(step * TILE, TILE), TILE)
        packed_c[:, cols] = jnp.dot(
            pick[...], cotangent[:, cols], preferred_element_type=wide
        ).astype(low)

    gather_end(1)
    stores = [
        pltpu.make_async_copy(source, target, out_s.at[at])
        for at, (source, target) in (
            (0, (weights, attn_w)),
            (2, (qkv, qkv_h)),
            (3, (probs, probs_h)),
            (4, (normed_a, normed_h)),
            (5, (context, context_h)),
            (7, (packed_c, packed_h)),
            (6, (hidden, hidden_h)),
        )
    ]
    for store in stores[:-1]:
        store.start()

    @pl.loop(0, width // TILE)
    def _(step):
        cols = pl.ds(pl.multiple_of(step * TILE, TILE), TILE)
        sum_here = tokens[:, cols].astype(wide) + jnp.dot(
            context[...], weights[3, :, cols], preferred_element_type=wide
        )
        hidden[:, cols] = sum_here
        packed_x[:, cols] = jnp.dot(
            pick[...], sum_here.astype(low), preferred_element_type=wide
        ).astype(low)

    dispatch(packed_x, 0)
    stores[-1].start()

    counted = small_all.shape[0]
    own_rows = spread_m.shape[1]
    count_lane = lax.broadcasted_iota(jnp.int32, (counted, 128), 1)
    mine = jnp.sum(
        jnp.where(count_lane == group, small_all[...], 0.0), axis=1, keepdims=True
    )
    mine = jnp.broadcast_to(mine, (counted, 128))
    table_down = lax.broadcasted_iota(jnp.int32, (counted, counted), 0)
    table_along = lax.broadcasted_iota(jnp.int32, (counted, counted), 1)
    ahead = ((table_along // 16 < table_down // 16) & (table_along % 16 == 0)).astype(wide).astype(low)
    offsets[0] = jnp.dot(ahead, mine.astype(low), preferred_element_type=wide)
    offsets[1] = mine
    slot_iota = lax.broadcasted_iota(jnp.int32, (slots, own_rows), 0)
    row_iota = lax.broadcasted_iota(jnp.int32, (slots, own_rows), 1)

    @pl.loop(0, exp_size)
    def _(at):
        eight = pl.ds(pl.multiple_of(at * 16, 16), 8)
        start = offsets[0, eight, :][:1, :1].astype(jnp.int32)
        limit = offsets[1, eight, :][:1, :1].astype(jnp.int32)
        spread_m[slot_rows(at), :] = (
            ((slot_iota + start) == row_iota) & (slot_iota < limit)
        ).astype(wide).astype(low)

    spread_store = pltpu.make_async_copy(spread_m, spread_h, out_s.at[1])
    spread_store.start()
    for copy in inner_copies(3):
        copy.wait_recv()
    forward_copy.start()

    for store in stores:
        store.wait()
    outer_copy.wait()
    forward_copy.wait()
    for mask in range(1, rep_size):
        for copy in inner_copies(mask):
            if mask == 3:
                copy.wait_send()
            else:
                copy.wait()
    for kind in range(2):
        side_copy(kind, group).wait_send()

        @pl.loop(0, groups)
        def _(source):
            @pl.when(source != group)
            def _():
                side_copy(kind, source).wait_send()

            @pl.when((source <= group) & (group + 1 < groups))
            def _():
                line_copy(kind, source, 1).wait_send()

            @pl.when((source >= group) & (group >= 1))
            def _():
                line_copy(kind, source, -1).wait_send()

        @pl.loop(0, exp_size)
        def _(at):
            @pl.when(at != exp_at)
            def _():
                core_copy(kind, at).wait_send()

    spread_store.wait()
    cent_own.wait()
    gain_own.wait()
    for mask in range(1, rep_size):
        gain_copy(mask).wait()
    for mask, flip in cent_pairs:
        cent_copy(mask, flip).wait()

    def disp_wait(source):
        return remote(
            packed_x.at[slot_rows(source // 2)],
            arrived.at[slot_rows(source)],
            disp_s.at[source],
            disp_r.at[source],
            (rep_at, source),
        )

    @pl.loop(0, groups)
    def _(at):
        @pl.when(2 * at != exp_at)
        def _():
            disp_wait(2 * at).wait_send()

    @pl.when(side == 0)
    def _():
        pltpu.make_async_copy(
            packed_x.at[slot_rows(group)], arrived.at[slot_rows(exp_at)], disp_s.at[exp_at]
        ).wait()

        @pl.loop(1, exp_size)
        def _(at):
            disp_wait(exp_at ^ at).wait_recv()


def run_attend(exp_size, rep_size, slots, tokens, cotangent, doc, expert_of, attn, gain_a, w_inner, w_outer, gain_e, cent):
    rows_n, width = tokens.shape
    low = jnp.bfloat16
    wide = jnp.float32
    groups = exp_size // 2
    depth = w_inner.shape[0]
    ff_block = w_outer.shape[0]
    anyplace = pl.BlockSpec(memory_space=pl.ANY)
    inside = pl.BlockSpec(memory_space=pltpu.VMEM)
    dma = pltpu.SemaphoreType.DMA
    shape = jax.ShapeDtypeStruct
    return pl.pallas_call(
        functools.partial(attend_kernel, exp_size, rep_size, slots),
        out_shape=(
            shape((4, width, width), low),
            shape((width, 2 * ff_block), low),
            shape((ff_block - DEFER, width), low),
            shape((exp_size * slots, width), low),
            shape((exp_size * slots, 2 * rows_n), low),
            shape((2 * rep_size * 8, cent.shape[1]), wide),
            shape((rep_size * 8, depth), wide),
            shape((groups * slots, width), low),
            shape((rows_n, width), wide),
            shape((3, rows_n, width), low),
            shape((HEADS * rows_n, rows_n), low),
            shape((rows_n, width), low),
            shape((rows_n, width), low),
            shape((groups * slots, rows_n), low),
            shape((1, width), wide),
        ),
        in_specs=[inside, inside, pl.BlockSpec(memory_space=pltpu.SMEM), inside]
        + [anyplace] * 4
        + [inside, anyplace, anyplace, inside, inside],
        out_specs=(anyplace,) * 13 + (inside,) * 2,
        scratch_shapes=[
            pltpu.VMEM((rows_n, width), wide),
            pltpu.VMEM((3, rows_n, width), low),
            pltpu.VMEM((HEADS * rows_n, rows_n), low),
            pltpu.VMEM((rows_n, width), low),
            pltpu.VMEM((rows_n, width), low),
            pltpu.VMEM((4, width, width), low),
            pltpu.VMEM((depth, 2 * ff_block), low),
            pltpu.VMEM((exp_size * slots, 2 * rows_n), low),
            pltpu.VMEM((2, exp_size * 16, 128), wide),
            pltpu.VMEM((exp_size * 16, 128), wide),
            pltpu.VMEM((8, depth), wide),
            pltpu.VMEM((groups * slots, width), low),
            pltpu.VMEM((groups * slots, width), low),
            pltpu.VMEM((rows_n, rows_n), wide),
            pltpu.VMEM((16, 128), wide),
            pltpu.VMEM((8, cent.shape[1]), wide),
            dma((6,)),
            dma((2, 2, groups)),
            dma((2, groups)),
            dma((2, groups)),
            dma((2, groups)),
            dma((2, exp_size)),
            dma((2, exp_size)),
            dma((2 + 2 * rep_size,)),
            dma((2 + 2 * rep_size,)),
            dma((exp_size,)),
            dma((exp_size,)),
            dma((exp_size,)),
            dma((exp_size,)),
            dma((2 * rep_size,)),
            dma((2 * rep_size,)),
            dma((rep_size,)),
            dma((rep_size,)),
            dma((8,)),
        ],
        compiler_params=pltpu.CompilerParams(
            collective_id=1, has_side_effects=True, vmem_limit_bytes=56 << 20
        ),
        cost_estimate=pl.CostEstimate(
            flops=10 * rows_n * width * width,
            bytes_accessed=40 << 20,
            transcendentals=HEADS * rows_n * rows_n,
        ),
        name="attend",
    )(tokens, cotangent, doc, expert_of, *attn, gain_a, w_inner, w_outer, gain_e, cent)


def expert_kernel(
    exp_size,
    rep_size,
    slots,
    arrived_h,
    packed_h,
    inner_h,
    outer_h,
    w_inner,
    w_outer,
    spread_h,
    cents,
    gains_e,
    home,
    branch,
    branch_got,
    outer_keep,
    outer_send,
    outer_got,
    inner_sum,
    centre_parts,
    arrived,
    spread_m,
    cent_b,
    gain,
    centre_grad,
    centre_v,
    inner_w,
    outer_w,
    own_x,
    own_cot,
    normed,
    active,
    slope,
    states,
    part_send,
    part_recv,
    hop,
    back,
    spread,
    relay,
    acc,
    gates,
    gate_grads,
    outer_keep_v,
    outer_send_v,
    inner_send_v,
    load_sem,
    disp_s,
    disp_r,
    bran_s,
    bran_r,
    centre_s,
    centre_r,
    norm_s,
    norm_r,
    state_s,
    state_r,
    part_s,
    part_r,
    grad_s,
    grad_r,
    hop_s,
    hop_r,
    gate_s,
    gate_r,
    ret_s,
    ret_r,
    relay_s,
    relay_r,
    early_s,
    early_r,
    out_sem,
    inner_s,
    out_r,
):
    low = jnp.bfloat16
    wide = jnp.float32
    rep_at = lax.axis_index("rep")
    exp_at = lax.axis_index("exp")
    first = exp_at % 2 == 0
    second = exp_at % 2 == 1
    core_peer = (rep_at ^ 1, exp_at)
    side_peer = (rep_at, exp_at ^ 1)
    width = own_x.shape[1]
    own_rows = own_x.shape[0]
    part = own_rows // CHUNKS
    wide_ff = inner_w.shape[1]
    block = wide_ff // 2
    depth = width // rep_size

    def slot_rows(at):
        return pl.ds(pl.multiple_of(at * slots, slots), slots)

    def inner_rows(mask):
        return pl.ds(pl.multiple_of((rep_at ^ mask) * depth, depth), depth)

    rows_load = pltpu.make_async_copy(arrived_h, arrived, load_sem.at[0])
    spread_load = pltpu.make_async_copy(spread_h, spread_m, load_sem.at[8])
    spread_load.start()

    @pl.when(first)
    def _():
        rows_load.start()

    loads = [
        pltpu.make_async_copy(w_outer, outer_w.at[:block], load_sem.at[1]),
        pltpu.make_async_copy(outer_h, outer_w.at[block : 2 * block - DEFER], load_sem.at[2]),
    ]
    for side in range(2):
        at = rep_at ^ (2 * side)
        loads.append(
            pltpu.make_async_copy(
                w_inner.at[:, pl.ds(pl.multiple_of(at * block, block), block)],
                inner_w.at[inner_rows(0), side * block : (side + 1) * block],
                load_sem.at[3 + side],
            )
        )
    for mask in range(1, rep_size):
        loads.append(
            pltpu.make_async_copy(
                inner_h.at[inner_rows(mask)], inner_w.at[inner_rows(mask)], load_sem.at[4 + mask]
            )
        )
    for load in loads:
        load.start()

    barrier = pltpu.get_barrier_semaphore()
    for mask in range(1, rep_size):
        for flip in range(2):
            pl.semaphore_signal(
                barrier, inc=1, device_id=(rep_at ^ mask, exp_at ^ flip), device_id_type=MESH
            )

    @pl.loop(1, exp_size)
    def _(at):
        pl.semaphore_signal(barrier, inc=1, device_id=(rep_at, exp_at ^ at), device_id_type=MESH)

    group = exp_at // 2
    pl.semaphore_wait(barrier, exp_size - 1 + 2 * (rep_size - 1))
    row_peer = (rep_at ^ 2, exp_at)
    late_copy = remote(
        w_outer.at[block - DEFER :],
        outer_w.at[2 * block - DEFER :],
        early_s.at[0],
        early_r.at[0],
        row_peer,
    )
    late_copy.start()

    def disp_copy(which):
        return remote(
            packed_h.at[slot_rows(which)],
            arrived.at[slot_rows(exp_at)],
            disp_s.at[which],
            disp_r.at[exp_at],
            (rep_at, 2 * which + 1),
        )

    disp_own = pltpu.make_async_copy(
        packed_h.at[slot_rows(group)], arrived.at[slot_rows(exp_at)], disp_s.at[group]
    )

    @pl.loop(0, exp_size // 2)
    def _(step):
        which = group ^ (exp_size // 2 - 1 - step)

        @pl.when(2 * which + 1 != exp_at)
        def _():
            disp_copy(which).start()

        @pl.when(2 * which + 1 == exp_at)
        def _():
            disp_own.start()

    piece = cents.shape[1]
    for at in range(width // piece):
        cent_b[:, at * piece : (at + 1) * piece] = jnp.broadcast_to(
            cents[at * 8 : at * 8 + 1, :], (cent_b.shape[0], piece)
        ).astype(low)
    for at in range(rep_size):
        gain[:, at * depth : (at + 1) * depth] = gains_e[at * 8 : at * 8 + 1, :]
    def compact_rows():
        return lax.dot_general(
            spread_m[...], arrived[...], (((0,), (0,)), ((), ())), preferred_element_type=wide
        ).astype(low)

    spread_load.wait()

    @pl.when(first)
    def _():
        rows_load.wait()
        own_x[...] = compact_rows()


    gate_copy = remote(gates, gates, gate_s.at[0], gate_r.at[0], side_peer)

    def part_rows(at):
        return pl.ds(pl.multiple_of(at * part, part), part)

    def both_rows(at):
        return pl.ds(pl.multiple_of(at * 2 * part, 2 * part), 2 * part)

    def own_slice(at):
        return pl.ds(pl.multiple_of(at * 2 * part + part, part), part)

    def other_slice(at):
        return pl.ds(pl.multiple_of(at * 2 * part, part), part)

    def grad_copy(at):
        rows = part_rows(at)
        return remote(
            gate_grads.at[rows], gate_grads.at[rows], grad_s.at[at], grad_r.at[at], side_peer
        )

    def hop_forward(at):
        rows = part_rows(at)
        return remote(hop.at[rows], own_x.at[rows], hop_s.at[at], hop_r.at[at], side_peer)

    def hop_backward(at):
        return remote(
            hop.at[part_rows(at)], states.at[own_slice(at)], hop_s.at[at], hop_r.at[at], side_peer
        )

    def norm_copy(at):
        return remote(
            normed.at[own_slice(at)], normed.at[other_slice(at)], norm_s.at[at], norm_r.at[at], core_peer
        )

    def state_copy(at):
        return remote(
            states.at[own_slice(at)], states.at[other_slice(at)], state_s.at[at], state_r.at[at], core_peer
        )

    def part_copy(kind, at):
        count = kind * CHUNKS + at
        rows = part_rows(count)
        return remote(
            part_send.at[rows], part_recv.at[rows], part_s.at[count], part_r.at[count], core_peer
        )

    def norm_rows(at):
        @pl.loop(0, part // ROWS)
        def _(step):
            off = pl.multiple_of(step * ROWS, ROWS)
            unit, _ = row_stats(own_x[pl.ds(at * part + off, ROWS), :].astype(wide))
            normed[pl.ds(at * 2 * part + part + off, ROWS), :] = (unit * gain[...]).astype(low)

        norm_copy(at).start()

    steps = 2 * CHUNKS

    def is_forward(step):
        early = step < CHUNKS
        mixed = (step == 0) | ((step % 2 == 1) & (step < steps - 1))
        return (first & early) | (second & mixed)

    def chunk_at(step):
        of_first = jnp.where(step < CHUNKS, step, step - CHUNKS)
        mixed = (step == 0) | ((step % 2 == 1) & (step < steps - 1))
        of_second = jnp.where(
            mixed,
            (step + 1) // 2,
            jnp.where(step == steps - 1, CHUNKS - 1, (step - 2) // 2),
        )
        return jnp.where(first, of_first, of_second)

    @pl.when(first)
    def _():
        @pl.loop(0, CHUNKS)
        def _(at):
            norm_rows(at)

        logit = lax.dot_general(
            own_x[...], cent_b[...], (((1,), (1,)), ((), ())), preferred_element_type=wide
        )
        gates[...] = jax.nn.sigmoid(logit)
        gate_copy.start()

    @pl.when(second)
    def _():
        hop_forward(0).wait_recv()
        norm_rows(0)

    def take_cotangent():
        disp_own.wait()

        @pl.loop(1, exp_size)
        def _(at):
            source = exp_at ^ at
            remote(
                packed_h.at[slot_rows(0)],
                arrived.at[slot_rows(source)],
                disp_s.at[0],
                disp_r.at[source],
                side_peer,
            ).wait_recv()

        own_cot[...] = compact_rows()
        gate_copy.wait_recv()

        @pl.loop(0, CHUNKS)
        def _(at):
            @pl.loop(0, part // ROWS)
            def _(step):
                off = pl.multiple_of(step * ROWS, ROWS)
                here = pl.ds(at * part + off, ROWS)
                states[pl.ds(at * 2 * part + part + off, ROWS), :] = (
                    gates[here, :][:, :1] * own_cot[here, :].astype(wide)
                ).astype(low)

            state_copy(at).start()

    for load in loads:
        load.wait()
    centre_grad[...] = jnp.zeros_like(centre_grad)

    def finish_forward(step, at):
        part_copy(0, at).wait_recv()

        @pl.loop(0, part // ROWS)
        def _(tile):
            off = pl.multiple_of(tile * ROWS, ROWS)
            here = pl.ds(at * part + off, ROWS)
            result = (
                own_x[here, :].astype(wide)
                + acc[step % 2, pl.ds(off, ROWS), :]
                + part_recv[here, :].astype(wide)
            )

            @pl.when(first)
            def _():
                hop[here, :] = result.astype(low)

            @pl.when(second)
            def _():
                cot = own_cot[here, :].astype(wide)
                back[here, :] = (gates[here, :][:, :1] * result).astype(low)
                gate_grads[here, :] = jnp.broadcast_to(
                    jnp.sum(cot * result, axis=1, keepdims=True), (ROWS, gate_grads.shape[1])
                )

        @pl.when(first)
        def _():
            hop_forward(at).start()

        @pl.when(second)
        def _():
            grad_copy(at).start()

    def finish_backward(step, at):
        part_copy(1, at).wait_recv()

        @pl.when(first)
        def _():
            grad_copy(at).wait_recv()

        @pl.loop(0, part // ROWS)
        def _(tile):
            off = pl.multiple_of(tile * ROWS, ROWS)
            here = pl.ds(at * part + off, ROWS)
            rows_in = own_x[here, :].astype(wide)
            unit, inv_scale = row_stats(rows_in)
            grad_unit = (
                acc[step % 2, pl.ds(off, ROWS), :]
                + part_recv[pl.ds((CHUNKS + at) * part + off, ROWS), :].astype(wide)
            ) * gain[...]
            grad_in = (
                grad_unit
                - jnp.mean(grad_unit, axis=-1, keepdims=True)
                - unit * jnp.mean(grad_unit * unit, axis=-1, keepdims=True)
            ) * inv_scale
            gate = gates[here, :][:, :1]

            @pl.when(second)
            def _():
                state = gate * own_cot[here, :].astype(wide) + grad_in
                hop[here, :] = state.astype(low)

            @pl.when(first)
            def _():
                state = states[pl.ds(at * 2 * part + part + off, ROWS), :].astype(wide) + grad_in
                grad_logit = gate_grads[here, :][:, :1] * gate * (1.0 - gate)
                back[here, :] = (state + grad_logit * cent_b[:1, :].astype(wide)).astype(low)
                centre_grad[...] += jnp.sum(grad_logit * rows_in, axis=0, keepdims=True)

        @pl.when(second)
        def _():
            hop_backward(at).start()

    def finish(step):
        at = chunk_at(step)
        forward = is_forward(step)

        @pl.when(forward)
        def _():
            finish_forward(step, at)

        @pl.when(jnp.logical_not(forward))
        def _():
            finish_backward(step, at)

    @pl.loop(0, steps)
    def _(step):
        at = chunk_at(step)
        forward = is_forward(step)
        rows = both_rows(at)

        @pl.when(forward)
        def _():
            norm_copy(at).wait_recv()

            @pl.loop(0, wide_ff // BIG)
            def _(tile):
                cols = pl.ds(pl.multiple_of(tile * BIG, BIG), BIG)
                inner = jnp.dot(normed[rows, :], inner_w[:, cols], preferred_element_type=wide)
                normal = 0.5 * (1.0 + lax.erf(inner * ROOT_HALF))
                active[rows, cols] = (inner * normal).astype(low)
                slope[rows, cols] = (
                    normal + inner * jnp.exp(-0.5 * inner * inner) * INV_ROOT_TAU
                ).astype(low)

        @pl.when(jnp.logical_not(forward))
        def _():
            state_copy(at).wait_recv()

            @pl.loop(0, wide_ff // BIG)
            def _(tile):
                cols = pl.ds(pl.multiple_of(tile * BIG, BIG), BIG)
                grad_active = lax.dot_general(
                    states[rows, :],
                    outer_w[cols, :],
                    (((1,), (1,)), ((), ())),
                    preferred_element_type=wide,
                )
                slope[rows, cols] = (grad_active * slope[rows, cols].astype(wide)).astype(low)

        @pl.when((step > 0) & jnp.logical_not(first & (step == CHUNKS)))
        def _():
            finish(step - 1)

        @pl.when(step == 0)
        def _():
            late_copy.wait_recv()

        @pl.when(forward)
        def _():
            both = jnp.dot(active[rows, :], outer_w[...], preferred_element_type=wide)
            part_send[part_rows(at), :] = both[:part].astype(low)
            acc[step % 2] = both[part:]
            part_copy(0, at).start()

        @pl.when(jnp.logical_not(forward))
        def _():
            both = lax.dot_general(
                slope[rows, :],
                inner_w[...],
                (((1,), (1,)), ((), ())),
                preferred_element_type=wide,
            )
            part_send[part_rows(CHUNKS + at), :] = both[:part].astype(low)
            acc[step % 2] = both[part:]
            part_copy(1, at).start()

        @pl.when(first & (step == CHUNKS - 1))
        def _():
            finish(step)

        @pl.when(second & (step == 0))
        def _():
            take_cotangent()

        after = step + 1
        after_at = chunk_at(after)

        @pl.when(first & (after >= CHUNKS) & (after < steps))
        def _():
            hop_backward(after_at).wait_recv()
            state_copy(after_at).start()

        @pl.when(second & is_forward(after) & (after < steps))
        def _():
            hop_forward(after_at).wait_recv()
            norm_rows(after_at)

    finish(steps - 1)

    groups = exp_size // 2

    def ret_copy(source, dest):
        return remote(
            source,
            home.at[slot_rows(group)],
            ret_s.at[dest],
            ret_r.at[group],
            (rep_at, dest),
        )

    def relay_copy(which):
        return remote(
            spread.at[slot_rows(2 * which + 1)],
            relay.at[slot_rows(which)],
            relay_s.at[which],
            relay_r.at[which],
            side_peer,
        )

    ret_own = pltpu.make_async_copy(
        spread.at[slot_rows(exp_at)], home.at[slot_rows(group)], ret_s.at[exp_at]
    )

    def make_spread():
        @pl.loop(0, width // TILE)
        def _(step):
            cols = pl.ds(pl.multiple_of(step * TILE, TILE), TILE)
            spread[:, cols] = jnp.dot(
                spread_m[...], back[:, cols], preferred_element_type=wide
            ).astype(low)

    def send_step(step):
        which = group ^ (groups - step)
        relay_copy(which).start()
        ret_copy(spread.at[slot_rows(2 * which)], 2 * which).start()

    def send_end():
        ret_copy(spread.at[slot_rows(exp_at + 1)], exp_at + 1).start()
        ret_own.start()

    def eight_rows(at):
        return pl.ds(pl.multiple_of(at * 8, 8), 8)

    def centre_copy(mask, flip):
        dest = rep_at ^ mask
        return remote(
            centre_v.at[eight_rows(flip * rep_size + dest)],
            centre_parts.at[eight_rows(rep_at)],
            centre_s.at[flip * rep_size + mask],
            centre_r.at[mask],
            (dest, exp_at ^ flip),
        )

    centre_own = pltpu.make_async_copy(
        centre_v.at[eight_rows(rep_at)], centre_parts.at[eight_rows(rep_at)], centre_s.at[0]
    )
    centre_pairs = [(m, f) for m in range(rep_size) for f in range(2) if m or f]

    make_spread()

    def bran_copy(which):
        return remote(
            spread.at[slot_rows(2 * which + 1)],
            branch_got.at[slot_rows(group)],
            bran_s.at[which],
            bran_r.at[group],
            (rep_at, 2 * which + 1),
        )

    bran_own = pltpu.make_async_copy(
        spread.at[slot_rows(exp_at)], branch_got.at[slot_rows(group)], bran_s.at[group]
    )

    @pl.when(second)
    def _():
        bran_own.start()

        @pl.loop(1, groups)
        def _(step):
            bran_copy(group ^ (groups - step)).start()

    spans = 4

    def send_span(span):
        @pl.when(first)
        def _():
            @pl.loop(1 + -(-span * (groups - 1) // spans), 1 + -(-(span + 1) * (groups - 1) // spans))
            def _(step):
                send_step(step)

    @pl.when(first)
    def _():
        for at in range(width // piece):
            centre_v[at * 8 : (at + 1) * 8, :] = jnp.broadcast_to(
                centre_grad[:, at * piece : (at + 1) * piece], (8, piece)
            )
        centre_own.start()
        for mask, flip in centre_pairs:
            centre_copy(mask, flip).start()

    outs = []
    tiles = block // TILE
    early_copy = remote(
        outer_send_v.at[:EARLY], outer_got, early_s.at[1], early_r.at[1], row_peer
    )
    for place, at in enumerate(list(range(tiles, 2 * tiles)) + list(range(tiles))):
        if place % 2 == 0 and place // 2 < spans:
            send_span(place // 2)
        rows = slice(at * TILE, (at + 1) * TILE)
        grad = lax.dot_general(
            active[:, rows], states[...], (((0,), (0,)), ((), ())), preferred_element_type=wide
        )
        if at < tiles:
            outer_keep_v[rows, :] = grad.astype(low)
            outs.append((outer_keep_v.at[rows], outer_keep.at[rows]))
        else:
            top = at * TILE - block
            outer_send_v[top : top + TILE, :] = grad.astype(low)
            if top + TILE == EARLY:
                early_copy.start()
            if top < EARLY:
                continue
            outs.append(
                (outer_send_v.at[top : top + TILE], outer_send.at[top - EARLY : top - EARLY + TILE])
            )
        pltpu.make_async_copy(outs[-1][0], outs[-1][1], out_sem.at[len(outs) - 1]).start()
    outs.append((spread, branch))
    pltpu.make_async_copy(spread, branch, out_sem.at[len(outs) - 1]).start()

    def inner_copy(mask, side):
        at = rep_at ^ (2 * side)
        cols = pl.ds(pl.multiple_of(at * block, block), block)
        target = inner_sum.at[mask // 2, :, cols]
        source = inner_send_v.at[mask, side]
        count = 2 * mask + side
        if mask % 2 == 0:
            return pltpu.make_async_copy(source, target, inner_s.at[count])
        return remote(source, target, inner_s.at[count], out_r.at[count], core_peer)

    inner_order = [(m, f) for m in (3, 1, 2, 0) for f in range(2)]
    @pl.when(first)
    def _():
        send_end()

    for mask, side in inner_order:
        cols = slice(side * block, (side + 1) * block)
        grad = lax.dot_general(
            normed[:, inner_rows(mask)],
            slope[:, cols],
            (((0,), (0,)), ((), ())),
            preferred_element_type=wide,
        )
        inner_send_v[mask, side] = grad.astype(low)
        inner_copy(mask, side).start()

    @pl.when(second)
    def _():
        @pl.loop(1, groups)
        def _(step):
            which = group ^ (groups - step)
            relay_copy(which).wait_recv()
            ret_copy(relay.at[slot_rows(which)], 2 * which + 1).start()

    late_copy.wait_send()
    early_copy.wait()
    for at, (source, target) in enumerate(outs):
        pltpu.make_async_copy(source, target, out_sem.at[at]).wait()
    for mask, side in inner_order:
        inner_copy(mask, side).wait()
    for at in range(CHUNKS):
        norm_copy(at).wait_send()
        state_copy(at).wait_send()
        part_copy(0, at).wait_send()
        part_copy(1, at).wait_send()

        @pl.when(first)
        def _():
            hop_forward(at).wait_send()

        @pl.when(second)
        def _():
            hop_backward(at).wait_send()
            grad_copy(at).wait_send()

    @pl.loop(0, groups)
    def _(which):
        @pl.when(2 * which + 1 != exp_at)
        def _():
            disp_copy(which).wait_send()

    @pl.when(second)
    def _():
        bran_own.wait()

        @pl.loop(1, groups)
        def _(step):
            which = group ^ step
            bran_copy(which).wait_send()
            remote(
                spread.at[slot_rows(which)],
                branch_got.at[slot_rows(which)],
                bran_s.at[which],
                bran_r.at[which],
                side_peer,
            ).wait_recv()

    @pl.when(first)
    def _():
        gate_copy.wait_send()

    @pl.when(first)
    def _():
        centre_own.wait()
        for mask, flip in centre_pairs:
            centre_copy(mask, flip).wait_send()
        for mask in range(1, rep_size):
            centre_copy(mask, 0).wait_recv()

    @pl.when(second)
    def _():
        for mask in range(rep_size):
            centre_copy(mask, 1).wait_recv()

    @pl.when(first)
    def _():
        ret_own.wait()
        ret_copy(spread.at[slot_rows(exp_at + 1)], exp_at + 1).wait_send()

        @pl.loop(1, groups)
        def _(step):
            which = group ^ step
            relay_copy(which).wait_send()
            ret_copy(spread.at[slot_rows(2 * which)], 2 * which).wait_send()

    @pl.when(second)
    def _():
        @pl.loop(1, groups)
        def _(step):
            which = group ^ step
            ret_copy(relay.at[slot_rows(which)], 2 * which + 1).wait_send()

        remote(
            relay.at[slot_rows(group)],
            home.at[slot_rows(group)],
            relay_s.at[group],
            ret_r.at[group],
            side_peer,
        ).wait_recv()

    @pl.loop(1, groups)
    def _(step):
        source = group ^ step
        remote(
            relay.at[slot_rows(source)],
            home.at[slot_rows(source)],
            relay_s.at[source],
            ret_r.at[source],
            side_peer,
        ).wait_recv()


def run_experts(
    exp_size, rep_size, slots, own_rows, arrived, packed, inner_w, outer_w, w_inner, w_outer, spread, cents, gains_e
):
    width = arrived.shape[1]
    depth = width // rep_size
    block = w_outer.shape[0]
    low = jnp.bfloat16
    wide = jnp.float32
    total = exp_size * slots
    all_rows = 2 * own_rows
    part = own_rows // CHUNKS
    piece = cents.shape[1]
    anyplace = pl.BlockSpec(memory_space=pl.ANY)
    inside = pl.BlockSpec(memory_space=pltpu.VMEM)
    dma = pltpu.SemaphoreType.DMA
    n_out = (2 * block - EARLY) // TILE + 1
    scratch = [
        pltpu.VMEM((total, width), low),
        pltpu.VMEM((total, own_rows), low),
        pltpu.VMEM((128, width), low),
        pltpu.VMEM((1, width), wide),
        pltpu.VMEM((1, width), wide),
        pltpu.VMEM((2 * rep_size * 8, piece), wide),
        pltpu.VMEM((width, 2 * block), low),
        pltpu.VMEM((2 * block, width), low),
        pltpu.VMEM((own_rows, width), low),
        pltpu.VMEM((own_rows, width), low),
        pltpu.VMEM((all_rows, width), low),
        pltpu.VMEM((all_rows, 2 * block), low),
        pltpu.VMEM((all_rows, 2 * block), low),
        pltpu.VMEM((all_rows, width), low),
        pltpu.VMEM((2 * own_rows, width), low),
        pltpu.VMEM((2 * own_rows, width), low),
        pltpu.VMEM((own_rows, width), low),
        pltpu.VMEM((own_rows, width), low),
        pltpu.VMEM((total, width), low),
        pltpu.VMEM((total // 2, width), low),
        pltpu.VMEM((2, part, width), wide),
        pltpu.VMEM((own_rows, 128), wide),
        pltpu.VMEM((own_rows, 128), wide),
        pltpu.VMEM((block, width), low),
        pltpu.VMEM((block, width), low),
        pltpu.VMEM((rep_size, 2, depth, block), low),
        dma((9,)),
        dma((exp_size // 2,)),
        dma((exp_size,)),
        dma((exp_size // 2,)),
        dma((exp_size // 2,)),
        dma((2 * rep_size,)),
        dma((rep_size,)),
    ]
    scratch += [dma((CHUNKS,)) for _ in range(4)]
    scratch += [dma((2 * CHUNKS,)), dma((2 * CHUNKS,))]
    scratch += [dma((CHUNKS,)) for _ in range(4)]
    scratch += [dma((1,)), dma((1,)), dma((exp_size,)), dma((exp_size // 2,))]
    scratch += [dma((exp_size // 2,)), dma((exp_size // 2,)), dma((2,)), dma((2,)), dma((n_out,))]
    scratch += [dma((2 * rep_size,)), dma((2 * rep_size,))]
    flops = 2 * all_rows * width * 2 * block * 6
    return pl.pallas_call(
        functools.partial(expert_kernel, exp_size, rep_size, slots),
        out_shape=(
            jax.ShapeDtypeStruct((total // 2, width), low),
            jax.ShapeDtypeStruct((total, width), low),
            jax.ShapeDtypeStruct((total // 2, width), low),
            jax.ShapeDtypeStruct((block, width), low),
            jax.ShapeDtypeStruct((block - EARLY, width), low),
            jax.ShapeDtypeStruct((EARLY, width), low),
            jax.ShapeDtypeStruct((2, depth, rep_size * block), low),
            jax.ShapeDtypeStruct((rep_size * 8, piece), wide),
        ),
        in_specs=[anyplace] * 7 + [inside] * 2,
        out_specs=(anyplace,) * 8,
        scratch_shapes=scratch,
        compiler_params=pltpu.CompilerParams(
            collective_id=0, has_side_effects=True, vmem_limit_bytes=62 << 20
        ),
        cost_estimate=pl.CostEstimate(
            flops=flops, bytes_accessed=40 << 20, transcendentals=2 * all_rows * 2 * block
        ),
        name="experts",
    )(arrived, packed, inner_w, outer_w, w_inner, w_outer, spread, cents, gains_e)


def finish_kernel(
    exp_size,
    rep_size,
    home,
    branch,
    branch_got,
    pick,
    hidden_h,
    cotangent,
    tokens_h,
    gain_row,
    qkv_h,
    probs_h,
    normed_h,
    context_h,
    attn_w,
    outer_send,
    outer_got,
    inner_sum,
    output,
    grad_tokens,
    shares,
    outer_recv,
    inner_recv,
    hidden,
    tokens,
    qkv,
    probs,
    normed_a,
    context,
    normed_t,
    context_t,
    branch_in,
    early_rows,
    weights,
    grad_hidden,
    grad_attn,
    grad_context,
    grads3,
    keep,
    core_out,
    core_in,
    side_out,
    side_in,
    line_out,
    line_in,
    total,
    row_out,
    row_in,
    half_out,
    half_in,
    load_s,
    branch_s,
    branch_r,
    expert_s,
    expert_r,
    core_s,
    core_r,
    side_s,
    side_r,
    line_s,
    line_r,
    row_s,
    row_r,
    half_s,
    half_r,
):
    low = jnp.bfloat16
    wide = jnp.float32
    rep_at = lax.axis_index("rep")
    exp_at = lax.axis_index("exp")
    core = rep_at % 2
    group = exp_at // 2
    side = exp_at % 2
    groups = exp_size // 2
    rows_n, width = cotangent.shape
    half = width // 2
    block = width // exp_size
    core_peer = (rep_at ^ 1, exp_at)
    side_peer = (rep_at, exp_at ^ 1)
    row_peer = (rep_at ^ 2, exp_at)

    loads = [
        pltpu.make_async_copy(source, target, load_s.at[at])
        for at, (source, target) in enumerate(
            (
                (context_h, context),
                (attn_w, weights),
                (qkv_h, qkv),
                (probs_h, probs),
                (normed_h, normed_a),
                (tokens_h, tokens),
                (hidden_h, hidden),
                (outer_got, early_rows),
            )
        )
    ]
    for load in loads:
        load.start()

    barrier = pltpu.get_barrier_semaphore()
    for mask in range(1, 3):
        pl.semaphore_signal(
            barrier, inc=1, device_id=(rep_at ^ mask, exp_at), device_id_type=MESH
        )

    @pl.loop(1, exp_size)
    def _(at):
        pl.semaphore_signal(barrier, inc=1, device_id=(rep_at, exp_at ^ at), device_id_type=MESH)

    pl.semaphore_wait(barrier, exp_size + 1)

    outer_copy = remote(
        outer_send, outer_recv.at[EARLY:], expert_s.at[0], expert_r.at[0], row_peer
    )
    early_store = pltpu.make_async_copy(early_rows, outer_recv.at[:EARLY], load_s.at[8])

    inner_copy = remote(inner_sum.at[1], inner_recv, expert_s.at[1], expert_r.at[1], row_peer)
    inner_copy.start()
    outer_copy.start()

    slots = pick.shape[0] // groups

    def slot_rows(at):
        return pl.ds(pl.multiple_of(at * slots, slots), slots)

    def branch_copy(dest):
        return remote(
            branch.at[slot_rows(dest)],
            branch_in.at[slot_rows(group)],
            branch_s.at[dest],
            branch_r.at[group],
            (rep_at, dest),
        )

    branch_own = pltpu.make_async_copy(branch_got, branch_in, branch_s.at[exp_at])

    @pl.when(side == 1)
    def _():
        branch_own.start()

        @pl.loop(0, groups)
        def _(at):
            branch_copy(2 * (group ^ (groups - 1 - at))).start()

    back_rows = lax.dot_general(
        pick[...], home[...], (((0,), (0,)), ((), ())), preferred_element_type=wide
    )
    grad_hidden[...] = cotangent[...].astype(wide) + back_rows
    grad_attn[...] = grad_hidden[...].astype(low)
    loads[0].wait()
    context_t[...] = context[...].T

    own_half = pl.ds(pl.multiple_of(core * half, half), half)
    other_half = pl.ds(pl.multiple_of((1 - core) * half, half), half)

    def core_copy(at):
        return remote(core_out.at[at], core_in.at[at], core_s.at[at], core_r.at[at], core_peer)

    def product(at, left, right, cols, target, kind):
        @pl.loop(0, width // 512)
        def _(step):
            rows = pl.ds(pl.multiple_of(step * 512, 512), 512)
            target[at, rows, :] = jnp.dot(
                left[rows, :], right[:, cols], preferred_element_type=wide
            ).astype(kind)

    def share_start(at, left, right):
        product(at, left, right, other_half, core_out, low)
        core_copy(at).start()
        product(at, left, right, own_half, keep, wide)

    def block_rows(at):
        return pl.ds(pl.multiple_of(at * block, block), block)

    def side_copy(at):
        return remote(side_out.at[at], side_in.at[at], side_s.at[at], side_r.at[at], side_peer)

    def share_side(at):
        core_copy(at).wait_recv()

        @pl.loop(0, groups)
        def _(which):
            rows = block_rows(2 * which + 1 - side)
            side_out[at, block_rows(which), :] = (
                keep[at, rows, :] + core_in[at, rows, :].astype(wide)
            ).astype(low)

        side_copy(at).start()

        @pl.loop(0, groups)
        def _(which):
            rows = block_rows(2 * which + side)
            keep[at, rows, :] = keep[at, rows, :] + core_in[at, rows, :].astype(wide)

    def line_copy(at, mask):
        dest = group ^ mask
        return remote(
            line_out.at[at, block_rows(dest)],
            line_in.at[at, block_rows(group)],
            line_s.at[at, mask],
            line_r.at[at, mask],
            (rep_at, 2 * dest + side),
        )

    def share_line(at):
        side_copy(at).wait_recv()

        @pl.loop(1, groups)
        def _(mask):
            dest = group ^ mask
            line_out[at, block_rows(dest), :] = (
                keep[at, block_rows(2 * dest + side), :] + side_in[at, block_rows(dest), :].astype(wide)
            ).astype(low)
            line_copy(at, mask).start()

        total[at] = keep[at, block_rows(exp_at), :] + side_in[at, block_rows(group), :].astype(wide)

    def row_copy(at):
        return remote(row_out.at[at], row_in.at[at], row_s.at[at], row_r.at[at], row_peer)

    def share_row(at):
        @pl.loop(1, groups)
        def _(mask):
            line_copy(at, mask).wait_recv()
            total[at] = total[at] + line_in[at, block_rows(group ^ mask), :].astype(wide)

        row_out[at] = total[at].astype(low)
        row_copy(at).start()

    def half_copy(at):
        return remote(half_out.at[at], half_in.at[at], half_s.at[at], half_r.at[at], core_peer)

    def share_half(at):
        row_copy(at).wait_recv()
        summed = row_out[at].astype(wide) + row_in[at].astype(wide)
        half_out[at] = summed
        half_copy(at).start()
        shares[at, :, own_half] = summed

    def share_end(at):
        half_copy(at).wait_recv()
        shares[at, :, other_half] = half_in[at]

    share_start(3, context_t, grad_attn)
    loads[1].wait()

    @pl.loop(0, width // TILE)
    def _(step):
        rows = pl.ds(pl.multiple_of(step * TILE, TILE), TILE)
        grad_context[:, rows] = lax.dot_general(
            grad_attn[...], weights[3, rows, :], (((1,), (1,)), ((), ())), preferred_element_type=wide
        ).astype(low)

    share_side(3)

    head_dim = width // HEADS
    pair = 2 * head_dim
    factor = head_dim ** (-0.5)
    lane = lax.broadcasted_iota(jnp.int32, (rows_n, pair), 1)

    def heads(which_half):
        @pl.loop(0, HEADS // 4)
        def _(step):
            at = which_half * (HEADS // 4) + step
            cols = pl.ds(pl.multiple_of(at * pair, pair), pair)
            q_pair = qkv[0, :, cols]
            k_pair = qkv[1, :, cols]
            v_pair = qkv[2, :, cols]
            c_pair = grad_context[:, cols]
            found = []
            for which in range(2):
                chosen = (lane >= head_dim) if which else (lane < head_dim)
                c_one = jnp.where(chosen, c_pair, jnp.zeros_like(c_pair))
                prob = probs[pl.ds(pl.multiple_of((2 * at + which) * rows_n, rows_n), rows_n), :]
                grad_prob = lax.dot_general(
                    c_one, v_pair, (((1,), (1,)), ((), ())), preferred_element_type=wide
                )
                weighted = prob.astype(wide) * grad_prob
                row_sum = jnp.sum(weighted, axis=1, keepdims=True)
                grad_score = (weighted - prob.astype(wide) * row_sum).astype(low)
                found.append(
                    (
                        jnp.dot(grad_score, k_pair, preferred_element_type=wide) * factor,
                        lax.dot_general(
                            grad_score,
                            q_pair,
                            (((0,), (0,)), ((), ())),
                            preferred_element_type=wide,
                        )
                        * factor,
                        lax.dot_general(
                            prob, c_pair, (((0,), (0,)), ((), ())), preferred_element_type=wide
                        ),
                    )
                )
            for which in range(3):
                grads3[which, :, cols] = jnp.where(
                    lane < head_dim, found[0][which], found[1][which]
                ).astype(low)

    loads[7].wait()
    early_store.start()
    loads[2].wait()
    loads[3].wait()
    heads(1 - core)
    loads[4].wait()
    normed_t[...] = normed_a[...].T
    for at in range(3):
        product(at, normed_t, grads3.at[at], other_half, core_out, low)
        core_copy(at).start()
    share_line(3)
    heads(core)
    for at in range(3):
        product(at, normed_t, grads3.at[at], own_half, keep, wide)
        share_side(at)
    loads[5].wait()
    @pl.loop(0, width // TILE)
    def _(step):
        rows = pl.ds(pl.multiple_of(step * TILE, TILE), TILE)
        grad_normed = jnp.zeros((rows_n, TILE), wide)
        for at in range(3):
            grad_normed = grad_normed + lax.dot_general(
                grads3[at], weights[at, rows, :], (((1,), (1,)), ((), ())), preferred_element_type=wide
            )
        grad_tokens[:, rows] = grad_normed

    @pl.loop(0, rows_n // ROWS)
    def _(step):
        here = pl.ds(pl.multiple_of(step * ROWS, ROWS), ROWS)
        unit, inv_scale = row_stats(tokens[here, :].astype(wide))
        grad_unit = grad_tokens[here, :] * gain_row[...]
        grad_in = (
            grad_unit
            - jnp.mean(grad_unit, axis=-1, keepdims=True)
            - unit * jnp.mean(grad_unit * unit, axis=-1, keepdims=True)
        ) * inv_scale
        grad_tokens[here, :] = grad_hidden[here, :] + grad_in

    share_row(3)
    for at in range(3):
        share_line(at)

    for at in range(3):
        share_row(at)
    def branch_wait(which):
        remote(
            branch.at[slot_rows(which)],
            branch_in.at[slot_rows(which)],
            branch_s.at[which],
            branch_r.at[which],
            side_peer,
        ).wait_recv()

    @pl.when(side == 0)
    def _():
        @pl.loop(0, groups)
        def _(at):
            branch_wait(at)

    @pl.when(side == 1)
    def _():
        branch_own.wait()

    loads[6].wait()
    rows = lax.dot_general(
        pick[...], branch_in[...], (((0,), (0,)), ((), ())), preferred_element_type=wide
    )
    output[...] = (hidden[...] + rows).astype(low)

    for at in (3, 0, 1, 2):
        share_half(at)
    for at in (3, 0, 1, 2):
        share_end(at)

    @pl.when(side == 1)
    def _():
        @pl.loop(0, groups)
        def _(at):
            branch_copy(2 * at).wait_send()

    for at in range(4):
        core_copy(at).wait_send()
        side_copy(at).wait_send()
        row_copy(at).wait_send()
        half_copy(at).wait_send()

        @pl.loop(1, groups)
        def _(mask):
            line_copy(at, mask).wait_send()

    inner_copy.wait()
    outer_copy.wait()
    early_store.wait()


def run_finish(exp_size, rep_size, home, branch, branch_got, pick, hidden, cotangent, tokens, gain_row, qkv, probs, normed_a, context, attn_w, outer_send, outer_got, inner_sum):
    rows_n, width = tokens.shape
    low = jnp.bfloat16
    wide = jnp.float32
    half = width // 2
    groups = exp_size // 2
    block = width // exp_size
    anyplace = pl.BlockSpec(memory_space=pl.ANY)
    inside = pl.BlockSpec(memory_space=pltpu.VMEM)
    dma = pltpu.SemaphoreType.DMA
    shape = jax.ShapeDtypeStruct
    return pl.pallas_call(
        functools.partial(finish_kernel, exp_size, rep_size),
        out_shape=(
            shape((rows_n, width), low),
            shape((rows_n, width), wide),
            shape((4, block, width), wide),
            shape((outer_send.shape[0] + EARLY, width), low),
            shape(inner_sum.shape[1:], low),
        ),
        in_specs=[inside, anyplace, anyplace, inside, anyplace, inside, anyplace, inside]
        + [anyplace] * 8,
        out_specs=(inside,) * 3 + (anyplace,) * 2,
        scratch_shapes=[
            pltpu.VMEM((rows_n, width), wide),
            pltpu.VMEM((rows_n, width), low),
            pltpu.VMEM(qkv.shape, low),
            pltpu.VMEM(probs.shape, low),
            pltpu.VMEM((rows_n, width), low),
            pltpu.VMEM((rows_n, width), low),
            pltpu.VMEM((width, rows_n), low),
            pltpu.VMEM((width, rows_n), low),
            pltpu.VMEM(pick.shape[:1] + (width,), low),
            pltpu.VMEM((EARLY, width), low),
            pltpu.VMEM((4, width, width), low),
            pltpu.VMEM((rows_n, width), wide),
            pltpu.VMEM((rows_n, width), low),
            pltpu.VMEM((rows_n, width), low),
            pltpu.VMEM((3, rows_n, width), low),
            pltpu.VMEM((4, width, half), wide),
            pltpu.VMEM((4, width, half), low),
            pltpu.VMEM((4, width, half), low),
            pltpu.VMEM((4, width // 2, half), low),
            pltpu.VMEM((4, width // 2, half), low),
            pltpu.VMEM((4, width // 2, half), low),
            pltpu.VMEM((4, width // 2, half), low),
            pltpu.VMEM((4, block, half), wide),
            pltpu.VMEM((4, block, half), low),
            pltpu.VMEM((4, block, half), low),
            pltpu.VMEM((4, block, half), wide),
            pltpu.VMEM((4, block, half), wide),
            dma((9,)),
            dma((exp_size,)),
            dma((groups,)),
            dma((2,)),
            dma((2,)),
            dma((4,)),
            dma((4,)),
            dma((4,)),
            dma((4,)),
            dma((4, groups)),
            dma((4, groups)),
            dma((4,)),
            dma((4,)),
            dma((4,)),
            dma((4,)),
        ],
        compiler_params=pltpu.CompilerParams(
            collective_id=2, has_side_effects=True, vmem_limit_bytes=60 << 20
        ),
        cost_estimate=pl.CostEstimate(
            flops=20 * rows_n * width * width, bytes_accessed=60 << 20, transcendentals=0
        ),
        name="finish",
    )(
        home,
        branch,
        branch_got,
        pick,
        hidden,
        cotangent,
        tokens,
        gain_row,
        qkv,
        probs,
        normed_a,
        context,
        attn_w,
        outer_send,
        outer_got,
        inner_sum,
    )


def shards(
    tokens,
    cotangent,
    doc_lengths,
    expert_of_token,
    w_query,
    w_key,
    w_value,
    w_output,
    attn_gain,
    w_inner,
    w_outer,
    expert_gain,
    centroids,
):
    exp_size = lax.axis_size("exp")
    rep_size = lax.axis_size("rep")
    row_count = tokens.shape[0]
    wide = jnp.float32

    slots = -(-3 * row_count // exp_size // 16) * 16
    (
        attn_w,
        inner_w,
        outer_w,
        arrived,
        spread,
        cents,
        gains_e,
        packed,
        hidden,
        qkv,
        probs,
        normed_a,
        context,
        pick,
        gain_row,
    ) = run_attend(
        exp_size,
        rep_size,
        slots,
        tokens,
        cotangent,
        doc_lengths,
        expert_of_token[None],
        (w_query, w_key, w_value, w_output),
        attn_gain[None],
        w_inner[0],
        w_outer[0],
        expert_gain,
        centroids,
    )
    home, branch, branch_got, outer_keep, outer_send, outer_got, inner_sum, centre_parts = run_experts(
        exp_size,
        rep_size,
        slots,
        2 * row_count,
        arrived,
        packed,
        inner_w,
        outer_w,
        w_inner[0],
        w_outer[0],
        spread,
        cents,
        gains_e,
    )
    output, grad_tokens, shares, outer_recv, inner_recv = run_finish(
        exp_size,
        rep_size,
        home,
        branch,
        branch_got,
        pick,
        hidden,
        cotangent,
        tokens,
        gain_row,
        qkv,
        probs,
        normed_a,
        context,
        attn_w,
        outer_send,
        outer_got,
        inner_sum,
    )
    grad_centroids = jnp.sum(centre_parts.reshape(rep_size, 8, -1)[:, 0], axis=0)[None]
    grad_w_outer = (outer_keep.astype(wide) + outer_recv.astype(wide))[None]
    summed = inner_sum[0].astype(wide) + inner_recv.astype(wide)
    grad_w_inner = summed[None]
    grad_expert_gain = jnp.sum(summed * w_inner[0].astype(wide), axis=1)[None] / expert_gain.astype(
        wide
    )
    share_gain = sum(
        jnp.sum(shares[i] * w.astype(wide), axis=1) for i, w in enumerate((w_query, w_key, w_value))
    ) / attn_gain.astype(wide)
    return (
        output,
        grad_tokens,
        shares[0],
        shares[1],
        shares[2],
        shares[3],
        share_gain,
        grad_w_inner,
        grad_w_outer,
        grad_expert_gain,
        grad_centroids,
    )


def solution(mesh):
    placed = (
        P(("rep", "exp"), None),
        P(("rep", "exp"), None),
        P(("rep", "exp"), None),
        P(("rep", "exp")),
        P("exp", None),
        P("exp", None),
        P("exp", None),
        P("exp", None),
        P("exp"),
        P("exp", "rep", None),
        P("exp", "rep", None),
        P("exp", "rep"),
        P("exp", "rep"),
    )
    return jax.shard_map(
        shards,
        mesh=mesh,
        in_specs=placed,
        out_specs=(
            P(("rep", "exp"), None),
            P(("rep", "exp"), None),
            P("exp", None),
            P("exp", None),
            P("exp", None),
            P("exp", None),
            P("exp"),
            P("exp", "rep", None),
            P("exp", "rep", None),
            P("exp", "rep"),
            P("exp", "rep"),
        ),
        check_vma=False,
    )
```

```python
import functools

import jax
import jax.numpy as jnp
from jax import lax
from jax.experimental import pallas as pl
from jax.experimental.pallas import tpu as pltpu
from jax.sharding import PartitionSpec as P

HEADS = 16
EPS = 1e-05
ROOT_HALF = 0.7071067811865476
INV_ROOT_TAU = 0.3989422804014327
CHUNKS = 4
DEFER = 384
EARLY = 512


MESH = pl.DeviceIdType.MESH
TILE = 256
ROWS = 128
BIG = 2048


def remote(src, dst, send_sem, recv_sem, device):
    return pltpu.make_async_remote_copy(
        src_ref=src,
        dst_ref=dst,
        send_sem=send_sem,
        recv_sem=recv_sem,
        device_id=device,
        device_id_type=MESH,
    )


def row_stats(rows):
    row_mean = jnp.mean(rows, axis=-1, keepdims=True)
    centered = rows - row_mean
    variance = jnp.mean(centered * centered, axis=-1, keepdims=True)
    inv_scale = lax.rsqrt(variance + EPS)
    return centered * inv_scale, inv_scale


def attend_kernel(
    exp_size,
    rep_size,
    slots,
    tokens,
    cotangent,
    doc,
    expert_of,
    w_query,
    w_key,
    w_value,
    w_output,
    gain_a,
    w_inner,
    w_outer,
    gain_e,
    cent,
    attn_w,
    inner_w,
    outer_w,
    arrived,
    spread_h,
    cents,
    gains_e,
    packed_h,
    hidden_h,
    qkv_h,
    probs_h,
    normed_h,
    context_h,
    pick,
    gain_row,
    hidden,
    qkv,
    probs,
    normed_a,
    context,
    weights,
    staging,
    spread_m,
    offsets,
    small_all,
    gain_v,
    packed_x,
    packed_c,
    bias,
    counts_v,
    cent_v,
    own_s,
    line_s,
    line_r,
    side_s,
    side_r,
    core_s,
    core_r,
    weight_s,
    weight_r,
    disp_s,
    disp_r,
    count_s,
    count_r,
    cent_s,
    cent_r,
    gain_s,
    gain_r,
    out_s,
):
    low = jnp.bfloat16
    wide = jnp.float32
    rep_at = lax.axis_index("rep")
    exp_at = lax.axis_index("exp")
    core = rep_at % 2
    group = exp_at // 2
    side = exp_at % 2
    groups = exp_size // 2
    rows_n, width = tokens.shape
    half = width // 2
    block = w_query.shape[0]
    depth = w_inner.shape[0]
    ff_block = w_outer.shape[0]
    core_peer = (rep_at ^ 1, exp_at)
    side_peer = (rep_at, exp_at ^ 1)

    def block_rows(at):
        return pl.ds(pl.multiple_of(at * block, block), block)

    own_loads = []
    for at, source in enumerate((w_query, w_key, w_value, w_output)):
        own_loads.append(
            pltpu.make_async_copy(source, weights.at[at, block_rows(exp_at)], own_s.at[at])
        )
    for load in own_loads:
        load.start()

    barrier = pltpu.get_barrier_semaphore()
    for mask in range(1, rep_size):
        for flip in range(2):
            pl.semaphore_signal(
                barrier, inc=1, device_id=(rep_at ^ mask, exp_at ^ flip), device_id_type=MESH
            )

    @pl.loop(1, exp_size)
    def _(at):
        pl.semaphore_signal(barrier, inc=1, device_id=(rep_at, exp_at ^ at), device_id_type=MESH)

    pl.semaphore_wait(barrier, exp_size - 1 + 2 * (rep_size - 1))

    outer_copy = remote(
        w_outer.at[: ff_block - DEFER],
        outer_w,
        weight_s.at[0],
        weight_r.at[0],
        (rep_at ^ 2, exp_at),
    )

    for load in own_loads:
        load.wait()

    picks = (slice(0, 3), slice(3, 4))
    own_half = pl.ds(pl.multiple_of(core * half, half), half)

    def view(kind, at):
        return weights.at[picks[kind], block_rows(at), own_half]

    def line_copy(kind, source, step):
        at = 2 * source + side
        return remote(
            view(kind, at),
            view(kind, at),
            line_s.at[kind, (1 + step) // 2, source],
            line_r.at[kind, source],
            (rep_at, exp_at + 2 * step),
        )

    def line_wait(kind, source):
        at = 2 * source + side
        remote(
            view(kind, at), view(kind, at), line_s.at[kind, 0, source], line_r.at[kind, source], side_peer
        ).wait_recv()

    def side_copy(kind, source):
        at = 2 * source + side
        return remote(
            view(kind, at), view(kind, at), side_s.at[kind, source], side_r.at[kind, source], side_peer
        )

    def side_wait(kind, source):
        at = 2 * source + 1 - side
        remote(
            view(kind, at), view(kind, at), side_s.at[kind, source], side_r.at[kind, source], side_peer
        ).wait_recv()

    def core_copy(kind, at):
        return remote(view(kind, at), view(kind, at), core_s.at[kind, at], core_r.at[kind, at], core_peer)

    def core_wait(kind, at):
        other = pl.ds(pl.multiple_of((1 - core) * half, half), half)
        there = weights.at[picks[kind], block_rows(at), other]
        remote(there, there, core_s.at[kind, at], core_r.at[kind, at], core_peer).wait_recv()

    def first_sends(kind):
        @pl.when(group + 1 < groups)
        def _():
            line_copy(kind, group, 1).start()

        @pl.when(group >= 1)
        def _():
            line_copy(kind, group, -1).start()

        side_copy(kind, group).start()

    def take_side(kind, source):
        side_wait(kind, source)
        core_copy(kind, 2 * source + 1 - side).start()

    def gather_step(kind, step):
        @pl.when(group - step >= 0)
        def _():
            source = group - step
            line_wait(kind, source)

            @pl.when(group + 1 < groups)
            def _():
                line_copy(kind, source, 1).start()

            side_copy(kind, source).start()
            core_copy(kind, 2 * source + side).start()

        @pl.when(group + step < groups)
        def _():
            source = group + step
            line_wait(kind, source)

            @pl.when(group >= 1)
            def _():
                line_copy(kind, source, -1).start()

            side_copy(kind, source).start()
            core_copy(kind, 2 * source + side).start()

        @pl.when(group - step + 1 >= 0)
        def _():
            take_side(kind, group - step + 1)

        @pl.when((step > 1) & (group + step - 1 < groups))
        def _():
            take_side(kind, group + step - 1)

    def gather_end(kind):
        last = groups - 1

        @pl.when(group - last >= 0)
        def _():
            take_side(kind, group - last)

        @pl.when((groups > 1) & (group + last < groups))
        def _():
            take_side(kind, group + last)

        @pl.loop(0, exp_size)
        def _(at):
            @pl.when(at != exp_at)
            def _():
                core_wait(kind, at)

    first_sends(0)
    first_sends(1)

    inner_rows = pl.ds(pl.multiple_of(rep_at * depth, depth), depth)

    def ff_cols(at):
        return pl.ds(pl.multiple_of(at * ff_block, ff_block), ff_block)

    def inner_copies(mask):
        dest = rep_at ^ mask
        found = []
        for part in range(2):
            source = w_inner.at[:, ff_cols(dest ^ (2 * part))]
            cols = slice(part * ff_block, (part + 1) * ff_block)
            at = 1 + 2 * mask + part
            if mask == 3:
                found.append(
                    remote(
                        source,
                        staging.at[:, cols],
                        weight_s.at[at],
                        weight_r.at[at],
                        (rep_at ^ 2, exp_at),
                    )
                )
            else:
                found.append(
                    remote(
                        source,
                        inner_w.at[inner_rows, cols],
                        weight_s.at[at],
                        weight_r.at[at],
                        (dest, exp_at),
                    )
                )
        return found

    far_rows = pl.ds(pl.multiple_of((rep_at ^ 2) * depth, depth), depth)
    forward_copy = remote(
        staging,
        inner_w.at[far_rows],
        weight_s.at[1 + 2 * rep_size],
        weight_r.at[1 + 2 * rep_size],
        core_peer,
    )

    for mask in (3, 2, 1):
        for copy in inner_copies(mask):
            copy.start()
    outer_copy.start()

    lanes = counts_v.shape[1]
    expert_row = expert_of[...]
    onehot = (
        lax.broadcasted_iota(jnp.int32, (lanes, rows_n), 0) == expert_row
    ).astype(wide)
    before = (
        lax.broadcasted_iota(jnp.int32, (rows_n, rows_n), 0)
        < lax.broadcasted_iota(jnp.int32, (rows_n, rows_n), 1)
    ).astype(low)
    earlier = jnp.dot(onehot.astype(low), before, preferred_element_type=wide)
    rank = jnp.sum(earlier * onehot, axis=0, keepdims=True).astype(jnp.int32)
    position = expert_row * slots + rank
    pick[...] = (
        lax.broadcasted_iota(jnp.int32, pick.shape, 0) == position
    ).astype(wide).astype(low)
    counts_v[...] = jnp.zeros_like(counts_v)
    counts_v[:8, :] = lax.dot_general(
        jnp.ones((8, rows_n), low),
        onehot.astype(low),
        (((1,), (1,)), ((), ())),
        preferred_element_type=wide,
    )
    counts_v[8:, :block] = jnp.broadcast_to(gain_a[...].astype(wide), (8, block))
    cent_v[...] = jnp.broadcast_to(cent[...].astype(wide), cent_v.shape)
    gain_v[...] = jnp.broadcast_to(gain_e[...].astype(wide), gain_v.shape)

    def eight(at):
        return pl.ds(pl.multiple_of(at * 8, 8), 8)

    def sixteen(at):
        return pl.ds(pl.multiple_of(at * 16, 16), 16)

    def count_copy(dest):
        return remote(
            counts_v, small_all.at[sixteen(exp_at)], count_s.at[dest], count_r.at[exp_at], (rep_at, dest)
        )

    count_own = pltpu.make_async_copy(counts_v, small_all.at[sixteen(exp_at)], count_s.at[exp_at])
    count_own.start()

    @pl.loop(1, exp_size)
    def _(at):
        count_copy(exp_at ^ at).start()

    cent_at = side * rep_size + rep_at

    def cent_copy(mask, flip):
        return remote(
            cent_v,
            cents.at[eight(cent_at)],
            cent_s.at[flip * rep_size + mask],
            cent_r.at[flip * rep_size + mask],
            (rep_at ^ mask, exp_at ^ flip),
        )

    cent_own = pltpu.make_async_copy(cent_v, cents.at[eight(cent_at)], cent_s.at[0])
    cent_own.start()
    cent_pairs = [(m, f) for m in range(rep_size) for f in range(2) if m or f]
    for mask, flip in cent_pairs:
        cent_copy(mask, flip).start()

    def gain_copy(mask):
        return remote(
            gain_v, gains_e.at[eight(rep_at)], gain_s.at[mask], gain_r.at[mask], (rep_at ^ mask, exp_at)
        )

    gain_own = pltpu.make_async_copy(gain_v, gains_e.at[eight(rep_at)], gain_s.at[0])
    gain_own.start()
    for mask in range(1, rep_size):
        gain_copy(mask).start()

    count_own.wait()

    @pl.loop(1, exp_size)
    def _(at):
        source = exp_at ^ at
        remote(
            counts_v, small_all.at[sixteen(source)], count_s.at[source], count_r.at[source], (rep_at, source)
        ).wait()

    tiled = jnp.dot(
        small_all[...].astype(low),
        (
            lax.broadcasted_iota(jnp.int32, (lanes, width), 1) % block
            == lax.broadcasted_iota(jnp.int32, (lanes, width), 0)
        ).astype(wide).astype(low),
        preferred_element_type=wide,
    )
    chosen_row = lax.broadcasted_iota(jnp.int32, (16 * exp_size, width), 0) == (
        16 * (lax.broadcasted_iota(jnp.int32, (16 * exp_size, width), 1) // block) + 8
    )
    gain_row[...] = jnp.sum(jnp.where(chosen_row, tiled, 0.0), axis=0, keepdims=True)

    @pl.loop(0, rows_n // ROWS)
    def _(step):
        here = pl.ds(pl.multiple_of(step * ROWS, ROWS), ROWS)
        unit, _ = row_stats(tokens[here, :].astype(wide))
        normed_a[here, :] = (unit * gain_row[...]).astype(low)

    down = lax.broadcasted_iota(jnp.int32, (rows_n, rows_n), 0)
    along = lax.broadcasted_iota(jnp.int32, (rows_n, rows_n), 1)
    end = jnp.int32(0)
    seg_down = jnp.zeros((rows_n, rows_n), jnp.int32)
    seg_along = jnp.zeros((rows_n, rows_n), jnp.int32)
    for at in range(doc.shape[1]):
        end = end + doc[0, at]
        seg_down = seg_down + (down >= end).astype(jnp.int32)
        seg_along = seg_along + (along >= end).astype(jnp.int32)
    bias[...] = jnp.where((seg_down == seg_along) & (down >= along), 0.0, -1e30)

    @pl.loop(1, groups)
    def _(step):
        gather_step(0, step)

    gather_end(0)

    def slot_rows(at):
        return pl.ds(pl.multiple_of(at * slots, slots), slots)

    def disp_copy(source, dest):
        return remote(
            source.at[slot_rows(dest // 2)],
            arrived.at[slot_rows(exp_at)],
            disp_s.at[dest],
            disp_r.at[exp_at],
            (rep_at, dest),
        )

    def dispatch(source, flip):
        @pl.loop(0, groups)
        def _(at):
            dest = 2 * (group ^ at) + flip

            @pl.when(dest != exp_at)
            def _():
                disp_copy(source, dest).start()

            @pl.when(dest == exp_at)
            def _():
                pltpu.make_async_copy(
                    source.at[slot_rows(group)], arrived.at[slot_rows(exp_at)], disp_s.at[exp_at]
                ).start()

    @pl.loop(1, 1 + (groups - 1 + 2) // 3)
    def _(step):
        gather_step(1, step)

    for at in range(3):

        @pl.loop(0, width // TILE)
        def _(step):
            cols = pl.ds(pl.multiple_of(step * TILE, TILE), TILE)
            qkv[at, :, cols] = jnp.dot(
                normed_a[...], weights[at, :, cols], preferred_element_type=wide
            ).astype(low)

    head_dim = width // HEADS
    pair = 2 * head_dim
    factor = head_dim ** (-0.5)
    lane = lax.broadcasted_iota(jnp.int32, (rows_n, pair), 1)
    pairs = HEADS // 2
    parts = 2
    begun = (groups - 1 + 2) // 3
    for part in range(parts):
        low_step = 1 + begun + part * (groups - 1 - begun) // parts
        high_step = 1 + begun + (part + 1) * (groups - 1 - begun) // parts

        @pl.loop(low_step, high_step)
        def _(step):
            gather_step(1, step)

        @pl.loop(part * pairs // parts, (part + 1) * pairs // parts)
        def _(at):
            cols = pl.ds(pl.multiple_of(at * pair, pair), pair)
            q_pair = qkv[0, :, cols]
            k_pair = qkv[1, :, cols]
            v_pair = qkv[2, :, cols]
            found = []
            for which in range(2):
                chosen = (lane >= head_dim) if which else (lane < head_dim)
                q_one = jnp.where(chosen, q_pair, jnp.zeros_like(q_pair))
                scores = (
                    lax.dot_general(
                        q_one, k_pair, (((1,), (1,)), ((), ())), preferred_element_type=wide
                    )
                    * factor
                    + bias[...]
                )
                top = jnp.max(scores, axis=1, keepdims=True)
                raised = jnp.exp(scores - top)
                total = jnp.sum(raised, axis=1, keepdims=True)
                prob = (raised * (1.0 / total)).astype(low)
                probs[pl.ds(pl.multiple_of((2 * at + which) * rows_n, rows_n), rows_n), :] = prob
                found.append(jnp.dot(prob, v_pair, preferred_element_type=wide))
            context[:, cols] = jnp.where(lane < head_dim, found[0], found[1]).astype(low)

    @pl.loop(0, width // TILE)
    def _(step):
        cols = pl.ds(pl.multiple_of(step * TILE, TILE), TILE)
        packed_c[:, cols] = jnp.dot(
            pick[...], cotangent[:, cols], preferred_element_type=wide
        ).astype(low)

    gather_end(1)
    stores = [
        pltpu.make_async_copy(source, target, out_s.at[at])
        for at, (source, target) in (
            (0, (weights, attn_w)),
            (2, (qkv, qkv_h)),
            (3, (probs, probs_h)),
            (4, (normed_a, normed_h)),
            (5, (context, context_h)),
            (7, (packed_c, packed_h)),
            (6, (hidden, hidden_h)),
        )
    ]
    for store in stores[:-1]:
        store.start()

    @pl.loop(0, width // TILE)
    def _(step):
        cols = pl.ds(pl.multiple_of(step * TILE, TILE), TILE)
        sum_here = tokens[:, cols].astype(wide) + jnp.dot(
            context[...], weights[3, :, cols], preferred_element_type=wide
        )
        hidden[:, cols] = sum_here
        packed_x[:, cols] = jnp.dot(
            pick[...], sum_here.astype(low), preferred_element_type=wide
        ).astype(low)

    dispatch(packed_x, 0)
    stores[-1].start()

    counted = small_all.shape[0]
    own_rows = spread_m.shape[1]
    count_lane = lax.broadcasted_iota(jnp.int32, (counted, 128), 1)
    mine = jnp.sum(
        jnp.where(count_lane == group, small_all[...], 0.0), axis=1, keepdims=True
    )
    mine = jnp.broadcast_to(mine, (counted, 128))
    table_down = lax.broadcasted_iota(jnp.int32, (counted, counted), 0)
    table_along = lax.broadcasted_iota(jnp.int32, (counted, counted), 1)
    ahead = ((table_along // 16 < table_down // 16) & (table_along % 16 == 0)).astype(wide).astype(low)
    offsets[0] = jnp.dot(ahead, mine.astype(low), preferred_element_type=wide)
    offsets[1] = mine
    slot_iota = lax.broadcasted_iota(jnp.int32, (slots, own_rows), 0)
    row_iota = lax.broadcasted_iota(jnp.int32, (slots, own_rows), 1)

    @pl.loop(0, exp_size)
    def _(at):
        eight = pl.ds(pl.multiple_of(at * 16, 16), 8)
        start = offsets[0, eight, :][:1, :1].astype(jnp.int32)
        limit = offsets[1, eight, :][:1, :1].astype(jnp.int32)
        spread_m[slot_rows(at), :] = (
            ((slot_iota + start) == row_iota) & (slot_iota < limit)
        ).astype(wide).astype(low)

    spread_store = pltpu.make_async_copy(spread_m, spread_h, out_s.at[1])
    spread_store.start()
    for copy in inner_copies(3):
        copy.wait_recv()
    forward_copy.start()

    for store in stores:
        store.wait()
    outer_copy.wait()
    forward_copy.wait()
    for mask in range(1, rep_size):
        for copy in inner_copies(mask):
            if mask == 3:
                copy.wait_send()
            else:
                copy.wait()
    for kind in range(2):
        side_copy(kind, group).wait_send()

        @pl.loop(0, groups)
        def _(source):
            @pl.when(source != group)
            def _():
                side_copy(kind, source).wait_send()

            @pl.when((source <= group) & (group + 1 < groups))
            def _():
                line_copy(kind, source, 1).wait_send()

            @pl.when((source >= group) & (group >= 1))
            def _():
                line_copy(kind, source, -1).wait_send()

        @pl.loop(0, exp_size)
        def _(at):
            @pl.when(at != exp_at)
            def _():
                core_copy(kind, at).wait_send()

    spread_store.wait()
    cent_own.wait()
    gain_own.wait()
    for mask in range(1, rep_size):
        gain_copy(mask).wait()
    for mask, flip in cent_pairs:
        cent_copy(mask, flip).wait()

    def disp_wait(source):
        return remote(
            packed_x.at[slot_rows(source // 2)],
            arrived.at[slot_rows(source)],
            disp_s.at[source],
            disp_r.at[source],
            (rep_at, source),
        )

    @pl.loop(0, groups)
    def _(at):
        @pl.when(2 * at != exp_at)
        def _():
            disp_wait(2 * at).wait_send()

    @pl.when(side == 0)
    def _():
        pltpu.make_async_copy(
            packed_x.at[slot_rows(group)], arrived.at[slot_rows(exp_at)], disp_s.at[exp_at]
        ).wait()

        @pl.loop(1, exp_size)
        def _(at):
            disp_wait(exp_at ^ at).wait_recv()


def run_attend(exp_size, rep_size, slots, tokens, cotangent, doc, expert_of, attn, gain_a, w_inner, w_outer, gain_e, cent):
    rows_n, width = tokens.shape
    low = jnp.bfloat16
    wide = jnp.float32
    groups = exp_size // 2
    depth = w_inner.shape[0]
    ff_block = w_outer.shape[0]
    anyplace = pl.BlockSpec(memory_space=pl.ANY)
    inside = pl.BlockSpec(memory_space=pltpu.VMEM)
    dma = pltpu.SemaphoreType.DMA
    shape = jax.ShapeDtypeStruct
    return pl.pallas_call(
        functools.partial(attend_kernel, exp_size, rep_size, slots),
        out_shape=(
            shape((4, width, width), low),
            shape((width, 2 * ff_block), low),
            shape((ff_block - DEFER, width), low),
            shape((exp_size * slots, width), low),
            shape((exp_size * slots, 2 * rows_n), low),
            shape((2 * rep_size * 8, cent.shape[1]), wide),
            shape((rep_size * 8, depth), wide),
            shape((groups * slots, width), low),
            shape((rows_n, width), wide),
            shape((3, rows_n, width), low),
            shape((HEADS * rows_n, rows_n), low),
            shape((rows_n, width), low),
            shape((rows_n, width), low),
            shape((groups * slots, rows_n), low),
            shape((1, width), wide),
        ),
        in_specs=[inside, inside, pl.BlockSpec(memory_space=pltpu.SMEM), inside]
        + [anyplace] * 4
        + [inside, anyplace, anyplace, inside, inside],
        out_specs=(anyplace,) * 13 + (inside,) * 2,
        scratch_shapes=[
            pltpu.VMEM((rows_n, width), wide),
            pltpu.VMEM((3, rows_n, width), low),
            pltpu.VMEM((HEADS * rows_n, rows_n), low),
            pltpu.VMEM((rows_n, width), low),
            pltpu.VMEM((rows_n, width), low),
            pltpu.VMEM((4, width, width), low),
            pltpu.VMEM((depth, 2 * ff_block), low),
            pltpu.VMEM((exp_size * slots, 2 * rows_n), low),
            pltpu.VMEM((2, exp_size * 16, 128), wide),
            pltpu.VMEM((exp_size * 16, 128), wide),
            pltpu.VMEM((8, depth), wide),
            pltpu.VMEM((groups * slots, width), low),
            pltpu.VMEM((groups * slots, width), low),
            pltpu.VMEM((rows_n, rows_n), wide),
            pltpu.VMEM((16, 128), wide),
            pltpu.VMEM((8, cent.shape[1]), wide),
            dma((6,)),
            dma((2, 2, groups)),
            dma((2, groups)),
            dma((2, groups)),
            dma((2, groups)),
            dma((2, exp_size)),
            dma((2, exp_size)),
            dma((2 + 2 * rep_size,)),
            dma((2 + 2 * rep_size,)),
            dma((exp_size,)),
            dma((exp_size,)),
            dma((exp_size,)),
            dma((exp_size,)),
            dma((2 * rep_size,)),
            dma((2 * rep_size,)),
            dma((rep_size,)),
            dma((rep_size,)),
            dma((8,)),
        ],
        compiler_params=pltpu.CompilerParams(
            collective_id=1, has_side_effects=True, vmem_limit_bytes=56 << 20
        ),
        cost_estimate=pl.CostEstimate(
            flops=10 * rows_n * width * width,
            bytes_accessed=40 << 20,
            transcendentals=HEADS * rows_n * rows_n,
        ),
        name="attend",
    )(tokens, cotangent, doc, expert_of, *attn, gain_a, w_inner, w_outer, gain_e, cent)


def expert_kernel(
    exp_size,
    rep_size,
    slots,
    arrived_h,
    packed_h,
    inner_h,
    outer_h,
    w_inner,
    w_outer,
    spread_h,
    cents,
    gains_e,
    home,
    branch,
    branch_got,
    outer_keep,
    outer_send,
    outer_got,
    inner_sum,
    centre_parts,
    arrived,
    spread_m,
    cent_b,
    gain,
    centre_grad,
    centre_v,
    inner_w,
    outer_w,
    own_x,
    own_cot,
    normed,
    active,
    slope,
    states,
    part_send,
    part_recv,
    hop,
    back,
    spread,
    relay,
    acc,
    gates,
    gate_grads,
    outer_keep_v,
    outer_send_v,
    inner_send_v,
    load_sem,
    disp_s,
    disp_r,
    bran_s,
    bran_r,
    centre_s,
    centre_r,
    norm_s,
    norm_r,
    state_s,
    state_r,
    part_s,
    part_r,
    grad_s,
    grad_r,
    hop_s,
    hop_r,
    gate_s,
    gate_r,
    ret_s,
    ret_r,
    relay_s,
    relay_r,
    early_s,
    early_r,
    out_sem,
    inner_s,
    out_r,
):
    low = jnp.bfloat16
    wide = jnp.float32
    rep_at = lax.axis_index("rep")
    exp_at = lax.axis_index("exp")
    first = exp_at % 2 == 0
    second = exp_at % 2 == 1
    core_peer = (rep_at ^ 1, exp_at)
    side_peer = (rep_at, exp_at ^ 1)
    width = own_x.shape[1]
    own_rows = own_x.shape[0]
    part = own_rows // CHUNKS
    wide_ff = inner_w.shape[1]
    block = wide_ff // 2
    depth = width // rep_size

    def slot_rows(at):
        return pl.ds(pl.multiple_of(at * slots, slots), slots)

    def inner_rows(mask):
        return pl.ds(pl.multiple_of((rep_at ^ mask) * depth, depth), depth)

    rows_load = pltpu.make_async_copy(arrived_h, arrived, load_sem.at[0])
    spread_load = pltpu.make_async_copy(spread_h, spread_m, load_sem.at[8])
    spread_load.start()

    @pl.when(first)
    def _():
        rows_load.start()

    loads = [
        pltpu.make_async_copy(w_outer, outer_w.at[:block], load_sem.at[1]),
        pltpu.make_async_copy(outer_h, outer_w.at[block : 2 * block - DEFER], load_sem.at[2]),
    ]
    for side in range(2):
        at = rep_at ^ (2 * side)
        loads.append(
            pltpu.make_async_copy(
                w_inner.at[:, pl.ds(pl.multiple_of(at * block, block), block)],
                inner_w.at[inner_rows(0), side * block : (side + 1) * block],
                load_sem.at[3 + side],
            )
        )
    for mask in range(1, rep_size):
        loads.append(
            pltpu.make_async_copy(
                inner_h.at[inner_rows(mask)], inner_w.at[inner_rows(mask)], load_sem.at[4 + mask]
            )
        )
    for load in loads:
        load.start()

    barrier = pltpu.get_barrier_semaphore()
    for mask in range(1, rep_size):
        for flip in range(2):
            pl.semaphore_signal(
                barrier, inc=1, device_id=(rep_at ^ mask, exp_at ^ flip), device_id_type=MESH
            )

    @pl.loop(1, exp_size)
    def _(at):
        pl.semaphore_signal(barrier, inc=1, device_id=(rep_at, exp_at ^ at), device_id_type=MESH)

    group = exp_at // 2
    pl.semaphore_wait(barrier, exp_size - 1 + 2 * (rep_size - 1))
    row_peer = (rep_at ^ 2, exp_at)
    late_copy = remote(
        w_outer.at[block - DEFER :],
        outer_w.at[2 * block - DEFER :],
        early_s.at[0],
        early_r.at[0],
        row_peer,
    )
    late_copy.start()

    def disp_copy(which):
        return remote(
            packed_h.at[slot_rows(which)],
            arrived.at[slot_rows(exp_at)],
            disp_s.at[which],
            disp_r.at[exp_at],
            (rep_at, 2 * which + 1),
        )

    disp_own = pltpu.make_async_copy(
        packed_h.at[slot_rows(group)], arrived.at[slot_rows(exp_at)], disp_s.at[group]
    )

    @pl.loop(0, exp_size // 2)
    def _(step):
        which = group ^ (exp_size // 2 - 1 - step)

        @pl.when(2 * which + 1 != exp_at)
        def _():
            disp_copy(which).start()

        @pl.when(2 * which + 1 == exp_at)
        def _():
            disp_own.start()

    piece = cents.shape[1]
    for at in range(width // piece):
        cent_b[:, at * piece : (at + 1) * piece] = jnp.broadcast_to(
            cents[at * 8 : at * 8 + 1, :], (cent_b.shape[0], piece)
        ).astype(low)
    for at in range(rep_size):
        gain[:, at * depth : (at + 1) * depth] = gains_e[at * 8 : at * 8 + 1, :]
    def compact_rows():
        return lax.dot_general(
            spread_m[...], arrived[...], (((0,), (0,)), ((), ())), preferred_element_type=wide
        ).astype(low)

    spread_load.wait()

    @pl.when(first)
    def _():
        rows_load.wait()
        own_x[...] = compact_rows()


    gate_copy = remote(gates, gates, gate_s.at[0], gate_r.at[0], side_peer)

    def part_rows(at):
        return pl.ds(pl.multiple_of(at * part, part), part)

    def both_rows(at):
        return pl.ds(pl.multiple_of(at * 2 * part, 2 * part), 2 * part)

    def own_slice(at):
        return pl.ds(pl.multiple_of(at * 2 * part + part, part), part)

    def other_slice(at):
        return pl.ds(pl.multiple_of(at * 2 * part, part), part)

    def grad_copy(at):
        rows = part_rows(at)
        return remote(
            gate_grads.at[rows], gate_grads.at[rows], grad_s.at[at], grad_r.at[at], side_peer
        )

    def hop_forward(at):
        rows = part_rows(at)
        return remote(hop.at[rows], own_x.at[rows], hop_s.at[at], hop_r.at[at], side_peer)

    def hop_backward(at):
        return remote(
            hop.at[part_rows(at)], states.at[own_slice(at)], hop_s.at[at], hop_r.at[at], side_peer
        )

    def norm_copy(at):
        return remote(
            normed.at[own_slice(at)], normed.at[other_slice(at)], norm_s.at[at], norm_r.at[at], core_peer
        )

    def state_copy(at):
        return remote(
            states.at[own_slice(at)], states.at[other_slice(at)], state_s.at[at], state_r.at[at], core_peer
        )

    def part_copy(kind, at):
        count = kind * CHUNKS + at
        rows = part_rows(count)
        return remote(
            part_send.at[rows], part_recv.at[rows], part_s.at[count], part_r.at[count], core_peer
        )

    def norm_rows(at):
        @pl.loop(0, part // ROWS)
        def _(step):
            off = pl.multiple_of(step * ROWS, ROWS)
            unit, _ = row_stats(own_x[pl.ds(at * part + off, ROWS), :].astype(wide))
            normed[pl.ds(at * 2 * part + part + off, ROWS), :] = (unit * gain[...]).astype(low)

        norm_copy(at).start()

    steps = 2 * CHUNKS

    def is_forward(step):
        early = step < CHUNKS
        mixed = (step == 0) | ((step % 2 == 1) & (step < steps - 1))
        return (first & early) | (second & mixed)

    def chunk_at(step):
        of_first = jnp.where(step < CHUNKS, step, step - CHUNKS)
        mixed = (step == 0) | ((step % 2 == 1) & (step < steps - 1))
        of_second = jnp.where(
            mixed,
            (step + 1) // 2,
            jnp.where(step == steps - 1, CHUNKS - 1, (step - 2) // 2),
        )
        return jnp.where(first, of_first, of_second)

    @pl.when(first)
    def _():
        @pl.loop(0, CHUNKS)
        def _(at):
            norm_rows(at)

        logit = lax.dot_general(
            own_x[...], cent_b[...], (((1,), (1,)), ((), ())), preferred_element_type=wide
        )
        gates[...] = jax.nn.sigmoid(logit)
        gate_copy.start()

    @pl.when(second)
    def _():
        hop_forward(0).wait_recv()
        norm_rows(0)

    def take_cotangent():
        disp_own.wait()

        @pl.loop(1, exp_size)
        def _(at):
            source = exp_at ^ at
            remote(
                packed_h.at[slot_rows(0)],
                arrived.at[slot_rows(source)],
                disp_s.at[0],
                disp_r.at[source],
                side_peer,
            ).wait_recv()

        own_cot[...] = compact_rows()
        gate_copy.wait_recv()

        @pl.loop(0, CHUNKS)
        def _(at):
            @pl.loop(0, part // ROWS)
            def _(step):
                off = pl.multiple_of(step * ROWS, ROWS)
                here = pl.ds(at * part + off, ROWS)
                states[pl.ds(at * 2 * part + part + off, ROWS), :] = (
                    gates[here, :][:, :1] * own_cot[here, :].astype(wide)
                ).astype(low)

            state_copy(at).start()

    for load in loads:
        load.wait()
    centre_grad[...] = jnp.zeros_like(centre_grad)

    def finish_forward(step, at):
        part_copy(0, at).wait_recv()

        @pl.loop(0, part // ROWS)
        def _(tile):
            off = pl.multiple_of(tile * ROWS, ROWS)
            here = pl.ds(at * part + off, ROWS)
            result = (
                own_x[here, :].astype(wide)
                + acc[step % 2, pl.ds(off, ROWS), :]
                + part_recv[here, :].astype(wide)
            )

            @pl.when(first)
            def _():
                hop[here, :] = result.astype(low)

            @pl.when(second)
            def _():
                cot = own_cot[here, :].astype(wide)
                back[here, :] = (gates[here, :][:, :1] * result).astype(low)
                gate_grads[here, :] = jnp.broadcast_to(
                    jnp.sum(cot * result, axis=1, keepdims=True), (ROWS, gate_grads.shape[1])
                )

        @pl.when(first)
        def _():
            hop_forward(at).start()

        @pl.when(second)
        def _():
            grad_copy(at).start()

    def finish_backward(step, at):
        part_copy(1, at).wait_recv()

        @pl.when(first)
        def _():
            grad_copy(at).wait_recv()

        @pl.loop(0, part // ROWS)
        def _(tile):
            off = pl.multiple_of(tile * ROWS, ROWS)
            here = pl.ds(at * part + off, ROWS)
            rows_in = own_x[here, :].astype(wide)
            unit, inv_scale = row_stats(rows_in)
            grad_unit = (
                acc[step % 2, pl.ds(off, ROWS), :]
                + part_recv[pl.ds((CHUNKS + at) * part + off, ROWS), :].astype(wide)
            ) * gain[...]
            grad_in = (
                grad_unit
                - jnp.mean(grad_unit, axis=-1, keepdims=True)
                - unit * jnp.mean(grad_unit * unit, axis=-1, keepdims=True)
            ) * inv_scale
            gate = gates[here, :][:, :1]

            @pl.when(second)
            def _():
                state = gate * own_cot[here, :].astype(wide) + grad_in
                hop[here, :] = state.astype(low)

            @pl.when(first)
            def _():
                state = states[pl.ds(at * 2 * part + part + off, ROWS), :].astype(wide) + grad_in
                grad_logit = gate_grads[here, :][:, :1] * gate * (1.0 - gate)
                back[here, :] = (state + grad_logit * cent_b[:1, :].astype(wide)).astype(low)
                centre_grad[...] += jnp.sum(grad_logit * rows_in, axis=0, keepdims=True)

        @pl.when(second)
        def _():
            hop_backward(at).start()

    def finish(step):
        at = chunk_at(step)
        forward = is_forward(step)

        @pl.when(forward)
        def _():
            finish_forward(step, at)

        @pl.when(jnp.logical_not(forward))
        def _():
            finish_backward(step, at)

    @pl.loop(0, steps)
    def _(step):
        at = chunk_at(step)
        forward = is_forward(step)
        rows = both_rows(at)

        @pl.when(forward)
        def _():
            norm_copy(at).wait_recv()

            @pl.loop(0, wide_ff // BIG)
            def _(tile):
                cols = pl.ds(pl.multiple_of(tile * BIG, BIG), BIG)
                inner = jnp.dot(normed[rows, :], inner_w[:, cols], preferred_element_type=wide)
                normal = 0.5 * (1.0 + lax.erf(inner * ROOT_HALF))
                active[rows, cols] = (inner * normal).astype(low)
                slope[rows, cols] = (
                    normal + inner * jnp.exp(-0.5 * inner * inner) * INV_ROOT_TAU
                ).astype(low)

        @pl.when(jnp.logical_not(forward))
        def _():
            state_copy(at).wait_recv()

            @pl.loop(0, wide_ff // BIG)
            def _(tile):
                cols = pl.ds(pl.multiple_of(tile * BIG, BIG), BIG)
                grad_active = lax.dot_general(
                    states[rows, :],
                    outer_w[cols, :],
                    (((1,), (1,)), ((), ())),
                    preferred_element_type=wide,
                )
                slope[rows, cols] = (grad_active * slope[rows, cols].astype(wide)).astype(low)

        @pl.when((step > 0) & jnp.logical_not(first & (step == CHUNKS)))
        def _():
            finish(step - 1)

        @pl.when(step == 0)
        def _():
            late_copy.wait_recv()

        @pl.when(forward)
        def _():
            both = jnp.dot(active[rows, :], outer_w[...], preferred_element_type=wide)
            part_send[part_rows(at), :] = both[:part].astype(low)
            acc[step % 2] = both[part:]
            part_copy(0, at).start()

        @pl.when(jnp.logical_not(forward))
        def _():
            both = lax.dot_general(
                slope[rows, :],
                inner_w[...],
                (((1,), (1,)), ((), ())),
                preferred_element_type=wide,
            )
            part_send[part_rows(CHUNKS + at), :] = both[:part].astype(low)
            acc[step % 2] = both[part:]
            part_copy(1, at).start()

        @pl.when(first & (step == CHUNKS - 1))
        def _():
            finish(step)

        @pl.when(second & (step == 0))
        def _():
            take_cotangent()

        after = step + 1
        after_at = chunk_at(after)

        @pl.when(first & (after >= CHUNKS) & (after < steps))
        def _():
            hop_backward(after_at).wait_recv()
            state_copy(after_at).start()

        @pl.when(second & is_forward(after) & (after < steps))
        def _():
            hop_forward(after_at).wait_recv()
            norm_rows(after_at)

    finish(steps - 1)

    groups = exp_size // 2

    def ret_copy(source, dest):
        return remote(
            source,
            home.at[slot_rows(group)],
            ret_s.at[dest],
            ret_r.at[group],
            (rep_at, dest),
        )

    def relay_copy(which):
        return remote(
            spread.at[slot_rows(2 * which + 1)],
            relay.at[slot_rows(which)],
            relay_s.at[which],
            relay_r.at[which],
            side_peer,
        )

    ret_own = pltpu.make_async_copy(
        spread.at[slot_rows(exp_at)], home.at[slot_rows(group)], ret_s.at[exp_at]
    )

    def make_spread():
        @pl.loop(0, width // TILE)
        def _(step):
            cols = pl.ds(pl.multiple_of(step * TILE, TILE), TILE)
            spread[:, cols] = jnp.dot(
                spread_m[...], back[:, cols], preferred_element_type=wide
            ).astype(low)

    def send_step(step):
        which = group ^ (groups - step)
        relay_copy(which).start()
        ret_copy(spread.at[slot_rows(2 * which)], 2 * which).start()

    def send_end():
        ret_copy(spread.at[slot_rows(exp_at + 1)], exp_at + 1).start()
        ret_own.start()

    def eight_rows(at):
        return pl.ds(pl.multiple_of(at * 8, 8), 8)

    def centre_copy(mask, flip):
        dest = rep_at ^ mask
        return remote(
            centre_v.at[eight_rows(flip * rep_size + dest)],
            centre_parts.at[eight_rows(rep_at)],
            centre_s.at[flip * rep_size + mask],
            centre_r.at[mask],
            (dest, exp_at ^ flip),
        )

    centre_own = pltpu.make_async_copy(
        centre_v.at[eight_rows(rep_at)], centre_parts.at[eight_rows(rep_at)], centre_s.at[0]
    )
    centre_pairs = [(m, f) for m in range(rep_size) for f in range(2) if m or f]

    make_spread()

    def bran_copy(which):
        return remote(
            spread.at[slot_rows(2 * which + 1)],
            branch_got.at[slot_rows(group)],
            bran_s.at[which],
            bran_r.at[group],
            (rep_at, 2 * which + 1),
        )

    bran_own = pltpu.make_async_copy(
        spread.at[slot_rows(exp_at)], branch_got.at[slot_rows(group)], bran_s.at[group]
    )

    @pl.when(second)
    def _():
        bran_own.start()

        @pl.loop(1, groups)
        def _(step):
            bran_copy(group ^ (groups - step)).start()

    spans = 4

    def send_span(span):
        @pl.when(first)
        def _():
            @pl.loop(1 + -(-span * (groups - 1) // spans), 1 + -(-(span + 1) * (groups - 1) // spans))
            def _(step):
                send_step(step)

    @pl.when(first)
    def _():
        for at in range(width // piece):
            centre_v[at * 8 : (at + 1) * 8, :] = jnp.broadcast_to(
                centre_grad[:, at * piece : (at + 1) * piece], (8, piece)
            )
        centre_own.start()
        for mask, flip in centre_pairs:
            centre_copy(mask, flip).start()

    outs = []
    tiles = block // TILE
    early_copy = remote(
        outer_send_v.at[:EARLY], outer_got, early_s.at[1], early_r.at[1], row_peer
    )
    for place, at in enumerate(list(range(tiles, 2 * tiles)) + list(range(tiles))):
        if place % 2 == 0 and place // 2 < spans:
            send_span(place // 2)
        rows = slice(at * TILE, (at + 1) * TILE)
        grad = lax.dot_general(
            active[:, rows], states[...], (((0,), (0,)), ((), ())), preferred_element_type=wide
        )
        if at < tiles:
            outer_keep_v[rows, :] = grad.astype(low)
            outs.append((outer_keep_v.at[rows], outer_keep.at[rows]))
        else:
            top = at * TILE - block
            outer_send_v[top : top + TILE, :] = grad.astype(low)
            if top + TILE == EARLY:
                early_copy.start()
            if top < EARLY:
                continue
            outs.append(
                (outer_send_v.at[top : top + TILE], outer_send.at[top - EARLY : top - EARLY + TILE])
            )
        pltpu.make_async_copy(outs[-1][0], outs[-1][1], out_sem.at[len(outs) - 1]).start()
    outs.append((spread, branch))
    pltpu.make_async_copy(spread, branch, out_sem.at[len(outs) - 1]).start()

    def inner_copy(mask, side):
        at = rep_at ^ (2 * side)
        cols = pl.ds(pl.multiple_of(at * block, block), block)
        target = inner_sum.at[mask // 2, :, cols]
        source = inner_send_v.at[mask, side]
        count = 2 * mask + side
        if mask % 2 == 0:
            return pltpu.make_async_copy(source, target, inner_s.at[count])
        return remote(source, target, inner_s.at[count], out_r.at[count], core_peer)

    inner_order = [(m, f) for m in (3, 1, 2, 0) for f in range(2)]
    @pl.when(first)
    def _():
        send_end()

    for mask, side in inner_order:
        cols = slice(side * block, (side + 1) * block)
        grad = lax.dot_general(
            normed[:, inner_rows(mask)],
            slope[:, cols],
            (((0,), (0,)), ((), ())),
            preferred_element_type=wide,
        )
        inner_send_v[mask, side] = grad.astype(low)
        inner_copy(mask, side).start()

    @pl.when(second)
    def _():
        @pl.loop(1, groups)
        def _(step):
            which = group ^ (groups - step)
            relay_copy(which).wait_recv()
            ret_copy(relay.at[slot_rows(which)], 2 * which + 1).start()

    late_copy.wait_send()
    early_copy.wait()
    for at, (source, target) in enumerate(outs):
        pltpu.make_async_copy(source, target, out_sem.at[at]).wait()
    for mask, side in inner_order:
        inner_copy(mask, side).wait()
    for at in range(CHUNKS):
        norm_copy(at).wait_send()
        state_copy(at).wait_send()
        part_copy(0, at).wait_send()
        part_copy(1, at).wait_send()

        @pl.when(first)
        def _():
            hop_forward(at).wait_send()

        @pl.when(second)
        def _():
            hop_backward(at).wait_send()
            grad_copy(at).wait_send()

    @pl.loop(0, groups)
    def _(which):
        @pl.when(2 * which + 1 != exp_at)
        def _():
            disp_copy(which).wait_send()

    @pl.when(second)
    def _():
        bran_own.wait()

        @pl.loop(1, groups)
        def _(step):
            which = group ^ step
            bran_copy(which).wait_send()
            remote(
                spread.at[slot_rows(which)],
                branch_got.at[slot_rows(which)],
                bran_s.at[which],
                bran_r.at[which],
                side_peer,
            ).wait_recv()

    @pl.when(first)
    def _():
        gate_copy.wait_send()

    @pl.when(first)
    def _():
        centre_own.wait()
        for mask, flip in centre_pairs:
            centre_copy(mask, flip).wait_send()
        for mask in range(1, rep_size):
            centre_copy(mask, 0).wait_recv()

    @pl.when(second)
    def _():
        for mask in range(rep_size):
            centre_copy(mask, 1).wait_recv()

    @pl.when(first)
    def _():
        ret_own.wait()
        ret_copy(spread.at[slot_rows(exp_at + 1)], exp_at + 1).wait_send()

        @pl.loop(1, groups)
        def _(step):
            which = group ^ step
            relay_copy(which).wait_send()
            ret_copy(spread.at[slot_rows(2 * which)], 2 * which).wait_send()

    @pl.when(second)
    def _():
        @pl.loop(1, groups)
        def _(step):
            which = group ^ step
            ret_copy(relay.at[slot_rows(which)], 2 * which + 1).wait_send()

        remote(
            relay.at[slot_rows(group)],
            home.at[slot_rows(group)],
            relay_s.at[group],
            ret_r.at[group],
            side_peer,
        ).wait_recv()

    @pl.loop(1, groups)
    def _(step):
        source = group ^ step
        remote(
            relay.at[slot_rows(source)],
            home.at[slot_rows(source)],
            relay_s.at[source],
            ret_r.at[source],
            side_peer,
        ).wait_recv()


def run_experts(
    exp_size, rep_size, slots, own_rows, arrived, packed, inner_w, outer_w, w_inner, w_outer, spread, cents, gains_e
):
    width = arrived.shape[1]
    depth = width // rep_size
    block = w_outer.shape[0]
    low = jnp.bfloat16
    wide = jnp.float32
    total = exp_size * slots
    all_rows = 2 * own_rows
    part = own_rows // CHUNKS
    piece = cents.shape[1]
    anyplace = pl.BlockSpec(memory_space=pl.ANY)
    inside = pl.BlockSpec(memory_space=pltpu.VMEM)
    dma = pltpu.SemaphoreType.DMA
    n_out = (2 * block - EARLY) // TILE + 1
    scratch = [
        pltpu.VMEM((total, width), low),
        pltpu.VMEM((total, own_rows), low),
        pltpu.VMEM((128, width), low),
        pltpu.VMEM((1, width), wide),
        pltpu.VMEM((1, width), wide),
        pltpu.VMEM((2 * rep_size * 8, piece), wide),
        pltpu.VMEM((width, 2 * block), low),
        pltpu.VMEM((2 * block, width), low),
        pltpu.VMEM((own_rows, width), low),
        pltpu.VMEM((own_rows, width), low),
        pltpu.VMEM((all_rows, width), low),
        pltpu.VMEM((all_rows, 2 * block), low),
        pltpu.VMEM((all_rows, 2 * block), low),
        pltpu.VMEM((all_rows, width), low),
        pltpu.VMEM((2 * own_rows, width), low),
        pltpu.VMEM((2 * own_rows, width), low),
        pltpu.VMEM((own_rows, width), low),
        pltpu.VMEM((own_rows, width), low),
        pltpu.VMEM((total, width), low),
        pltpu.VMEM((total // 2, width), low),
        pltpu.VMEM((2, part, width), wide),
        pltpu.VMEM((own_rows, 128), wide),
        pltpu.VMEM((own_rows, 128), wide),
        pltpu.VMEM((block, width), low),
        pltpu.VMEM((block, width), low),
        pltpu.VMEM((rep_size, 2, depth, block), low),
        dma((9,)),
        dma((exp_size // 2,)),
        dma((exp_size,)),
        dma((exp_size // 2,)),
        dma((exp_size // 2,)),
        dma((2 * rep_size,)),
        dma((rep_size,)),
    ]
    scratch += [dma((CHUNKS,)) for _ in range(4)]
    scratch += [dma((2 * CHUNKS,)), dma((2 * CHUNKS,))]
    scratch += [dma((CHUNKS,)) for _ in range(4)]
    scratch += [dma((1,)), dma((1,)), dma((exp_size,)), dma((exp_size // 2,))]
    scratch += [dma((exp_size // 2,)), dma((exp_size // 2,)), dma((2,)), dma((2,)), dma((n_out,))]
    scratch += [dma((2 * rep_size,)), dma((2 * rep_size,))]
    flops = 2 * all_rows * width * 2 * block * 6
    return pl.pallas_call(
        functools.partial(expert_kernel, exp_size, rep_size, slots),
        out_shape=(
            jax.ShapeDtypeStruct((total // 2, width), low),
            jax.ShapeDtypeStruct((total, width), low),
            jax.ShapeDtypeStruct((total // 2, width), low),
            jax.ShapeDtypeStruct((block, width), low),
            jax.ShapeDtypeStruct((block - EARLY, width), low),
            jax.ShapeDtypeStruct((EARLY, width), low),
            jax.ShapeDtypeStruct((2, depth, rep_size * block), low),
            jax.ShapeDtypeStruct((rep_size * 8, piece), wide),
        ),
        in_specs=[anyplace] * 7 + [inside] * 2,
        out_specs=(anyplace,) * 8,
        scratch_shapes=scratch,
        compiler_params=pltpu.CompilerParams(
            collective_id=0, has_side_effects=True, vmem_limit_bytes=62 << 20
        ),
        cost_estimate=pl.CostEstimate(
            flops=flops, bytes_accessed=40 << 20, transcendentals=2 * all_rows * 2 * block
        ),
        name="experts",
    )(arrived, packed, inner_w, outer_w, w_inner, w_outer, spread, cents, gains_e)


def finish_kernel(
    exp_size,
    rep_size,
    home,
    branch,
    branch_got,
    pick,
    hidden_h,
    cotangent,
    tokens_h,
    gain_row,
    qkv_h,
    probs_h,
    normed_h,
    context_h,
    attn_w,
    outer_send,
    outer_got,
    inner_sum,
    output,
    grad_tokens,
    shares,
    outer_recv,
    inner_recv,
    hidden,
    tokens,
    qkv,
    probs,
    normed_a,
    context,
    normed_t,
    context_t,
    branch_in,
    early_rows,
    weights,
    grad_hidden,
    grad_attn,
    grad_context,
    grads3,
    keep,
    core_out,
    core_in,
    side_out,
    side_in,
    line_out,
    line_in,
    total,
    row_out,
    row_in,
    half_out,
    half_in,
    load_s,
    branch_s,
    branch_r,
    expert_s,
    expert_r,
    core_s,
    core_r,
    side_s,
    side_r,
    line_s,
    line_r,
    row_s,
    row_r,
    half_s,
    half_r,
):
    low = jnp.bfloat16
    wide = jnp.float32
    rep_at = lax.axis_index("rep")
    exp_at = lax.axis_index("exp")
    core = rep_at % 2
    group = exp_at // 2
    side = exp_at % 2
    groups = exp_size // 2
    rows_n, width = cotangent.shape
    half = width // 2
    block = width // exp_size
    core_peer = (rep_at ^ 1, exp_at)
    side_peer = (rep_at, exp_at ^ 1)
    row_peer = (rep_at ^ 2, exp_at)

    loads = [
        pltpu.make_async_copy(source, target, load_s.at[at])
        for at, (source, target) in enumerate(
            (
                (context_h, context),
                (attn_w, weights),
                (qkv_h, qkv),
                (probs_h, probs),
                (normed_h, normed_a),
                (tokens_h, tokens),
                (hidden_h, hidden),
                (outer_got, early_rows),
            )
        )
    ]
    for load in loads:
        load.start()

    barrier = pltpu.get_barrier_semaphore()
    for mask in range(1, 3):
        pl.semaphore_signal(
            barrier, inc=1, device_id=(rep_at ^ mask, exp_at), device_id_type=MESH
        )

    @pl.loop(1, exp_size)
    def _(at):
        pl.semaphore_signal(barrier, inc=1, device_id=(rep_at, exp_at ^ at), device_id_type=MESH)

    pl.semaphore_wait(barrier, exp_size + 1)

    outer_copy = remote(
        outer_send, outer_recv.at[EARLY:], expert_s.at[0], expert_r.at[0], row_peer
    )
    early_store = pltpu.make_async_copy(early_rows, outer_recv.at[:EARLY], load_s.at[8])

    inner_copy = remote(inner_sum.at[1], inner_recv, expert_s.at[1], expert_r.at[1], row_peer)
    inner_copy.start()
    outer_copy.start()

    slots = pick.shape[0] // groups

    def slot_rows(at):
        return pl.ds(pl.multiple_of(at * slots, slots), slots)

    def branch_copy(dest):
        return remote(
            branch.at[slot_rows(dest)],
            branch_in.at[slot_rows(group)],
            branch_s.at[dest],
            branch_r.at[group],
            (rep_at, dest),
        )

    branch_own = pltpu.make_async_copy(branch_got, branch_in, branch_s.at[exp_at])

    @pl.when(side == 1)
    def _():
        branch_own.start()

        @pl.loop(0, groups)
        def _(at):
            branch_copy(2 * (group ^ (groups - 1 - at))).start()

    back_rows = lax.dot_general(
        pick[...], home[...], (((0,), (0,)), ((), ())), preferred_element_type=wide
    )
    grad_hidden[...] = cotangent[...].astype(wide) + back_rows
    grad_attn[...] = grad_hidden[...].astype(low)
    loads[0].wait()
    context_t[...] = context[...].T

    own_half = pl.ds(pl.multiple_of(core * half, half), half)
    other_half = pl.ds(pl.multiple_of((1 - core) * half, half), half)

    def core_copy(at):
        return remote(core_out.at[at], core_in.at[at], core_s.at[at], core_r.at[at], core_peer)

    def product(at, left, right, cols, target, kind):
        @pl.loop(0, width // 512)
        def _(step):
            rows = pl.ds(pl.multiple_of(step * 512, 512), 512)
            target[at, rows, :] = jnp.dot(
                left[rows, :], right[:, cols], preferred_element_type=wide
            ).astype(kind)

    def share_start(at, left, right):
        product(at, left, right, other_half, core_out, low)
        core_copy(at).start()
        product(at, left, right, own_half, keep, wide)

    def block_rows(at):
        return pl.ds(pl.multiple_of(at * block, block), block)

    def side_copy(at):
        return remote(side_out.at[at], side_in.at[at], side_s.at[at], side_r.at[at], side_peer)

    def share_side(at):
        core_copy(at).wait_recv()

        @pl.loop(0, groups)
        def _(which):
            rows = block_rows(2 * which + 1 - side)
            side_out[at, block_rows(which), :] = (
                keep[at, rows, :] + core_in[at, rows, :].astype(wide)
            ).astype(low)

        side_copy(at).start()

        @pl.loop(0, groups)
        def _(which):
            rows = block_rows(2 * which + side)
            keep[at, rows, :] = keep[at, rows, :] + core_in[at, rows, :].astype(wide)

    def line_copy(at, mask):
        dest = group ^ mask
        return remote(
            line_out.at[at, block_rows(dest)],
            line_in.at[at, block_rows(group)],
            line_s.at[at, mask],
            line_r.at[at, mask],
            (rep_at, 2 * dest + side),
        )

    def share_line(at):
        side_copy(at).wait_recv()

        @pl.loop(1, groups)
        def _(mask):
            dest = group ^ mask
            line_out[at, block_rows(dest), :] = (
                keep[at, block_rows(2 * dest + side), :] + side_in[at, block_rows(dest), :].astype(wide)
            ).astype(low)
            line_copy(at, mask).start()

        total[at] = keep[at, block_rows(exp_at), :] + side_in[at, block_rows(group), :].astype(wide)

    def row_copy(at):
        return remote(row_out.at[at], row_in.at[at], row_s.at[at], row_r.at[at], row_peer)

    def share_row(at):
        @pl.loop(1, groups)
        def _(mask):
            line_copy(at, mask).wait_recv()
            total[at] = total[at] + line_in[at, block_rows(group ^ mask), :].astype(wide)

        row_out[at] = total[at].astype(low)
        row_copy(at).start()

    def half_copy(at):
        return remote(half_out.at[at], half_in.at[at], half_s.at[at], half_r.at[at], core_peer)

    def share_half(at):
        row_copy(at).wait_recv()
        summed = row_out[at].astype(wide) + row_in[at].astype(wide)
        half_out[at] = summed
        half_copy(at).start()
        shares[at, :, own_half] = summed

    def share_end(at):
        half_copy(at).wait_recv()
        shares[at, :, other_half] = half_in[at]

    share_start(3, context_t, grad_attn)
    loads[1].wait()

    @pl.loop(0, width // TILE)
    def _(step):
        rows = pl.ds(pl.multiple_of(step * TILE, TILE), TILE)
        grad_context[:, rows] = lax.dot_general(
            grad_attn[...], weights[3, rows, :], (((1,), (1,)), ((), ())), preferred_element_type=wide
        ).astype(low)

    share_side(3)

    head_dim = width // HEADS
    pair = 2 * head_dim
    factor = head_dim ** (-0.5)
    lane = lax.broadcasted_iota(jnp.int32, (rows_n, pair), 1)

    def heads(which_half):
        @pl.loop(0, HEADS // 4)
        def _(step):
            at = which_half * (HEADS // 4) + step
            cols = pl.ds(pl.multiple_of(at * pair, pair), pair)
            q_pair = qkv[0, :, cols]
            k_pair = qkv[1, :, cols]
            v_pair = qkv[2, :, cols]
            c_pair = grad_context[:, cols]
            found = []
            for which in range(2):
                chosen = (lane >= head_dim) if which else (lane < head_dim)
                c_one = jnp.where(chosen, c_pair, jnp.zeros_like(c_pair))
                prob = probs[pl.ds(pl.multiple_of((2 * at + which) * rows_n, rows_n), rows_n), :]
                grad_prob = lax.dot_general(
                    c_one, v_pair, (((1,), (1,)), ((), ())), preferred_element_type=wide
                )
                weighted = prob.astype(wide) * grad_prob
                row_sum = jnp.sum(weighted, axis=1, keepdims=True)
                grad_score = (weighted - prob.astype(wide) * row_sum).astype(low)
                found.append(
                    (
                        jnp.dot(grad_score, k_pair, preferred_element_type=wide) * factor,
                        lax.dot_general(
                            grad_score,
                            q_pair,
                            (((0,), (0,)), ((), ())),
                            preferred_element_type=wide,
                        )
                        * factor,
                        lax.dot_general(
                            prob, c_pair, (((0,), (0,)), ((), ())), preferred_element_type=wide
                        ),
                    )
                )
            for which in range(3):
                grads3[which, :, cols] = jnp.where(
                    lane < head_dim, found[0][which], found[1][which]
                ).astype(low)

    loads[7].wait()
    early_store.start()
    loads[2].wait()
    loads[3].wait()
    heads(1 - core)
    loads[4].wait()
    normed_t[...] = normed_a[...].T
    for at in range(3):
        product(at, normed_t, grads3.at[at], other_half, core_out, low)
        core_copy(at).start()
    share_line(3)
    heads(core)
    for at in range(3):
        product(at, normed_t, grads3.at[at], own_half, keep, wide)
        share_side(at)
    loads[5].wait()
    @pl.loop(0, width // TILE)
    def _(step):
        rows = pl.ds(pl.multiple_of(step * TILE, TILE), TILE)
        grad_normed = jnp.zeros((rows_n, TILE), wide)
        for at in range(3):
            grad_normed = grad_normed + lax.dot_general(
                grads3[at], weights[at, rows, :], (((1,), (1,)), ((), ())), preferred_element_type=wide
            )
        grad_tokens[:, rows] = grad_normed

    @pl.loop(0, rows_n // ROWS)
    def _(step):
        here = pl.ds(pl.multiple_of(step * ROWS, ROWS), ROWS)
        unit, inv_scale = row_stats(tokens[here, :].astype(wide))
        grad_unit = grad_tokens[here, :] * gain_row[...]
        grad_in = (
            grad_unit
            - jnp.mean(grad_unit, axis=-1, keepdims=True)
            - unit * jnp.mean(grad_unit * unit, axis=-1, keepdims=True)
        ) * inv_scale
        grad_tokens[here, :] = grad_hidden[here, :] + grad_in

    share_row(3)
    for at in range(3):
        share_line(at)

    for at in range(3):
        share_row(at)
    def branch_wait(which):
        remote(
            branch.at[slot_rows(which)],
            branch_in.at[slot_rows(which)],
            branch_s.at[which],
            branch_r.at[which],
            side_peer,
        ).wait_recv()

    @pl.when(side == 0)
    def _():
        @pl.loop(0, groups)
        def _(at):
            branch_wait(at)

    @pl.when(side == 1)
    def _():
        branch_own.wait()

    loads[6].wait()
    rows = lax.dot_general(
        pick[...], branch_in[...], (((0,), (0,)), ((), ())), preferred_element_type=wide
    )
    output[...] = (hidden[...] + rows).astype(low)

    for at in (3, 0, 1, 2):
        share_half(at)
    for at in (3, 0, 1, 2):
        share_end(at)

    @pl.when(side == 1)
    def _():
        @pl.loop(0, groups)
        def _(at):
            branch_copy(2 * at).wait_send()

    for at in range(4):
        core_copy(at).wait_send()
        side_copy(at).wait_send()
        row_copy(at).wait_send()
        half_copy(at).wait_send()

        @pl.loop(1, groups)
        def _(mask):
            line_copy(at, mask).wait_send()

    inner_copy.wait()
    outer_copy.wait()
    early_store.wait()


def run_finish(exp_size, rep_size, home, branch, branch_got, pick, hidden, cotangent, tokens, gain_row, qkv, probs, normed_a, context, attn_w, outer_send, outer_got, inner_sum):
    rows_n, width = tokens.shape
    low = jnp.bfloat16
    wide = jnp.float32
    half = width // 2
    groups = exp_size // 2
    block = width // exp_size
    anyplace = pl.BlockSpec(memory_space=pl.ANY)
    inside = pl.BlockSpec(memory_space=pltpu.VMEM)
    dma = pltpu.SemaphoreType.DMA
    shape = jax.ShapeDtypeStruct
    return pl.pallas_call(
        functools.partial(finish_kernel, exp_size, rep_size),
        out_shape=(
            shape((rows_n, width), low),
            shape((rows_n, width), wide),
            shape((4, block, width), wide),
            shape((outer_send.shape[0] + EARLY, width), low),
            shape(inner_sum.shape[1:], low),
        ),
        in_specs=[inside, anyplace, anyplace, inside, anyplace, inside, anyplace, inside]
        + [anyplace] * 8,
        out_specs=(inside,) * 3 + (anyplace,) * 2,
        scratch_shapes=[
            pltpu.VMEM((rows_n, width), wide),
            pltpu.VMEM((rows_n, width), low),
            pltpu.VMEM(qkv.shape, low),
            pltpu.VMEM(probs.shape, low),
            pltpu.VMEM((rows_n, width), low),
            pltpu.VMEM((rows_n, width), low),
            pltpu.VMEM((width, rows_n), low),
            pltpu.VMEM((width, rows_n), low),
            pltpu.VMEM(pick.shape[:1] + (width,), low),
            pltpu.VMEM((EARLY, width), low),
            pltpu.VMEM((4, width, width), low),
            pltpu.VMEM((rows_n, width), wide),
            pltpu.VMEM((rows_n, width), low),
            pltpu.VMEM((rows_n, width), low),
            pltpu.VMEM((3, rows_n, width), low),
            pltpu.VMEM((4, width, half), wide),
            pltpu.VMEM((4, width, half), low),
            pltpu.VMEM((4, width, half), low),
            pltpu.VMEM((4, width // 2, half), low),
            pltpu.VMEM((4, width // 2, half), low),
            pltpu.VMEM((4, width // 2, half), low),
            pltpu.VMEM((4, width // 2, half), low),
            pltpu.VMEM((4, block, half), wide),
            pltpu.VMEM((4, block, half), low),
            pltpu.VMEM((4, block, half), low),
            pltpu.VMEM((4, block, half), wide),
            pltpu.VMEM((4, block, half), wide),
            dma((9,)),
            dma((exp_size,)),
            dma((groups,)),
            dma((2,)),
            dma((2,)),
            dma((4,)),
            dma((4,)),
            dma((4,)),
            dma((4,)),
            dma((4, groups)),
            dma((4, groups)),
            dma((4,)),
            dma((4,)),
            dma((4,)),
            dma((4,)),
        ],
        compiler_params=pltpu.CompilerParams(
            collective_id=2, has_side_effects=True, vmem_limit_bytes=60 << 20
        ),
        cost_estimate=pl.CostEstimate(
            flops=20 * rows_n * width * width, bytes_accessed=60 << 20, transcendentals=0
        ),
        name="finish",
    )(
        home,
        branch,
        branch_got,
        pick,
        hidden,
        cotangent,
        tokens,
        gain_row,
        qkv,
        probs,
        normed_a,
        context,
        attn_w,
        outer_send,
        outer_got,
        inner_sum,
    )


def shards(
    tokens,
    cotangent,
    doc_lengths,
    expert_of_token,
    w_query,
    w_key,
    w_value,
    w_output,
    attn_gain,
    w_inner,
    w_outer,
    expert_gain,
    centroids,
):
    exp_size = lax.axis_size("exp")
    rep_size = lax.axis_size("rep")
    row_count = tokens.shape[0]
    wide = jnp.float32

    slots = -(-3 * row_count // exp_size // 16) * 16
    (
        attn_w,
        inner_w,
        outer_w,
        arrived,
        spread,
        cents,
        gains_e,
        packed,
        hidden,
        qkv,
        probs,
        normed_a,
        context,
        pick,
        gain_row,
    ) = run_attend(
        exp_size,
        rep_size,
        slots,
        tokens,
        cotangent,
        doc_lengths,
        expert_of_token[None],
        (w_query, w_key, w_value, w_output),
        attn_gain[None],
        w_inner[0],
        w_outer[0],
        expert_gain,
        centroids,
    )
    home, branch, branch_got, outer_keep, outer_send, outer_got, inner_sum, centre_parts = run_experts(
        exp_size,
        rep_size,
        slots,
        2 * row_count,
        arrived,
        packed,
        inner_w,
        outer_w,
        w_inner[0],
        w_outer[0],
        spread,
        cents,
        gains_e,
    )
    output, grad_tokens, shares, outer_recv, inner_recv = run_finish(
        exp_size,
        rep_size,
        home,
        branch,
        branch_got,
        pick,
        hidden,
        cotangent,
        tokens,
        gain_row,
        qkv,
        probs,
        normed_a,
        context,
        attn_w,
        outer_send,
        outer_got,
        inner_sum,
    )
    grad_centroids = jnp.sum(centre_parts.reshape(rep_size, 8, -1)[:, 0], axis=0)[None]
    grad_w_outer = (outer_keep.astype(wide) + outer_recv.astype(wide))[None]
    summed = inner_sum[0].astype(wide) + inner_recv.astype(wide)
    grad_w_inner = summed[None]
    grad_expert_gain = jnp.sum(summed * w_inner[0].astype(wide), axis=1)[None] / expert_gain.astype(
        wide
    )
    share_gain = sum(
        jnp.sum(shares[i] * w.astype(wide), axis=1) for i, w in enumerate((w_query, w_key, w_value))
    ) / attn_gain.astype(wide)
    return (
        output,
        grad_tokens,
        shares[0],
        shares[1],
        shares[2],
        shares[3],
        share_gain,
        grad_w_inner,
        grad_w_outer,
        grad_expert_gain,
        grad_centroids,
    )


def solution(mesh):
    placed = (
        P(("rep", "exp"), None),
        P(("rep", "exp"), None),
        P(("rep", "exp"), None),
        P(("rep", "exp")),
        P("exp", None),
        P("exp", None),
        P("exp", None),
        P("exp", None),
        P("exp"),
        P("exp", "rep", None),
        P("exp", "rep", None),
        P("exp", "rep"),
        P("exp", "rep"),
    )
    return jax.shard_map(
        shards,
        mesh=mesh,
        in_specs=placed,
        out_specs=(
            P(("rep", "exp"), None),
            P(("rep", "exp"), None),
            P("exp", None),
            P("exp", None),
            P("exp", None),
            P("exp", None),
            P("exp"),
            P("exp", "rep", None),
            P("exp", "rep", None),
            P("exp", "rep"),
            P("exp", "rep"),
        ),
        check_vma=False,
    )
```

```python
import functools

import jax
import jax.numpy as jnp
from jax import lax
from jax.experimental import pallas as pl
from jax.experimental.pallas import tpu as pltpu
from jax.sharding import PartitionSpec as P

HEADS = 16
EPS = 1e-05
ROOT_HALF = 0.7071067811865476
INV_ROOT_TAU = 0.3989422804014327
CHUNKS = 4
DEFER = 448
EARLY = 512


MESH = pl.DeviceIdType.MESH
TILE = 256
ROWS = 128
BIG = 2048


def remote(src, dst, send_sem, recv_sem, device):
    return pltpu.make_async_remote_copy(
        src_ref=src,
        dst_ref=dst,
        send_sem=send_sem,
        recv_sem=recv_sem,
        device_id=device,
        device_id_type=MESH,
    )


def row_stats(rows):
    row_mean = jnp.mean(rows, axis=-1, keepdims=True)
    centered = rows - row_mean
    variance = jnp.mean(centered * centered, axis=-1, keepdims=True)
    inv_scale = lax.rsqrt(variance + EPS)
    return centered * inv_scale, inv_scale


def attend_kernel(
    exp_size,
    rep_size,
    slots,
    tokens,
    cotangent,
    doc,
    expert_of,
    w_query,
    w_key,
    w_value,
    w_output,
    gain_a,
    w_inner,
    w_outer,
    gain_e,
    cent,
    attn_w,
    inner_w,
    outer_w,
    arrived,
    spread_h,
    cents,
    gains_e,
    packed_h,
    hidden_h,
    qkv_h,
    probs_h,
    normed_h,
    context_h,
    pick,
    gain_row,
    hidden,
    qkv,
    probs,
    normed_a,
    context,
    weights,
    staging,
    spread_m,
    offsets,
    small_all,
    gain_v,
    packed_x,
    packed_c,
    bias,
    counts_v,
    cent_v,
    own_s,
    line_s,
    line_r,
    side_s,
    side_r,
    core_s,
    core_r,
    weight_s,
    weight_r,
    disp_s,
    disp_r,
    count_s,
    count_r,
    cent_s,
    cent_r,
    gain_s,
    gain_r,
    out_s,
):
    low = jnp.bfloat16
    wide = jnp.float32
    rep_at = lax.axis_index("rep")
    exp_at = lax.axis_index("exp")
    core = rep_at % 2
    group = exp_at // 2
    side = exp_at % 2
    groups = exp_size // 2
    rows_n, width = tokens.shape
    half = width // 2
    block = w_query.shape[0]
    depth = w_inner.shape[0]
    ff_block = w_outer.shape[0]
    core_peer = (rep_at ^ 1, exp_at)
    side_peer = (rep_at, exp_at ^ 1)

    def block_rows(at):
        return pl.ds(pl.multiple_of(at * block, block), block)

    own_loads = []
    for at, source in enumerate((w_query, w_key, w_value, w_output)):
        own_loads.append(
            pltpu.make_async_copy(source, weights.at[at, block_rows(exp_at)], own_s.at[at])
        )
    for load in own_loads:
        load.start()

    barrier = pltpu.get_barrier_semaphore()
    for mask in range(1, rep_size):
        for flip in range(2):
            pl.semaphore_signal(
                barrier, inc=1, device_id=(rep_at ^ mask, exp_at ^ flip), device_id_type=MESH
            )

    @pl.loop(1, exp_size)
    def _(at):
        pl.semaphore_signal(barrier, inc=1, device_id=(rep_at, exp_at ^ at), device_id_type=MESH)

    pl.semaphore_wait(barrier, exp_size - 1 + 2 * (rep_size - 1))

    outer_copy = remote(
        w_outer.at[: ff_block - DEFER],
        outer_w,
        weight_s.at[0],
        weight_r.at[0],
        (rep_at ^ 2, exp_at),
    )

    for load in own_loads:
        load.wait()

    picks = (slice(0, 3), slice(3, 4))
    own_half = pl.ds(pl.multiple_of(core * half, half), half)

    def view(kind, at):
        return weights.at[picks[kind], block_rows(at), own_half]

    def line_copy(kind, source, step):
        at = 2 * source + side
        return remote(
            view(kind, at),
            view(kind, at),
            line_s.at[kind, (1 + step) // 2, source],
            line_r.at[kind, source],
            (rep_at, exp_at + 2 * step),
        )

    def line_wait(kind, source):
        at = 2 * source + side
        remote(
            view(kind, at), view(kind, at), line_s.at[kind, 0, source], line_r.at[kind, source], side_peer
        ).wait_recv()

    def side_copy(kind, source):
        at = 2 * source + side
        return remote(
            view(kind, at), view(kind, at), side_s.at[kind, source], side_r.at[kind, source], side_peer
        )

    def side_wait(kind, source):
        at = 2 * source + 1 - side
        remote(
            view(kind, at), view(kind, at), side_s.at[kind, source], side_r.at[kind, source], side_peer
        ).wait_recv()

    def core_copy(kind, at):
        return remote(view(kind, at), view(kind, at), core_s.at[kind, at], core_r.at[kind, at], core_peer)

    def core_wait(kind, at):
        other = pl.ds(pl.multiple_of((1 - core) * half, half), half)
        there = weights.at[picks[kind], block_rows(at), other]
        remote(there, there, core_s.at[kind, at], core_r.at[kind, at], core_peer).wait_recv()

    def first_sends(kind):
        @pl.when(group + 1 < groups)
        def _():
            line_copy(kind, group, 1).start()

        @pl.when(group >= 1)
        def _():
            line_copy(kind, group, -1).start()

        side_copy(kind, group).start()

    def take_side(kind, source):
        side_wait(kind, source)
        core_copy(kind, 2 * source + 1 - side).start()

    def gather_step(kind, step):
        @pl.when(group - step >= 0)
        def _():
            source = group - step
            line_wait(kind, source)

            @pl.when(group + 1 < groups)
            def _():
                line_copy(kind, source, 1).start()

            side_copy(kind, source).start()
            core_copy(kind, 2 * source + side).start()

        @pl.when(group + step < groups)
        def _():
            source = group + step
            line_wait(kind, source)

            @pl.when(group >= 1)
            def _():
                line_copy(kind, source, -1).start()

            side_copy(kind, source).start()
            core_copy(kind, 2 * source + side).start()

        @pl.when(group - step + 1 >= 0)
        def _():
            take_side(kind, group - step + 1)

        @pl.when((step > 1) & (group + step - 1 < groups))
        def _():
            take_side(kind, group + step - 1)

    def gather_end(kind):
        last = groups - 1

        @pl.when(group - last >= 0)
        def _():
            take_side(kind, group - last)

        @pl.when((groups > 1) & (group + last < groups))
        def _():
            take_side(kind, group + last)

        @pl.loop(0, exp_size)
        def _(at):
            @pl.when(at != exp_at)
            def _():
                core_wait(kind, at)

    first_sends(0)
    first_sends(1)

    inner_rows = pl.ds(pl.multiple_of(rep_at * depth, depth), depth)

    def ff_cols(at):
        return pl.ds(pl.multiple_of(at * ff_block, ff_block), ff_block)

    def inner_copies(mask):
        dest = rep_at ^ mask
        found = []
        for part in range(2):
            source = w_inner.at[:, ff_cols(dest ^ (2 * part))]
            cols = slice(part * ff_block, (part + 1) * ff_block)
            at = 1 + 2 * mask + part
            if mask == 3:
                found.append(
                    remote(
                        source,
                        staging.at[:, cols],
                        weight_s.at[at],
                        weight_r.at[at],
                        (rep_at ^ 2, exp_at),
                    )
                )
            else:
                found.append(
                    remote(
                        source,
                        inner_w.at[inner_rows, cols],
                        weight_s.at[at],
                        weight_r.at[at],
                        (dest, exp_at),
                    )
                )
        return found

    far_rows = pl.ds(pl.multiple_of((rep_at ^ 2) * depth, depth), depth)
    forward_copy = remote(
        staging,
        inner_w.at[far_rows],
        weight_s.at[1 + 2 * rep_size],
        weight_r.at[1 + 2 * rep_size],
        core_peer,
    )

    for mask in (3, 2, 1):
        for copy in inner_copies(mask):
            copy.start()
    outer_copy.start()

    lanes = counts_v.shape[1]
    expert_row = expert_of[...]
    onehot = (
        lax.broadcasted_iota(jnp.int32, (lanes, rows_n), 0) == expert_row
    ).astype(wide)
    before = (
        lax.broadcasted_iota(jnp.int32, (rows_n, rows_n), 0)
        < lax.broadcasted_iota(jnp.int32, (rows_n, rows_n), 1)
    ).astype(low)
    earlier = jnp.dot(onehot.astype(low), before, preferred_element_type=wide)
    rank = jnp.sum(earlier * onehot, axis=0, keepdims=True).astype(jnp.int32)
    position = expert_row * slots + rank
    pick[...] = (
        lax.broadcasted_iota(jnp.int32, pick.shape, 0) == position
    ).astype(wide).astype(low)
    counts_v[...] = jnp.zeros_like(counts_v)
    counts_v[:8, :] = lax.dot_general(
        jnp.ones((8, rows_n), low),
        onehot.astype(low),
        (((1,), (1,)), ((), ())),
        preferred_element_type=wide,
    )
    counts_v[8:, :block] = jnp.broadcast_to(gain_a[...].astype(wide), (8, block))
    cent_v[...] = jnp.broadcast_to(cent[...].astype(wide), cent_v.shape)
    gain_v[...] = jnp.broadcast_to(gain_e[...].astype(wide), gain_v.shape)

    def eight(at):
        return pl.ds(pl.multiple_of(at * 8, 8), 8)

    def sixteen(at):
        return pl.ds(pl.multiple_of(at * 16, 16), 16)

    def count_copy(dest):
        return remote(
            counts_v, small_all.at[sixteen(exp_at)], count_s.at[dest], count_r.at[exp_at], (rep_at, dest)
        )

    count_own = pltpu.make_async_copy(counts_v, small_all.at[sixteen(exp_at)], count_s.at[exp_at])
    count_own.start()

    @pl.loop(1, exp_size)
    def _(at):
        count_copy(exp_at ^ at).start()

    cent_at = side * rep_size + rep_at

    def cent_copy(mask, flip):
        return remote(
            cent_v,
            cents.at[eight(cent_at)],
            cent_s.at[flip * rep_size + mask],
            cent_r.at[flip * rep_size + mask],
            (rep_at ^ mask, exp_at ^ flip),
        )

    cent_own = pltpu.make_async_copy(cent_v, cents.at[eight(cent_at)], cent_s.at[0])
    cent_own.start()
    cent_pairs = [(m, f) for m in range(rep_size) for f in range(2) if m or f]
    for mask, flip in cent_pairs:
        cent_copy(mask, flip).start()

    def gain_copy(mask):
        return remote(
            gain_v, gains_e.at[eight(rep_at)], gain_s.at[mask], gain_r.at[mask], (rep_at ^ mask, exp_at)
        )

    gain_own = pltpu.make_async_copy(gain_v, gains_e.at[eight(rep_at)], gain_s.at[0])
    gain_own.start()
    for mask in range(1, rep_size):
        gain_copy(mask).start()

    count_own.wait()

    @pl.loop(1, exp_size)
    def _(at):
        source = exp_at ^ at
        remote(
            counts_v, small_all.at[sixteen(source)], count_s.at[source], count_r.at[source], (rep_at, source)
        ).wait()

    tiled = jnp.dot(
        small_all[...].astype(low),
        (
            lax.broadcasted_iota(jnp.int32, (lanes, width), 1) % block
            == lax.broadcasted_iota(jnp.int32, (lanes, width), 0)
        ).astype(wide).astype(low),
        preferred_element_type=wide,
    )
    chosen_row = lax.broadcasted_iota(jnp.int32, (16 * exp_size, width), 0) == (
        16 * (lax.broadcasted_iota(jnp.int32, (16 * exp_size, width), 1) // block) + 8
    )
    gain_row[...] = jnp.sum(jnp.where(chosen_row, tiled, 0.0), axis=0, keepdims=True)

    @pl.loop(0, rows_n // ROWS)
    def _(step):
        here = pl.ds(pl.multiple_of(step * ROWS, ROWS), ROWS)
        unit, _ = row_stats(tokens[here, :].astype(wide))
        normed_a[here, :] = (unit * gain_row[...]).astype(low)

    down = lax.broadcasted_iota(jnp.int32, (rows_n, rows_n), 0)
    along = lax.broadcasted_iota(jnp.int32, (rows_n, rows_n), 1)
    end = jnp.int32(0)
    seg_down = jnp.zeros((rows_n, rows_n), jnp.int32)
    seg_along = jnp.zeros((rows_n, rows_n), jnp.int32)
    for at in range(doc.shape[1]):
        end = end + doc[0, at]
        seg_down = seg_down + (down >= end).astype(jnp.int32)
        seg_along = seg_along + (along >= end).astype(jnp.int32)
    bias[...] = jnp.where((seg_down == seg_along) & (down >= along), 0.0, -1e30)

    @pl.loop(1, groups)
    def _(step):
        gather_step(0, step)

    gather_end(0)

    def slot_rows(at):
        return pl.ds(pl.multiple_of(at * slots, slots), slots)

    def disp_copy(source, dest):
        return remote(
            source.at[slot_rows(dest // 2)],
            arrived.at[slot_rows(exp_at)],
            disp_s.at[dest],
            disp_r.at[exp_at],
            (rep_at, dest),
        )

    def dispatch(source, flip):
        @pl.loop(0, groups)
        def _(at):
            dest = 2 * (group ^ at) + flip

            @pl.when(dest != exp_at)
            def _():
                disp_copy(source, dest).start()

            @pl.when(dest == exp_at)
            def _():
                pltpu.make_async_copy(
                    source.at[slot_rows(group)], arrived.at[slot_rows(exp_at)], disp_s.at[exp_at]
                ).start()

    @pl.loop(1, 1 + (groups - 1 + 2) // 3)
    def _(step):
        gather_step(1, step)

    for at in range(3):

        @pl.loop(0, width // TILE)
        def _(step):
            cols = pl.ds(pl.multiple_of(step * TILE, TILE), TILE)
            qkv[at, :, cols] = jnp.dot(
                normed_a[...], weights[at, :, cols], preferred_element_type=wide
            ).astype(low)

    head_dim = width // HEADS
    pair = 2 * head_dim
    factor = head_dim ** (-0.5)
    lane = lax.broadcasted_iota(jnp.int32, (rows_n, pair), 1)
    pairs = HEADS // 2
    parts = 2
    begun = (groups - 1 + 2) // 3
    for part in range(parts):
        low_step = 1 + begun + part * (groups - 1 - begun) // parts
        high_step = 1 + begun + (part + 1) * (groups - 1 - begun) // parts

        @pl.loop(low_step, high_step)
        def _(step):
            gather_step(1, step)

        @pl.loop(part * pairs // parts, (part + 1) * pairs // parts)
        def _(at):
            cols = pl.ds(pl.multiple_of(at * pair, pair), pair)
            q_pair = qkv[0, :, cols]
            k_pair = qkv[1, :, cols]
            v_pair = qkv[2, :, cols]
            found = []
            for which in range(2):
                chosen = (lane >= head_dim) if which else (lane < head_dim)
                q_one = jnp.where(chosen, q_pair, jnp.zeros_like(q_pair))
                scores = (
                    lax.dot_general(
                        q_one, k_pair, (((1,), (1,)), ((), ())), preferred_element_type=wide
                    )
                    * factor
                    + bias[...]
                )
                top = jnp.max(scores, axis=1, keepdims=True)
                raised = jnp.exp(scores - top)
                total = jnp.sum(raised, axis=1, keepdims=True)
                prob = (raised * (1.0 / total)).astype(low)
                probs[pl.ds(pl.multiple_of((2 * at + which) * rows_n, rows_n), rows_n), :] = prob
                found.append(jnp.dot(prob, v_pair, preferred_element_type=wide))
            context[:, cols] = jnp.where(lane < head_dim, found[0], found[1]).astype(low)

    @pl.loop(0, width // TILE)
    def _(step):
        cols = pl.ds(pl.multiple_of(step * TILE, TILE), TILE)
        packed_c[:, cols] = jnp.dot(
            pick[...], cotangent[:, cols], preferred_element_type=wide
        ).astype(low)

    gather_end(1)
    stores = [
        pltpu.make_async_copy(source, target, out_s.at[at])
        for at, (source, target) in (
            (0, (weights, attn_w)),
            (2, (qkv, qkv_h)),
            (3, (probs, probs_h)),
            (4, (normed_a, normed_h)),
            (5, (context, context_h)),
            (7, (packed_c, packed_h)),
            (6, (hidden, hidden_h)),
        )
    ]
    for store in stores[:-1]:
        store.start()

    @pl.loop(0, width // TILE)
    def _(step):
        cols = pl.ds(pl.multiple_of(step * TILE, TILE), TILE)
        sum_here = tokens[:, cols].astype(wide) + jnp.dot(
            context[...], weights[3, :, cols], preferred_element_type=wide
        )
        hidden[:, cols] = sum_here
        packed_x[:, cols] = jnp.dot(
            pick[...], sum_here.astype(low), preferred_element_type=wide
        ).astype(low)

    dispatch(packed_x, 0)
    stores[-1].start()

    counted = small_all.shape[0]
    own_rows = spread_m.shape[1]
    count_lane = lax.broadcasted_iota(jnp.int32, (counted, 128), 1)
    mine = jnp.sum(
        jnp.where(count_lane == group, small_all[...], 0.0), axis=1, keepdims=True
    )
    mine = jnp.broadcast_to(mine, (counted, 128))
    table_down = lax.broadcasted_iota(jnp.int32, (counted, counted), 0)
    table_along = lax.broadcasted_iota(jnp.int32, (counted, counted), 1)
    ahead = ((table_along // 16 < table_down // 16) & (table_along % 16 == 0)).astype(wide).astype(low)
    offsets[0] = jnp.dot(ahead, mine.astype(low), preferred_element_type=wide)
    offsets[1] = mine
    slot_iota = lax.broadcasted_iota(jnp.int32, (slots, own_rows), 0)
    row_iota = lax.broadcasted_iota(jnp.int32, (slots, own_rows), 1)

    @pl.loop(0, exp_size)
    def _(at):
        eight = pl.ds(pl.multiple_of(at * 16, 16), 8)
        start = offsets[0, eight, :][:1, :1].astype(jnp.int32)
        limit = offsets[1, eight, :][:1, :1].astype(jnp.int32)
        spread_m[slot_rows(at), :] = (
            ((slot_iota + start) == row_iota) & (slot_iota < limit)
        ).astype(wide).astype(low)

    spread_store = pltpu.make_async_copy(spread_m, spread_h, out_s.at[1])
    spread_store.start()
    for copy in inner_copies(3):
        copy.wait_recv()
    forward_copy.start()

    for store in stores:
        store.wait()
    outer_copy.wait()
    forward_copy.wait()
    for mask in range(1, rep_size):
        for copy in inner_copies(mask):
            if mask == 3:
                copy.wait_send()
            else:
                copy.wait()
    for kind in range(2):
        side_copy(kind, group).wait_send()

        @pl.loop(0, groups)
        def _(source):
            @pl.when(source != group)
            def _():
                side_copy(kind, source).wait_send()

            @pl.when((source <= group) & (group + 1 < groups))
            def _():
                line_copy(kind, source, 1).wait_send()

            @pl.when((source >= group) & (group >= 1))
            def _():
                line_copy(kind, source, -1).wait_send()

        @pl.loop(0, exp_size)
        def _(at):
            @pl.when(at != exp_at)
            def _():
                core_copy(kind, at).wait_send()

    spread_store.wait()
    cent_own.wait()
    gain_own.wait()
    for mask in range(1, rep_size):
        gain_copy(mask).wait()
    for mask, flip in cent_pairs:
        cent_copy(mask, flip).wait()

    def disp_wait(source):
        return remote(
            packed_x.at[slot_rows(source // 2)],
            arrived.at[slot_rows(source)],
            disp_s.at[source],
            disp_r.at[source],
            (rep_at, source),
        )

    @pl.loop(0, groups)
    def _(at):
        @pl.when(2 * at != exp_at)
        def _():
            disp_wait(2 * at).wait_send()

    @pl.when(side == 0)
    def _():
        pltpu.make_async_copy(
            packed_x.at[slot_rows(group)], arrived.at[slot_rows(exp_at)], disp_s.at[exp_at]
        ).wait()

        @pl.loop(1, exp_size)
        def _(at):
            disp_wait(exp_at ^ at).wait_recv()


def run_attend(exp_size, rep_size, slots, tokens, cotangent, doc, expert_of, attn, gain_a, w_inner, w_outer, gain_e, cent):
    rows_n, width = tokens.shape
    low = jnp.bfloat16
    wide = jnp.float32
    groups = exp_size // 2
    depth = w_inner.shape[0]
    ff_block = w_outer.shape[0]
    anyplace = pl.BlockSpec(memory_space=pl.ANY)
    inside = pl.BlockSpec(memory_space=pltpu.VMEM)
    dma = pltpu.SemaphoreType.DMA
    shape = jax.ShapeDtypeStruct
    return pl.pallas_call(
        functools.partial(attend_kernel, exp_size, rep_size, slots),
        out_shape=(
            shape((4, width, width), low),
            shape((width, 2 * ff_block), low),
            shape((ff_block - DEFER, width), low),
            shape((exp_size * slots, width), low),
            shape((exp_size * slots, 2 * rows_n), low),
            shape((2 * rep_size * 8, cent.shape[1]), wide),
            shape((rep_size * 8, depth), wide),
            shape((groups * slots, width), low),
            shape((rows_n, width), wide),
            shape((3, rows_n, width), low),
            shape((HEADS * rows_n, rows_n), low),
            shape((rows_n, width), low),
            shape((rows_n, width), low),
            shape((groups * slots, rows_n), low),
            shape((1, width), wide),
        ),
        in_specs=[inside, inside, pl.BlockSpec(memory_space=pltpu.SMEM), inside]
        + [anyplace] * 4
        + [inside, anyplace, anyplace, inside, inside],
        out_specs=(anyplace,) * 13 + (inside,) * 2,
        scratch_shapes=[
            pltpu.VMEM((rows_n, width), wide),
            pltpu.VMEM((3, rows_n, width), low),
            pltpu.VMEM((HEADS * rows_n, rows_n), low),
            pltpu.VMEM((rows_n, width), low),
            pltpu.VMEM((rows_n, width), low),
            pltpu.VMEM((4, width, width), low),
            pltpu.VMEM((depth, 2 * ff_block), low),
            pltpu.VMEM((exp_size * slots, 2 * rows_n), low),
            pltpu.VMEM((2, exp_size * 16, 128), wide),
            pltpu.VMEM((exp_size * 16, 128), wide),
            pltpu.VMEM((8, depth), wide),
            pltpu.VMEM((groups * slots, width), low),
            pltpu.VMEM((groups * slots, width), low),
            pltpu.VMEM((rows_n, rows_n), wide),
            pltpu.VMEM((16, 128), wide),
            pltpu.VMEM((8, cent.shape[1]), wide),
            dma((6,)),
            dma((2, 2, groups)),
            dma((2, groups)),
            dma((2, groups)),
            dma((2, groups)),
            dma((2, exp_size)),
            dma((2, exp_size)),
            dma((2 + 2 * rep_size,)),
            dma((2 + 2 * rep_size,)),
            dma((exp_size,)),
            dma((exp_size,)),
            dma((exp_size,)),
            dma((exp_size,)),
            dma((2 * rep_size,)),
            dma((2 * rep_size,)),
            dma((rep_size,)),
            dma((rep_size,)),
            dma((8,)),
        ],
        compiler_params=pltpu.CompilerParams(
            collective_id=1, has_side_effects=True, vmem_limit_bytes=56 << 20
        ),
        cost_estimate=pl.CostEstimate(
            flops=10 * rows_n * width * width,
            bytes_accessed=40 << 20,
            transcendentals=HEADS * rows_n * rows_n,
        ),
        name="attend",
    )(tokens, cotangent, doc, expert_of, *attn, gain_a, w_inner, w_outer, gain_e, cent)


def expert_kernel(
    exp_size,
    rep_size,
    slots,
    arrived_h,
    packed_h,
    inner_h,
    outer_h,
    w_inner,
    w_outer,
    spread_h,
    cents,
    gains_e,
    home,
    branch,
    branch_got,
    outer_keep,
    outer_send,
    outer_got,
    inner_sum,
    centre_parts,
    arrived,
    spread_m,
    cent_b,
    gain,
    centre_grad,
    centre_v,
    inner_w,
    outer_w,
    own_x,
    own_cot,
    normed,
    active,
    slope,
    states,
    part_send,
    part_recv,
    hop,
    back,
    spread,
    relay,
    acc,
    gates,
    gate_grads,
    outer_keep_v,
    outer_send_v,
    inner_send_v,
    load_sem,
    disp_s,
    disp_r,
    bran_s,
    bran_r,
    centre_s,
    centre_r,
    norm_s,
    norm_r,
    state_s,
    state_r,
    part_s,
    part_r,
    grad_s,
    grad_r,
    hop_s,
    hop_r,
    gate_s,
    gate_r,
    ret_s,
    ret_r,
    relay_s,
    relay_r,
    early_s,
    early_r,
    out_sem,
    inner_s,
    out_r,
):
    low = jnp.bfloat16
    wide = jnp.float32
    rep_at = lax.axis_index("rep")
    exp_at = lax.axis_index("exp")
    first = exp_at % 2 == 0
    second = exp_at % 2 == 1
    core_peer = (rep_at ^ 1, exp_at)
    side_peer = (rep_at, exp_at ^ 1)
    width = own_x.shape[1]
    own_rows = own_x.shape[0]
    part = own_rows // CHUNKS
    wide_ff = inner_w.shape[1]
    block = wide_ff // 2
    depth = width // rep_size

    def slot_rows(at):
        return pl.ds(pl.multiple_of(at * slots, slots), slots)

    def inner_rows(mask):
        return pl.ds(pl.multiple_of((rep_at ^ mask) * depth, depth), depth)

    rows_load = pltpu.make_async_copy(arrived_h, arrived, load_sem.at[0])
    spread_load = pltpu.make_async_copy(spread_h, spread_m, load_sem.at[8])
    spread_load.start()

    @pl.when(first)
    def _():
        rows_load.start()

    loads = [
        pltpu.make_async_copy(w_outer, outer_w.at[:block], load_sem.at[1]),
        pltpu.make_async_copy(outer_h, outer_w.at[block : 2 * block - DEFER], load_sem.at[2]),
    ]
    for side in range(2):
        at = rep_at ^ (2 * side)
        loads.append(
            pltpu.make_async_copy(
                w_inner.at[:, pl.ds(pl.multiple_of(at * block, block), block)],
                inner_w.at[inner_rows(0), side * block : (side + 1) * block],
                load_sem.at[3 + side],
            )
        )
    for mask in range(1, rep_size):
        loads.append(
            pltpu.make_async_copy(
                inner_h.at[inner_rows(mask)], inner_w.at[inner_rows(mask)], load_sem.at[4 + mask]
            )
        )
    for load in loads:
        load.start()

    barrier = pltpu.get_barrier_semaphore()
    for mask in range(1, rep_size):
        for flip in range(2):
            pl.semaphore_signal(
                barrier, inc=1, device_id=(rep_at ^ mask, exp_at ^ flip), device_id_type=MESH
            )

    @pl.loop(1, exp_size)
    def _(at):
        pl.semaphore_signal(barrier, inc=1, device_id=(rep_at, exp_at ^ at), device_id_type=MESH)

    group = exp_at // 2
    pl.semaphore_wait(barrier, exp_size - 1 + 2 * (rep_size - 1))
    row_peer = (rep_at ^ 2, exp_at)
    late_copy = remote(
        w_outer.at[block - DEFER :],
        outer_w.at[2 * block - DEFER :],
        early_s.at[0],
        early_r.at[0],
        row_peer,
    )
    late_copy.start()

    def disp_copy(which):
        return remote(
            packed_h.at[slot_rows(which)],
            arrived.at[slot_rows(exp_at)],
            disp_s.at[which],
            disp_r.at[exp_at],
            (rep_at, 2 * which + 1),
        )

    disp_own = pltpu.make_async_copy(
        packed_h.at[slot_rows(group)], arrived.at[slot_rows(exp_at)], disp_s.at[group]
    )

    @pl.loop(0, exp_size // 2)
    def _(step):
        which = group ^ (exp_size // 2 - 1 - step)

        @pl.when(2 * which + 1 != exp_at)
        def _():
            disp_copy(which).start()

        @pl.when(2 * which + 1 == exp_at)
        def _():
            disp_own.start()

    piece = cents.shape[1]
    for at in range(width // piece):
        cent_b[:, at * piece : (at + 1) * piece] = jnp.broadcast_to(
            cents[at * 8 : at * 8 + 1, :], (cent_b.shape[0], piece)
        ).astype(low)
    for at in range(rep_size):
        gain[:, at * depth : (at + 1) * depth] = gains_e[at * 8 : at * 8 + 1, :]
    def compact_rows():
        return lax.dot_general(
            spread_m[...], arrived[...], (((0,), (0,)), ((), ())), preferred_element_type=wide
        ).astype(low)

    spread_load.wait()

    @pl.when(first)
    def _():
        rows_load.wait()
        own_x[...] = compact_rows()


    gate_copy = remote(gates, gates, gate_s.at[0], gate_r.at[0], side_peer)

    def part_rows(at):
        return pl.ds(pl.multiple_of(at * part, part), part)

    def both_rows(at):
        return pl.ds(pl.multiple_of(at * 2 * part, 2 * part), 2 * part)

    def own_slice(at):
        return pl.ds(pl.multiple_of(at * 2 * part + part, part), part)

    def other_slice(at):
        return pl.ds(pl.multiple_of(at * 2 * part, part), part)

    def grad_copy(at):
        rows = part_rows(at)
        return remote(
            gate_grads.at[rows], gate_grads.at[rows], grad_s.at[at], grad_r.at[at], side_peer
        )

    def hop_forward(at):
        rows = part_rows(at)
        return remote(hop.at[rows], own_x.at[rows], hop_s.at[at], hop_r.at[at], side_peer)

    def hop_backward(at):
        return remote(
            hop.at[part_rows(at)], states.at[own_slice(at)], hop_s.at[at], hop_r.at[at], side_peer
        )

    def norm_copy(at):
        return remote(
            normed.at[own_slice(at)], normed.at[other_slice(at)], norm_s.at[at], norm_r.at[at], core_peer
        )

    def state_copy(at):
        return remote(
            states.at[own_slice(at)], states.at[other_slice(at)], state_s.at[at], state_r.at[at], core_peer
        )

    def part_copy(kind, at):
        count = kind * CHUNKS + at
        rows = part_rows(count)
        return remote(
            part_send.at[rows], part_recv.at[rows], part_s.at[count], part_r.at[count], core_peer
        )

    def norm_rows(at):
        @pl.loop(0, part // ROWS)
        def _(step):
            off = pl.multiple_of(step * ROWS, ROWS)
            unit, _ = row_stats(own_x[pl.ds(at * part + off, ROWS), :].astype(wide))
            normed[pl.ds(at * 2 * part + part + off, ROWS), :] = (unit * gain[...]).astype(low)

        norm_copy(at).start()

    steps = 2 * CHUNKS

    def is_forward(step):
        early = step < CHUNKS
        mixed = (step == 0) | ((step % 2 == 1) & (step < steps - 1))
        return (first & early) | (second & mixed)

    def chunk_at(step):
        of_first = jnp.where(step < CHUNKS, step, step - CHUNKS)
        mixed = (step == 0) | ((step % 2 == 1) & (step < steps - 1))
        of_second = jnp.where(
            mixed,
            (step + 1) // 2,
            jnp.where(step == steps - 1, CHUNKS - 1, (step - 2) // 2),
        )
        return jnp.where(first, of_first, of_second)

    @pl.when(first)
    def _():
        @pl.loop(0, CHUNKS)
        def _(at):
            norm_rows(at)

        logit = lax.dot_general(
            own_x[...], cent_b[...], (((1,), (1,)), ((), ())), preferred_element_type=wide
        )
        gates[...] = jax.nn.sigmoid(logit)
        gate_copy.start()

    @pl.when(second)
    def _():
        hop_forward(0).wait_recv()
        norm_rows(0)

    def take_cotangent():
        disp_own.wait()

        @pl.loop(1, exp_size)
        def _(at):
            source = exp_at ^ at
            remote(
                packed_h.at[slot_rows(0)],
                arrived.at[slot_rows(source)],
                disp_s.at[0],
                disp_r.at[source],
                side_peer,
            ).wait_recv()

        own_cot[...] = compact_rows()
        gate_copy.wait_recv()

        @pl.loop(0, CHUNKS)
        def _(at):
            @pl.loop(0, part // ROWS)
            def _(step):
                off = pl.multiple_of(step * ROWS, ROWS)
                here = pl.ds(at * part + off, ROWS)
                states[pl.ds(at * 2 * part + part + off, ROWS), :] = (
                    gates[here, :][:, :1] * own_cot[here, :].astype(wide)
                ).astype(low)

            state_copy(at).start()

    for load in loads:
        load.wait()
    centre_grad[...] = jnp.zeros_like(centre_grad)

    def finish_forward(step, at):
        part_copy(0, at).wait_recv()

        @pl.loop(0, part // ROWS)
        def _(tile):
            off = pl.multiple_of(tile * ROWS, ROWS)
            here = pl.ds(at * part + off, ROWS)
            result = (
                own_x[here, :].astype(wide)
                + acc[step % 2, pl.ds(off, ROWS), :]
                + part_recv[here, :].astype(wide)
            )

            @pl.when(first)
            def _():
                hop[here, :] = result.astype(low)

            @pl.when(second)
            def _():
                cot = own_cot[here, :].astype(wide)
                back[here, :] = (gates[here, :][:, :1] * result).astype(low)
                gate_grads[here, :] = jnp.broadcast_to(
                    jnp.sum(cot * result, axis=1, keepdims=True), (ROWS, gate_grads.shape[1])
                )

        @pl.when(first)
        def _():
            hop_forward(at).start()

        @pl.when(second)
        def _():
            grad_copy(at).start()

    def finish_backward(step, at):
        part_copy(1, at).wait_recv()

        @pl.when(first)
        def _():
            grad_copy(at).wait_recv()

        @pl.loop(0, part // ROWS)
        def _(tile):
            off = pl.multiple_of(tile * ROWS, ROWS)
            here = pl.ds(at * part + off, ROWS)
            rows_in = own_x[here, :].astype(wide)
            unit, inv_scale = row_stats(rows_in)
            grad_unit = (
                acc[step % 2, pl.ds(off, ROWS), :]
                + part_recv[pl.ds((CHUNKS + at) * part + off, ROWS), :].astype(wide)
            ) * gain[...]
            grad_in = (
                grad_unit
                - jnp.mean(grad_unit, axis=-1, keepdims=True)
                - unit * jnp.mean(grad_unit * unit, axis=-1, keepdims=True)
            ) * inv_scale
            gate = gates[here, :][:, :1]

            @pl.when(second)
            def _():
                state = gate * own_cot[here, :].astype(wide) + grad_in
                hop[here, :] = state.astype(low)

            @pl.when(first)
            def _():
                state = states[pl.ds(at * 2 * part + part + off, ROWS), :].astype(wide) + grad_in
                grad_logit = gate_grads[here, :][:, :1] * gate * (1.0 - gate)
                back[here, :] = (state + grad_logit * cent_b[:1, :].astype(wide)).astype(low)
                centre_grad[...] += jnp.sum(grad_logit * rows_in, axis=0, keepdims=True)

        @pl.when(second)
        def _():
            hop_backward(at).start()

    def finish(step):
        at = chunk_at(step)
        forward = is_forward(step)

        @pl.when(forward)
        def _():
            finish_forward(step, at)

        @pl.when(jnp.logical_not(forward))
        def _():
            finish_backward(step, at)

    @pl.loop(0, steps)
    def _(step):
        at = chunk_at(step)
        forward = is_forward(step)
        rows = both_rows(at)

        @pl.when(forward)
        def _():
            norm_copy(at).wait_recv()

            @pl.loop(0, wide_ff // BIG)
            def _(tile):
                cols = pl.ds(pl.multiple_of(tile * BIG, BIG), BIG)
                inner = jnp.dot(normed[rows, :], inner_w[:, cols], preferred_element_type=wide)
                normal = 0.5 * (1.0 + lax.erf(inner * ROOT_HALF))
                active[rows, cols] = (inner * normal).astype(low)
                slope[rows, cols] = (
                    normal + inner * jnp.exp(-0.5 * inner * inner) * INV_ROOT_TAU
                ).astype(low)

        @pl.when(jnp.logical_not(forward))
        def _():
            state_copy(at).wait_recv()

            @pl.loop(0, wide_ff // BIG)
            def _(tile):
                cols = pl.ds(pl.multiple_of(tile * BIG, BIG), BIG)
                grad_active = lax.dot_general(
                    states[rows, :],
                    outer_w[cols, :],
                    (((1,), (1,)), ((), ())),
                    preferred_element_type=wide,
                )
                slope[rows, cols] = (grad_active * slope[rows, cols].astype(wide)).astype(low)

        @pl.when((step > 0) & jnp.logical_not(first & (step == CHUNKS)))
        def _():
            finish(step - 1)

        @pl.when(step == 0)
        def _():
            late_copy.wait_recv()

        @pl.when(forward)
        def _():
            both = jnp.dot(active[rows, :], outer_w[...], preferred_element_type=wide)
            part_send[part_rows(at), :] = both[:part].astype(low)
            acc[step % 2] = both[part:]
            part_copy(0, at).start()

        @pl.when(jnp.logical_not(forward))
        def _():
            both = lax.dot_general(
                slope[rows, :],
                inner_w[...],
                (((1,), (1,)), ((), ())),
                preferred_element_type=wide,
            )
            part_send[part_rows(CHUNKS + at), :] = both[:part].astype(low)
            acc[step % 2] = both[part:]
            part_copy(1, at).start()

        @pl.when(first & (step == CHUNKS - 1))
        def _():
            finish(step)

        @pl.when(second & (step == 0))
        def _():
            take_cotangent()

        after = step + 1
        after_at = chunk_at(after)

        @pl.when(first & (after >= CHUNKS) & (after < steps))
        def _():
            hop_backward(after_at).wait_recv()
            state_copy(after_at).start()

        @pl.when(second & is_forward(after) & (after < steps))
        def _():
            hop_forward(after_at).wait_recv()
            norm_rows(after_at)

    finish(steps - 1)

    groups = exp_size // 2

    def ret_copy(source, dest):
        return remote(
            source,
            home.at[slot_rows(group)],
            ret_s.at[dest],
            ret_r.at[group],
            (rep_at, dest),
        )

    def relay_copy(which):
        return remote(
            spread.at[slot_rows(2 * which + 1)],
            relay.at[slot_rows(which)],
            relay_s.at[which],
            relay_r.at[which],
            side_peer,
        )

    ret_own = pltpu.make_async_copy(
        spread.at[slot_rows(exp_at)], home.at[slot_rows(group)], ret_s.at[exp_at]
    )

    def make_spread():
        @pl.loop(0, width // TILE)
        def _(step):
            cols = pl.ds(pl.multiple_of(step * TILE, TILE), TILE)
            spread[:, cols] = jnp.dot(
                spread_m[...], back[:, cols], preferred_element_type=wide
            ).astype(low)

    def send_step(step):
        which = group ^ (groups - step)
        relay_copy(which).start()
        ret_copy(spread.at[slot_rows(2 * which)], 2 * which).start()

    def send_end():
        ret_copy(spread.at[slot_rows(exp_at + 1)], exp_at + 1).start()
        ret_own.start()

    def eight_rows(at):
        return pl.ds(pl.multiple_of(at * 8, 8), 8)

    def centre_copy(mask, flip):
        dest = rep_at ^ mask
        return remote(
            centre_v.at[eight_rows(flip * rep_size + dest)],
            centre_parts.at[eight_rows(rep_at)],
            centre_s.at[flip * rep_size + mask],
            centre_r.at[mask],
            (dest, exp_at ^ flip),
        )

    centre_own = pltpu.make_async_copy(
        centre_v.at[eight_rows(rep_at)], centre_parts.at[eight_rows(rep_at)], centre_s.at[0]
    )
    centre_pairs = [(m, f) for m in range(rep_size) for f in range(2) if m or f]

    make_spread()

    def bran_copy(which):
        return remote(
            spread.at[slot_rows(2 * which + 1)],
            branch_got.at[slot_rows(group)],
            bran_s.at[which],
            bran_r.at[group],
            (rep_at, 2 * which + 1),
        )

    bran_own = pltpu.make_async_copy(
        spread.at[slot_rows(exp_at)], branch_got.at[slot_rows(group)], bran_s.at[group]
    )

    @pl.when(second)
    def _():
        bran_own.start()

        @pl.loop(1, groups)
        def _(step):
            bran_copy(group ^ (groups - step)).start()

    spans = 4

    def send_span(span):
        @pl.when(first)
        def _():
            @pl.loop(1 + -(-span * (groups - 1) // spans), 1 + -(-(span + 1) * (groups - 1) // spans))
            def _(step):
                send_step(step)

    @pl.when(first)
    def _():
        for at in range(width // piece):
            centre_v[at * 8 : (at + 1) * 8, :] = jnp.broadcast_to(
                centre_grad[:, at * piece : (at + 1) * piece], (8, piece)
            )
        centre_own.start()
        for mask, flip in centre_pairs:
            centre_copy(mask, flip).start()

    outs = []
    tiles = block // TILE
    early_copy = remote(
        outer_send_v.at[:EARLY], outer_got, early_s.at[1], early_r.at[1], row_peer
    )
    for place, at in enumerate(list(range(tiles, 2 * tiles)) + list(range(tiles))):
        if place % 2 == 0 and place // 2 < spans:
            send_span(place // 2)
        rows = slice(at * TILE, (at + 1) * TILE)
        grad = lax.dot_general(
            active[:, rows], states[...], (((0,), (0,)), ((), ())), preferred_element_type=wide
        )
        if at < tiles:
            outer_keep_v[rows, :] = grad.astype(low)
            outs.append((outer_keep_v.at[rows], outer_keep.at[rows]))
        else:
            top = at * TILE - block
            outer_send_v[top : top + TILE, :] = grad.astype(low)
            if top + TILE == EARLY:
                early_copy.start()
            if top < EARLY:
                continue
            outs.append(
                (outer_send_v.at[top : top + TILE], outer_send.at[top - EARLY : top - EARLY + TILE])
            )
        pltpu.make_async_copy(outs[-1][0], outs[-1][1], out_sem.at[len(outs) - 1]).start()
    outs.append((spread, branch))
    pltpu.make_async_copy(spread, branch, out_sem.at[len(outs) - 1]).start()

    def inner_copy(mask, side):
        at = rep_at ^ (2 * side)
        cols = pl.ds(pl.multiple_of(at * block, block), block)
        target = inner_sum.at[mask // 2, :, cols]
        source = inner_send_v.at[mask, side]
        count = 2 * mask + side
        if mask % 2 == 0:
            return pltpu.make_async_copy(source, target, inner_s.at[count])
        return remote(source, target, inner_s.at[count], out_r.at[count], core_peer)

    inner_order = [(m, f) for m in (3, 1, 2, 0) for f in range(2)]
    @pl.when(first)
    def _():
        send_end()

    for mask, side in inner_order:
        cols = slice(side * block, (side + 1) * block)
        grad = lax.dot_general(
            normed[:, inner_rows(mask)],
            slope[:, cols],
            (((0,), (0,)), ((), ())),
            preferred_element_type=wide,
        )
        inner_send_v[mask, side] = grad.astype(low)
        inner_copy(mask, side).start()

    @pl.when(second)
    def _():
        @pl.loop(1, groups)
        def _(step):
            which = group ^ (groups - step)
            relay_copy(which).wait_recv()
            ret_copy(relay.at[slot_rows(which)], 2 * which + 1).start()

    late_copy.wait_send()
    early_copy.wait()
    for at, (source, target) in enumerate(outs):
        pltpu.make_async_copy(source, target, out_sem.at[at]).wait()
    for mask, side in inner_order:
        inner_copy(mask, side).wait()
    for at in range(CHUNKS):
        norm_copy(at).wait_send()
        state_copy(at).wait_send()
        part_copy(0, at).wait_send()
        part_copy(1, at).wait_send()

        @pl.when(first)
        def _():
            hop_forward(at).wait_send()

        @pl.when(second)
        def _():
            hop_backward(at).wait_send()
            grad_copy(at).wait_send()

    @pl.loop(0, groups)
    def _(which):
        @pl.when(2 * which + 1 != exp_at)
        def _():
            disp_copy(which).wait_send()

    @pl.when(second)
    def _():
        bran_own.wait()

        @pl.loop(1, groups)
        def _(step):
            which = group ^ step
            bran_copy(which).wait_send()
            remote(
                spread.at[slot_rows(which)],
                branch_got.at[slot_rows(which)],
                bran_s.at[which],
                bran_r.at[which],
                side_peer,
            ).wait_recv()

    @pl.when(first)
    def _():
        gate_copy.wait_send()

    @pl.when(first)
    def _():
        centre_own.wait()
        for mask, flip in centre_pairs:
            centre_copy(mask, flip).wait_send()
        for mask in range(1, rep_size):
            centre_copy(mask, 0).wait_recv()

    @pl.when(second)
    def _():
        for mask in range(rep_size):
            centre_copy(mask, 1).wait_recv()

    @pl.when(first)
    def _():
        ret_own.wait()
        ret_copy(spread.at[slot_rows(exp_at + 1)], exp_at + 1).wait_send()

        @pl.loop(1, groups)
        def _(step):
            which = group ^ step
            relay_copy(which).wait_send()
            ret_copy(spread.at[slot_rows(2 * which)], 2 * which).wait_send()

    @pl.when(second)
    def _():
        @pl.loop(1, groups)
        def _(step):
            which = group ^ step
            ret_copy(relay.at[slot_rows(which)], 2 * which + 1).wait_send()

        remote(
            relay.at[slot_rows(group)],
            home.at[slot_rows(group)],
            relay_s.at[group],
            ret_r.at[group],
            side_peer,
        ).wait_recv()

    @pl.loop(1, groups)
    def _(step):
        source = group ^ step
        remote(
            relay.at[slot_rows(source)],
            home.at[slot_rows(source)],
            relay_s.at[source],
            ret_r.at[source],
            side_peer,
        ).wait_recv()


def run_experts(
    exp_size, rep_size, slots, own_rows, arrived, packed, inner_w, outer_w, w_inner, w_outer, spread, cents, gains_e
):
    width = arrived.shape[1]
    depth = width // rep_size
    block = w_outer.shape[0]
    low = jnp.bfloat16
    wide = jnp.float32
    total = exp_size * slots
    all_rows = 2 * own_rows
    part = own_rows // CHUNKS
    piece = cents.shape[1]
    anyplace = pl.BlockSpec(memory_space=pl.ANY)
    inside = pl.BlockSpec(memory_space=pltpu.VMEM)
    dma = pltpu.SemaphoreType.DMA
    n_out = (2 * block - EARLY) // TILE + 1
    scratch = [
        pltpu.VMEM((total, width), low),
        pltpu.VMEM((total, own_rows), low),
        pltpu.VMEM((128, width), low),
        pltpu.VMEM((1, width), wide),
        pltpu.VMEM((1, width), wide),
        pltpu.VMEM((2 * rep_size * 8, piece), wide),
        pltpu.VMEM((width, 2 * block), low),
        pltpu.VMEM((2 * block, width), low),
        pltpu.VMEM((own_rows, width), low),
        pltpu.VMEM((own_rows, width), low),
        pltpu.VMEM((all_rows, width), low),
        pltpu.VMEM((all_rows, 2 * block), low),
        pltpu.VMEM((all_rows, 2 * block), low),
        pltpu.VMEM((all_rows, width), low),
        pltpu.VMEM((2 * own_rows, width), low),
        pltpu.VMEM((2 * own_rows, width), low),
        pltpu.VMEM((own_rows, width), low),
        pltpu.VMEM((own_rows, width), low),
        pltpu.VMEM((total, width), low),
        pltpu.VMEM((total // 2, width), low),
        pltpu.VMEM((2, part, width), wide),
        pltpu.VMEM((own_rows, 128), wide),
        pltpu.VMEM((own_rows, 128), wide),
        pltpu.VMEM((block, width), low),
        pltpu.VMEM((block, width), low),
        pltpu.VMEM((rep_size, 2, depth, block), low),
        dma((9,)),
        dma((exp_size // 2,)),
        dma((exp_size,)),
        dma((exp_size // 2,)),
        dma((exp_size // 2,)),
        dma((2 * rep_size,)),
        dma((rep_size,)),
    ]
    scratch += [dma((CHUNKS,)) for _ in range(4)]
    scratch += [dma((2 * CHUNKS,)), dma((2 * CHUNKS,))]
    scratch += [dma((CHUNKS,)) for _ in range(4)]
    scratch += [dma((1,)), dma((1,)), dma((exp_size,)), dma((exp_size // 2,))]
    scratch += [dma((exp_size // 2,)), dma((exp_size // 2,)), dma((2,)), dma((2,)), dma((n_out,))]
    scratch += [dma((2 * rep_size,)), dma((2 * rep_size,))]
    flops = 2 * all_rows * width * 2 * block * 6
    return pl.pallas_call(
        functools.partial(expert_kernel, exp_size, rep_size, slots),
        out_shape=(
            jax.ShapeDtypeStruct((total // 2, width), low),
            jax.ShapeDtypeStruct((total, width), low),
            jax.ShapeDtypeStruct((total // 2, width), low),
            jax.ShapeDtypeStruct((block, width), low),
            jax.ShapeDtypeStruct((block - EARLY, width), low),
            jax.ShapeDtypeStruct((EARLY, width), low),
            jax.ShapeDtypeStruct((2, depth, rep_size * block), low),
            jax.ShapeDtypeStruct((rep_size * 8, piece), wide),
        ),
        in_specs=[anyplace] * 7 + [inside] * 2,
        out_specs=(anyplace,) * 8,
        scratch_shapes=scratch,
        compiler_params=pltpu.CompilerParams(
            collective_id=0, has_side_effects=True, vmem_limit_bytes=62 << 20
        ),
        cost_estimate=pl.CostEstimate(
            flops=flops, bytes_accessed=40 << 20, transcendentals=2 * all_rows * 2 * block
        ),
        name="experts",
    )(arrived, packed, inner_w, outer_w, w_inner, w_outer, spread, cents, gains_e)


def finish_kernel(
    exp_size,
    rep_size,
    home,
    branch,
    branch_got,
    pick,
    hidden_h,
    cotangent,
    tokens_h,
    gain_row,
    qkv_h,
    probs_h,
    normed_h,
    context_h,
    attn_w,
    outer_send,
    outer_got,
    inner_sum,
    output,
    grad_tokens,
    shares,
    outer_recv,
    inner_recv,
    hidden,
    tokens,
    qkv,
    probs,
    normed_a,
    context,
    normed_t,
    context_t,
    branch_in,
    early_rows,
    weights,
    grad_hidden,
    grad_attn,
    grad_context,
    grads3,
    keep,
    core_out,
    core_in,
    side_out,
    side_in,
    line_out,
    line_in,
    total,
    row_out,
    row_in,
    half_out,
    half_in,
    load_s,
    branch_s,
    branch_r,
    expert_s,
    expert_r,
    core_s,
    core_r,
    side_s,
    side_r,
    line_s,
    line_r,
    row_s,
    row_r,
    half_s,
    half_r,
):
    low = jnp.bfloat16
    wide = jnp.float32
    rep_at = lax.axis_index("rep")
    exp_at = lax.axis_index("exp")
    core = rep_at % 2
    group = exp_at // 2
    side = exp_at % 2
    groups = exp_size // 2
    rows_n, width = cotangent.shape
    half = width // 2
    block = width // exp_size
    core_peer = (rep_at ^ 1, exp_at)
    side_peer = (rep_at, exp_at ^ 1)
    row_peer = (rep_at ^ 2, exp_at)

    loads = [
        pltpu.make_async_copy(source, target, load_s.at[at])
        for at, (source, target) in enumerate(
            (
                (context_h, context),
                (attn_w, weights),
                (qkv_h, qkv),
                (probs_h, probs),
                (normed_h, normed_a),
                (tokens_h, tokens),
                (hidden_h, hidden),
                (outer_got, early_rows),
            )
        )
    ]
    for load in loads:
        load.start()

    barrier = pltpu.get_barrier_semaphore()
    for mask in range(1, 3):
        pl.semaphore_signal(
            barrier, inc=1, device_id=(rep_at ^ mask, exp_at), device_id_type=MESH
        )

    @pl.loop(1, exp_size)
    def _(at):
        pl.semaphore_signal(barrier, inc=1, device_id=(rep_at, exp_at ^ at), device_id_type=MESH)

    pl.semaphore_wait(barrier, exp_size + 1)

    outer_copy = remote(
        outer_send, outer_recv.at[EARLY:], expert_s.at[0], expert_r.at[0], row_peer
    )
    early_store = pltpu.make_async_copy(early_rows, outer_recv.at[:EARLY], load_s.at[8])

    inner_copy = remote(inner_sum.at[1], inner_recv, expert_s.at[1], expert_r.at[1], row_peer)
    inner_copy.start()
    outer_copy.start()

    slots = pick.shape[0] // groups

    def slot_rows(at):
        return pl.ds(pl.multiple_of(at * slots, slots), slots)

    def branch_copy(dest):
        return remote(
            branch.at[slot_rows(dest)],
            branch_in.at[slot_rows(group)],
            branch_s.at[dest],
            branch_r.at[group],
            (rep_at, dest),
        )

    branch_own = pltpu.make_async_copy(branch_got, branch_in, branch_s.at[exp_at])

    @pl.when(side == 1)
    def _():
        branch_own.start()

        @pl.loop(0, groups)
        def _(at):
            branch_copy(2 * (group ^ (groups - 1 - at))).start()

    back_rows = lax.dot_general(
        pick[...], home[...], (((0,), (0,)), ((), ())), preferred_element_type=wide
    )
    grad_hidden[...] = cotangent[...].astype(wide) + back_rows
    grad_attn[...] = grad_hidden[...].astype(low)
    loads[0].wait()
    context_t[...] = context[...].T

    own_half = pl.ds(pl.multiple_of(core * half, half), half)
    other_half = pl.ds(pl.multiple_of((1 - core) * half, half), half)

    def core_copy(at):
        return remote(core_out.at[at], core_in.at[at], core_s.at[at], core_r.at[at], core_peer)

    def product(at, left, right, cols, target, kind):
        @pl.loop(0, width // 512)
        def _(step):
            rows = pl.ds(pl.multiple_of(step * 512, 512), 512)
            target[at, rows, :] = jnp.dot(
                left[rows, :], right[:, cols], preferred_element_type=wide
            ).astype(kind)

    def share_start(at, left, right):
        product(at, left, right, other_half, core_out, low)
        core_copy(at).start()
        product(at, left, right, own_half, keep, wide)

    def block_rows(at):
        return pl.ds(pl.multiple_of(at * block, block), block)

    def side_copy(at):
        return remote(side_out.at[at], side_in.at[at], side_s.at[at], side_r.at[at], side_peer)

    def share_side(at):
        core_copy(at).wait_recv()

        @pl.loop(0, groups)
        def _(which):
            rows = block_rows(2 * which + 1 - side)
            side_out[at, block_rows(which), :] = (
                keep[at, rows, :] + core_in[at, rows, :].astype(wide)
            ).astype(low)

        side_copy(at).start()

        @pl.loop(0, groups)
        def _(which):
            rows = block_rows(2 * which + side)
            keep[at, rows, :] = keep[at, rows, :] + core_in[at, rows, :].astype(wide)

    def line_copy(at, mask):
        dest = group ^ mask
        return remote(
            line_out.at[at, block_rows(dest)],
            line_in.at[at, block_rows(group)],
            line_s.at[at, mask],
            line_r.at[at, mask],
            (rep_at, 2 * dest + side),
        )

    def share_line(at):
        side_copy(at).wait_recv()

        @pl.loop(1, groups)
        def _(mask):
            dest = group ^ mask
            line_out[at, block_rows(dest), :] = (
                keep[at, block_rows(2 * dest + side), :] + side_in[at, block_rows(dest), :].astype(wide)
            ).astype(low)
            line_copy(at, mask).start()

        total[at] = keep[at, block_rows(exp_at), :] + side_in[at, block_rows(group), :].astype(wide)

    def row_copy(at):
        return remote(row_out.at[at], row_in.at[at], row_s.at[at], row_r.at[at], row_peer)

    def share_row(at):
        @pl.loop(1, groups)
        def _(mask):
            line_copy(at, mask).wait_recv()
            total[at] = total[at] + line_in[at, block_rows(group ^ mask), :].astype(wide)

        row_out[at] = total[at].astype(low)
        row_copy(at).start()

    def half_copy(at):
        return remote(half_out.at[at], half_in.at[at], half_s.at[at], half_r.at[at], core_peer)

    def share_half(at):
        row_copy(at).wait_recv()
        summed = row_out[at].astype(wide) + row_in[at].astype(wide)
        half_out[at] = summed
        half_copy(at).start()
        shares[at, :, own_half] = summed

    def share_end(at):
        half_copy(at).wait_recv()
        shares[at, :, other_half] = half_in[at]

    share_start(3, context_t, grad_attn)
    loads[1].wait()

    @pl.loop(0, width // TILE)
    def _(step):
        rows = pl.ds(pl.multiple_of(step * TILE, TILE), TILE)
        grad_context[:, rows] = lax.dot_general(
            grad_attn[...], weights[3, rows, :], (((1,), (1,)), ((), ())), preferred_element_type=wide
        ).astype(low)

    share_side(3)

    head_dim = width // HEADS
    pair = 2 * head_dim
    factor = head_dim ** (-0.5)
    lane = lax.broadcasted_iota(jnp.int32, (rows_n, pair), 1)

    def heads(which_half):
        @pl.loop(0, HEADS // 4)
        def _(step):
            at = which_half * (HEADS // 4) + step
            cols = pl.ds(pl.multiple_of(at * pair, pair), pair)
            q_pair = qkv[0, :, cols]
            k_pair = qkv[1, :, cols]
            v_pair = qkv[2, :, cols]
            c_pair = grad_context[:, cols]
            found = []
            for which in range(2):
                chosen = (lane >= head_dim) if which else (lane < head_dim)
                c_one = jnp.where(chosen, c_pair, jnp.zeros_like(c_pair))
                prob = probs[pl.ds(pl.multiple_of((2 * at + which) * rows_n, rows_n), rows_n), :]
                grad_prob = lax.dot_general(
                    c_one, v_pair, (((1,), (1,)), ((), ())), preferred_element_type=wide
                )
                weighted = prob.astype(wide) * grad_prob
                row_sum = jnp.sum(weighted, axis=1, keepdims=True)
                grad_score = (weighted - prob.astype(wide) * row_sum).astype(low)
                found.append(
                    (
                        jnp.dot(grad_score, k_pair, preferred_element_type=wide) * factor,
                        lax.dot_general(
                            grad_score,
                            q_pair,
                            (((0,), (0,)), ((), ())),
                            preferred_element_type=wide,
                        )
                        * factor,
                        lax.dot_general(
                            prob, c_pair, (((0,), (0,)), ((), ())), preferred_element_type=wide
                        ),
                    )
                )
            for which in range(3):
                grads3[which, :, cols] = jnp.where(
                    lane < head_dim, found[0][which], found[1][which]
                ).astype(low)

    loads[7].wait()
    early_store.start()
    loads[2].wait()
    loads[3].wait()
    heads(1 - core)
    loads[4].wait()
    normed_t[...] = normed_a[...].T
    for at in range(3):
        product(at, normed_t, grads3.at[at], other_half, core_out, low)
        core_copy(at).start()
    share_line(3)
    heads(core)
    for at in range(3):
        product(at, normed_t, grads3.at[at], own_half, keep, wide)
        share_side(at)
    loads[5].wait()
    @pl.loop(0, width // TILE)
    def _(step):
        rows = pl.ds(pl.multiple_of(step * TILE, TILE), TILE)
        grad_normed = jnp.zeros((rows_n, TILE), wide)
        for at in range(3):
            grad_normed = grad_normed + lax.dot_general(
                grads3[at], weights[at, rows, :], (((1,), (1,)), ((), ())), preferred_element_type=wide
            )
        grad_tokens[:, rows] = grad_normed

    @pl.loop(0, rows_n // ROWS)
    def _(step):
        here = pl.ds(pl.multiple_of(step * ROWS, ROWS), ROWS)
        unit, inv_scale = row_stats(tokens[here, :].astype(wide))
        grad_unit = grad_tokens[here, :] * gain_row[...]
        grad_in = (
            grad_unit
            - jnp.mean(grad_unit, axis=-1, keepdims=True)
            - unit * jnp.mean(grad_unit * unit, axis=-1, keepdims=True)
        ) * inv_scale
        grad_tokens[here, :] = grad_hidden[here, :] + grad_in

    share_row(3)
    for at in range(3):
        share_line(at)

    for at in range(3):
        share_row(at)
    def branch_wait(which):
        remote(
            branch.at[slot_rows(which)],
            branch_in.at[slot_rows(which)],
            branch_s.at[which],
            branch_r.at[which],
            side_peer,
        ).wait_recv()

    @pl.when(side == 0)
    def _():
        @pl.loop(0, groups)
        def _(at):
            branch_wait(at)

    @pl.when(side == 1)
    def _():
        branch_own.wait()

    loads[6].wait()
    rows = lax.dot_general(
        pick[...], branch_in[...], (((0,), (0,)), ((), ())), preferred_element_type=wide
    )
    output[...] = (hidden[...] + rows).astype(low)

    for at in (3, 0, 1, 2):
        share_half(at)
    for at in (3, 0, 1, 2):
        share_end(at)

    @pl.when(side == 1)
    def _():
        @pl.loop(0, groups)
        def _(at):
            branch_copy(2 * at).wait_send()

    for at in range(4):
        core_copy(at).wait_send()
        side_copy(at).wait_send()
        row_copy(at).wait_send()
        half_copy(at).wait_send()

        @pl.loop(1, groups)
        def _(mask):
            line_copy(at, mask).wait_send()

    inner_copy.wait()
    outer_copy.wait()
    early_store.wait()


def run_finish(exp_size, rep_size, home, branch, branch_got, pick, hidden, cotangent, tokens, gain_row, qkv, probs, normed_a, context, attn_w, outer_send, outer_got, inner_sum):
    rows_n, width = tokens.shape
    low = jnp.bfloat16
    wide = jnp.float32
    half = width // 2
    groups = exp_size // 2
    block = width // exp_size
    anyplace = pl.BlockSpec(memory_space=pl.ANY)
    inside = pl.BlockSpec(memory_space=pltpu.VMEM)
    dma = pltpu.SemaphoreType.DMA
    shape = jax.ShapeDtypeStruct
    return pl.pallas_call(
        functools.partial(finish_kernel, exp_size, rep_size),
        out_shape=(
            shape((rows_n, width), low),
            shape((rows_n, width), wide),
            shape((4, block, width), wide),
            shape((outer_send.shape[0] + EARLY, width), low),
            shape(inner_sum.shape[1:], low),
        ),
        in_specs=[inside, anyplace, anyplace, inside, anyplace, inside, anyplace, inside]
        + [anyplace] * 8,
        out_specs=(inside,) * 3 + (anyplace,) * 2,
        scratch_shapes=[
            pltpu.VMEM((rows_n, width), wide),
            pltpu.VMEM((rows_n, width), low),
            pltpu.VMEM(qkv.shape, low),
            pltpu.VMEM(probs.shape, low),
            pltpu.VMEM((rows_n, width), low),
            pltpu.VMEM((rows_n, width), low),
            pltpu.VMEM((width, rows_n), low),
            pltpu.VMEM((width, rows_n), low),
            pltpu.VMEM(pick.shape[:1] + (width,), low),
            pltpu.VMEM((EARLY, width), low),
            pltpu.VMEM((4, width, width), low),
            pltpu.VMEM((rows_n, width), wide),
            pltpu.VMEM((rows_n, width), low),
            pltpu.VMEM((rows_n, width), low),
            pltpu.VMEM((3, rows_n, width), low),
            pltpu.VMEM((4, width, half), wide),
            pltpu.VMEM((4, width, half), low),
            pltpu.VMEM((4, width, half), low),
            pltpu.VMEM((4, width // 2, half), low),
            pltpu.VMEM((4, width // 2, half), low),
            pltpu.VMEM((4, width // 2, half), low),
            pltpu.VMEM((4, width // 2, half), low),
            pltpu.VMEM((4, block, half), wide),
            pltpu.VMEM((4, block, half), low),
            pltpu.VMEM((4, block, half), low),
            pltpu.VMEM((4, block, half), wide),
            pltpu.VMEM((4, block, half), wide),
            dma((9,)),
            dma((exp_size,)),
            dma((groups,)),
            dma((2,)),
            dma((2,)),
            dma((4,)),
            dma((4,)),
            dma((4,)),
            dma((4,)),
            dma((4, groups)),
            dma((4, groups)),
            dma((4,)),
            dma((4,)),
            dma((4,)),
            dma((4,)),
        ],
        compiler_params=pltpu.CompilerParams(
            collective_id=2, has_side_effects=True, vmem_limit_bytes=60 << 20
        ),
        cost_estimate=pl.CostEstimate(
            flops=20 * rows_n * width * width, bytes_accessed=60 << 20, transcendentals=0
        ),
        name="finish",
    )(
        home,
        branch,
        branch_got,
        pick,
        hidden,
        cotangent,
        tokens,
        gain_row,
        qkv,
        probs,
        normed_a,
        context,
        attn_w,
        outer_send,
        outer_got,
        inner_sum,
    )


def shards(
    tokens,
    cotangent,
    doc_lengths,
    expert_of_token,
    w_query,
    w_key,
    w_value,
    w_output,
    attn_gain,
    w_inner,
    w_outer,
    expert_gain,
    centroids,
):
    exp_size = lax.axis_size("exp")
    rep_size = lax.axis_size("rep")
    row_count = tokens.shape[0]
    wide = jnp.float32

    slots = -(-3 * row_count // exp_size // 16) * 16
    (
        attn_w,
        inner_w,
        outer_w,
        arrived,
        spread,
        cents,
        gains_e,
        packed,
        hidden,
        qkv,
        probs,
        normed_a,
        context,
        pick,
        gain_row,
    ) = run_attend(
        exp_size,
        rep_size,
        slots,
        tokens,
        cotangent,
        doc_lengths,
        expert_of_token[None],
        (w_query, w_key, w_value, w_output),
        attn_gain[None],
        w_inner[0],
        w_outer[0],
        expert_gain,
        centroids,
    )
    home, branch, branch_got, outer_keep, outer_send, outer_got, inner_sum, centre_parts = run_experts(
        exp_size,
        rep_size,
        slots,
        2 * row_count,
        arrived,
        packed,
        inner_w,
        outer_w,
        w_inner[0],
        w_outer[0],
        spread,
        cents,
        gains_e,
    )
    output, grad_tokens, shares, outer_recv, inner_recv = run_finish(
        exp_size,
        rep_size,
        home,
        branch,
        branch_got,
        pick,
        hidden,
        cotangent,
        tokens,
        gain_row,
        qkv,
        probs,
        normed_a,
        context,
        attn_w,
        outer_send,
        outer_got,
        inner_sum,
    )
    grad_centroids = jnp.sum(centre_parts.reshape(rep_size, 8, -1)[:, 0], axis=0)[None]
    grad_w_outer = (outer_keep.astype(wide) + outer_recv.astype(wide))[None]
    summed = inner_sum[0].astype(wide) + inner_recv.astype(wide)
    grad_w_inner = summed[None]
    grad_expert_gain = jnp.sum(summed * w_inner[0].astype(wide), axis=1)[None] / expert_gain.astype(
        wide
    )
    share_gain = sum(
        jnp.sum(shares[i] * w.astype(wide), axis=1) for i, w in enumerate((w_query, w_key, w_value))
    ) / attn_gain.astype(wide)
    return (
        output,
        grad_tokens,
        shares[0],
        shares[1],
        shares[2],
        shares[3],
        share_gain,
        grad_w_inner,
        grad_w_outer,
        grad_expert_gain,
        grad_centroids,
    )


def solution(mesh):
    placed = (
        P(("rep", "exp"), None),
        P(("rep", "exp"), None),
        P(("rep", "exp"), None),
        P(("rep", "exp")),
        P("exp", None),
        P("exp", None),
        P("exp", None),
        P("exp", None),
        P("exp"),
        P("exp", "rep", None),
        P("exp", "rep", None),
        P("exp", "rep"),
        P("exp", "rep"),
    )
    return jax.shard_map(
        shards,
        mesh=mesh,
        in_specs=placed,
        out_specs=(
            P(("rep", "exp"), None),
            P(("rep", "exp"), None),
            P("exp", None),
            P("exp", None),
            P("exp", None),
            P("exp", None),
            P("exp"),
            P("exp", "rep", None),
            P("exp", "rep", None),
            P("exp", "rep"),
            P("exp", "rep"),
        ),
        check_vma=False,
    )
```
